512 devices in a mesh: tm: 16 (over x, z_hi, core), rep: 32 (over y, z_lo).
Axes of the slice: x: 4, y: 4, z: 16 (z_hi: 2, z_lo: 8; z = z_hi * 8 + z_lo), core: 2. Of those that a mesh axis runs over, the one named last changes fastest.
Arguments:
- samples: bfloat16 [32, 8192, 512], P('rep', 'tm'), may hold values from -5 to 5
- grad_out: bfloat16 [32, 8192, 512], P('rep', 'tm'), may hold values from -4 to 4
- w_conv: bfloat16 [1024, 1024], replicated, may hold values from -0.1875 to 0.1875
- w_res: bfloat16 [512, 512], replicated, may hold values from -0.25 to 0.25
- lengths: int32 [32], P('rep'), may hold values from 2048 to 8192
Outputs:
- grad_in: bfloat16 [32, 8192, 512], P('rep', 'tm')
- grad_conv: float32 [1024, 1024], P('tm', 'rep')
- grad_res: float32 [512, 512], P('tm', 'rep')
The draws below stay inside these ranges and needn't reach their ends.
All inputs are finite; a program needn't handle non-finite values.
Results may differ from the reference program's by a relative error of at most 0.015.
Values may be sent and summed in bfloat16 or wider, within the bound.
A program may use at most 64 MiB of HBM per device.

```python
import jax
import jax.numpy as jnp
from jax import lax

RESIDUAL_WIDTH = 512
TOK_DEV = 512
DILATION_STEP = 256
SEQUENCE_SAMPLES = 8192
SEQS = 32
TOKENS = 262144
N_TM = 16


def place_ends(result, key, smallest, top_value):
    longest = result.shape.index(max(result.shape))
    spots = []
    for shift in (0, 1):
        where = [jax.random.randint(jax.random.fold_in(key, axis), (), 0, length) for axis, length in enumerate(result.shape)]
        where[longest] = (where[longest] + shift) % result.shape[longest]
        spots.append(tuple(where))
    return result.at[spots[0]].set(smallest).at[spots[1]].set(top_value)


def raised(values, key, source, target, blocks, factor):
    def block_of(position):
        return (jnp.arange(values.shape[position]) // (values.shape[position] // blocks)).reshape((-1,) + (1,) * (values.ndim - 1 - position))

    one_side = jax.random.permutation(key, blocks)[block_of(target)]
    far = (block_of(target) + blocks // 2) % blocks
    return jnp.where((block_of(source) == one_side) | (block_of(source) == far), factor * values, values)


def block_scale(rng, dims, shards, smallest, top_value):
    gain = 1.0
    for dim, shards_of in shards:
        draws = jax.random.uniform(jax.random.fold_in(jax.random.fold_in(rng, 6), dim), (shards_of,), jnp.float32, smallest / len(shards), top_value / len(shards))
        gain = gain * jnp.repeat(jnp.exp(draws), dims[dim] // shards_of).reshape((-1,) + (1,) * (len(dims) - 1 - dim))
    return gain


def noise(stream_key, shape, scale, limit, pieces=(), held_as=jnp.bfloat16):
    entries = scale * jax.random.normal(stream_key, shape, jnp.float32)
    if pieces:
        entries = entries * block_scale(stream_key, shape, pieces, -0.22, 0.18)
    return jnp.clip(entries, -limit, limit).astype(held_as)


def bell_draw_with(own_key, extent, spread, limit, cuts, heavy, kind=jnp.bfloat16):
    drawn = spread * jax.random.normal(own_key, extent, jnp.float32)
    if cuts:
        drawn = drawn * block_scale(own_key, extent, cuts, -0.22, 0.18)
    return jnp.clip(raised(drawn, jax.random.fold_in(own_key, 3), *heavy), -limit, limit).astype(kind)


def setup_inputs(seed: int = 0) -> dict:
    streams_of = jax.random.split(jax.random.key(seed), 6)
    return {
        "samples": bell_draw_with(streams_of[0], (SEQS, SEQUENCE_SAMPLES, RESIDUAL_WIDTH), 0.6, 5.0, ((0, 32), (1, 16)), (1, 2, 16, 2.0)),
        "grad_out": noise(streams_of[1], (SEQS, SEQUENCE_SAMPLES, RESIDUAL_WIDTH), 0.5, 4.0, ((0, 32), (1, 16))),
        "w_conv": noise(streams_of[2], (2 * RESIDUAL_WIDTH, 2 * RESIDUAL_WIDTH), (2 * RESIDUAL_WIDTH) ** -0.5, 0.1875),
        "w_res": noise(streams_of[3], (RESIDUAL_WIDTH, RESIDUAL_WIDTH), RESIDUAL_WIDTH ** -0.5, 0.25),
        "lengths": place_ends(jax.random.randint(streams_of[4], (SEQS,), SEQUENCE_SAMPLES // 4, SEQUENCE_SAMPLES + 1), jax.random.fold_in(streams_of[4], 1), SEQUENCE_SAMPLES // 4, SEQUENCE_SAMPLES).astype(jnp.int32),
    }


def gate_backward(inputs, cotangent, in_length, w_conv, w_res):
    channel_count = w_res.shape[0]
    pre_act = jnp.dot(inputs, w_conv, preferred_element_type=jnp.float32)
    tanh_f = jnp.tanh(pre_act[:, :channel_count])
    sig_g = jax.nn.sigmoid(pre_act[:, channel_count:])
    gated = (in_length * tanh_f * sig_g).astype(jnp.bfloat16)
    gated_grad = in_length * jnp.dot(cotangent, w_res.T, preferred_element_type=jnp.float32)
    pre_grad = jnp.concatenate([gated_grad * sig_g * (1.0 - tanh_f * tanh_f),
                                gated_grad * tanh_f * sig_g * (1.0 - sig_g)], 1).astype(jnp.bfloat16)
    return gated, pre_grad


def block_terms(left, right):
    left_blocks = left.reshape(N_TM, TOK_DEV, left.shape[1]).astype(jnp.float32)
    right_blocks = right.reshape(N_TM, TOK_DEV, right.shape[1]).astype(jnp.float32)
    terms = jnp.einsum('btk,btn->bkn', left_blocks, right_blocks).astype(jnp.bfloat16)
    terms = lax.optimization_barrier(terms)
    return jnp.sum(terms.astype(jnp.float32), axis=0)


def reference(samples, grad_out, w_conv, w_res, lengths):
    def one_sequence(carry, item):
        sequence_rows, cotangent, seq_len = item
        prior_samples = jnp.concatenate([jnp.zeros((DILATION_STEP, RESIDUAL_WIDTH), jnp.bfloat16), sequence_rows[:SEQUENCE_SAMPLES - DILATION_STEP]], 0)
        inputs = jnp.concatenate([prior_samples, sequence_rows], 1)
        in_length = (jnp.arange(SEQUENCE_SAMPLES) < seq_len).astype(jnp.float32)[:, None]
        gated, pre_grad = gate_backward(inputs, cotangent, in_length, w_conv, w_res)
        input_gradient = jnp.dot(pre_grad, w_conv.T, preferred_element_type=jnp.float32)
        delayed_gradient = jnp.concatenate([input_gradient[DILATION_STEP:, :RESIDUAL_WIDTH], jnp.zeros((DILATION_STEP, RESIDUAL_WIDTH), jnp.float32)], 0)
        grad_rows = (cotangent.astype(jnp.float32) + input_gradient[:, RESIDUAL_WIDTH:] + delayed_gradient).astype(jnp.bfloat16)
        sum_conv = carry[0] + block_terms(inputs, pre_grad)
        sum_res = carry[1] + block_terms(gated, cotangent)
        return (sum_conv, sum_res), grad_rows

    start = (jnp.zeros((2 * RESIDUAL_WIDTH, 2 * RESIDUAL_WIDTH), jnp.float32), jnp.zeros((RESIDUAL_WIDTH, RESIDUAL_WIDTH), jnp.float32))
    (sum_conv, sum_res), grad_in = lax.scan(one_sequence, start, (samples, grad_out, lengths))
    grad_scale = float(TOKENS) ** -0.5
    return grad_in, sum_conv * grad_scale, sum_res * grad_scale
```

```python
import jax
import jax.numpy as jnp
from jax import lax
from jax.sharding import Mesh, PartitionSpec as P

DILATION_STEP = 256
TM = ("x", "zh", "c")
REP = ("y", "zl")


def passed_along(array, axis, by, length):
    pairs = [(i, i + by) for i in range(length) if 0 <= i + by < length]
    return lax.ppermute(array, axis, pairs)


def gate_backward(inputs, cotangent, in_length, w_conv, w_res):
    channel_count = w_res.shape[0]
    pre_act = jnp.dot(inputs, w_conv, preferred_element_type=jnp.float32)
    tanh_f = jnp.tanh(pre_act[:, :channel_count])
    sig_g = jax.nn.sigmoid(pre_act[:, channel_count:])
    gated = (in_length * tanh_f * sig_g).astype(jnp.bfloat16)
    gated_grad = in_length * jnp.dot(cotangent, w_res.T, preferred_element_type=jnp.float32)
    pre_grad = jnp.concatenate(
        [gated_grad * sig_g * (1.0 - tanh_f * tanh_f), gated_grad * tanh_f * sig_g * (1.0 - sig_g)],
        1,
    ).astype(jnp.bfloat16)
    return (gated, pre_grad)


def reduce_over(packed, axis, position, out_type):
    moved = lax.all_to_all(packed, axis, position, position, tiled=True)
    return jnp.sum(moved.astype(jnp.float32), axis=position).astype(out_type)


def make_body(sizes):
    nx, nzh, nc, ny, nzl = sizes
    n_tm = nx * nzh * nc
    n_rep = ny * nzl

    def body(samples, grad_out, w_conv, w_res, lengths):
        sequence_rows = samples[0]
        cotangent = grad_out[0]
        seq_len = lengths[0]
        count_of_rows = sequence_rows.shape[0]
        channel_count = sequence_rows.shape[1]
        start_row = lax.axis_index(TM) * count_of_rows
        trailing_rows = sequence_rows[count_of_rows - DILATION_STEP :]
        arrived = passed_along(trailing_rows, TM, 1, n_tm)
        prior_samples = jnp.concatenate(
            [arrived, sequence_rows[: count_of_rows - DILATION_STEP]], 0
        )
        inputs = jnp.concatenate([prior_samples, sequence_rows], 1)
        in_length = (start_row + jnp.arange(count_of_rows) < seq_len).astype(jnp.float32)[:, None]
        gated, pre_grad = gate_backward(inputs, cotangent, in_length, w_conv, w_res)
        input_gradient = jnp.dot(pre_grad, w_conv.T, preferred_element_type=jnp.float32)
        incoming_gradient = passed_along(input_gradient[:DILATION_STEP, :channel_count], TM, -1, n_tm)
        delayed_gradient = jnp.concatenate(
            [input_gradient[DILATION_STEP:, :channel_count], incoming_gradient], 0
        )
        grad_rows = (
            cotangent.astype(jnp.float32) + input_gradient[:, channel_count:] + delayed_gradient
        ).astype(jnp.bfloat16)
        term_conv = jnp.einsum("tk,tn->kn", inputs, pre_grad, preferred_element_type=jnp.float32)
        term_res = jnp.einsum("tk,tn->kn", gated, cotangent, preferred_element_type=jnp.float32)
        kc, nconv = term_conv.shape
        kr, nres = term_res.shape
        rc, cc = kc // n_tm, nconv // n_rep
        rr, cr = kr // n_tm, nres // n_rep
        conv_blocks = (
            term_conv.astype(jnp.bfloat16)
            .reshape(nx, nzh, nc, rc, ny, nzl, cc)
            .transpose(0, 1, 2, 4, 5, 3, 6)
            .reshape(nx, nzh, nc, ny, nzl, rc * cc)
        )
        res_blocks = (
            term_res.astype(jnp.bfloat16)
            .reshape(nx, nzh, nc, rr, ny, nzl, cr)
            .transpose(0, 1, 2, 4, 5, 3, 6)
            .reshape(nx, nzh, nc, ny, nzl, rr * cr)
        )
        packed = jnp.concatenate([conv_blocks, res_blocks], -1)
        packed = reduce_over(packed, "c", 2, jnp.bfloat16)
        packed = reduce_over(packed, "x", 0, jnp.bfloat16)
        packed = reduce_over(packed, "y", 1, jnp.float32)
        packed = packed.reshape(nzh * nzl, -1)
        total = reduce_over(packed, ("zh", "zl"), 0, jnp.float32)
        all_tokens = count_of_rows * n_tm * n_rep
        grad_scale = float(all_tokens) ** (-0.5)
        sum_conv = total[: rc * cc].reshape(rc, cc) * grad_scale
        sum_res = total[rc * cc :].reshape(rr, cr) * grad_scale
        return (grad_rows[None], sum_conv, sum_res)

    return body


def solution(mesh):
    n_tm, n_rep = mesh.devices.shape
    nc = 2
    nzh = 2
    nx = n_tm // (nc * nzh)
    nzl = 8
    ny = n_rep // nzl
    sizes = (nx, nzh, nc, ny, nzl)
    fine = Mesh(mesh.devices.reshape(sizes), ("x", "zh", "c", "y", "zl"))
    return jax.shard_map(
        make_body(sizes),
        mesh=fine,
        in_specs=(P(REP, TM, None), P(REP, TM, None), P(), P(), P(REP)),
        out_specs=(P(REP, TM, None), P(TM, REP), P(TM, REP)),
        check_vma=False,
    )
```

```python
import jax
import jax.numpy as jnp
from jax import lax
from jax.experimental import pallas as pl
from jax.experimental.pallas import tpu as pltpu
from jax.sharding import Mesh, PartitionSpec as P

DILATION_STEP = 256
TM = ("x", "zh", "c")
REP = ("y", "zl")


def passed_along(array, axis, by, length):
    pairs = [(i, i + by) for i in range(length) if 0 <= i + by < length]
    return lax.ppermute(array, axis, pairs)


def gate_backward(inputs, cotangent, in_length, w_conv, w_res):
    channel_count = w_res.shape[0]
    pre_act = jnp.dot(inputs, w_conv, preferred_element_type=jnp.float32)
    tanh_f = jnp.tanh(pre_act[:, :channel_count])
    sig_g = jax.nn.sigmoid(pre_act[:, channel_count:])
    gated = (in_length * tanh_f * sig_g).astype(jnp.bfloat16)
    gated_grad = in_length * jnp.dot(cotangent, w_res.T, preferred_element_type=jnp.float32)
    pre_grad = jnp.concatenate(
        [gated_grad * sig_g * (1.0 - tanh_f * tanh_f), gated_grad * tanh_f * sig_g * (1.0 - sig_g)],
        1,
    ).astype(jnp.bfloat16)
    return (gated, pre_grad)


def make_reducer(sizes, rc, n_conv, rr, n_res, scale):
    nx, nzh, nc, ny, nzl = sizes
    nz = nzh * nzl
    cyc, cyr = n_conv // ny, n_res // ny
    cc, cr = cyc // nzl, cyr // nzl
    base_x, base_y, base_z = 1, 1 + nx, 1 + nx + ny
    n_slots = base_z + nz
    n_peers = (nc - 1) + (nx - 1) + (ny - 1) + (nz - 1)
    mesh_id = pl.DeviceIdType.MESH

    def kernel(conv_ref, res_ref, conv_out, res_out,
               rc_conv, rc_res, sx_conv, sx_res, rx_conv, rx_res,
               sy_conv, sy_res, ry_conv, ry_res, sz_conv, sz_res, rz_conv, rz_res,
               send_sems, recv_sems):
        me_x = lax.axis_index("x")
        me_zh = lax.axis_index("zh")
        me_c = lax.axis_index("c")
        me_y = lax.axis_index("y")
        me_zl = lax.axis_index("zl")
        me_z = me_zh * nzl + me_zl
        other_c = 1 - me_c

        def dev(x=None, zh=None, c=None, y=None, zl=None):
            return (me_x if x is None else x, me_zh if zh is None else zh,
                    me_c if c is None else c, me_y if y is None else y,
                    me_zl if zl is None else zl)

        peers = [dev(c=other_c)]
        peers += [dev(x=lax.rem(me_x + d, nx)) for d in range(1, nx)]
        peers += [dev(y=lax.rem(me_y + d, ny)) for d in range(1, ny)]
        for d in range(1, nz):
            q = lax.rem(me_z + d, nz)
            peers.append(dev(zh=q // nzl, zl=lax.rem(q, nzl)))
        barrier = pltpu.get_barrier_semaphore()
        for peer in peers:
            pl.semaphore_signal(barrier, inc=1, device_id=peer, device_id_type=mesh_id)
        pl.semaphore_wait(barrier, n_peers)

        sends = []

        def send(kind, src, dst, slot, peer):
            copy = pltpu.make_async_remote_copy(
                src_ref=src, dst_ref=dst, send_sem=send_sems.at[kind, slot],
                recv_sem=recv_sems.at[kind, slot], device_id=peer, device_id_type=mesh_id)
            copy.start()
            sends.append(copy)

        def arrive(kind, src, dst, slot):
            pltpu.make_async_remote_copy(
                src_ref=src, dst_ref=dst, send_sem=send_sems.at[kind, slot],
                recv_sem=recv_sems.at[kind, slot], device_id=dev(),
                device_id_type=mesh_id).wait_recv()

        send(0, conv_ref.at[:, :, pl.ds(other_c, 1)], rc_conv, 0, peers[0])
        send(1, res_ref.at[:, :, pl.ds(other_c, 1)], rc_res, 0, peers[0])
        arrive(0, conv_ref.at[:, :, pl.ds(other_c, 1)], rc_conv, 0)
        arrive(1, res_ref.at[:, :, pl.ds(other_c, 1)], rc_res, 0)
        for x in range(nx):
            for zh in range(nzh):
                own_c = conv_ref[x, zh, pl.ds(me_c, 1)][0].astype(jnp.float32)
                sx_conv[x, zh] = (own_c + rc_conv[x, zh, 0].astype(jnp.float32)).astype(jnp.bfloat16)
                own_r = res_ref[x, zh, pl.ds(me_c, 1)][0].astype(jnp.float32)
                sx_res[x, zh] = (own_r + rc_res[x, zh, 0].astype(jnp.float32)).astype(jnp.bfloat16)

        for d in range(1, nx):
            tx = lax.rem(me_x + d, nx)
            send(0, sx_conv.at[tx], rx_conv.at[me_x], base_x + me_x, peers[d])
            send(1, sx_res.at[tx], rx_res.at[me_x], base_x + me_x, peers[d])
        for d in range(1, nx):
            sx = lax.rem(me_x + nx - d, nx)
            arrive(0, sx_conv.at[sx], rx_conv.at[sx], base_x + sx)
            arrive(1, sx_res.at[sx], rx_res.at[sx], base_x + sx)
        acc_c = sx_conv[me_x].astype(jnp.float32)
        acc_r = sx_res[me_x].astype(jnp.float32)
        for d in range(1, nx):
            sx = lax.rem(me_x + nx - d, nx)
            acc_c = acc_c + rx_conv[sx].astype(jnp.float32)
            acc_r = acc_r + rx_res[sx].astype(jnp.float32)
        for y in range(ny):
            sy_conv[y] = acc_c[:, :, y * cyc:(y + 1) * cyc].astype(jnp.bfloat16)
            sy_res[y] = acc_r[:, :, y * cyr:(y + 1) * cyr].astype(jnp.bfloat16)

        for d in range(1, ny):
            ty = lax.rem(me_y + d, ny)
            peer = peers[nx - 1 + d]
            send(0, sy_conv.at[ty], ry_conv.at[me_y], base_y + me_y, peer)
            send(1, sy_res.at[ty], ry_res.at[me_y], base_y + me_y, peer)
        for d in range(1, ny):
            sy = lax.rem(me_y + ny - d, ny)
            arrive(0, sy_conv.at[sy], ry_conv.at[sy], base_y + sy)
            arrive(1, sy_res.at[sy], ry_res.at[sy], base_y + sy)
        acc_c = sy_conv[me_y].astype(jnp.float32)
        acc_r = sy_res[me_y].astype(jnp.float32)
        for d in range(1, ny):
            sy = lax.rem(me_y + ny - d, ny)
            acc_c = acc_c + ry_conv[sy].astype(jnp.float32)
            acc_r = acc_r + ry_res[sy].astype(jnp.float32)
        for zh in range(nzh):
            for zl in range(nzl):
                sz_conv[zh * nzl + zl] = acc_c[zh, :, zl * cc:(zl + 1) * cc]
                sz_res[zh * nzl + zl] = acc_r[zh, :, zl * cr:(zl + 1) * cr]

        for d in range(1, nz):
            tz = lax.rem(me_z + d, nz)
            peer = peers[nx + ny - 2 + d]
            send(0, sz_conv.at[tz], rz_conv.at[me_z], base_z + me_z, peer)
            send(1, sz_res.at[tz], rz_res.at[me_z], base_z + me_z, peer)
        for d in range(1, nz):
            sz = lax.rem(me_z + nz - d, nz)
            arrive(0, sz_conv.at[sz], rz_conv.at[sz], base_z + sz)
            arrive(1, sz_res.at[sz], rz_res.at[sz], base_z + sz)
        acc_c = sz_conv[me_z]
        acc_r = sz_res[me_z]
        for d in range(1, nz):
            sz = lax.rem(me_z + nz - d, nz)
            acc_c = acc_c + rz_conv[sz]
            acc_r = acc_r + rz_res[sz]
        conv_out[...] = acc_c * scale
        res_out[...] = acc_r * scale
        for copy in sends:
            copy.wait_send()

    vmem = pl.BlockSpec(memory_space=pltpu.VMEM)
    bf16, f32 = jnp.bfloat16, jnp.float32
    return pl.pallas_call(
        kernel,
        out_shape=(jax.ShapeDtypeStruct((rc, cc), f32), jax.ShapeDtypeStruct((rr, cr), f32)),
        in_specs=[vmem, vmem],
        out_specs=(vmem, vmem),
        scratch_shapes=[
            pltpu.VMEM((nx, nzh, 1, rc, n_conv), bf16),
            pltpu.VMEM((nx, nzh, 1, rr, n_res), bf16),
            pltpu.VMEM((nx, nzh, rc, n_conv), bf16),
            pltpu.VMEM((nx, nzh, rr, n_res), bf16),
            pltpu.VMEM((nx, nzh, rc, n_conv), bf16),
            pltpu.VMEM((nx, nzh, rr, n_res), bf16),
            pltpu.VMEM((ny, nzh, rc, cyc), bf16),
            pltpu.VMEM((ny, nzh, rr, cyr), bf16),
            pltpu.VMEM((ny, nzh, rc, cyc), bf16),
            pltpu.VMEM((ny, nzh, rr, cyr), bf16),
            pltpu.VMEM((nz, rc, cc), f32),
            pltpu.VMEM((nz, rr, cr), f32),
            pltpu.VMEM((nz, rc, cc), f32),
            pltpu.VMEM((nz, rr, cr), f32),
            pltpu.SemaphoreType.DMA((2, n_slots)),
            pltpu.SemaphoreType.DMA((2, n_slots)),
        ],
        compiler_params=pltpu.CompilerParams(collective_id=0, has_side_effects=True),
    )


def make_body(sizes):
    nx, nzh, nc, ny, nzl = sizes
    n_tm = nx * nzh * nc
    n_rep = ny * nzl

    def body(samples, grad_out, w_conv, w_res, lengths):
        sequence_rows = samples[0]
        cotangent = grad_out[0]
        seq_len = lengths[0]
        count_of_rows = sequence_rows.shape[0]
        channel_count = sequence_rows.shape[1]
        start_row = lax.axis_index(TM) * count_of_rows
        trailing_rows = sequence_rows[count_of_rows - DILATION_STEP :]
        arrived = passed_along(trailing_rows, TM, 1, n_tm)
        prior_samples = jnp.concatenate(
            [arrived, sequence_rows[: count_of_rows - DILATION_STEP]], 0
        )
        inputs = jnp.concatenate([prior_samples, sequence_rows], 1)
        in_length = (start_row + jnp.arange(count_of_rows) < seq_len).astype(jnp.float32)[:, None]
        gated, pre_grad = gate_backward(inputs, cotangent, in_length, w_conv, w_res)
        input_gradient = jnp.dot(pre_grad, w_conv.T, preferred_element_type=jnp.float32)
        incoming_gradient = passed_along(input_gradient[:DILATION_STEP, :channel_count], TM, -1, n_tm)
        delayed_gradient = jnp.concatenate(
            [input_gradient[DILATION_STEP:, :channel_count], incoming_gradient], 0
        )
        grad_rows = (
            cotangent.astype(jnp.float32) + input_gradient[:, channel_count:] + delayed_gradient
        ).astype(jnp.bfloat16)
        term_conv = jnp.einsum("tk,tn->kn", inputs, pre_grad, preferred_element_type=jnp.float32)
        term_res = jnp.einsum("tk,tn->kn", gated, cotangent, preferred_element_type=jnp.float32)
        kc, n_conv = term_conv.shape
        kr, n_res = term_res.shape
        rc, rr = kc // n_tm, kr // n_tm
        all_tokens = count_of_rows * n_tm * n_rep
        reducer = make_reducer(sizes, rc, n_conv, rr, n_res, float(all_tokens) ** (-0.5))
        sum_conv, sum_res = reducer(
            term_conv.astype(jnp.bfloat16).reshape(nx, nzh, nc, rc, n_conv),
            term_res.astype(jnp.bfloat16).reshape(nx, nzh, nc, rr, n_res),
        )
        return (grad_rows[None], sum_conv, sum_res)

    return body


def solution(mesh):
    n_tm, n_rep = mesh.devices.shape
    nc = 2
    nzh = 2
    nx = n_tm // (nc * nzh)
    nzl = 8
    ny = n_rep // nzl
    sizes = (nx, nzh, nc, ny, nzl)
    fine = Mesh(mesh.devices.reshape(sizes), ("x", "zh", "c", "y", "zl"))
    return jax.shard_map(
        make_body(sizes),
        mesh=fine,
        in_specs=(P(REP, TM, None), P(REP, TM, None), P(), P(), P(REP)),
        out_specs=(P(REP, TM, None), P(TM, REP), P(TM, REP)),
        check_vma=False,
    )
```

```python
import jax
import jax.numpy as jnp
from jax import lax
from jax.experimental import pallas as pl
from jax.experimental.pallas import tpu as pltpu
from jax.sharding import Mesh, PartitionSpec as P

DILATION_STEP = 256
TM = ("x", "zh", "c")
REP = ("y", "zl")


def passed_along(array, axis, by, length):
    pairs = [(i, i + by) for i in range(length) if 0 <= i + by < length]
    return lax.ppermute(array, axis, pairs)


def gate_backward(inputs, cotangent, in_length, w_conv, w_res):
    channel_count = w_res.shape[0]
    pre_act = jnp.dot(inputs, w_conv, preferred_element_type=jnp.float32)
    tanh_f = jnp.tanh(pre_act[:, :channel_count])
    sig_g = jax.nn.sigmoid(pre_act[:, channel_count:])
    gated = (in_length * tanh_f * sig_g).astype(jnp.bfloat16)
    gated_grad = in_length * jnp.dot(cotangent, w_res.T, preferred_element_type=jnp.float32)
    pre_grad = jnp.concatenate(
        [gated_grad * sig_g * (1.0 - tanh_f * tanh_f), gated_grad * tanh_f * sig_g * (1.0 - sig_g)],
        1,
    ).astype(jnp.bfloat16)
    return (gated, pre_grad)


def make_reducer(sizes, rc, n_conv, rr, n_res, scale):
    nx, nzh, nc, ny, nzl = sizes
    nz = nzh * nzl
    cyc, cyr = n_conv // ny, n_res // ny
    cc, cr = cyc // nzl, cyr // nzl
    base_x, base_y, base_z = 1, 1 + nx, 1 + nx + ny
    n_slots = base_z + nz
    n_peers = (nc - 1) + (nx - 1) + (ny - 1) + (nz - 1)
    mesh_id = pl.DeviceIdType.MESH

    def kernel(conv_ref, res_ref, conv_out, res_out,
               rc_conv, rc_res, sx_conv, sx_res, rx_conv, rx_res,
               sy_conv, sy_res, ry_conv, ry_res, sz_conv, sz_res, rz_conv, rz_res,
               send_sems, recv_sems):
        me_x = lax.axis_index("x")
        me_zh = lax.axis_index("zh")
        me_c = lax.axis_index("c")
        me_y = lax.axis_index("y")
        me_zl = lax.axis_index("zl")
        me_z = me_zh * nzl + me_zl
        other_c = 1 - me_c

        def dev(x=None, zh=None, c=None, y=None, zl=None):
            return (me_x if x is None else x, me_zh if zh is None else zh,
                    me_c if c is None else c, me_y if y is None else y,
                    me_zl if zl is None else zl)

        peers = [dev(c=other_c)]
        peers += [dev(x=lax.rem(me_x + d, nx)) for d in range(1, nx)]
        peers += [dev(y=lax.rem(me_y + d, ny)) for d in range(1, ny)]
        for d in range(1, nz):
            q = lax.rem(me_z + d, nz)
            peers.append(dev(zh=q // nzl, zl=lax.rem(q, nzl)))
        barrier = pltpu.get_barrier_semaphore()
        for peer in peers:
            pl.semaphore_signal(barrier, inc=1, device_id=peer, device_id_type=mesh_id)
        pl.semaphore_wait(barrier, n_peers)

        sends = []

        def send(kind, src, dst, slot, peer):
            copy = pltpu.make_async_remote_copy(
                src_ref=src, dst_ref=dst, send_sem=send_sems.at[kind, slot],
                recv_sem=recv_sems.at[kind, slot], device_id=peer, device_id_type=mesh_id)
            copy.start()
            sends.append(copy)

        def arrive(kind, src, dst, slot):
            pltpu.make_async_remote_copy(
                src_ref=src, dst_ref=dst, send_sem=send_sems.at[kind, slot],
                recv_sem=recv_sems.at[kind, slot], device_id=dev(),
                device_id_type=mesh_id).wait_recv()

        send(0, conv_ref.at[:, :, pl.ds(other_c, 1)], rc_conv, 0, peers[0])
        send(1, res_ref.at[:, :, pl.ds(other_c, 1)], rc_res, 0, peers[0])
        arrive(0, conv_ref.at[:, :, pl.ds(other_c, 1)], rc_conv, 0)
        arrive(1, res_ref.at[:, :, pl.ds(other_c, 1)], rc_res, 0)
        for x in range(nx):
            for zh in range(nzh):
                own_c = conv_ref[x, zh, pl.ds(me_c, 1)][0].astype(jnp.float32)
                sx_conv[x, zh] = (own_c + rc_conv[x, zh, 0].astype(jnp.float32)).astype(jnp.bfloat16)
                own_r = res_ref[x, zh, pl.ds(me_c, 1)][0].astype(jnp.float32)
                sx_res[x, zh] = (own_r + rc_res[x, zh, 0].astype(jnp.float32)).astype(jnp.bfloat16)

        for d in range(1, nx):
            tx = lax.rem(me_x + d, nx)
            send(0, sx_conv.at[tx], rx_conv.at[me_x], base_x + me_x, peers[d])
            send(1, sx_res.at[tx], rx_res.at[me_x], base_x + me_x, peers[d])
        for d in range(1, nx):
            sx = lax.rem(me_x + nx - d, nx)
            arrive(0, sx_conv.at[sx], rx_conv.at[sx], base_x + sx)
            arrive(1, sx_res.at[sx], rx_res.at[sx], base_x + sx)
        acc_c = sx_conv[me_x].astype(jnp.float32)
        acc_r = sx_res[me_x].astype(jnp.float32)
        for d in range(1, nx):
            sx = lax.rem(me_x + nx - d, nx)
            acc_c = acc_c + rx_conv[sx].astype(jnp.float32)
            acc_r = acc_r + rx_res[sx].astype(jnp.float32)
        for y in range(ny):
            sy_conv[y] = acc_c[:, :, y * cyc:(y + 1) * cyc].astype(jnp.bfloat16)
            sy_res[y] = acc_r[:, :, y * cyr:(y + 1) * cyr].astype(jnp.bfloat16)

        for d in range(1, ny):
            ty = lax.rem(me_y + d, ny)
            peer = peers[nx - 1 + d]
            send(0, sy_conv.at[ty], ry_conv.at[me_y], base_y + me_y, peer)
            send(1, sy_res.at[ty], ry_res.at[me_y], base_y + me_y, peer)
        for d in range(1, ny):
            sy = lax.rem(me_y + ny - d, ny)
            arrive(0, sy_conv.at[sy], ry_conv.at[sy], base_y + sy)
            arrive(1, sy_res.at[sy], ry_res.at[sy], base_y + sy)
        acc_c = sy_conv[me_y].astype(jnp.float32)
        acc_r = sy_res[me_y].astype(jnp.float32)
        for d in range(1, ny):
            sy = lax.rem(me_y + ny - d, ny)
            acc_c = acc_c + ry_conv[sy].astype(jnp.float32)
            acc_r = acc_r + ry_res[sy].astype(jnp.float32)
        for zh in range(nzh):
            flip_c = acc_c[zh].T
            flip_r = acc_r[zh].T
            for zl in range(nzl):
                sz_conv[zh * nzl + zl] = flip_c[zl * cc:(zl + 1) * cc, :].astype(jnp.bfloat16)
                sz_res[zh * nzl + zl] = flip_r[zl * cr:(zl + 1) * cr, :].astype(jnp.bfloat16)

        for d in range(1, nz):
            tz = lax.rem(me_z + d, nz)
            peer = peers[nx + ny - 2 + d]
            send(0, sz_conv.at[tz], rz_conv.at[me_z], base_z + me_z, peer)
            send(1, sz_res.at[tz], rz_res.at[me_z], base_z + me_z, peer)
        for d in range(1, nz):
            sz = lax.rem(me_z + nz - d, nz)
            arrive(0, sz_conv.at[sz], rz_conv.at[sz], base_z + sz)
            arrive(1, sz_res.at[sz], rz_res.at[sz], base_z + sz)
        acc_c = sz_conv[me_z].astype(jnp.float32)
        acc_r = sz_res[me_z].astype(jnp.float32)
        for d in range(1, nz):
            sz = lax.rem(me_z + nz - d, nz)
            acc_c = acc_c + rz_conv[sz].astype(jnp.float32)
            acc_r = acc_r + rz_res[sz].astype(jnp.float32)
        conv_out[...] = acc_c.T * scale
        res_out[...] = acc_r.T * scale
        for copy in sends:
            copy.wait_send()

    vmem = pl.BlockSpec(memory_space=pltpu.VMEM)
    bf16, f32 = jnp.bfloat16, jnp.float32
    return pl.pallas_call(
        kernel,
        out_shape=(jax.ShapeDtypeStruct((rc, cc), f32), jax.ShapeDtypeStruct((rr, cr), f32)),
        in_specs=[vmem, vmem],
        out_specs=(vmem, vmem),
        scratch_shapes=[
            pltpu.VMEM((nx, nzh, 1, rc, n_conv), bf16),
            pltpu.VMEM((nx, nzh, 1, rr, n_res), bf16),
            pltpu.VMEM((nx, nzh, rc, n_conv), bf16),
            pltpu.VMEM((nx, nzh, rr, n_res), bf16),
            pltpu.VMEM((nx, nzh, rc, n_conv), bf16),
            pltpu.VMEM((nx, nzh, rr, n_res), bf16),
            pltpu.VMEM((ny, nzh, rc, cyc), bf16),
            pltpu.VMEM((ny, nzh, rr, cyr), bf16),
            pltpu.VMEM((ny, nzh, rc, cyc), bf16),
            pltpu.VMEM((ny, nzh, rr, cyr), bf16),
            pltpu.VMEM((nz, cc, rc), bf16),
            pltpu.VMEM((nz, cr, rr), bf16),
            pltpu.VMEM((nz, cc, rc), bf16),
            pltpu.VMEM((nz, cr, rr), bf16),
            pltpu.SemaphoreType.DMA((2, n_slots)),
            pltpu.SemaphoreType.DMA((2, n_slots)),
        ],
        compiler_params=pltpu.CompilerParams(collective_id=0, has_side_effects=True),
    )


def make_body(sizes):
    nx, nzh, nc, ny, nzl = sizes
    n_tm = nx * nzh * nc
    n_rep = ny * nzl

    def body(samples, grad_out, w_conv, w_res, lengths):
        sequence_rows = samples[0]
        cotangent = grad_out[0]
        seq_len = lengths[0]
        count_of_rows = sequence_rows.shape[0]
        channel_count = sequence_rows.shape[1]
        start_row = lax.axis_index(TM) * count_of_rows
        trailing_rows = sequence_rows[count_of_rows - DILATION_STEP :]
        arrived = passed_along(trailing_rows, TM, 1, n_tm)
        prior_samples = jnp.concatenate(
            [arrived, sequence_rows[: count_of_rows - DILATION_STEP]], 0
        )
        inputs = jnp.concatenate([prior_samples, sequence_rows], 1)
        in_length = (start_row + jnp.arange(count_of_rows) < seq_len).astype(jnp.float32)[:, None]
        gated, pre_grad = gate_backward(inputs, cotangent, in_length, w_conv, w_res)
        input_gradient = jnp.dot(pre_grad, w_conv.T, preferred_element_type=jnp.float32)
        incoming_gradient = passed_along(input_gradient[:DILATION_STEP, :channel_count], TM, -1, n_tm)
        delayed_gradient = jnp.concatenate(
            [input_gradient[DILATION_STEP:, :channel_count], incoming_gradient], 0
        )
        grad_rows = (
            cotangent.astype(jnp.float32) + input_gradient[:, channel_count:] + delayed_gradient
        ).astype(jnp.bfloat16)
        term_conv = jnp.einsum("tk,tn->kn", inputs, pre_grad, preferred_element_type=jnp.float32)
        term_res = jnp.einsum("tk,tn->kn", gated, cotangent, preferred_element_type=jnp.float32)
        kc, n_conv = term_conv.shape
        kr, n_res = term_res.shape
        rc, rr = kc // n_tm, kr // n_tm
        all_tokens = count_of_rows * n_tm * n_rep
        reducer = make_reducer(sizes, rc, n_conv, rr, n_res, float(all_tokens) ** (-0.5))
        sum_conv, sum_res = reducer(
            term_conv.astype(jnp.bfloat16).reshape(nx, nzh, nc, rc, n_conv),
            term_res.astype(jnp.bfloat16).reshape(nx, nzh, nc, rr, n_res),
        )
        return (grad_rows[None], sum_conv, sum_res)

    return body


def solution(mesh):
    n_tm, n_rep = mesh.devices.shape
    nc = 2
    nzh = 2
    nx = n_tm // (nc * nzh)
    nzl = 8
    ny = n_rep // nzl
    sizes = (nx, nzh, nc, ny, nzl)
    fine = Mesh(mesh.devices.reshape(sizes), ("x", "zh", "c", "y", "zl"))
    return jax.shard_map(
        make_body(sizes),
        mesh=fine,
        in_specs=(P(REP, TM, None), P(REP, TM, None), P(), P(), P(REP)),
        out_specs=(P(REP, TM, None), P(TM, REP), P(TM, REP)),
        check_vma=False,
    )
```

```python
import jax
import jax.numpy as jnp
from jax import lax
from jax.experimental import pallas as pl
from jax.experimental.pallas import tpu as pltpu
from jax.sharding import Mesh, PartitionSpec as P

DILATION_STEP = 256
TM = ("x", "zh", "c")
REP = ("y", "zl")


def passed_along(array, axis, by, length):
    pairs = [(i, i + by) for i in range(length) if 0 <= i + by < length]
    return lax.ppermute(array, axis, pairs)


def gate_backward(inputs, cotangent, in_length, w_conv, w_res):
    channel_count = w_res.shape[0]
    pre_act = jnp.dot(inputs, w_conv, preferred_element_type=jnp.float32)
    tanh_f = jnp.tanh(pre_act[:, :channel_count])
    sig_g = jax.nn.sigmoid(pre_act[:, channel_count:])
    gated = (in_length * tanh_f * sig_g).astype(jnp.bfloat16)
    gated_grad = in_length * jnp.dot(cotangent, w_res.T, preferred_element_type=jnp.float32)
    pre_grad = jnp.concatenate(
        [gated_grad * sig_g * (1.0 - tanh_f * tanh_f), gated_grad * tanh_f * sig_g * (1.0 - sig_g)],
        1,
    ).astype(jnp.bfloat16)
    return (gated, pre_grad)


def make_reducer(sizes, rc, n_conv, rr, n_res, scale):
    nx, nzh, nc, ny, nzl = sizes
    nz = nzh * nzl
    cyc, cyr = n_conv // ny, n_res // ny
    cc, cr = cyc // nzl, cyr // nzl
    hc, hr = rc // 2, rr // 2
    base_xa, base_yb = 1, 1 + nx
    base_ya, base_xb = 1 + nx + ny, 1 + nx + 2 * ny
    base_z = 1 + 2 * nx + 2 * ny
    n_slots = base_z + nz
    n_peers = (nc - 1) + (nx - 1) + (ny - 1) + (nz - 1)
    mesh_id = pl.DeviceIdType.MESH

    def kernel(conv_ref, res_ref, conv_out, res_out,
               rc_conv, rc_res, sx_conv, sx_res,
               rxa_conv, rxa_res, ryb_conv, ryb_res,
               sa_conv, sa_res, rya_conv, rya_res,
               sb_conv, sb_res, rxb_conv, rxb_res,
               sz_conv, sz_res, rz_conv, rz_res,
               send_sems, recv_sems, local_sems):
        me_x = lax.axis_index("x")
        me_zh = lax.axis_index("zh")
        me_c = lax.axis_index("c")
        me_y = lax.axis_index("y")
        me_zl = lax.axis_index("zl")
        me_z = me_zh * nzl + me_zl
        other_c = 1 - me_c

        def dev(x=None, zh=None, c=None, y=None, zl=None):
            return (me_x if x is None else x, me_zh if zh is None else zh,
                    me_c if c is None else c, me_y if y is None else y,
                    me_zl if zl is None else zl)

        peers = [dev(c=other_c)]
        x_peers = [dev(x=lax.rem(me_x + d, nx)) for d in range(1, nx)]
        y_peers = [dev(y=lax.rem(me_y + d, ny)) for d in range(1, ny)]
        z_peers = []
        for d in range(1, nz):
            q = lax.rem(me_z + d, nz)
            z_peers.append(dev(zh=q // nzl, zl=lax.rem(q, nzl)))
        barrier = pltpu.get_barrier_semaphore()
        for peer in peers + x_peers + y_peers + z_peers:
            pl.semaphore_signal(barrier, inc=1, device_id=peer, device_id_type=mesh_id)
        pl.semaphore_wait(barrier, n_peers)

        sends = []

        def send(kind, src, dst, slot, peer):
            copy = pltpu.make_async_remote_copy(
                src_ref=src, dst_ref=dst, send_sem=send_sems.at[kind, slot],
                recv_sem=recv_sems.at[kind, slot], device_id=peer, device_id_type=mesh_id)
            copy.start()
            sends.append(copy)

        def arrive(kind, src, dst, slot):
            pltpu.make_async_remote_copy(
                src_ref=src, dst_ref=dst, send_sem=send_sems.at[kind, slot],
                recv_sem=recv_sems.at[kind, slot], device_id=dev(),
                device_id_type=mesh_id).wait_recv()

        def keep(kind, which, src, dst):
            copy = pltpu.make_async_copy(src, dst, local_sems.at[kind, which])
            copy.start()
            return copy

        send(0, conv_ref.at[:, :, pl.ds(other_c, 1)], rc_conv, 0, peers[0])
        send(1, res_ref.at[:, :, pl.ds(other_c, 1)], rc_res, 0, peers[0])
        arrive(0, conv_ref.at[:, :, pl.ds(other_c, 1)], rc_conv, 0)
        arrive(1, res_ref.at[:, :, pl.ds(other_c, 1)], rc_res, 0)
        for x in range(nx):
            for zh in range(nzh):
                own_c = conv_ref[x, zh, pl.ds(me_c, 1)][0].astype(jnp.float32)
                sx_conv[x, zh] = (own_c + rc_conv[x, zh, 0].astype(jnp.float32)).astype(jnp.bfloat16)
                own_r = res_ref[x, zh, pl.ds(me_c, 1)][0].astype(jnp.float32)
                sx_res[x, zh] = (own_r + rc_res[x, zh, 0].astype(jnp.float32)).astype(jnp.bfloat16)

        for d in range(1, nx):
            tx = lax.rem(me_x + d, nx)
            send(0, sx_conv.at[tx, :, pl.ds(0, hc)], rxa_conv.at[me_x], base_xa + me_x, x_peers[d - 1])
            send(1, sx_res.at[tx, :, pl.ds(0, hr)], rxa_res.at[me_x], base_xa + me_x, x_peers[d - 1])
        for d in range(1, ny):
            ty = lax.rem(me_y + d, ny)
            send(0, sx_conv.at[:, :, pl.ds(hc, hc), pl.ds(ty * cyc, cyc)], ryb_conv.at[me_y],
                 base_yb + me_y, y_peers[d - 1])
            send(1, sx_res.at[:, :, pl.ds(hr, hr), pl.ds(ty * cyr, cyr)], ryb_res.at[me_y],
                 base_yb + me_y, y_peers[d - 1])
        own_b = [keep(0, 0, sx_conv.at[:, :, pl.ds(hc, hc), pl.ds(me_y * cyc, cyc)], ryb_conv.at[me_y]),
                 keep(1, 0, sx_res.at[:, :, pl.ds(hr, hr), pl.ds(me_y * cyr, cyr)], ryb_res.at[me_y])]

        for d in range(1, nx):
            sx = lax.rem(me_x + nx - d, nx)
            arrive(0, sx_conv.at[sx, :, pl.ds(0, hc)], rxa_conv.at[sx], base_xa + sx)
            arrive(1, sx_res.at[sx, :, pl.ds(0, hr)], rxa_res.at[sx], base_xa + sx)
        acc_c = sx_conv[me_x, :, :hc].astype(jnp.float32)
        acc_r = sx_res[me_x, :, :hr].astype(jnp.float32)
        for d in range(1, nx):
            sx = lax.rem(me_x + nx - d, nx)
            acc_c = acc_c + rxa_conv[sx].astype(jnp.float32)
            acc_r = acc_r + rxa_res[sx].astype(jnp.float32)
        sa_conv[...] = acc_c.astype(jnp.bfloat16)
        sa_res[...] = acc_r.astype(jnp.bfloat16)
        for d in range(1, ny):
            ty = lax.rem(me_y + d, ny)
            send(0, sa_conv.at[:, :, pl.ds(ty * cyc, cyc)], rya_conv.at[me_y], base_ya + me_y, y_peers[d - 1])
            send(1, sa_res.at[:, :, pl.ds(ty * cyr, cyr)], rya_res.at[me_y], base_ya + me_y, y_peers[d - 1])
        own_a = [keep(0, 1, sa_conv.at[:, :, pl.ds(me_y * cyc, cyc)], rya_conv.at[me_y]),
                 keep(1, 1, sa_res.at[:, :, pl.ds(me_y * cyr, cyr)], rya_res.at[me_y])]

        for d in range(1, ny):
            sy = lax.rem(me_y + ny - d, ny)
            arrive(0, sx_conv.at[:, :, pl.ds(hc, hc), pl.ds(0, cyc)], ryb_conv.at[sy], base_yb + sy)
            arrive(1, sx_res.at[:, :, pl.ds(hr, hr), pl.ds(0, cyr)], ryb_res.at[sy], base_yb + sy)
        for copy in own_b:
            copy.wait()
        acc_c = ryb_conv[0].astype(jnp.float32)
        acc_r = ryb_res[0].astype(jnp.float32)
        for s in range(1, ny):
            acc_c = acc_c + ryb_conv[s].astype(jnp.float32)
            acc_r = acc_r + ryb_res[s].astype(jnp.float32)
        sb_conv[...] = acc_c.astype(jnp.bfloat16)
        sb_res[...] = acc_r.astype(jnp.bfloat16)
        for d in range(1, nx):
            tx = lax.rem(me_x + d, nx)
            send(0, sb_conv.at[tx], rxb_conv.at[me_x], base_xb + me_x, x_peers[d - 1])
            send(1, sb_res.at[tx], rxb_res.at[me_x], base_xb + me_x, x_peers[d - 1])

        for d in range(1, ny):
            sy = lax.rem(me_y + ny - d, ny)
            arrive(0, sa_conv.at[:, :, pl.ds(0, cyc)], rya_conv.at[sy], base_ya + sy)
            arrive(1, sa_res.at[:, :, pl.ds(0, cyr)], rya_res.at[sy], base_ya + sy)
        for copy in own_a:
            copy.wait()
        for d in range(1, nx):
            sx = lax.rem(me_x + nx - d, nx)
            arrive(0, sb_conv.at[sx], rxb_conv.at[sx], base_xb + sx)
            arrive(1, sb_res.at[sx], rxb_res.at[sx], base_xb + sx)
        top_c = rya_conv[0].astype(jnp.float32)
        top_r = rya_res[0].astype(jnp.float32)
        for s in range(1, ny):
            top_c = top_c + rya_conv[s].astype(jnp.float32)
            top_r = top_r + rya_res[s].astype(jnp.float32)
        low_c = sb_conv[me_x].astype(jnp.float32)
        low_r = sb_res[me_x].astype(jnp.float32)
        for d in range(1, nx):
            sx = lax.rem(me_x + nx - d, nx)
            low_c = low_c + rxb_conv[sx].astype(jnp.float32)
            low_r = low_r + rxb_res[sx].astype(jnp.float32)
        acc_c = jnp.concatenate([top_c, low_c], axis=1)
        acc_r = jnp.concatenate([top_r, low_r], axis=1)
        for zh in range(nzh):
            flip_c = acc_c[zh].T
            flip_r = acc_r[zh].T
            for zl in range(nzl):
                sz_conv[zh * nzl + zl] = flip_c[zl * cc:(zl + 1) * cc, :].astype(jnp.bfloat16)
                sz_res[zh * nzl + zl] = flip_r[zl * cr:(zl + 1) * cr, :].astype(jnp.bfloat16)

        for d in range(1, nz):
            tz = lax.rem(me_z + d, nz)
            send(0, sz_conv.at[tz], rz_conv.at[me_z], base_z + me_z, z_peers[d - 1])
            send(1, sz_res.at[tz], rz_res.at[me_z], base_z + me_z, z_peers[d - 1])
        for d in range(1, nz):
            sz = lax.rem(me_z + nz - d, nz)
            arrive(0, sz_conv.at[sz], rz_conv.at[sz], base_z + sz)
            arrive(1, sz_res.at[sz], rz_res.at[sz], base_z + sz)
        acc_c = sz_conv[me_z].astype(jnp.float32)
        acc_r = sz_res[me_z].astype(jnp.float32)
        for d in range(1, nz):
            sz = lax.rem(me_z + nz - d, nz)
            acc_c = acc_c + rz_conv[sz].astype(jnp.float32)
            acc_r = acc_r + rz_res[sz].astype(jnp.float32)
        conv_out[...] = acc_c.T * scale
        res_out[...] = acc_r.T * scale
        for copy in sends:
            copy.wait_send()

    vmem = pl.BlockSpec(memory_space=pltpu.VMEM)
    bf16, f32 = jnp.bfloat16, jnp.float32
    return pl.pallas_call(
        kernel,
        out_shape=(jax.ShapeDtypeStruct((rc, cc), f32), jax.ShapeDtypeStruct((rr, cr), f32)),
        in_specs=[vmem, vmem],
        out_specs=(vmem, vmem),
        scratch_shapes=[
            pltpu.VMEM((nx, nzh, 1, rc, n_conv), bf16),
            pltpu.VMEM((nx, nzh, 1, rr, n_res), bf16),
            pltpu.VMEM((nx, nzh, rc, n_conv), bf16),
            pltpu.VMEM((nx, nzh, rr, n_res), bf16),
            pltpu.VMEM((nx, nzh, hc, n_conv), bf16),
            pltpu.VMEM((nx, nzh, hr, n_res), bf16),
            pltpu.VMEM((ny, nx, nzh, hc, cyc), bf16),
            pltpu.VMEM((ny, nx, nzh, hr, cyr), bf16),
            pltpu.VMEM((nzh, hc, n_conv), bf16),
            pltpu.VMEM((nzh, hr, n_res), bf16),
            pltpu.VMEM((ny, nzh, hc, cyc), bf16),
            pltpu.VMEM((ny, nzh, hr, cyr), bf16),
            pltpu.VMEM((nx, nzh, hc, cyc), bf16),
            pltpu.VMEM((nx, nzh, hr, cyr), bf16),
            pltpu.VMEM((nx, nzh, hc, cyc), bf16),
            pltpu.VMEM((nx, nzh, hr, cyr), bf16),
            pltpu.VMEM((nz, cc, rc), bf16),
            pltpu.VMEM((nz, cr, rr), bf16),
            pltpu.VMEM((nz, cc, rc), bf16),
            pltpu.VMEM((nz, cr, rr), bf16),
            pltpu.SemaphoreType.DMA((2, n_slots)),
            pltpu.SemaphoreType.DMA((2, n_slots)),
            pltpu.SemaphoreType.DMA((2, 2)),
        ],
        compiler_params=pltpu.CompilerParams(collective_id=0, has_side_effects=True),
    )


def make_body(sizes):
    nx, nzh, nc, ny, nzl = sizes
    n_tm = nx * nzh * nc
    n_rep = ny * nzl

    def body(samples, grad_out, w_conv, w_res, lengths):
        sequence_rows = samples[0]
        cotangent = grad_out[0]
        seq_len = lengths[0]
        count_of_rows = sequence_rows.shape[0]
        channel_count = sequence_rows.shape[1]
        start_row = lax.axis_index(TM) * count_of_rows
        trailing_rows = sequence_rows[count_of_rows - DILATION_STEP :]
        arrived = passed_along(trailing_rows, TM, 1, n_tm)
        prior_samples = jnp.concatenate(
            [arrived, sequence_rows[: count_of_rows - DILATION_STEP]], 0
        )
        inputs = jnp.concatenate([prior_samples, sequence_rows], 1)
        in_length = (start_row + jnp.arange(count_of_rows) < seq_len).astype(jnp.float32)[:, None]
        gated, pre_grad = gate_backward(inputs, cotangent, in_length, w_conv, w_res)
        input_gradient = jnp.dot(pre_grad, w_conv.T, preferred_element_type=jnp.float32)
        incoming_gradient = passed_along(input_gradient[:DILATION_STEP, :channel_count], TM, -1, n_tm)
        delayed_gradient = jnp.concatenate(
            [input_gradient[DILATION_STEP:, :channel_count], incoming_gradient], 0
        )
        grad_rows = (
            cotangent.astype(jnp.float32) + input_gradient[:, channel_count:] + delayed_gradient
        ).astype(jnp.bfloat16)
        term_conv = jnp.einsum("tk,tn->kn", inputs, pre_grad, preferred_element_type=jnp.float32)
        term_res = jnp.einsum("tk,tn->kn", gated, cotangent, preferred_element_type=jnp.float32)
        kc, n_conv = term_conv.shape
        kr, n_res = term_res.shape
        rc, rr = kc // n_tm, kr // n_tm
        all_tokens = count_of_rows * n_tm * n_rep
        reducer = make_reducer(sizes, rc, n_conv, rr, n_res, float(all_tokens) ** (-0.5))
        sum_conv, sum_res = reducer(
            term_conv.astype(jnp.bfloat16).reshape(nx, nzh, nc, rc, n_conv),
            term_res.astype(jnp.bfloat16).reshape(nx, nzh, nc, rr, n_res),
        )
        return (grad_rows[None], sum_conv, sum_res)

    return body


def solution(mesh):
    n_tm, n_rep = mesh.devices.shape
    nc = 2
    nzh = 2
    nx = n_tm // (nc * nzh)
    nzl = 8
    ny = n_rep // nzl
    sizes = (nx, nzh, nc, ny, nzl)
    fine = Mesh(mesh.devices.reshape(sizes), ("x", "zh", "c", "y", "zl"))
    return jax.shard_map(
        make_body(sizes),
        mesh=fine,
        in_specs=(P(REP, TM, None), P(REP, TM, None), P(), P(), P(REP)),
        out_specs=(P(REP, TM, None), P(TM, REP), P(TM, REP)),
        check_vma=False,
    )
```

```python
import jax
import jax.numpy as jnp
from jax import lax
from jax.experimental import pallas as pl
from jax.experimental.pallas import tpu as pltpu
from jax.sharding import Mesh, PartitionSpec as P

DILATION_STEP = 256
TM = ("x", "zh", "c")
REP = ("y", "zl")


def passed_along(array, axis, by, length):
    pairs = [(i, i + by) for i in range(length) if 0 <= i + by < length]
    return lax.ppermute(array, axis, pairs)


def gate_backward(inputs, cotangent, in_length, w_conv, w_res):
    channel_count = w_res.shape[0]
    pre_act = jnp.dot(inputs, w_conv, preferred_element_type=jnp.float32)
    tanh_f = jnp.tanh(pre_act[:, :channel_count])
    sig_g = jax.nn.sigmoid(pre_act[:, channel_count:])
    gated = (in_length * tanh_f * sig_g).astype(jnp.bfloat16)
    gated_grad = in_length * jnp.dot(cotangent, w_res.T, preferred_element_type=jnp.float32)
    pre_grad = jnp.concatenate(
        [gated_grad * sig_g * (1.0 - tanh_f * tanh_f), gated_grad * tanh_f * sig_g * (1.0 - sig_g)],
        1,
    ).astype(jnp.bfloat16)
    return (gated, pre_grad)


def make_reducer(sizes, rc, n_conv, rr, n_res, scale):
    nx, nzh, nc, ny, nzl = sizes
    nz = nzh * nzl
    cyc, cyr = n_conv // ny, n_res // ny
    cc, cr = cyc // nzl, cyr // nzl
    hc, hr = rc // 2, rr // 2
    base_xa, base_yb = 1, 1 + nx
    base_ya, base_xb = 1 + nx + ny, 1 + nx + 2 * ny
    base_z = 1 + 2 * nx + 2 * ny
    n_slots = base_z + nz
    n_peers = (nc - 1) + (nx - 1) + (ny - 1) + (nz - 1)
    mesh_id = pl.DeviceIdType.MESH

    def kernel(conv_ref, res_ref, conv_out, res_out,
               rc_conv, rc_res, sx_conv, sx_res,
               rxa_conv, rxa_res, ryb_conv, ryb_res,
               sa_conv, sa_res, rya_conv, rya_res,
               sb_conv, sb_res, rxb_conv, rxb_res,
               sz_conv, sz_res, rz_conv, rz_res,
               send_sems, recv_sems, local_sems):
        me_x = lax.axis_index("x")
        me_zh = lax.axis_index("zh")
        me_c = lax.axis_index("c")
        me_y = lax.axis_index("y")
        me_zl = lax.axis_index("zl")
        me_z = me_zh * nzl + me_zl
        other_c = 1 - me_c

        def dev(x=None, zh=None, c=None, y=None, zl=None):
            return (me_x if x is None else x, me_zh if zh is None else zh,
                    me_c if c is None else c, me_y if y is None else y,
                    me_zl if zl is None else zl)

        peers = [dev(c=other_c)]
        x_peers = [dev(x=lax.rem(me_x + d, nx)) for d in range(1, nx)]
        y_peers = [dev(y=lax.rem(me_y + d, ny)) for d in range(1, ny)]
        z_peers = []
        for d in range(1, nz):
            q = lax.rem(me_z + d, nz)
            z_peers.append(dev(zh=q // nzl, zl=lax.rem(q, nzl)))
        barrier = pltpu.get_barrier_semaphore()
        for peer in peers + x_peers + y_peers + z_peers:
            pl.semaphore_signal(barrier, inc=1, device_id=peer, device_id_type=mesh_id)
        pl.semaphore_wait(barrier, n_peers)

        sends = []

        def send(kind, src, dst, slot, peer):
            copy = pltpu.make_async_remote_copy(
                src_ref=src, dst_ref=dst, send_sem=send_sems.at[kind, slot],
                recv_sem=recv_sems.at[kind, slot], device_id=peer, device_id_type=mesh_id)
            copy.start()
            sends.append(copy)

        def arrive(kind, src, dst, slot):
            pltpu.make_async_remote_copy(
                src_ref=src, dst_ref=dst, send_sem=send_sems.at[kind, slot],
                recv_sem=recv_sems.at[kind, slot], device_id=dev(),
                device_id_type=mesh_id).wait_recv()

        def keep(kind, which, src, dst):
            copy = pltpu.make_async_copy(src, dst, local_sems.at[kind, which])
            copy.start()
            return copy

        send(0, conv_ref.at[:, :, pl.ds(other_c, 1)], rc_conv, 0, peers[0])
        send(1, res_ref.at[:, :, pl.ds(other_c, 1)], rc_res, 0, peers[0])
        arrive(0, conv_ref.at[:, :, pl.ds(other_c, 1)], rc_conv, 0)
        arrive(1, res_ref.at[:, :, pl.ds(other_c, 1)], rc_res, 0)
        for x in range(nx):
            for zh in range(nzh):
                own_c = conv_ref[x, zh, pl.ds(me_c, 1)][0].astype(jnp.float32)
                sx_conv[x, zh] = (own_c + rc_conv[x, zh, 0].astype(jnp.float32)).astype(jnp.bfloat16)
                own_r = res_ref[x, zh, pl.ds(me_c, 1)][0].astype(jnp.float32)
                sx_res[x, zh] = (own_r + rc_res[x, zh, 0].astype(jnp.float32)).astype(jnp.bfloat16)

        for d in range(1, nx):
            tx = lax.rem(me_x + d, nx)
            send(0, sx_conv.at[tx, :, pl.ds(0, hc)], rxa_conv.at[me_x], base_xa + me_x, x_peers[d - 1])
            send(1, sx_res.at[tx, :, pl.ds(0, hr)], rxa_res.at[me_x], base_xa + me_x, x_peers[d - 1])
        for d in range(1, ny):
            ty = lax.rem(me_y + d, ny)
            send(0, sx_conv.at[:, :, pl.ds(hc, hc), pl.ds(ty * cyc, cyc)], ryb_conv.at[me_y],
                 base_yb + me_y, y_peers[d - 1])
            send(1, sx_res.at[:, :, pl.ds(hr, hr), pl.ds(ty * cyr, cyr)], ryb_res.at[me_y],
                 base_yb + me_y, y_peers[d - 1])
        own_b = [keep(0, 0, sx_conv.at[:, :, pl.ds(hc, hc), pl.ds(me_y * cyc, cyc)], ryb_conv.at[me_y]),
                 keep(1, 0, sx_res.at[:, :, pl.ds(hr, hr), pl.ds(me_y * cyr, cyr)], ryb_res.at[me_y])]

        for d in range(1, nx):
            sx = lax.rem(me_x + nx - d, nx)
            arrive(0, sx_conv.at[sx, :, pl.ds(0, hc)], rxa_conv.at[sx], base_xa + sx)
            arrive(1, sx_res.at[sx, :, pl.ds(0, hr)], rxa_res.at[sx], base_xa + sx)
        acc_c = sx_conv[me_x, :, :hc].astype(jnp.float32)
        acc_r = sx_res[me_x, :, :hr].astype(jnp.float32)
        for d in range(1, nx):
            sx = lax.rem(me_x + nx - d, nx)
            acc_c = acc_c + rxa_conv[sx].astype(jnp.float32)
            acc_r = acc_r + rxa_res[sx].astype(jnp.float32)
        sa_conv[...] = acc_c.astype(jnp.bfloat16)
        sa_res[...] = acc_r.astype(jnp.bfloat16)
        for d in range(1, ny):
            ty = lax.rem(me_y + d, ny)
            send(0, sa_conv.at[:, :, pl.ds(ty * cyc, cyc)], rya_conv.at[me_y], base_ya + me_y, y_peers[d - 1])
            send(1, sa_res.at[:, :, pl.ds(ty * cyr, cyr)], rya_res.at[me_y], base_ya + me_y, y_peers[d - 1])
        own_a = [keep(0, 1, sa_conv.at[:, :, pl.ds(me_y * cyc, cyc)], rya_conv.at[me_y]),
                 keep(1, 1, sa_res.at[:, :, pl.ds(me_y * cyr, cyr)], rya_res.at[me_y])]

        for d in range(1, ny):
            sy = lax.rem(me_y + ny - d, ny)
            arrive(0, sx_conv.at[:, :, pl.ds(hc, hc), pl.ds(0, cyc)], ryb_conv.at[sy], base_yb + sy)
            arrive(1, sx_res.at[:, :, pl.ds(hr, hr), pl.ds(0, cyr)], ryb_res.at[sy], base_yb + sy)
        for copy in own_b:
            copy.wait()
        acc_c = ryb_conv[0].astype(jnp.float32)
        acc_r = ryb_res[0].astype(jnp.float32)
        for s in range(1, ny):
            acc_c = acc_c + ryb_conv[s].astype(jnp.float32)
            acc_r = acc_r + ryb_res[s].astype(jnp.float32)
        sb_conv[...] = acc_c.astype(jnp.bfloat16)
        sb_res[...] = acc_r.astype(jnp.bfloat16)
        for d in range(1, nx):
            tx = lax.rem(me_x + d, nx)
            send(0, sb_conv.at[tx], rxb_conv.at[me_x], base_xb + me_x, x_peers[d - 1])
            send(1, sb_res.at[tx], rxb_res.at[me_x], base_xb + me_x, x_peers[d - 1])

        for d in range(1, ny):
            sy = lax.rem(me_y + ny - d, ny)
            arrive(0, sa_conv.at[:, :, pl.ds(0, cyc)], rya_conv.at[sy], base_ya + sy)
            arrive(1, sa_res.at[:, :, pl.ds(0, cyr)], rya_res.at[sy], base_ya + sy)
        for copy in own_a:
            copy.wait()
        for d in range(1, nx):
            sx = lax.rem(me_x + nx - d, nx)
            arrive(0, sb_conv.at[sx], rxb_conv.at[sx], base_xb + sx)
            arrive(1, sb_res.at[sx], rxb_res.at[sx], base_xb + sx)
        top_c = rya_conv[0].astype(jnp.float32)
        top_r = rya_res[0].astype(jnp.float32)
        for s in range(1, ny):
            top_c = top_c + rya_conv[s].astype(jnp.float32)
            top_r = top_r + rya_res[s].astype(jnp.float32)
        low_c = sb_conv[me_x].astype(jnp.float32)
        low_r = sb_res[me_x].astype(jnp.float32)
        for d in range(1, nx):
            sx = lax.rem(me_x + nx - d, nx)
            low_c = low_c + rxb_conv[sx].astype(jnp.float32)
            low_r = low_r + rxb_res[sx].astype(jnp.float32)
        acc_c = jnp.concatenate([top_c, low_c], axis=1)
        acc_r = jnp.concatenate([top_r, low_r], axis=1)
        for zh in range(nzh):
            flip_c = acc_c[zh].T
            flip_r = acc_r[zh].T
            for zl in range(nzl):
                sz_conv[zh * nzl + zl] = flip_c[zl * cc:(zl + 1) * cc, :].astype(jnp.bfloat16)
                sz_res[zh * nzl + zl] = flip_r[zl * cr:(zl + 1) * cr, :].astype(jnp.bfloat16)

        for d in range(1, nz):
            tz = lax.rem(me_z + d, nz)
            send(0, sz_conv.at[tz], rz_conv.at[me_z], base_z + me_z, z_peers[d - 1])
            send(1, sz_res.at[tz], rz_res.at[me_z], base_z + me_z, z_peers[d - 1])
        for d in range(1, nz):
            sz = lax.rem(me_z + nz - d, nz)
            arrive(0, sz_conv.at[sz], rz_conv.at[sz], base_z + sz)
            arrive(1, sz_res.at[sz], rz_res.at[sz], base_z + sz)
        acc_c = sz_conv[me_z].astype(jnp.float32)
        acc_r = sz_res[me_z].astype(jnp.float32)
        for d in range(1, nz):
            sz = lax.rem(me_z + nz - d, nz)
            acc_c = acc_c + rz_conv[sz].astype(jnp.float32)
            acc_r = acc_r + rz_res[sz].astype(jnp.float32)
        conv_out[...] = acc_c.T * scale
        res_out[...] = acc_r.T * scale
        for copy in sends:
            copy.wait_send()

    vmem = pl.BlockSpec(memory_space=pltpu.VMEM)
    bf16, f32 = jnp.bfloat16, jnp.float32
    return pl.pallas_call(
        kernel,
        out_shape=(jax.ShapeDtypeStruct((rc, cc), f32), jax.ShapeDtypeStruct((rr, cr), f32)),
        in_specs=[vmem, vmem],
        out_specs=(vmem, vmem),
        scratch_shapes=[
            pltpu.VMEM((nx, nzh, 1, rc, n_conv), bf16),
            pltpu.VMEM((nx, nzh, 1, rr, n_res), bf16),
            pltpu.VMEM((nx, nzh, rc, n_conv), bf16),
            pltpu.VMEM((nx, nzh, rr, n_res), bf16),
            pltpu.VMEM((nx, nzh, hc, n_conv), bf16),
            pltpu.VMEM((nx, nzh, hr, n_res), bf16),
            pltpu.VMEM((ny, nx, nzh, hc, cyc), bf16),
            pltpu.VMEM((ny, nx, nzh, hr, cyr), bf16),
            pltpu.VMEM((nzh, hc, n_conv), bf16),
            pltpu.VMEM((nzh, hr, n_res), bf16),
            pltpu.VMEM((ny, nzh, hc, cyc), bf16),
            pltpu.VMEM((ny, nzh, hr, cyr), bf16),
            pltpu.VMEM((nx, nzh, hc, cyc), bf16),
            pltpu.VMEM((nx, nzh, hr, cyr), bf16),
            pltpu.VMEM((nx, nzh, hc, cyc), bf16),
            pltpu.VMEM((nx, nzh, hr, cyr), bf16),
            pltpu.VMEM((nz, cc, rc), bf16),
            pltpu.VMEM((nz, cr, rr), bf16),
            pltpu.VMEM((nz, cc, rc), bf16),
            pltpu.VMEM((nz, cr, rr), bf16),
            pltpu.SemaphoreType.DMA((2, n_slots)),
            pltpu.SemaphoreType.DMA((2, n_slots)),
            pltpu.SemaphoreType.DMA((2, 2)),
        ],
        compiler_params=pltpu.CompilerParams(collective_id=0, has_side_effects=True),
    )


def make_body(sizes):
    nx, nzh, nc, ny, nzl = sizes
    n_tm = nx * nzh * nc
    n_rep = ny * nzl

    def body(samples, grad_out, w_conv, w_res, lengths):
        sequence_rows = samples[0]
        cotangent = grad_out[0]
        seq_len = lengths[0]
        count_of_rows = sequence_rows.shape[0]
        channel_count = sequence_rows.shape[1]
        step = DILATION_STEP
        start_row = lax.axis_index(TM) * count_of_rows
        arrived = passed_along(sequence_rows[count_of_rows - step :], TM, 1, n_tm)
        in_length = (start_row + jnp.arange(count_of_rows) < seq_len).astype(jnp.float32)[:, None]
        w_earlier, w_current = w_conv[:channel_count], w_conv[channel_count:]
        current_part = jnp.dot(sequence_rows, w_current, preferred_element_type=jnp.float32)
        gated_grad = in_length * jnp.dot(cotangent, w_res.T, preferred_element_type=jnp.float32)

        def rows_of(lo, hi, prior):
            pre_act = current_part[lo:hi] + jnp.dot(prior, w_earlier, preferred_element_type=jnp.float32)
            tanh_f = jnp.tanh(pre_act[:, :channel_count])
            sig_g = jax.nn.sigmoid(pre_act[:, channel_count:])
            gated = (in_length[lo:hi] * tanh_f * sig_g).astype(jnp.bfloat16)
            grad = gated_grad[lo:hi]
            pre_grad = jnp.concatenate(
                [grad * sig_g * (1.0 - tanh_f * tanh_f), grad * tanh_f * sig_g * (1.0 - sig_g)], 1
            ).astype(jnp.bfloat16)
            inputs = jnp.concatenate([prior, sequence_rows[lo:hi]], 1)
            input_gradient = jnp.dot(pre_grad, w_conv.T, preferred_element_type=jnp.float32)
            term_conv = jnp.einsum("tk,tn->kn", inputs, pre_grad, preferred_element_type=jnp.float32)
            term_res = jnp.einsum("tk,tn->kn", gated, cotangent[lo:hi], preferred_element_type=jnp.float32)
            return input_gradient, term_conv, term_res

        late_grad, late_conv, late_res = rows_of(step, count_of_rows, sequence_rows[: count_of_rows - step])
        early_grad, early_conv, early_res = rows_of(0, step, arrived)
        incoming_gradient = passed_along(early_grad[:, :channel_count].astype(jnp.bfloat16), TM, -1, n_tm)
        delayed_gradient = jnp.concatenate(
            [early_grad[step:, :channel_count], late_grad[:, :channel_count],
             incoming_gradient.astype(jnp.float32)], 0
        )
        current_gradient = jnp.concatenate([early_grad[:, channel_count:], late_grad[:, channel_count:]], 0)
        grad_rows = (cotangent.astype(jnp.float32) + current_gradient + delayed_gradient).astype(jnp.bfloat16)
        term_conv = early_conv + late_conv
        term_res = early_res + late_res
        kc, n_conv = term_conv.shape
        kr, n_res = term_res.shape
        rc, rr = kc // n_tm, kr // n_tm
        all_tokens = count_of_rows * n_tm * n_rep
        reducer = make_reducer(sizes, rc, n_conv, rr, n_res, float(all_tokens) ** (-0.5))
        sum_conv, sum_res = reducer(
            term_conv.astype(jnp.bfloat16).reshape(nx, nzh, nc, rc, n_conv),
            term_res.astype(jnp.bfloat16).reshape(nx, nzh, nc, rr, n_res),
        )
        return (grad_rows[None], sum_conv, sum_res)

    return body


def solution(mesh):
    n_tm, n_rep = mesh.devices.shape
    nc = 2
    nzh = 2
    nx = n_tm // (nc * nzh)
    nzl = 8
    ny = n_rep // nzl
    sizes = (nx, nzh, nc, ny, nzl)
    fine = Mesh(mesh.devices.reshape(sizes), ("x", "zh", "c", "y", "zl"))
    return jax.shard_map(
        make_body(sizes),
        mesh=fine,
        in_specs=(P(REP, TM, None), P(REP, TM, None), P(), P(), P(REP)),
        out_specs=(P(REP, TM, None), P(TM, REP), P(TM, REP)),
        check_vma=False,
    )
```

```python
import jax
import jax.numpy as jnp
from jax import lax
from jax.experimental import pallas as pl
from jax.experimental.pallas import tpu as pltpu
from jax.sharding import Mesh, PartitionSpec as P

DILATION_STEP = 256
TM = ("x", "zh", "c")
REP = ("y", "zl")


def passed_along(array, axis, by, length):
    pairs = [(i, i + by) for i in range(length) if 0 <= i + by < length]
    return lax.ppermute(array, axis, pairs)


def gate_backward(inputs, cotangent, in_length, w_conv, w_res):
    channel_count = w_res.shape[0]
    pre_act = jnp.dot(inputs, w_conv, preferred_element_type=jnp.float32)
    tanh_f = jnp.tanh(pre_act[:, :channel_count])
    sig_g = jax.nn.sigmoid(pre_act[:, channel_count:])
    gated = (in_length * tanh_f * sig_g).astype(jnp.bfloat16)
    gated_grad = in_length * jnp.dot(cotangent, w_res.T, preferred_element_type=jnp.float32)
    pre_grad = jnp.concatenate(
        [gated_grad * sig_g * (1.0 - tanh_f * tanh_f), gated_grad * tanh_f * sig_g * (1.0 - sig_g)],
        1,
    ).astype(jnp.bfloat16)
    return (gated, pre_grad)


def make_reducer(sizes, rc, n_conv, rr, n_res, scale):
    nx, nzh, nc, ny, nzl = sizes
    nz = nzh * nzl
    cyc, cyr = n_conv // ny, n_res // ny
    cc, cr = cyc // nzl, cyr // nzl
    hc, hr = rc // 2, rr // 2
    base_xa, base_yb = 1, 1 + nx
    base_ya, base_xb = 1 + nx + ny, 1 + nx + 2 * ny
    base_z = 1 + 2 * nx + 2 * ny
    n_slots = base_z + nz
    n_peers = (nc - 1) + (nx - 1) + (ny - 1) + (nz - 1)
    mesh_id = pl.DeviceIdType.MESH

    def kernel(conv_ref, res_ref, conv_out, res_out,
               rc_conv, rc_res, sx_conv, sx_res,
               rxa_conv, rxa_res, ryb_conv, ryb_res,
               sa_conv, sa_res, rya_conv, rya_res,
               sb_conv, sb_res, rxb_conv, rxb_res,
               sz_conv, sz_res, rz_conv, rz_res,
               send_sems, recv_sems, local_sems):
        me_x = lax.axis_index("x")
        me_zh = lax.axis_index("zh")
        me_c = lax.axis_index("c")
        me_y = lax.axis_index("y")
        me_zl = lax.axis_index("zl")
        me_z = me_zh * nzl + me_zl
        other_c = 1 - me_c

        def dev(x=None, zh=None, c=None, y=None, zl=None):
            return (me_x if x is None else x, me_zh if zh is None else zh,
                    me_c if c is None else c, me_y if y is None else y,
                    me_zl if zl is None else zl)

        peers = [dev(c=other_c)]
        x_peers = [dev(x=lax.rem(me_x + d, nx)) for d in range(1, nx)]
        y_peers = [dev(y=lax.rem(me_y + d, ny)) for d in range(1, ny)]
        z_peers = []
        for d in range(1, nz):
            q = lax.rem(me_z + d, nz)
            z_peers.append(dev(zh=q // nzl, zl=lax.rem(q, nzl)))
        barrier = pltpu.get_barrier_semaphore()
        for peer in peers + x_peers + y_peers + z_peers:
            pl.semaphore_signal(barrier, inc=1, device_id=peer, device_id_type=mesh_id)
        pl.semaphore_wait(barrier, n_peers)

        sends = []

        def send(kind, src, dst, slot, peer):
            copy = pltpu.make_async_remote_copy(
                src_ref=src, dst_ref=dst, send_sem=send_sems.at[kind, slot],
                recv_sem=recv_sems.at[kind, slot], device_id=peer, device_id_type=mesh_id)
            copy.start()
            sends.append(copy)

        def arrive(kind, src, dst, slot):
            pltpu.make_async_remote_copy(
                src_ref=src, dst_ref=dst, send_sem=send_sems.at[kind, slot],
                recv_sem=recv_sems.at[kind, slot], device_id=dev(),
                device_id_type=mesh_id).wait_recv()

        def keep(kind, which, src, dst):
            copy = pltpu.make_async_copy(src, dst, local_sems.at[kind, which])
            copy.start()
            return copy

        send(0, conv_ref.at[:, :, pl.ds(other_c, 1)], rc_conv, 0, peers[0])
        send(1, res_ref.at[:, :, pl.ds(other_c, 1)], rc_res, 0, peers[0])
        arrive(0, conv_ref.at[:, :, pl.ds(other_c, 1)], rc_conv, 0)
        arrive(1, res_ref.at[:, :, pl.ds(other_c, 1)], rc_res, 0)
        for x in range(nx):
            for zh in range(nzh):
                own_c = conv_ref[x, zh, pl.ds(me_c, 1)][0].astype(jnp.float32)
                sx_conv[x, zh] = (own_c + rc_conv[x, zh, 0].astype(jnp.float32)).astype(jnp.bfloat16)
                own_r = res_ref[x, zh, pl.ds(me_c, 1)][0].astype(jnp.float32)
                sx_res[x, zh] = (own_r + rc_res[x, zh, 0].astype(jnp.float32)).astype(jnp.bfloat16)

        for d in range(1, nx):
            tx = lax.rem(me_x + d, nx)
            send(0, sx_conv.at[tx, :, pl.ds(0, hc)], rxa_conv.at[me_x], base_xa + me_x, x_peers[d - 1])
            send(1, sx_res.at[tx, :, pl.ds(0, hr)], rxa_res.at[me_x], base_xa + me_x, x_peers[d - 1])
        for d in range(1, ny):
            ty = lax.rem(me_y + d, ny)
            send(0, sx_conv.at[:, :, pl.ds(hc, hc), pl.ds(ty * cyc, cyc)], ryb_conv.at[me_y],
                 base_yb + me_y, y_peers[d - 1])
            send(1, sx_res.at[:, :, pl.ds(hr, hr), pl.ds(ty * cyr, cyr)], ryb_res.at[me_y],
                 base_yb + me_y, y_peers[d - 1])
        own_b = [keep(0, 0, sx_conv.at[:, :, pl.ds(hc, hc), pl.ds(me_y * cyc, cyc)], ryb_conv.at[me_y]),
                 keep(1, 0, sx_res.at[:, :, pl.ds(hr, hr), pl.ds(me_y * cyr, cyr)], ryb_res.at[me_y])]

        for d in range(1, nx):
            sx = lax.rem(me_x + nx - d, nx)
            arrive(0, sx_conv.at[sx, :, pl.ds(0, hc)], rxa_conv.at[sx], base_xa + sx)
            arrive(1, sx_res.at[sx, :, pl.ds(0, hr)], rxa_res.at[sx], base_xa + sx)
        acc_c = sx_conv[me_x, :, :hc].astype(jnp.float32)
        acc_r = sx_res[me_x, :, :hr].astype(jnp.float32)
        for d in range(1, nx):
            sx = lax.rem(me_x + nx - d, nx)
            acc_c = acc_c + rxa_conv[sx].astype(jnp.float32)
            acc_r = acc_r + rxa_res[sx].astype(jnp.float32)
        sa_conv[...] = acc_c.astype(jnp.bfloat16)
        sa_res[...] = acc_r.astype(jnp.bfloat16)
        for d in range(1, ny):
            ty = lax.rem(me_y + d, ny)
            send(0, sa_conv.at[:, :, pl.ds(ty * cyc, cyc)], rya_conv.at[me_y], base_ya + me_y, y_peers[d - 1])
            send(1, sa_res.at[:, :, pl.ds(ty * cyr, cyr)], rya_res.at[me_y], base_ya + me_y, y_peers[d - 1])
        own_a = [keep(0, 1, sa_conv.at[:, :, pl.ds(me_y * cyc, cyc)], rya_conv.at[me_y]),
                 keep(1, 1, sa_res.at[:, :, pl.ds(me_y * cyr, cyr)], rya_res.at[me_y])]

        for d in range(1, ny):
            sy = lax.rem(me_y + ny - d, ny)
            arrive(0, sx_conv.at[:, :, pl.ds(hc, hc), pl.ds(0, cyc)], ryb_conv.at[sy], base_yb + sy)
            arrive(1, sx_res.at[:, :, pl.ds(hr, hr), pl.ds(0, cyr)], ryb_res.at[sy], base_yb + sy)
        for copy in own_b:
            copy.wait()
        acc_c = ryb_conv[0].astype(jnp.float32)
        acc_r = ryb_res[0].astype(jnp.float32)
        for s in range(1, ny):
            acc_c = acc_c + ryb_conv[s].astype(jnp.float32)
            acc_r = acc_r + ryb_res[s].astype(jnp.float32)
        sb_conv[...] = acc_c.astype(jnp.bfloat16)
        sb_res[...] = acc_r.astype(jnp.bfloat16)
        for d in range(1, nx):
            tx = lax.rem(me_x + d, nx)
            send(0, sb_conv.at[tx], rxb_conv.at[me_x], base_xb + me_x, x_peers[d - 1])
            send(1, sb_res.at[tx], rxb_res.at[me_x], base_xb + me_x, x_peers[d - 1])

        for d in range(1, ny):
            sy = lax.rem(me_y + ny - d, ny)
            arrive(0, sa_conv.at[:, :, pl.ds(0, cyc)], rya_conv.at[sy], base_ya + sy)
            arrive(1, sa_res.at[:, :, pl.ds(0, cyr)], rya_res.at[sy], base_ya + sy)
        for copy in own_a:
            copy.wait()
        for d in range(1, nx):
            sx = lax.rem(me_x + nx - d, nx)
            arrive(0, sb_conv.at[sx], rxb_conv.at[sx], base_xb + sx)
            arrive(1, sb_res.at[sx], rxb_res.at[sx], base_xb + sx)
        top_c = rya_conv[0].astype(jnp.float32)
        top_r = rya_res[0].astype(jnp.float32)
        for s in range(1, ny):
            top_c = top_c + rya_conv[s].astype(jnp.float32)
            top_r = top_r + rya_res[s].astype(jnp.float32)
        low_c = sb_conv[me_x].astype(jnp.float32)
        low_r = sb_res[me_x].astype(jnp.float32)
        for d in range(1, nx):
            sx = lax.rem(me_x + nx - d, nx)
            low_c = low_c + rxb_conv[sx].astype(jnp.float32)
            low_r = low_r + rxb_res[sx].astype(jnp.float32)
        acc_c = jnp.concatenate([top_c, low_c], axis=1)
        acc_r = jnp.concatenate([top_r, low_r], axis=1)
        for zh in range(nzh):
            flip_c = acc_c[zh].T
            flip_r = acc_r[zh].T
            for zl in range(nzl):
                sz_conv[zh * nzl + zl] = flip_c[zl * cc:(zl + 1) * cc, :].astype(jnp.bfloat16)
                sz_res[zh * nzl + zl] = flip_r[zl * cr:(zl + 1) * cr, :].astype(jnp.bfloat16)

        for d in range(1, nz):
            tz = lax.rem(me_z + d, nz)
            send(0, sz_conv.at[tz], rz_conv.at[me_z], base_z + me_z, z_peers[d - 1])
            send(1, sz_res.at[tz], rz_res.at[me_z], base_z + me_z, z_peers[d - 1])
        for d in range(1, nz):
            sz = lax.rem(me_z + nz - d, nz)
            arrive(0, sz_conv.at[sz], rz_conv.at[sz], base_z + sz)
            arrive(1, sz_res.at[sz], rz_res.at[sz], base_z + sz)
        acc_c = sz_conv[me_z].astype(jnp.float32)
        acc_r = sz_res[me_z].astype(jnp.float32)
        for d in range(1, nz):
            sz = lax.rem(me_z + nz - d, nz)
            acc_c = acc_c + rz_conv[sz].astype(jnp.float32)
            acc_r = acc_r + rz_res[sz].astype(jnp.float32)
        conv_out[...] = acc_c * scale
        res_out[...] = acc_r * scale
        for copy in sends:
            copy.wait_send()

    vmem = pl.BlockSpec(memory_space=pltpu.VMEM)
    bf16, f32 = jnp.bfloat16, jnp.float32
    return pl.pallas_call(
        kernel,
        out_shape=(jax.ShapeDtypeStruct((cc, rc), f32), jax.ShapeDtypeStruct((cr, rr), f32)),
        in_specs=[vmem, vmem],
        out_specs=(vmem, vmem),
        scratch_shapes=[
            pltpu.VMEM((nx, nzh, 1, rc, n_conv), bf16),
            pltpu.VMEM((nx, nzh, 1, rr, n_res), bf16),
            pltpu.VMEM((nx, nzh, rc, n_conv), bf16),
            pltpu.VMEM((nx, nzh, rr, n_res), bf16),
            pltpu.VMEM((nx, nzh, hc, n_conv), bf16),
            pltpu.VMEM((nx, nzh, hr, n_res), bf16),
            pltpu.VMEM((ny, nx, nzh, hc, cyc), bf16),
            pltpu.VMEM((ny, nx, nzh, hr, cyr), bf16),
            pltpu.VMEM((nzh, hc, n_conv), bf16),
            pltpu.VMEM((nzh, hr, n_res), bf16),
            pltpu.VMEM((ny, nzh, hc, cyc), bf16),
            pltpu.VMEM((ny, nzh, hr, cyr), bf16),
            pltpu.VMEM((nx, nzh, hc, cyc), bf16),
            pltpu.VMEM((nx, nzh, hr, cyr), bf16),
            pltpu.VMEM((nx, nzh, hc, cyc), bf16),
            pltpu.VMEM((nx, nzh, hr, cyr), bf16),
            pltpu.VMEM((nz, cc, rc), bf16),
            pltpu.VMEM((nz, cr, rr), bf16),
            pltpu.VMEM((nz, cc, rc), bf16),
            pltpu.VMEM((nz, cr, rr), bf16),
            pltpu.SemaphoreType.DMA((2, n_slots)),
            pltpu.SemaphoreType.DMA((2, n_slots)),
            pltpu.SemaphoreType.DMA((2, 2)),
        ],
        compiler_params=pltpu.CompilerParams(collective_id=0, has_side_effects=True),
    )


def make_body(sizes):
    nx, nzh, nc, ny, nzl = sizes
    n_tm = nx * nzh * nc
    n_rep = ny * nzl

    def body(samples, grad_out, w_conv, w_res, lengths):
        sequence_rows = samples[0]
        cotangent = grad_out[0]
        seq_len = lengths[0]
        count_of_rows = sequence_rows.shape[0]
        channel_count = sequence_rows.shape[1]
        start_row = lax.axis_index(TM) * count_of_rows
        trailing_rows = sequence_rows[count_of_rows - DILATION_STEP :]
        arrived = passed_along(trailing_rows, TM, 1, n_tm)
        prior_samples = jnp.concatenate(
            [arrived, sequence_rows[: count_of_rows - DILATION_STEP]], 0
        )
        inputs = jnp.concatenate([prior_samples, sequence_rows], 1)
        in_length = (start_row + jnp.arange(count_of_rows) < seq_len).astype(jnp.float32)[:, None]
        gated, pre_grad = gate_backward(inputs, cotangent, in_length, w_conv, w_res)
        input_gradient = jnp.dot(pre_grad, w_conv.T, preferred_element_type=jnp.float32)
        incoming_gradient = passed_along(
            input_gradient[:DILATION_STEP, :channel_count].astype(jnp.bfloat16), TM, -1, n_tm
        ).astype(jnp.float32)
        delayed_gradient = jnp.concatenate(
            [input_gradient[DILATION_STEP:, :channel_count], incoming_gradient], 0
        )
        grad_rows = (
            cotangent.astype(jnp.float32) + input_gradient[:, channel_count:] + delayed_gradient
        ).astype(jnp.bfloat16)
        term_conv = jnp.einsum("tk,tn->kn", inputs, pre_grad, preferred_element_type=jnp.float32)
        term_res = jnp.einsum("tk,tn->kn", gated, cotangent, preferred_element_type=jnp.float32)
        kc, n_conv = term_conv.shape
        kr, n_res = term_res.shape
        rc, rr = kc // n_tm, kr // n_tm
        all_tokens = count_of_rows * n_tm * n_rep
        reducer = make_reducer(sizes, rc, n_conv, rr, n_res, float(all_tokens) ** (-0.5))
        flip_conv, flip_res = reducer(
            term_conv.astype(jnp.bfloat16).reshape(nx, nzh, nc, rc, n_conv),
            term_res.astype(jnp.bfloat16).reshape(nx, nzh, nc, rr, n_res),
        )
        return (grad_rows[None], flip_conv.T, flip_res.T)

    return body


def solution(mesh):
    n_tm, n_rep = mesh.devices.shape
    nc = 2
    nzh = 2
    nx = n_tm // (nc * nzh)
    nzl = 8
    ny = n_rep // nzl
    sizes = (nx, nzh, nc, ny, nzl)
    fine = Mesh(mesh.devices.reshape(sizes), ("x", "zh", "c", "y", "zl"))
    return jax.shard_map(
        make_body(sizes),
        mesh=fine,
        in_specs=(P(REP, TM, None), P(REP, TM, None), P(), P(), P(REP)),
        out_specs=(P(REP, TM, None), P(TM, REP), P(TM, REP)),
        check_vma=False,
    )
```

```python
import jax
import jax.numpy as jnp
from jax import lax
from jax.experimental import pallas as pl
from jax.experimental.pallas import tpu as pltpu
from jax.sharding import Mesh, PartitionSpec as P

DILATION_STEP = 256
TM = ("x", "zh", "c")
REP = ("y", "zl")


def passed_along(array, axis, by, length):
    pairs = [(i, i + by) for i in range(length) if 0 <= i + by < length]
    return lax.ppermute(array, axis, pairs)


def gate_backward(inputs, cotangent, in_length, w_conv, w_res):
    channel_count = w_res.shape[0]
    pre_act = jnp.dot(inputs, w_conv, preferred_element_type=jnp.float32)
    tanh_f = jnp.tanh(pre_act[:, :channel_count])
    sig_g = jax.nn.sigmoid(pre_act[:, channel_count:])
    gated = (in_length * tanh_f * sig_g).astype(jnp.bfloat16)
    gated_grad = in_length * jnp.dot(cotangent, w_res.T, preferred_element_type=jnp.float32)
    pre_grad = jnp.concatenate(
        [gated_grad * sig_g * (1.0 - tanh_f * tanh_f), gated_grad * tanh_f * sig_g * (1.0 - sig_g)],
        1,
    ).astype(jnp.bfloat16)
    return (gated, pre_grad)


def make_reducer(sizes, rc, n_conv, rr, n_res, scale):
    nx, nzh, nc, ny, nzl = sizes
    nz = nzh * nzl
    cyc, cyr = n_conv // ny, n_res // ny
    cc, cr = cyc // nzl, cyr // nzl
    hc, hr = rc // 2, rr // 2
    base_xa, base_yb = 1, 1 + nx
    base_ya, base_xb = 1 + nx + ny, 1 + nx + 2 * ny
    base_z = 1 + 2 * nx + 2 * ny
    n_slots = base_z + nz
    n_peers = (nc - 1) + (nx - 1) + (ny - 1) + (nz - 1)
    mesh_id = pl.DeviceIdType.MESH

    def kernel(conv_ref, res_ref, conv_out, res_out,
               rc_conv, rc_res, sx_conv, sx_res,
               rxa_conv, rxa_res, ryb_conv, ryb_res,
               sa_conv, sa_res, rya_conv, rya_res,
               sb_conv, sb_res, rxb_conv, rxb_res,
               sz_conv, sz_res, rz_conv, rz_res,
               send_sems, recv_sems, local_sems):
        me_x = lax.axis_index("x")
        me_zh = lax.axis_index("zh")
        me_c = lax.axis_index("c")
        me_y = lax.axis_index("y")
        me_zl = lax.axis_index("zl")
        me_z = me_zh * nzl + me_zl
        other_c = 1 - me_c

        def dev(x=None, zh=None, c=None, y=None, zl=None):
            return (me_x if x is None else x, me_zh if zh is None else zh,
                    me_c if c is None else c, me_y if y is None else y,
                    me_zl if zl is None else zl)

        peers = [dev(c=other_c)]
        x_peers = [dev(x=lax.rem(me_x + d, nx)) for d in range(1, nx)]
        y_peers = [dev(y=lax.rem(me_y + d, ny)) for d in range(1, ny)]
        z_peers = []
        for d in range(1, nz):
            q = lax.rem(me_z + d, nz)
            z_peers.append(dev(zh=q // nzl, zl=lax.rem(q, nzl)))
        barrier = pltpu.get_barrier_semaphore()
        for peer in peers + x_peers + y_peers + z_peers:
            pl.semaphore_signal(barrier, inc=1, device_id=peer, device_id_type=mesh_id)
        pl.semaphore_wait(barrier, n_peers)

        sends = []

        def send(kind, src, dst, slot, peer):
            copy = pltpu.make_async_remote_copy(
                src_ref=src, dst_ref=dst, send_sem=send_sems.at[kind, slot],
                recv_sem=recv_sems.at[kind, slot], device_id=peer, device_id_type=mesh_id)
            copy.start()
            sends.append(copy)

        def arrive(kind, src, dst, slot):
            pltpu.make_async_remote_copy(
                src_ref=src, dst_ref=dst, send_sem=send_sems.at[kind, slot],
                recv_sem=recv_sems.at[kind, slot], device_id=dev(),
                device_id_type=mesh_id).wait_recv()

        def keep(kind, which, src, dst):
            copy = pltpu.make_async_copy(src, dst, local_sems.at[kind, which])
            copy.start()
            return copy

        send(0, conv_ref.at[:, :, pl.ds(other_c, 1)], rc_conv, 0, peers[0])
        send(1, res_ref.at[:, :, pl.ds(other_c, 1)], rc_res, 0, peers[0])
        arrive(0, conv_ref.at[:, :, pl.ds(other_c, 1)], rc_conv, 0)
        arrive(1, res_ref.at[:, :, pl.ds(other_c, 1)], rc_res, 0)
        for x in range(nx):
            for zh in range(nzh):
                own_c = conv_ref[x, zh, pl.ds(me_c, 1)][0].astype(jnp.float32)
                sx_conv[x, zh] = (own_c + rc_conv[x, zh, 0].astype(jnp.float32)).astype(jnp.bfloat16)
                own_r = res_ref[x, zh, pl.ds(me_c, 1)][0].astype(jnp.float32)
                sx_res[x, zh] = (own_r + rc_res[x, zh, 0].astype(jnp.float32)).astype(jnp.bfloat16)

        for d in range(1, nx):
            tx = lax.rem(me_x + d, nx)
            send(0, sx_conv.at[tx, :, pl.ds(0, hc)], rxa_conv.at[me_x], base_xa + me_x, x_peers[d - 1])
            send(1, sx_res.at[tx, :, pl.ds(0, hr)], rxa_res.at[me_x], base_xa + me_x, x_peers[d - 1])
        for d in range(1, ny):
            ty = lax.rem(me_y + d, ny)
            send(0, sx_conv.at[:, :, pl.ds(hc, hc), pl.ds(ty * cyc, cyc)], ryb_conv.at[me_y],
                 base_yb + me_y, y_peers[d - 1])
            send(1, sx_res.at[:, :, pl.ds(hr, hr), pl.ds(ty * cyr, cyr)], ryb_res.at[me_y],
                 base_yb + me_y, y_peers[d - 1])
        own_b = [keep(0, 0, sx_conv.at[:, :, pl.ds(hc, hc), pl.ds(me_y * cyc, cyc)], ryb_conv.at[me_y]),
                 keep(1, 0, sx_res.at[:, :, pl.ds(hr, hr), pl.ds(me_y * cyr, cyr)], ryb_res.at[me_y])]

        for d in range(1, nx):
            sx = lax.rem(me_x + nx - d, nx)
            arrive(0, sx_conv.at[sx, :, pl.ds(0, hc)], rxa_conv.at[sx], base_xa + sx)
            arrive(1, sx_res.at[sx, :, pl.ds(0, hr)], rxa_res.at[sx], base_xa + sx)
        acc_c = sx_conv[me_x, :, :hc].astype(jnp.float32)
        acc_r = sx_res[me_x, :, :hr].astype(jnp.float32)
        for d in range(1, nx):
            sx = lax.rem(me_x + nx - d, nx)
            acc_c = acc_c + rxa_conv[sx].astype(jnp.float32)
            acc_r = acc_r + rxa_res[sx].astype(jnp.float32)
        sa_conv[...] = acc_c.astype(jnp.bfloat16)
        sa_res[...] = acc_r.astype(jnp.bfloat16)
        for d in range(1, ny):
            ty = lax.rem(me_y + d, ny)
            send(0, sa_conv.at[:, :, pl.ds(ty * cyc, cyc)], rya_conv.at[me_y], base_ya + me_y, y_peers[d - 1])
            send(1, sa_res.at[:, :, pl.ds(ty * cyr, cyr)], rya_res.at[me_y], base_ya + me_y, y_peers[d - 1])
        own_a = [keep(0, 1, sa_conv.at[:, :, pl.ds(me_y * cyc, cyc)], rya_conv.at[me_y]),
                 keep(1, 1, sa_res.at[:, :, pl.ds(me_y * cyr, cyr)], rya_res.at[me_y])]

        for d in range(1, ny):
            sy = lax.rem(me_y + ny - d, ny)
            arrive(0, sx_conv.at[:, :, pl.ds(hc, hc), pl.ds(0, cyc)], ryb_conv.at[sy], base_yb + sy)
            arrive(1, sx_res.at[:, :, pl.ds(hr, hr), pl.ds(0, cyr)], ryb_res.at[sy], base_yb + sy)
        for copy in own_b:
            copy.wait()
        acc_c = ryb_conv[0].astype(jnp.float32)
        acc_r = ryb_res[0].astype(jnp.float32)
        for s in range(1, ny):
            acc_c = acc_c + ryb_conv[s].astype(jnp.float32)
            acc_r = acc_r + ryb_res[s].astype(jnp.float32)
        sb_conv[...] = acc_c.astype(jnp.bfloat16)
        sb_res[...] = acc_r.astype(jnp.bfloat16)
        for d in range(1, nx):
            tx = lax.rem(me_x + d, nx)
            send(0, sb_conv.at[tx], rxb_conv.at[me_x], base_xb + me_x, x_peers[d - 1])
            send(1, sb_res.at[tx], rxb_res.at[me_x], base_xb + me_x, x_peers[d - 1])

        for d in range(1, ny):
            sy = lax.rem(me_y + ny - d, ny)
            arrive(0, sa_conv.at[:, :, pl.ds(0, cyc)], rya_conv.at[sy], base_ya + sy)
            arrive(1, sa_res.at[:, :, pl.ds(0, cyr)], rya_res.at[sy], base_ya + sy)
        for copy in own_a:
            copy.wait()
        for d in range(1, nx):
            sx = lax.rem(me_x + nx - d, nx)
            arrive(0, sb_conv.at[sx], rxb_conv.at[sx], base_xb + sx)
            arrive(1, sb_res.at[sx], rxb_res.at[sx], base_xb + sx)
        top_c = rya_conv[0].astype(jnp.float32)
        top_r = rya_res[0].astype(jnp.float32)
        for s in range(1, ny):
            top_c = top_c + rya_conv[s].astype(jnp.float32)
            top_r = top_r + rya_res[s].astype(jnp.float32)
        low_c = sb_conv[me_x].astype(jnp.float32)
        low_r = sb_res[me_x].astype(jnp.float32)
        for d in range(1, nx):
            sx = lax.rem(me_x + nx - d, nx)
            low_c = low_c + rxb_conv[sx].astype(jnp.float32)
            low_r = low_r + rxb_res[sx].astype(jnp.float32)
        acc_c = jnp.concatenate([top_c, low_c], axis=1)
        acc_r = jnp.concatenate([top_r, low_r], axis=1)
        for zh in range(nzh):
            flip_c = acc_c[zh].T
            flip_r = acc_r[zh].T
            for zl in range(nzl):
                sz_conv[zh * nzl + zl] = flip_c[zl * cc:(zl + 1) * cc, :].astype(jnp.bfloat16)
                sz_res[zh * nzl + zl] = flip_r[zl * cr:(zl + 1) * cr, :].astype(jnp.bfloat16)

        for d in range(1, nz):
            tz = lax.rem(me_z + d, nz)
            send(0, sz_conv.at[tz], rz_conv.at[me_z], base_z + me_z, z_peers[d - 1])
            send(1, sz_res.at[tz], rz_res.at[me_z], base_z + me_z, z_peers[d - 1])
        for d in range(1, nz):
            sz = lax.rem(me_z + nz - d, nz)
            arrive(0, sz_conv.at[sz], rz_conv.at[sz], base_z + sz)
            arrive(1, sz_res.at[sz], rz_res.at[sz], base_z + sz)
        acc_c = sz_conv[me_z].astype(jnp.float32)
        acc_r = sz_res[me_z].astype(jnp.float32)
        for d in range(1, nz):
            sz = lax.rem(me_z + nz - d, nz)
            acc_c = acc_c + rz_conv[sz].astype(jnp.float32)
            acc_r = acc_r + rz_res[sz].astype(jnp.float32)
        conv_out[...] = acc_c * scale
        res_out[...] = acc_r * scale
        for copy in sends:
            copy.wait_send()

    vmem = pl.BlockSpec(memory_space=pltpu.VMEM)
    bf16, f32 = jnp.bfloat16, jnp.float32
    return pl.pallas_call(
        kernel,
        out_shape=(jax.ShapeDtypeStruct((cc, rc), f32), jax.ShapeDtypeStruct((cr, rr), f32)),
        in_specs=[vmem, vmem],
        out_specs=(vmem, vmem),
        scratch_shapes=[
            pltpu.VMEM((nx, nzh, 1, rc, n_conv), bf16),
            pltpu.VMEM((nx, nzh, 1, rr, n_res), bf16),
            pltpu.VMEM((nx, nzh, rc, n_conv), bf16),
            pltpu.VMEM((nx, nzh, rr, n_res), bf16),
            pltpu.VMEM((nx, nzh, hc, n_conv), bf16),
            pltpu.VMEM((nx, nzh, hr, n_res), bf16),
            pltpu.VMEM((ny, nx, nzh, hc, cyc), bf16),
            pltpu.VMEM((ny, nx, nzh, hr, cyr), bf16),
            pltpu.VMEM((nzh, hc, n_conv), bf16),
            pltpu.VMEM((nzh, hr, n_res), bf16),
            pltpu.VMEM((ny, nzh, hc, cyc), bf16),
            pltpu.VMEM((ny, nzh, hr, cyr), bf16),
            pltpu.VMEM((nx, nzh, hc, cyc), bf16),
            pltpu.VMEM((nx, nzh, hr, cyr), bf16),
            pltpu.VMEM((nx, nzh, hc, cyc), bf16),
            pltpu.VMEM((nx, nzh, hr, cyr), bf16),
            pltpu.VMEM((nz, cc, rc), bf16),
            pltpu.VMEM((nz, cr, rr), bf16),
            pltpu.VMEM((nz, cc, rc), bf16),
            pltpu.VMEM((nz, cr, rr), bf16),
            pltpu.SemaphoreType.DMA((2, n_slots)),
            pltpu.SemaphoreType.DMA((2, n_slots)),
            pltpu.SemaphoreType.DMA((2, 2)),
        ],
        compiler_params=pltpu.CompilerParams(collective_id=0, has_side_effects=True),
    )


def make_halo(sizes):
    nx, nzh, nc, ny, nzl = sizes
    n_tm = nx * nzh * nc
    mesh_id = pl.DeviceIdType.MESH

    def kernel(src_ref, out_ref, buf, send_sem, recv_sem):
        me_y = lax.axis_index("y")
        me_zl = lax.axis_index("zl")
        t = (lax.axis_index("x") * nzh + lax.axis_index("zh")) * nc + lax.axis_index("c")

        def dev(u):
            return (u // (nzh * nc), lax.rem(u // nc, nzh), lax.rem(u, nc), me_y, me_zl)

        nxt = jnp.minimum(t + 1, n_tm - 1)
        prv = jnp.maximum(t - 1, 0)
        has_next = t < n_tm - 1
        has_prev = t > 0
        barrier = pltpu.get_barrier_semaphore()

        @pl.when(has_next)
        def _():
            pl.semaphore_signal(barrier, inc=1, device_id=dev(nxt), device_id_type=mesh_id)

        @pl.when(has_prev)
        def _():
            pl.semaphore_signal(barrier, inc=1, device_id=dev(prv), device_id_type=mesh_id)

        pl.semaphore_wait(barrier, (1 - (t + 1) // n_tm) + (t + n_tm - 1) // n_tm)

        copy = pltpu.make_async_remote_copy(
            src_ref=src_ref, dst_ref=buf, send_sem=send_sem, recv_sem=recv_sem,
            device_id=dev(nxt), device_id_type=mesh_id)

        @pl.when(has_next)
        def _():
            copy.start()

        @pl.when(has_prev)
        def _():
            copy.wait_recv()
            out_ref[...] = buf[...]

        @pl.when(t == 0)
        def _():
            out_ref[...] = jnp.zeros_like(out_ref)

        @pl.when(has_next)
        def _():
            copy.wait_send()

    vmem = pl.BlockSpec(memory_space=pltpu.VMEM)

    def call(rows):
        return pl.pallas_call(
            kernel,
            out_shape=jax.ShapeDtypeStruct(rows.shape, rows.dtype),
            in_specs=[vmem],
            out_specs=vmem,
            scratch_shapes=[
                pltpu.VMEM(rows.shape, rows.dtype),
                pltpu.SemaphoreType.DMA(()),
                pltpu.SemaphoreType.DMA(()),
            ],
            compiler_params=pltpu.CompilerParams(collective_id=1, has_side_effects=True),
        )(rows)

    return call


def make_body(sizes):
    nx, nzh, nc, ny, nzl = sizes
    n_tm = nx * nzh * nc
    n_rep = ny * nzl

    def body(samples, grad_out, w_conv, w_res, lengths):
        sequence_rows = samples[0]
        cotangent = grad_out[0]
        seq_len = lengths[0]
        count_of_rows = sequence_rows.shape[0]
        channel_count = sequence_rows.shape[1]
        start_row = lax.axis_index(TM) * count_of_rows
        trailing_rows = sequence_rows[count_of_rows - DILATION_STEP :]
        arrived = make_halo(sizes)(trailing_rows)
        prior_samples = jnp.concatenate(
            [arrived, sequence_rows[: count_of_rows - DILATION_STEP]], 0
        )
        inputs = jnp.concatenate([prior_samples, sequence_rows], 1)
        in_length = (start_row + jnp.arange(count_of_rows) < seq_len).astype(jnp.float32)[:, None]
        gated, pre_grad = gate_backward(inputs, cotangent, in_length, w_conv, w_res)
        input_gradient = jnp.dot(pre_grad, w_conv.T, preferred_element_type=jnp.float32)
        incoming_gradient = passed_along(
            input_gradient[:DILATION_STEP, :channel_count].astype(jnp.bfloat16), TM, -1, n_tm
        ).astype(jnp.float32)
        delayed_gradient = jnp.concatenate(
            [input_gradient[DILATION_STEP:, :channel_count], incoming_gradient], 0
        )
        grad_rows = (
            cotangent.astype(jnp.float32) + input_gradient[:, channel_count:] + delayed_gradient
        ).astype(jnp.bfloat16)
        term_conv = jnp.einsum("tk,tn->kn", inputs, pre_grad, preferred_element_type=jnp.float32)
        term_res = jnp.einsum("tk,tn->kn", gated, cotangent, preferred_element_type=jnp.float32)
        kc, n_conv = term_conv.shape
        kr, n_res = term_res.shape
        rc, rr = kc // n_tm, kr // n_tm
        all_tokens = count_of_rows * n_tm * n_rep
        reducer = make_reducer(sizes, rc, n_conv, rr, n_res, float(all_tokens) ** (-0.5))
        flip_conv, flip_res = reducer(
            term_conv.astype(jnp.bfloat16).reshape(nx, nzh, nc, rc, n_conv),
            term_res.astype(jnp.bfloat16).reshape(nx, nzh, nc, rr, n_res),
        )
        return (grad_rows[None], flip_conv.T, flip_res.T)

    return body


def solution(mesh):
    n_tm, n_rep = mesh.devices.shape
    nc = 2
    nzh = 2
    nx = n_tm // (nc * nzh)
    nzl = 8
    ny = n_rep // nzl
    sizes = (nx, nzh, nc, ny, nzl)
    fine = Mesh(mesh.devices.reshape(sizes), ("x", "zh", "c", "y", "zl"))
    return jax.shard_map(
        make_body(sizes),
        mesh=fine,
        in_specs=(P(REP, TM, None), P(REP, TM, None), P(), P(), P(REP)),
        out_specs=(P(REP, TM, None), P(TM, REP), P(TM, REP)),
        check_vma=False,
    )
```

```python
import jax
import jax.numpy as jnp
from jax import lax
from jax.experimental import pallas as pl
from jax.experimental.pallas import tpu as pltpu
from jax.sharding import Mesh, PartitionSpec as P

DILATION_STEP = 256
TM = ("x", "zh", "c")
REP = ("y", "zl")


def passed_along(array, axis, by, length):
    pairs = [(i, i + by) for i in range(length) if 0 <= i + by < length]
    return lax.ppermute(array, axis, pairs)


def gate_backward(inputs, cotangent, in_length, w_conv, w_res):
    channel_count = w_res.shape[0]
    pre_act = jnp.dot(inputs, w_conv, preferred_element_type=jnp.float32)
    tanh_f = jnp.tanh(pre_act[:, :channel_count])
    sig_g = jax.nn.sigmoid(pre_act[:, channel_count:])
    gated = (in_length * tanh_f * sig_g).astype(jnp.bfloat16)
    gated_grad = in_length * jnp.dot(cotangent, w_res.T, preferred_element_type=jnp.float32)
    pre_grad = jnp.concatenate(
        [gated_grad * sig_g * (1.0 - tanh_f * tanh_f), gated_grad * tanh_f * sig_g * (1.0 - sig_g)],
        1,
    ).astype(jnp.bfloat16)
    return (gated, pre_grad)


def make_reducer(sizes, rc, n_conv, rr, n_res, scale):
    nx, nzh, nc, ny, nzl = sizes
    nz = nzh * nzl
    cyc, cyr = n_conv // ny, n_res // ny
    cc, cr = cyc // nzl, cyr // nzl
    hc, hr = rc // 2, rr // 2
    base_xa, base_yb = 1, 1 + nx
    base_ya, base_xb = 1 + nx + ny, 1 + nx + 2 * ny
    base_z = 1 + 2 * nx + 2 * ny
    n_slots = base_z + nz
    n_peers = (nc - 1) + (nx - 1) + (ny - 1) + (nz - 1)
    mesh_id = pl.DeviceIdType.MESH

    def kernel(conv_ref, res_ref, conv_out, res_out,
               rc_conv, rc_res, sx_conv, sx_res,
               rxa_conv, rxa_res, ryb_conv, ryb_res,
               sa_conv, sa_res, rya_conv, rya_res,
               sb_conv, sb_res, rxb_conv, rxb_res,
               sz_conv, sz_res, rz_conv, rz_res,
               send_sems, recv_sems, local_sems):
        me_x = lax.axis_index("x")
        me_zh = lax.axis_index("zh")
        me_c = lax.axis_index("c")
        me_y = lax.axis_index("y")
        me_zl = lax.axis_index("zl")
        me_z = me_zh * nzl + me_zl
        other_c = 1 - me_c

        def dev(x=None, zh=None, c=None, y=None, zl=None):
            return (me_x if x is None else x, me_zh if zh is None else zh,
                    me_c if c is None else c, me_y if y is None else y,
                    me_zl if zl is None else zl)

        peers = [dev(c=other_c)]
        x_peers = [dev(x=lax.rem(me_x + d, nx)) for d in range(1, nx)]
        y_peers = [dev(y=lax.rem(me_y + d, ny)) for d in range(1, ny)]
        z_peers = []
        for d in range(1, nz):
            q = lax.rem(me_z + d, nz)
            z_peers.append(dev(zh=q // nzl, zl=lax.rem(q, nzl)))
        barrier = pltpu.get_barrier_semaphore()
        for peer in peers + x_peers + y_peers + z_peers:
            pl.semaphore_signal(barrier, inc=1, device_id=peer, device_id_type=mesh_id)
        pl.semaphore_wait(barrier, n_peers)

        sends = []

        def send(kind, src, dst, slot, peer):
            copy = pltpu.make_async_remote_copy(
                src_ref=src, dst_ref=dst, send_sem=send_sems.at[kind, slot],
                recv_sem=recv_sems.at[kind, slot], device_id=peer, device_id_type=mesh_id)
            copy.start()
            sends.append(copy)

        def arrive(kind, src, dst, slot):
            pltpu.make_async_remote_copy(
                src_ref=src, dst_ref=dst, send_sem=send_sems.at[kind, slot],
                recv_sem=recv_sems.at[kind, slot], device_id=dev(),
                device_id_type=mesh_id).wait_recv()

        def keep(kind, which, src, dst):
            copy = pltpu.make_async_copy(src, dst, local_sems.at[kind, which])
            copy.start()
            return copy

        send(0, conv_ref.at[:, :, pl.ds(other_c, 1)], rc_conv, 0, peers[0])
        send(1, res_ref.at[:, :, pl.ds(other_c, 1)], rc_res, 0, peers[0])
        arrive(0, conv_ref.at[:, :, pl.ds(other_c, 1)], rc_conv, 0)
        arrive(1, res_ref.at[:, :, pl.ds(other_c, 1)], rc_res, 0)
        for x in range(nx):
            for zh in range(nzh):
                own_c = conv_ref[x, zh, pl.ds(me_c, 1)][0].astype(jnp.float32)
                sx_conv[x, zh] = (own_c + rc_conv[x, zh, 0].astype(jnp.float32)).astype(jnp.bfloat16)
                own_r = res_ref[x, zh, pl.ds(me_c, 1)][0].astype(jnp.float32)
                sx_res[x, zh] = (own_r + rc_res[x, zh, 0].astype(jnp.float32)).astype(jnp.bfloat16)

        for d in range(1, nx):
            tx = lax.rem(me_x + d, nx)
            send(0, sx_conv.at[tx, :, pl.ds(0, hc)], rxa_conv.at[me_x], base_xa + me_x, x_peers[d - 1])
            send(1, sx_res.at[tx, :, pl.ds(0, hr)], rxa_res.at[me_x], base_xa + me_x, x_peers[d - 1])
        for d in range(1, ny):
            ty = lax.rem(me_y + d, ny)
            send(0, sx_conv.at[:, :, pl.ds(hc, hc), pl.ds(ty * cyc, cyc)], ryb_conv.at[me_y],
                 base_yb + me_y, y_peers[d - 1])
            send(1, sx_res.at[:, :, pl.ds(hr, hr), pl.ds(ty * cyr, cyr)], ryb_res.at[me_y],
                 base_yb + me_y, y_peers[d - 1])
        own_b = [keep(0, 0, sx_conv.at[:, :, pl.ds(hc, hc), pl.ds(me_y * cyc, cyc)], ryb_conv.at[me_y]),
                 keep(1, 0, sx_res.at[:, :, pl.ds(hr, hr), pl.ds(me_y * cyr, cyr)], ryb_res.at[me_y])]

        for d in range(1, nx):
            sx = lax.rem(me_x + nx - d, nx)
            arrive(0, sx_conv.at[sx, :, pl.ds(0, hc)], rxa_conv.at[sx], base_xa + sx)
            arrive(1, sx_res.at[sx, :, pl.ds(0, hr)], rxa_res.at[sx], base_xa + sx)
        acc_c = sx_conv[me_x, :, :hc].astype(jnp.float32)
        acc_r = sx_res[me_x, :, :hr].astype(jnp.float32)
        for d in range(1, nx):
            sx = lax.rem(me_x + nx - d, nx)
            acc_c = acc_c + rxa_conv[sx].astype(jnp.float32)
            acc_r = acc_r + rxa_res[sx].astype(jnp.float32)
        sa_conv[...] = acc_c.astype(jnp.bfloat16)
        sa_res[...] = acc_r.astype(jnp.bfloat16)
        for d in range(1, ny):
            ty = lax.rem(me_y + d, ny)
            send(0, sa_conv.at[:, :, pl.ds(ty * cyc, cyc)], rya_conv.at[me_y], base_ya + me_y, y_peers[d - 1])
            send(1, sa_res.at[:, :, pl.ds(ty * cyr, cyr)], rya_res.at[me_y], base_ya + me_y, y_peers[d - 1])
        own_a = [keep(0, 1, sa_conv.at[:, :, pl.ds(me_y * cyc, cyc)], rya_conv.at[me_y]),
                 keep(1, 1, sa_res.at[:, :, pl.ds(me_y * cyr, cyr)], rya_res.at[me_y])]

        for d in range(1, ny):
            sy = lax.rem(me_y + ny - d, ny)
            arrive(0, sx_conv.at[:, :, pl.ds(hc, hc), pl.ds(0, cyc)], ryb_conv.at[sy], base_yb + sy)
            arrive(1, sx_res.at[:, :, pl.ds(hr, hr), pl.ds(0, cyr)], ryb_res.at[sy], base_yb + sy)
        for copy in own_b:
            copy.wait()
        acc_c = ryb_conv[0].astype(jnp.float32)
        acc_r = ryb_res[0].astype(jnp.float32)
        for s in range(1, ny):
            acc_c = acc_c + ryb_conv[s].astype(jnp.float32)
            acc_r = acc_r + ryb_res[s].astype(jnp.float32)
        sb_conv[...] = acc_c.astype(jnp.bfloat16)
        sb_res[...] = acc_r.astype(jnp.bfloat16)
        for d in range(1, nx):
            tx = lax.rem(me_x + d, nx)
            send(0, sb_conv.at[tx], rxb_conv.at[me_x], base_xb + me_x, x_peers[d - 1])
            send(1, sb_res.at[tx], rxb_res.at[me_x], base_xb + me_x, x_peers[d - 1])

        for d in range(1, ny):
            sy = lax.rem(me_y + ny - d, ny)
            arrive(0, sa_conv.at[:, :, pl.ds(0, cyc)], rya_conv.at[sy], base_ya + sy)
            arrive(1, sa_res.at[:, :, pl.ds(0, cyr)], rya_res.at[sy], base_ya + sy)
        for copy in own_a:
            copy.wait()
        for d in range(1, nx):
            sx = lax.rem(me_x + nx - d, nx)
            arrive(0, sb_conv.at[sx], rxb_conv.at[sx], base_xb + sx)
            arrive(1, sb_res.at[sx], rxb_res.at[sx], base_xb + sx)
        top_c = rya_conv[0].astype(jnp.float32)
        top_r = rya_res[0].astype(jnp.float32)
        for s in range(1, ny):
            top_c = top_c + rya_conv[s].astype(jnp.float32)
            top_r = top_r + rya_res[s].astype(jnp.float32)
        low_c = sb_conv[me_x].astype(jnp.float32)
        low_r = sb_res[me_x].astype(jnp.float32)
        for d in range(1, nx):
            sx = lax.rem(me_x + nx - d, nx)
            low_c = low_c + rxb_conv[sx].astype(jnp.float32)
            low_r = low_r + rxb_res[sx].astype(jnp.float32)
        acc_c = jnp.concatenate([top_c, low_c], axis=1)
        acc_r = jnp.concatenate([top_r, low_r], axis=1)
        for zh in range(nzh):
            flip_c = acc_c[zh].T
            flip_r = acc_r[zh].T
            for zl in range(nzl):
                sz_conv[zh * nzl + zl] = flip_c[zl * cc:(zl + 1) * cc, :].astype(jnp.bfloat16)
                sz_res[zh * nzl + zl] = flip_r[zl * cr:(zl + 1) * cr, :].astype(jnp.bfloat16)

        for d in range(1, nz):
            tz = lax.rem(me_z + d, nz)
            send(0, sz_conv.at[tz], rz_conv.at[me_z], base_z + me_z, z_peers[d - 1])
            send(1, sz_res.at[tz], rz_res.at[me_z], base_z + me_z, z_peers[d - 1])
        for d in range(1, nz):
            sz = lax.rem(me_z + nz - d, nz)
            arrive(0, sz_conv.at[sz], rz_conv.at[sz], base_z + sz)
            arrive(1, sz_res.at[sz], rz_res.at[sz], base_z + sz)
        acc_c = sz_conv[me_z].astype(jnp.float32)
        acc_r = sz_res[me_z].astype(jnp.float32)
        for d in range(1, nz):
            sz = lax.rem(me_z + nz - d, nz)
            acc_c = acc_c + rz_conv[sz].astype(jnp.float32)
            acc_r = acc_r + rz_res[sz].astype(jnp.float32)
        conv_out[...] = acc_c * scale
        res_out[...] = acc_r * scale
        for copy in sends:
            copy.wait_send()

    vmem = pl.BlockSpec(memory_space=pltpu.VMEM)
    bf16, f32 = jnp.bfloat16, jnp.float32
    return pl.pallas_call(
        kernel,
        out_shape=(jax.ShapeDtypeStruct((cc, rc), f32), jax.ShapeDtypeStruct((cr, rr), f32)),
        in_specs=[vmem, vmem],
        out_specs=(vmem, vmem),
        scratch_shapes=[
            pltpu.VMEM((nx, nzh, 1, rc, n_conv), bf16),
            pltpu.VMEM((nx, nzh, 1, rr, n_res), bf16),
            pltpu.VMEM((nx, nzh, rc, n_conv), bf16),
            pltpu.VMEM((nx, nzh, rr, n_res), bf16),
            pltpu.VMEM((nx, nzh, hc, n_conv), bf16),
            pltpu.VMEM((nx, nzh, hr, n_res), bf16),
            pltpu.VMEM((ny, nx, nzh, hc, cyc), bf16),
            pltpu.VMEM((ny, nx, nzh, hr, cyr), bf16),
            pltpu.VMEM((nzh, hc, n_conv), bf16),
            pltpu.VMEM((nzh, hr, n_res), bf16),
            pltpu.VMEM((ny, nzh, hc, cyc), bf16),
            pltpu.VMEM((ny, nzh, hr, cyr), bf16),
            pltpu.VMEM((nx, nzh, hc, cyc), bf16),
            pltpu.VMEM((nx, nzh, hr, cyr), bf16),
            pltpu.VMEM((nx, nzh, hc, cyc), bf16),
            pltpu.VMEM((nx, nzh, hr, cyr), bf16),
            pltpu.VMEM((nz, cc, rc), bf16),
            pltpu.VMEM((nz, cr, rr), bf16),
            pltpu.VMEM((nz, cc, rc), bf16),
            pltpu.VMEM((nz, cr, rr), bf16),
            pltpu.SemaphoreType.DMA((2, n_slots)),
            pltpu.SemaphoreType.DMA((2, n_slots)),
            pltpu.SemaphoreType.DMA((2, 2)),
        ],
        compiler_params=pltpu.CompilerParams(collective_id=0, has_side_effects=True),
    )


def make_halo(sizes):
    nx, nzh, nc, ny, nzl = sizes
    n_tm = nx * nzh * nc
    nz = nzh * nzl
    quarter = nz // 4
    mesh_id = pl.DeviceIdType.MESH

    def kernel(src_ref, out_ref, buf_f, rel_a, rel_b, buf_a, buf_b, send_sems, recv_sems):
        me_x = lax.axis_index("x")
        me_c = lax.axis_index("c")
        me_y = lax.axis_index("y")
        me_zl = lax.axis_index("zl")
        me_z = lax.axis_index("zh") * nzl + me_zl
        t = (me_x * nzh + lax.axis_index("zh")) * nc + me_c
        half = src_ref.shape[0] // 2

        def dev(x, z, c):
            return (x, z // nzl, c, me_y, lax.rem(z, nzl))

        def dest_of(x, z):
            t_d = lax.rem((x * nzh + z // nzl) * nc + nc, n_tm)
            return dev(t_d // (nzh * nc), lax.rem(t_d // nc, nzh) * nzl + lax.rem(z, nzl), 0)

        def copy(src, dst, k, peer):
            return pltpu.make_async_remote_copy(
                src_ref=src, dst_ref=dst, send_sem=send_sems.at[k], recv_sem=recv_sems.at[k],
                device_id=peer, device_id_type=mesh_id)

        barrier = pltpu.get_barrier_semaphore()

        @pl.when(me_c == 0)
        def _():
            t_s = lax.rem(t + n_tm - 1, n_tm)
            x_s = t_s // (nzh * nc)
            z_s = lax.rem(t_s // nc, nzh) * nzl + me_zl
            partner = dev(me_x, me_z, 1)
            up = dev(x_s, lax.rem(z_s + quarter, nz), 1)
            down = dev(x_s, lax.rem(z_s + nz - quarter, nz), 1)
            for peer in (partner, up, down):
                pl.semaphore_signal(barrier, inc=1, device_id=peer, device_id_type=mesh_id)
            pl.semaphore_wait(barrier, 3)
            whole = copy(src_ref, buf_f, 0, partner)
            whole.start()
            copy(src_ref.at[pl.ds(0, half)], buf_a, 3, up).wait_recv()
            copy(src_ref.at[pl.ds(0, half)], buf_b, 4, down).wait_recv()

            @pl.when(t > 0)
            def _():
                out_ref[pl.ds(0, half)] = buf_a[...]
                out_ref[pl.ds(half, half)] = buf_b[...]

            @pl.when(t == 0)
            def _():
                out_ref[...] = jnp.zeros_like(out_ref)

            whole.wait_send()

        @pl.when(me_c == 1)
        def _():
            z_up = lax.rem(me_z + quarter, nz)
            z_down = lax.rem(me_z + nz - quarter, nz)
            partner = dev(me_x, me_z, 0)
            up = dev(me_x, z_up, 1)
            down = dev(me_x, z_down, 1)
            after_up = dest_of(me_x, z_up)
            after_down = dest_of(me_x, z_down)
            for peer in (partner, up, down, after_up, after_down):
                pl.semaphore_signal(barrier, inc=1, device_id=peer, device_id_type=mesh_id)
            pl.semaphore_wait(barrier, 5)
            first = copy(src_ref.at[pl.ds(0, half)], rel_a, 1, up)
            second = copy(src_ref.at[pl.ds(half, half)], rel_b, 2, down)
            first.start()
            second.start()
            first.wait_recv()
            on_a = copy(rel_a, buf_a, 3, after_down)
            on_a.start()
            second.wait_recv()
            on_b = copy(rel_b, buf_b, 4, after_up)
            on_b.start()
            copy(src_ref, buf_f, 0, partner).wait_recv()
            out_ref[...] = buf_f[...]
            first.wait_send()
            second.wait_send()
            on_a.wait_send()
            on_b.wait_send()

    vmem = pl.BlockSpec(memory_space=pltpu.VMEM)

    def call(rows):
        half_shape = (rows.shape[0] // 2, rows.shape[1])
        return pl.pallas_call(
            kernel,
            out_shape=jax.ShapeDtypeStruct(rows.shape, rows.dtype),
            in_specs=[vmem],
            out_specs=vmem,
            scratch_shapes=[
                pltpu.VMEM(rows.shape, rows.dtype),
                pltpu.VMEM(half_shape, rows.dtype),
                pltpu.VMEM(half_shape, rows.dtype),
                pltpu.VMEM(half_shape, rows.dtype),
                pltpu.VMEM(half_shape, rows.dtype),
                pltpu.SemaphoreType.DMA((5,)),
                pltpu.SemaphoreType.DMA((5,)),
            ],
            compiler_params=pltpu.CompilerParams(collective_id=1, has_side_effects=True),
        )(rows)

    return call


def make_body(sizes):
    nx, nzh, nc, ny, nzl = sizes
    n_tm = nx * nzh * nc
    n_rep = ny * nzl

    def body(samples, grad_out, w_conv, w_res, lengths):
        sequence_rows = samples[0]
        cotangent = grad_out[0]
        seq_len = lengths[0]
        count_of_rows = sequence_rows.shape[0]
        channel_count = sequence_rows.shape[1]
        start_row = lax.axis_index(TM) * count_of_rows
        trailing_rows = sequence_rows[count_of_rows - DILATION_STEP :]
        arrived = make_halo(sizes)(trailing_rows)
        prior_samples = jnp.concatenate(
            [arrived, sequence_rows[: count_of_rows - DILATION_STEP]], 0
        )
        inputs = jnp.concatenate([prior_samples, sequence_rows], 1)
        in_length = (start_row + jnp.arange(count_of_rows) < seq_len).astype(jnp.float32)[:, None]
        gated, pre_grad = gate_backward(inputs, cotangent, in_length, w_conv, w_res)
        input_gradient = jnp.dot(pre_grad, w_conv.T, preferred_element_type=jnp.float32)
        incoming_gradient = passed_along(
            input_gradient[:DILATION_STEP, :channel_count].astype(jnp.bfloat16), TM, -1, n_tm
        ).astype(jnp.float32)
        delayed_gradient = jnp.concatenate(
            [input_gradient[DILATION_STEP:, :channel_count], incoming_gradient], 0
        )
        grad_rows = (
            cotangent.astype(jnp.float32) + input_gradient[:, channel_count:] + delayed_gradient
        ).astype(jnp.bfloat16)
        term_conv = jnp.einsum("tk,tn->kn", inputs, pre_grad, preferred_element_type=jnp.float32)
        term_res = jnp.einsum("tk,tn->kn", gated, cotangent, preferred_element_type=jnp.float32)
        kc, n_conv = term_conv.shape
        kr, n_res = term_res.shape
        rc, rr = kc // n_tm, kr // n_tm
        all_tokens = count_of_rows * n_tm * n_rep
        reducer = make_reducer(sizes, rc, n_conv, rr, n_res, float(all_tokens) ** (-0.5))
        flip_conv, flip_res = reducer(
            term_conv.astype(jnp.bfloat16).reshape(nx, nzh, nc, rc, n_conv),
            term_res.astype(jnp.bfloat16).reshape(nx, nzh, nc, rr, n_res),
        )
        return (grad_rows[None], flip_conv.T, flip_res.T)

    return body


def solution(mesh):
    n_tm, n_rep = mesh.devices.shape
    nc = 2
    nzh = 2
    nx = n_tm // (nc * nzh)
    nzl = 8
    ny = n_rep // nzl
    sizes = (nx, nzh, nc, ny, nzl)
    fine = Mesh(mesh.devices.reshape(sizes), ("x", "zh", "c", "y", "zl"))
    return jax.shard_map(
        make_body(sizes),
        mesh=fine,
        in_specs=(P(REP, TM, None), P(REP, TM, None), P(), P(), P(REP)),
        out_specs=(P(REP, TM, None), P(TM, REP), P(TM, REP)),
        check_vma=False,
    )
```

```python
import jax
import jax.numpy as jnp
from jax import lax
from jax.experimental import pallas as pl
from jax.experimental.pallas import tpu as pltpu
from jax.sharding import Mesh, PartitionSpec as P

DILATION_STEP = 256
TM = ("x", "zh", "c")
REP = ("y", "zl")


def passed_along(array, axis, by, length):
    pairs = [(i, i + by) for i in range(length) if 0 <= i + by < length]
    return lax.ppermute(array, axis, pairs)


def gate_backward(inputs, cotangent, in_length, w_conv, w_res):
    channel_count = w_res.shape[0]
    pre_act = jnp.dot(inputs, w_conv, preferred_element_type=jnp.float32)
    tanh_f = jnp.tanh(pre_act[:, :channel_count])
    sig_g = jax.nn.sigmoid(pre_act[:, channel_count:])
    gated = (in_length * tanh_f * sig_g).astype(jnp.bfloat16)
    gated_grad = in_length * jnp.dot(cotangent, w_res.T, preferred_element_type=jnp.float32)
    pre_grad = jnp.concatenate(
        [gated_grad * sig_g * (1.0 - tanh_f * tanh_f), gated_grad * tanh_f * sig_g * (1.0 - sig_g)],
        1,
    ).astype(jnp.bfloat16)
    return (gated, pre_grad)


def make_reducer(sizes, rc, n_conv, rr, n_res, scale, edge_shape):
    nx, nzh, nc, ny, nzl = sizes
    nz = nzh * nzl
    cyc, cyr = n_conv // ny, n_res // ny
    cc, cr = cyc // nzl, cyr // nzl
    hc, hr = rc // 2, rr // 2
    base_xa, base_yb = 1, 1 + nx
    base_ya, base_xb = 1 + nx + ny, 1 + nx + 2 * ny
    base_z = 1 + 2 * nx + 2 * ny
    n_slots = base_z + nz
    n_peers = (nc - 1) + (nx - 1) + (ny - 1) + (nz - 1) + 2
    n_tm = nx * nzh * nc
    mesh_id = pl.DeviceIdType.MESH

    def kernel(conv_ref, res_ref, edge_ref, conv_out, res_out, edge_out,
               rc_conv, rc_res, sx_conv, sx_res,
               rxa_conv, rxa_res, ryb_conv, ryb_res,
               sa_conv, sa_res, rya_conv, rya_res,
               sb_conv, sb_res, rxb_conv, rxb_res,
               sz_conv, sz_res, rz_conv, rz_res,
               edge_buf, send_sems, recv_sems, local_sems):
        me_x = lax.axis_index("x")
        me_zh = lax.axis_index("zh")
        me_c = lax.axis_index("c")
        me_y = lax.axis_index("y")
        me_zl = lax.axis_index("zl")
        me_z = me_zh * nzl + me_zl
        other_c = 1 - me_c

        def dev(x=None, zh=None, c=None, y=None, zl=None):
            return (me_x if x is None else x, me_zh if zh is None else zh,
                    me_c if c is None else c, me_y if y is None else y,
                    me_zl if zl is None else zl)

        peers = [dev(c=other_c)]
        x_peers = [dev(x=lax.rem(me_x + d, nx)) for d in range(1, nx)]
        y_peers = [dev(y=lax.rem(me_y + d, ny)) for d in range(1, ny)]
        z_peers = []
        for d in range(1, nz):
            q = lax.rem(me_z + d, nz)
            z_peers.append(dev(zh=q // nzl, zl=lax.rem(q, nzl)))
        barrier = pltpu.get_barrier_semaphore()
        t = (me_x * nzh + me_zh) * nc + me_c

        def tm_dev(u):
            return dev(x=u // (nzh * nc), zh=lax.rem(u // nc, nzh), c=lax.rem(u, nc))

        before = tm_dev(lax.rem(t + n_tm - 1, n_tm))
        after = tm_dev(lax.rem(t + 1, n_tm))
        for peer in peers + x_peers + y_peers + z_peers + [before, after]:
            pl.semaphore_signal(barrier, inc=1, device_id=peer, device_id_type=mesh_id)
        pl.semaphore_wait(barrier, n_peers)

        sends = []

        def send(kind, src, dst, slot, peer):
            copy = pltpu.make_async_remote_copy(
                src_ref=src, dst_ref=dst, send_sem=send_sems.at[kind, slot],
                recv_sem=recv_sems.at[kind, slot], device_id=peer, device_id_type=mesh_id)
            copy.start()
            sends.append(copy)

        def arrive(kind, src, dst, slot):
            pltpu.make_async_remote_copy(
                src_ref=src, dst_ref=dst, send_sem=send_sems.at[kind, slot],
                recv_sem=recv_sems.at[kind, slot], device_id=dev(),
                device_id_type=mesh_id).wait_recv()

        def keep(kind, which, src, dst):
            copy = pltpu.make_async_copy(src, dst, local_sems.at[kind, which])
            copy.start()
            return copy

        edge = pltpu.make_async_remote_copy(
            src_ref=edge_ref, dst_ref=edge_buf, send_sem=local_sems.at[0, 2],
            recv_sem=local_sems.at[1, 2], device_id=before, device_id_type=mesh_id)
        edge.start()

        send(0, conv_ref.at[:, :, pl.ds(other_c, 1)], rc_conv, 0, peers[0])
        send(1, res_ref.at[:, :, pl.ds(other_c, 1)], rc_res, 0, peers[0])
        arrive(0, conv_ref.at[:, :, pl.ds(other_c, 1)], rc_conv, 0)
        arrive(1, res_ref.at[:, :, pl.ds(other_c, 1)], rc_res, 0)
        for x in range(nx):
            for zh in range(nzh):
                own_c = conv_ref[x, zh, pl.ds(me_c, 1)][0].astype(jnp.float32)
                sx_conv[x, zh] = (own_c + rc_conv[x, zh, 0].astype(jnp.float32)).astype(jnp.bfloat16)
                own_r = res_ref[x, zh, pl.ds(me_c, 1)][0].astype(jnp.float32)
                sx_res[x, zh] = (own_r + rc_res[x, zh, 0].astype(jnp.float32)).astype(jnp.bfloat16)

        for d in range(1, nx):
            tx = lax.rem(me_x + d, nx)
            send(0, sx_conv.at[tx, :, pl.ds(0, hc)], rxa_conv.at[me_x], base_xa + me_x, x_peers[d - 1])
            send(1, sx_res.at[tx, :, pl.ds(0, hr)], rxa_res.at[me_x], base_xa + me_x, x_peers[d - 1])
        for d in range(1, ny):
            ty = lax.rem(me_y + d, ny)
            send(0, sx_conv.at[:, :, pl.ds(hc, hc), pl.ds(ty * cyc, cyc)], ryb_conv.at[me_y],
                 base_yb + me_y, y_peers[d - 1])
            send(1, sx_res.at[:, :, pl.ds(hr, hr), pl.ds(ty * cyr, cyr)], ryb_res.at[me_y],
                 base_yb + me_y, y_peers[d - 1])
        own_b = [keep(0, 0, sx_conv.at[:, :, pl.ds(hc, hc), pl.ds(me_y * cyc, cyc)], ryb_conv.at[me_y]),
                 keep(1, 0, sx_res.at[:, :, pl.ds(hr, hr), pl.ds(me_y * cyr, cyr)], ryb_res.at[me_y])]

        for d in range(1, nx):
            sx = lax.rem(me_x + nx - d, nx)
            arrive(0, sx_conv.at[sx, :, pl.ds(0, hc)], rxa_conv.at[sx], base_xa + sx)
            arrive(1, sx_res.at[sx, :, pl.ds(0, hr)], rxa_res.at[sx], base_xa + sx)
        acc_c = sx_conv[me_x, :, :hc].astype(jnp.float32)
        acc_r = sx_res[me_x, :, :hr].astype(jnp.float32)
        for d in range(1, nx):
            sx = lax.rem(me_x + nx - d, nx)
            acc_c = acc_c + rxa_conv[sx].astype(jnp.float32)
            acc_r = acc_r + rxa_res[sx].astype(jnp.float32)
        sa_conv[...] = acc_c.astype(jnp.bfloat16)
        sa_res[...] = acc_r.astype(jnp.bfloat16)
        for d in range(1, ny):
            ty = lax.rem(me_y + d, ny)
            send(0, sa_conv.at[:, :, pl.ds(ty * cyc, cyc)], rya_conv.at[me_y], base_ya + me_y, y_peers[d - 1])
            send(1, sa_res.at[:, :, pl.ds(ty * cyr, cyr)], rya_res.at[me_y], base_ya + me_y, y_peers[d - 1])
        own_a = [keep(0, 1, sa_conv.at[:, :, pl.ds(me_y * cyc, cyc)], rya_conv.at[me_y]),
                 keep(1, 1, sa_res.at[:, :, pl.ds(me_y * cyr, cyr)], rya_res.at[me_y])]

        for d in range(1, ny):
            sy = lax.rem(me_y + ny - d, ny)
            arrive(0, sx_conv.at[:, :, pl.ds(hc, hc), pl.ds(0, cyc)], ryb_conv.at[sy], base_yb + sy)
            arrive(1, sx_res.at[:, :, pl.ds(hr, hr), pl.ds(0, cyr)], ryb_res.at[sy], base_yb + sy)
        for copy in own_b:
            copy.wait()
        acc_c = ryb_conv[0].astype(jnp.float32)
        acc_r = ryb_res[0].astype(jnp.float32)
        for s in range(1, ny):
            acc_c = acc_c + ryb_conv[s].astype(jnp.float32)
            acc_r = acc_r + ryb_res[s].astype(jnp.float32)
        sb_conv[...] = acc_c.astype(jnp.bfloat16)
        sb_res[...] = acc_r.astype(jnp.bfloat16)
        for d in range(1, nx):
            tx = lax.rem(me_x + d, nx)
            send(0, sb_conv.at[tx], rxb_conv.at[me_x], base_xb + me_x, x_peers[d - 1])
            send(1, sb_res.at[tx], rxb_res.at[me_x], base_xb + me_x, x_peers[d - 1])

        for d in range(1, ny):
            sy = lax.rem(me_y + ny - d, ny)
            arrive(0, sa_conv.at[:, :, pl.ds(0, cyc)], rya_conv.at[sy], base_ya + sy)
            arrive(1, sa_res.at[:, :, pl.ds(0, cyr)], rya_res.at[sy], base_ya + sy)
        for copy in own_a:
            copy.wait()
        for d in range(1, nx):
            sx = lax.rem(me_x + nx - d, nx)
            arrive(0, sb_conv.at[sx], rxb_conv.at[sx], base_xb + sx)
            arrive(1, sb_res.at[sx], rxb_res.at[sx], base_xb + sx)
        top_c = rya_conv[0].astype(jnp.float32)
        top_r = rya_res[0].astype(jnp.float32)
        for s in range(1, ny):
            top_c = top_c + rya_conv[s].astype(jnp.float32)
            top_r = top_r + rya_res[s].astype(jnp.float32)
        low_c = sb_conv[me_x].astype(jnp.float32)
        low_r = sb_res[me_x].astype(jnp.float32)
        for d in range(1, nx):
            sx = lax.rem(me_x + nx - d, nx)
            low_c = low_c + rxb_conv[sx].astype(jnp.float32)
            low_r = low_r + rxb_res[sx].astype(jnp.float32)
        acc_c = jnp.concatenate([top_c, low_c], axis=1)
        acc_r = jnp.concatenate([top_r, low_r], axis=1)
        for zh in range(nzh):
            flip_c = acc_c[zh].T
            flip_r = acc_r[zh].T
            for zl in range(nzl):
                sz_conv[zh * nzl + zl] = flip_c[zl * cc:(zl + 1) * cc, :].astype(jnp.bfloat16)
                sz_res[zh * nzl + zl] = flip_r[zl * cr:(zl + 1) * cr, :].astype(jnp.bfloat16)

        for d in range(1, nz):
            tz = lax.rem(me_z + d, nz)
            send(0, sz_conv.at[tz], rz_conv.at[me_z], base_z + me_z, z_peers[d - 1])
            send(1, sz_res.at[tz], rz_res.at[me_z], base_z + me_z, z_peers[d - 1])
        for d in range(1, nz):
            sz = lax.rem(me_z + nz - d, nz)
            arrive(0, sz_conv.at[sz], rz_conv.at[sz], base_z + sz)
            arrive(1, sz_res.at[sz], rz_res.at[sz], base_z + sz)
        acc_c = sz_conv[me_z].astype(jnp.float32)
        acc_r = sz_res[me_z].astype(jnp.float32)
        for d in range(1, nz):
            sz = lax.rem(me_z + nz - d, nz)
            acc_c = acc_c + rz_conv[sz].astype(jnp.float32)
            acc_r = acc_r + rz_res[sz].astype(jnp.float32)
        conv_out[...] = acc_c * scale
        res_out[...] = acc_r * scale
        edge.wait_recv()

        @pl.when(t < n_tm - 1)
        def _():
            edge_out[...] = edge_buf[...]

        @pl.when(t == n_tm - 1)
        def _():
            edge_out[...] = jnp.zeros_like(edge_out)

        for copy in sends:
            copy.wait_send()
        edge.wait_send()

    vmem = pl.BlockSpec(memory_space=pltpu.VMEM)
    bf16, f32 = jnp.bfloat16, jnp.float32
    return pl.pallas_call(
        kernel,
        out_shape=(jax.ShapeDtypeStruct((cc, rc), f32), jax.ShapeDtypeStruct((cr, rr), f32),
                   jax.ShapeDtypeStruct(edge_shape, bf16)),
        in_specs=[vmem, vmem, vmem],
        out_specs=(vmem, vmem, vmem),
        scratch_shapes=[
            pltpu.VMEM((nx, nzh, 1, rc, n_conv), bf16),
            pltpu.VMEM((nx, nzh, 1, rr, n_res), bf16),
            pltpu.VMEM((nx, nzh, rc, n_conv), bf16),
            pltpu.VMEM((nx, nzh, rr, n_res), bf16),
            pltpu.VMEM((nx, nzh, hc, n_conv), bf16),
            pltpu.VMEM((nx, nzh, hr, n_res), bf16),
            pltpu.VMEM((ny, nx, nzh, hc, cyc), bf16),
            pltpu.VMEM((ny, nx, nzh, hr, cyr), bf16),
            pltpu.VMEM((nzh, hc, n_conv), bf16),
            pltpu.VMEM((nzh, hr, n_res), bf16),
            pltpu.VMEM((ny, nzh, hc, cyc), bf16),
            pltpu.VMEM((ny, nzh, hr, cyr), bf16),
            pltpu.VMEM((nx, nzh, hc, cyc), bf16),
            pltpu.VMEM((nx, nzh, hr, cyr), bf16),
            pltpu.VMEM((nx, nzh, hc, cyc), bf16),
            pltpu.VMEM((nx, nzh, hr, cyr), bf16),
            pltpu.VMEM((nz, cc, rc), bf16),
            pltpu.VMEM((nz, cr, rr), bf16),
            pltpu.VMEM((nz, cc, rc), bf16),
            pltpu.VMEM((nz, cr, rr), bf16),
            pltpu.VMEM(edge_shape, bf16),
            pltpu.SemaphoreType.DMA((2, n_slots)),
            pltpu.SemaphoreType.DMA((2, n_slots)),
            pltpu.SemaphoreType.DMA((2, 3)),
        ],
        compiler_params=pltpu.CompilerParams(collective_id=0, has_side_effects=True),
    )


def make_body(sizes):
    nx, nzh, nc, ny, nzl = sizes
    n_tm = nx * nzh * nc
    n_rep = ny * nzl

    def body(samples, grad_out, w_conv, w_res, lengths):
        sequence_rows = samples[0]
        cotangent = grad_out[0]
        seq_len = lengths[0]
        count_of_rows = sequence_rows.shape[0]
        channel_count = sequence_rows.shape[1]
        start_row = lax.axis_index(TM) * count_of_rows
        trailing_rows = sequence_rows[count_of_rows - DILATION_STEP :]
        arrived = passed_along(trailing_rows, TM, 1, n_tm)
        prior_samples = jnp.concatenate(
            [arrived, sequence_rows[: count_of_rows - DILATION_STEP]], 0
        )
        inputs = jnp.concatenate([prior_samples, sequence_rows], 1)
        in_length = (start_row + jnp.arange(count_of_rows) < seq_len).astype(jnp.float32)[:, None]
        gated, pre_grad = gate_backward(inputs, cotangent, in_length, w_conv, w_res)
        input_gradient = jnp.dot(pre_grad, w_conv.T, preferred_element_type=jnp.float32)
        term_conv = jnp.einsum("tk,tn->kn", inputs, pre_grad, preferred_element_type=jnp.float32)
        term_res = jnp.einsum("tk,tn->kn", gated, cotangent, preferred_element_type=jnp.float32)
        kc, n_conv = term_conv.shape
        kr, n_res = term_res.shape
        rc, rr = kc // n_tm, kr // n_tm
        all_tokens = count_of_rows * n_tm * n_rep
        edge_rows = input_gradient[:DILATION_STEP, :channel_count].astype(jnp.bfloat16)
        reducer = make_reducer(sizes, rc, n_conv, rr, n_res, float(all_tokens) ** (-0.5), edge_rows.shape)
        flip_conv, flip_res, incoming_gradient = reducer(
            term_conv.astype(jnp.bfloat16).reshape(nx, nzh, nc, rc, n_conv),
            term_res.astype(jnp.bfloat16).reshape(nx, nzh, nc, rr, n_res),
            edge_rows,
        )
        delayed_gradient = jnp.concatenate(
            [input_gradient[DILATION_STEP:, :channel_count], incoming_gradient.astype(jnp.float32)], 0
        )
        grad_rows = (
            cotangent.astype(jnp.float32) + input_gradient[:, channel_count:] + delayed_gradient
        ).astype(jnp.bfloat16)
        return (grad_rows[None], flip_conv.T, flip_res.T)

    return body


def solution(mesh):
    n_tm, n_rep = mesh.devices.shape
    nc = 2
    nzh = 2
    nx = n_tm // (nc * nzh)
    nzl = 8
    ny = n_rep // nzl
    sizes = (nx, nzh, nc, ny, nzl)
    fine = Mesh(mesh.devices.reshape(sizes), ("x", "zh", "c", "y", "zl"))
    return jax.shard_map(
        make_body(sizes),
        mesh=fine,
        in_specs=(P(REP, TM, None), P(REP, TM, None), P(), P(), P(REP)),
        out_specs=(P(REP, TM, None), P(TM, REP), P(TM, REP)),
        check_vma=False,
    )
```

```python
import jax
import jax.numpy as jnp
from jax import lax
from jax.experimental import pallas as pl
from jax.experimental.pallas import tpu as pltpu
from jax.sharding import Mesh, PartitionSpec as P

DILATION_STEP = 256
TM = ("x", "zh", "c")
REP = ("y", "zl")


def passed_along(array, axis, by, length):
    pairs = [(i, i + by) for i in range(length) if 0 <= i + by < length]
    return lax.ppermute(array, axis, pairs)


def gate_backward(inputs, cotangent, in_length, w_conv, w_res):
    channel_count = w_res.shape[0]
    pre_act = jnp.dot(inputs, w_conv, preferred_element_type=jnp.float32)
    tanh_f = jnp.tanh(pre_act[:, :channel_count])
    sig_g = jax.nn.sigmoid(pre_act[:, channel_count:])
    gated = (in_length * tanh_f * sig_g).astype(jnp.bfloat16)
    gated_grad = in_length * jnp.dot(cotangent, w_res.T, preferred_element_type=jnp.float32)
    pre_grad = jnp.concatenate(
        [gated_grad * sig_g * (1.0 - tanh_f * tanh_f), gated_grad * tanh_f * sig_g * (1.0 - sig_g)],
        1,
    ).astype(jnp.bfloat16)
    return (gated, pre_grad)


def make_reducer(sizes, rc, n_conv, rr, n_res, scale, edge_shape):
    nx, nzh, nc, ny, nzl = sizes
    nz = nzh * nzl
    cyc, cyr = n_conv // ny, n_res // ny
    cc, cr = cyc // nzl, cyr // nzl
    hc, hr = rc // 2, rr // 2
    base_xa, base_yb = 1, 1 + nx
    base_ya, base_xb = 1 + nx + ny, 1 + nx + 2 * ny
    base_z = 1 + 2 * nx + 2 * ny
    n_slots = base_z + nz
    n_peers = (nc - 1) + (nx - 1) + (ny - 1) + (nz - 1) + 2
    n_tm = nx * nzh * nc
    mesh_id = pl.DeviceIdType.MESH

    def kernel(conv_ref, res_ref, edge_ref, conv_out, res_out, edge_out,
               rc_conv, rc_res, sx_conv, sx_res,
               rxa_conv, rxa_res, ryb_conv, ryb_res,
               sa_conv, sa_res, rya_conv, rya_res,
               sb_conv, sb_res, rxb_conv, rxb_res,
               sz_conv, sz_res, rz_conv, rz_res,
               edge_buf, send_sems, recv_sems, local_sems):
        me_x = lax.axis_index("x")
        me_zh = lax.axis_index("zh")
        me_c = lax.axis_index("c")
        me_y = lax.axis_index("y")
        me_zl = lax.axis_index("zl")
        me_z = me_zh * nzl + me_zl
        other_c = 1 - me_c

        def dev(x=None, zh=None, c=None, y=None, zl=None):
            return (me_x if x is None else x, me_zh if zh is None else zh,
                    me_c if c is None else c, me_y if y is None else y,
                    me_zl if zl is None else zl)

        peers = [dev(c=other_c)]
        x_peers = [dev(x=lax.rem(me_x + d, nx)) for d in range(1, nx)]
        y_peers = [dev(y=lax.rem(me_y + d, ny)) for d in range(1, ny)]
        z_peers = []
        for d in range(1, nz):
            q = lax.rem(me_z + d, nz)
            z_peers.append(dev(zh=q // nzl, zl=lax.rem(q, nzl)))
        barrier = pltpu.get_barrier_semaphore()
        t = (me_x * nzh + me_zh) * nc + me_c

        def tm_dev(u):
            return dev(x=u // (nzh * nc), zh=lax.rem(u // nc, nzh), c=lax.rem(u, nc))

        before = tm_dev(lax.rem(t + n_tm - 1, n_tm))
        after = tm_dev(lax.rem(t + 1, n_tm))
        for peer in peers + x_peers + y_peers + z_peers + [before, after]:
            pl.semaphore_signal(barrier, inc=1, device_id=peer, device_id_type=mesh_id)
        pl.semaphore_wait(barrier, n_peers)

        sends = []

        def send(kind, src, dst, slot, peer):
            copy = pltpu.make_async_remote_copy(
                src_ref=src, dst_ref=dst, send_sem=send_sems.at[kind, slot],
                recv_sem=recv_sems.at[kind, slot], device_id=peer, device_id_type=mesh_id)
            copy.start()
            sends.append(copy)

        def arrive(kind, src, dst, slot):
            pltpu.make_async_remote_copy(
                src_ref=src, dst_ref=dst, send_sem=send_sems.at[kind, slot],
                recv_sem=recv_sems.at[kind, slot], device_id=dev(),
                device_id_type=mesh_id).wait_recv()

        def keep(kind, which, src, dst):
            copy = pltpu.make_async_copy(src, dst, local_sems.at[kind, which])
            copy.start()
            return copy

        edge = pltpu.make_async_remote_copy(
            src_ref=edge_ref, dst_ref=edge_buf, send_sem=local_sems.at[0, 2],
            recv_sem=local_sems.at[1, 2], device_id=before, device_id_type=mesh_id)
        edge.start()

        send(0, conv_ref.at[:, :, pl.ds(other_c, 1)], rc_conv, 0, peers[0])
        send(1, res_ref.at[:, :, pl.ds(other_c, 1)], rc_res, 0, peers[0])
        arrive(0, conv_ref.at[:, :, pl.ds(other_c, 1)], rc_conv, 0)
        arrive(1, res_ref.at[:, :, pl.ds(other_c, 1)], rc_res, 0)
        for x in range(nx):
            for zh in range(nzh):
                own_c = conv_ref[x, zh, pl.ds(me_c, 1)][0].astype(jnp.float32)
                sx_conv[x, zh] = (own_c + rc_conv[x, zh, 0].astype(jnp.float32)).astype(jnp.bfloat16)
                own_r = res_ref[x, zh, pl.ds(me_c, 1)][0].astype(jnp.float32)
                sx_res[x, zh] = (own_r + rc_res[x, zh, 0].astype(jnp.float32)).astype(jnp.bfloat16)

        for d in range(1, nx):
            tx = lax.rem(me_x + d, nx)
            send(0, sx_conv.at[tx, :, pl.ds(0, hc)], rxa_conv.at[me_x], base_xa + me_x, x_peers[d - 1])
            send(1, sx_res.at[tx, :, pl.ds(0, hr)], rxa_res.at[me_x], base_xa + me_x, x_peers[d - 1])
        for d in range(1, ny):
            ty = lax.rem(me_y + d, ny)
            send(0, sx_conv.at[:, :, pl.ds(hc, hc), pl.ds(ty * cyc, cyc)], ryb_conv.at[me_y],
                 base_yb + me_y, y_peers[d - 1])
            send(1, sx_res.at[:, :, pl.ds(hr, hr), pl.ds(ty * cyr, cyr)], ryb_res.at[me_y],
                 base_yb + me_y, y_peers[d - 1])
        own_b = [keep(0, 0, sx_conv.at[:, :, pl.ds(hc, hc), pl.ds(me_y * cyc, cyc)], ryb_conv.at[me_y]),
                 keep(1, 0, sx_res.at[:, :, pl.ds(hr, hr), pl.ds(me_y * cyr, cyr)], ryb_res.at[me_y])]

        for d in range(1, nx):
            sx = lax.rem(me_x + nx - d, nx)
            arrive(0, sx_conv.at[sx, :, pl.ds(0, hc)], rxa_conv.at[sx], base_xa + sx)
            arrive(1, sx_res.at[sx, :, pl.ds(0, hr)], rxa_res.at[sx], base_xa + sx)
        acc_c = sx_conv[me_x, :, :hc].astype(jnp.float32)
        acc_r = sx_res[me_x, :, :hr].astype(jnp.float32)
        for d in range(1, nx):
            sx = lax.rem(me_x + nx - d, nx)
            acc_c = acc_c + rxa_conv[sx].astype(jnp.float32)
            acc_r = acc_r + rxa_res[sx].astype(jnp.float32)
        sa_conv[...] = acc_c.astype(jnp.bfloat16)
        sa_res[...] = acc_r.astype(jnp.bfloat16)
        for d in range(1, ny):
            ty = lax.rem(me_y + d, ny)
            send(0, sa_conv.at[:, :, pl.ds(ty * cyc, cyc)], rya_conv.at[me_y], base_ya + me_y, y_peers[d - 1])
            send(1, sa_res.at[:, :, pl.ds(ty * cyr, cyr)], rya_res.at[me_y], base_ya + me_y, y_peers[d - 1])
        own_a = [keep(0, 1, sa_conv.at[:, :, pl.ds(me_y * cyc, cyc)], rya_conv.at[me_y]),
                 keep(1, 1, sa_res.at[:, :, pl.ds(me_y * cyr, cyr)], rya_res.at[me_y])]

        for d in range(1, ny):
            sy = lax.rem(me_y + ny - d, ny)
            arrive(0, sx_conv.at[:, :, pl.ds(hc, hc), pl.ds(0, cyc)], ryb_conv.at[sy], base_yb + sy)
            arrive(1, sx_res.at[:, :, pl.ds(hr, hr), pl.ds(0, cyr)], ryb_res.at[sy], base_yb + sy)
        for copy in own_b:
            copy.wait()
        acc_c = ryb_conv[0].astype(jnp.float32)
        acc_r = ryb_res[0].astype(jnp.float32)
        for s in range(1, ny):
            acc_c = acc_c + ryb_conv[s].astype(jnp.float32)
            acc_r = acc_r + ryb_res[s].astype(jnp.float32)
        sb_conv[...] = acc_c.astype(jnp.bfloat16)
        sb_res[...] = acc_r.astype(jnp.bfloat16)
        for d in range(1, nx):
            tx = lax.rem(me_x + d, nx)
            send(0, sb_conv.at[tx], rxb_conv.at[me_x], base_xb + me_x, x_peers[d - 1])
            send(1, sb_res.at[tx], rxb_res.at[me_x], base_xb + me_x, x_peers[d - 1])

        for d in range(1, ny):
            sy = lax.rem(me_y + ny - d, ny)
            arrive(0, sa_conv.at[:, :, pl.ds(0, cyc)], rya_conv.at[sy], base_ya + sy)
            arrive(1, sa_res.at[:, :, pl.ds(0, cyr)], rya_res.at[sy], base_ya + sy)
        for copy in own_a:
            copy.wait()
        for d in range(1, nx):
            sx = lax.rem(me_x + nx - d, nx)
            arrive(0, sb_conv.at[sx], rxb_conv.at[sx], base_xb + sx)
            arrive(1, sb_res.at[sx], rxb_res.at[sx], base_xb + sx)
        top_c = rya_conv[0].astype(jnp.float32)
        top_r = rya_res[0].astype(jnp.float32)
        for s in range(1, ny):
            top_c = top_c + rya_conv[s].astype(jnp.float32)
            top_r = top_r + rya_res[s].astype(jnp.float32)
        low_c = sb_conv[me_x].astype(jnp.float32)
        low_r = sb_res[me_x].astype(jnp.float32)
        for d in range(1, nx):
            sx = lax.rem(me_x + nx - d, nx)
            low_c = low_c + rxb_conv[sx].astype(jnp.float32)
            low_r = low_r + rxb_res[sx].astype(jnp.float32)
        acc_c = jnp.concatenate([top_c, low_c], axis=1)
        acc_r = jnp.concatenate([top_r, low_r], axis=1)
        for zh in range(nzh):
            flip_c = acc_c[zh].T
            flip_r = acc_r[zh].T
            for zl in range(nzl):
                sz_conv[zh * nzl + zl] = flip_c[zl * cc:(zl + 1) * cc, :].astype(jnp.bfloat16)
                sz_res[zh * nzl + zl] = flip_r[zl * cr:(zl + 1) * cr, :].astype(jnp.bfloat16)

        for d in range(1, nz):
            tz = lax.rem(me_z + d, nz)
            send(0, sz_conv.at[tz], rz_conv.at[me_z], base_z + me_z, z_peers[d - 1])
            send(1, sz_res.at[tz], rz_res.at[me_z], base_z + me_z, z_peers[d - 1])
        for d in range(1, nz):
            sz = lax.rem(me_z + nz - d, nz)
            arrive(0, sz_conv.at[sz], rz_conv.at[sz], base_z + sz)
            arrive(1, sz_res.at[sz], rz_res.at[sz], base_z + sz)
        acc_c = sz_conv[me_z].astype(jnp.float32)
        acc_r = sz_res[me_z].astype(jnp.float32)
        for d in range(1, nz):
            sz = lax.rem(me_z + nz - d, nz)
            acc_c = acc_c + rz_conv[sz].astype(jnp.float32)
            acc_r = acc_r + rz_res[sz].astype(jnp.float32)
        conv_out[...] = acc_c * scale
        res_out[...] = acc_r * scale
        edge.wait_recv()

        @pl.when(t < n_tm - 1)
        def _():
            edge_out[...] = edge_buf[...]

        @pl.when(t == n_tm - 1)
        def _():
            edge_out[...] = jnp.zeros_like(edge_out)

        for copy in sends:
            copy.wait_send()
        edge.wait_send()

    vmem = pl.BlockSpec(memory_space=pltpu.VMEM)
    bf16, f32 = jnp.bfloat16, jnp.float32
    return pl.pallas_call(
        kernel,
        out_shape=(jax.ShapeDtypeStruct((cc, rc), f32), jax.ShapeDtypeStruct((cr, rr), f32),
                   jax.ShapeDtypeStruct(edge_shape, bf16)),
        in_specs=[vmem, vmem, vmem],
        out_specs=(vmem, vmem, vmem),
        scratch_shapes=[
            pltpu.VMEM((nx, nzh, 1, rc, n_conv), bf16),
            pltpu.VMEM((nx, nzh, 1, rr, n_res), bf16),
            pltpu.VMEM((nx, nzh, rc, n_conv), bf16),
            pltpu.VMEM((nx, nzh, rr, n_res), bf16),
            pltpu.VMEM((nx, nzh, hc, n_conv), bf16),
            pltpu.VMEM((nx, nzh, hr, n_res), bf16),
            pltpu.VMEM((ny, nx, nzh, hc, cyc), bf16),
            pltpu.VMEM((ny, nx, nzh, hr, cyr), bf16),
            pltpu.VMEM((nzh, hc, n_conv), bf16),
            pltpu.VMEM((nzh, hr, n_res), bf16),
            pltpu.VMEM((ny, nzh, hc, cyc), bf16),
            pltpu.VMEM((ny, nzh, hr, cyr), bf16),
            pltpu.VMEM((nx, nzh, hc, cyc), bf16),
            pltpu.VMEM((nx, nzh, hr, cyr), bf16),
            pltpu.VMEM((nx, nzh, hc, cyc), bf16),
            pltpu.VMEM((nx, nzh, hr, cyr), bf16),
            pltpu.VMEM((nz, cc, rc), bf16),
            pltpu.VMEM((nz, cr, rr), bf16),
            pltpu.VMEM((nz, cc, rc), bf16),
            pltpu.VMEM((nz, cr, rr), bf16),
            pltpu.VMEM(edge_shape, bf16),
            pltpu.SemaphoreType.DMA((2, n_slots)),
            pltpu.SemaphoreType.DMA((2, n_slots)),
            pltpu.SemaphoreType.DMA((2, 3)),
        ],
        compiler_params=pltpu.CompilerParams(collective_id=0, has_side_effects=True),
    )


def make_body(sizes):
    nx, nzh, nc, ny, nzl = sizes
    n_tm = nx * nzh * nc
    n_rep = ny * nzl

    def body(samples, grad_out, w_conv, w_res, lengths):
        sequence_rows = samples[0]
        cotangent = grad_out[0]
        seq_len = lengths[0]
        count_of_rows = sequence_rows.shape[0]
        channel_count = sequence_rows.shape[1]
        start_row = lax.axis_index(TM) * count_of_rows
        trailing_rows = sequence_rows[count_of_rows - DILATION_STEP :]
        arrived = passed_along(trailing_rows, TM, 1, n_tm)
        prior_samples = jnp.concatenate(
            [arrived, sequence_rows[: count_of_rows - DILATION_STEP]], 0
        )
        inputs = jnp.concatenate([prior_samples, sequence_rows], 1)
        in_length = (start_row + jnp.arange(count_of_rows) < seq_len).astype(jnp.float32)[:, None]
        gated, pre_grad = gate_backward(inputs, cotangent, in_length, w_conv, w_res)
        input_gradient = jnp.dot(pre_grad, w_conv.T, preferred_element_type=jnp.float32)
        term_conv = jnp.einsum("tk,tn->kn", inputs, pre_grad, preferred_element_type=jnp.float32)
        term_res = jnp.einsum("tk,tn->kn", gated, cotangent, preferred_element_type=jnp.float32)
        kc, n_conv = term_conv.shape
        kr, n_res = term_res.shape
        rc, rr = kc // n_tm, kr // n_tm
        all_tokens = count_of_rows * n_tm * n_rep
        edge_rows = input_gradient[:DILATION_STEP, :channel_count].astype(jnp.bfloat16)
        reducer = make_reducer(sizes, rc, n_conv, rr, n_res, float(all_tokens) ** (-0.5), edge_rows.shape)
        split = count_of_rows - DILATION_STEP
        head_rows = (
            cotangent[:split].astype(jnp.float32) + input_gradient[:split, channel_count:]
            + input_gradient[DILATION_STEP:, :channel_count]
        ).astype(jnp.bfloat16)
        conv_in = term_conv.astype(jnp.bfloat16).reshape(nx, nzh, nc, rc, n_conv)
        res_in = term_res.astype(jnp.bfloat16).reshape(nx, nzh, nc, rr, n_res)
        head_rows, conv_in, res_in, edge_rows = lax.optimization_barrier((head_rows, conv_in, res_in, edge_rows))
        flip_conv, flip_res, incoming_gradient = reducer(conv_in, res_in, edge_rows)
        tail_rows = (
            cotangent[split:].astype(jnp.float32) + input_gradient[split:, channel_count:]
            + incoming_gradient.astype(jnp.float32)
        ).astype(jnp.bfloat16)
        grad_rows = jnp.concatenate([head_rows, tail_rows], 0)
        return (grad_rows[None], flip_conv.T, flip_res.T)

    return body


def solution(mesh):
    n_tm, n_rep = mesh.devices.shape
    nc = 2
    nzh = 2
    nx = n_tm // (nc * nzh)
    nzl = 8
    ny = n_rep // nzl
    sizes = (nx, nzh, nc, ny, nzl)
    fine = Mesh(mesh.devices.reshape(sizes), ("x", "zh", "c", "y", "zl"))
    return jax.shard_map(
        make_body(sizes),
        mesh=fine,
        in_specs=(P(REP, TM, None), P(REP, TM, None), P(), P(), P(REP)),
        out_specs=(P(REP, TM, None), P(TM, REP), P(TM, REP)),
        check_vma=False,
    )
```

```python
import jax
import jax.numpy as jnp
from jax import lax
from jax.experimental import pallas as pl
from jax.experimental.pallas import tpu as pltpu
from jax.sharding import Mesh, PartitionSpec as P

DILATION_STEP = 256
TM = ("x", "zh", "c")
REP = ("y", "zl")


def passed_along(array, axis, by, length):
    pairs = [(i, i + by) for i in range(length) if 0 <= i + by < length]
    return lax.ppermute(array, axis, pairs)


def gate_backward(inputs, cotangent, in_length, w_conv, w_res):
    channel_count = w_res.shape[0]
    pre_act = jnp.dot(inputs, w_conv, preferred_element_type=jnp.float32)
    tanh_f = jnp.tanh(pre_act[:, :channel_count])
    sig_g = jax.nn.sigmoid(pre_act[:, channel_count:])
    gated = (in_length * tanh_f * sig_g).astype(jnp.bfloat16)
    gated_grad = in_length * jnp.dot(cotangent, w_res.T, preferred_element_type=jnp.float32)
    pre_grad = jnp.concatenate(
        [gated_grad * sig_g * (1.0 - tanh_f * tanh_f), gated_grad * tanh_f * sig_g * (1.0 - sig_g)],
        1,
    ).astype(jnp.bfloat16)
    return (gated, pre_grad)


def make_reducer(sizes, rc, n_conv, rr, n_res, scale, edge_shape):
    nx, nzh, nc, ny, nzl = sizes
    nz = nzh * nzl
    cyc, cyr = n_conv // ny, n_res // ny
    cc, cr = cyc // nzl, cyr // nzl
    hc, hr = rc // 2, rr // 2
    base_xa, base_yb = 1, 1 + nx
    base_ya, base_xb = 1 + nx + ny, 1 + nx + 2 * ny
    base_z = 1 + 2 * nx + 2 * ny
    n_slots = base_z + nz + 1
    slot_cb = base_z + nz
    n_peers = (nc - 1) + (nx - 1) + (ny - 1) + (nz - 1) + 2
    n_tm = nx * nzh * nc
    mesh_id = pl.DeviceIdType.MESH

    def kernel(conv_ref, res_ref, edge_ref, conv_out, res_out, edge_out,
               rc_conv, rc_res, sx_conv, sx_res,
               rxa_conv, rxa_res, ryb_conv, ryb_res,
               sa_conv, sa_res, rya_conv, rya_res,
               sb_conv, sb_res, rxb_conv, rxb_res,
               sz_conv, sz_res, rz_conv, rz_res,
               edge_buf, send_sems, recv_sems, local_sems):
        me_x = lax.axis_index("x")
        me_zh = lax.axis_index("zh")
        me_c = lax.axis_index("c")
        me_y = lax.axis_index("y")
        me_zl = lax.axis_index("zl")
        me_z = me_zh * nzl + me_zl
        other_c = 1 - me_c

        def dev(x=None, zh=None, c=None, y=None, zl=None):
            return (me_x if x is None else x, me_zh if zh is None else zh,
                    me_c if c is None else c, me_y if y is None else y,
                    me_zl if zl is None else zl)

        peers = [dev(c=other_c)]
        x_peers = [dev(x=lax.rem(me_x + d, nx)) for d in range(1, nx)]
        y_peers = [dev(y=lax.rem(me_y + d, ny)) for d in range(1, ny)]
        z_peers = []
        for d in range(1, nz):
            q = lax.rem(me_z + d, nz)
            z_peers.append(dev(zh=q // nzl, zl=lax.rem(q, nzl)))
        barrier = pltpu.get_barrier_semaphore()
        t = (me_x * nzh + me_zh) * nc + me_c

        def tm_dev(u):
            return dev(x=u // (nzh * nc), zh=lax.rem(u // nc, nzh), c=lax.rem(u, nc))

        before = tm_dev(lax.rem(t + n_tm - 1, n_tm))
        after = tm_dev(lax.rem(t + 1, n_tm))
        for peer in peers + x_peers + y_peers + z_peers + [before, after]:
            pl.semaphore_signal(barrier, inc=1, device_id=peer, device_id_type=mesh_id)
        pl.semaphore_wait(barrier, n_peers)

        sends = []

        def send(kind, src, dst, slot, peer):
            copy = pltpu.make_async_remote_copy(
                src_ref=src, dst_ref=dst, send_sem=send_sems.at[kind, slot],
                recv_sem=recv_sems.at[kind, slot], device_id=peer, device_id_type=mesh_id)
            copy.start()
            sends.append(copy)

        def arrive(kind, src, dst, slot):
            pltpu.make_async_remote_copy(
                src_ref=src, dst_ref=dst, send_sem=send_sems.at[kind, slot],
                recv_sem=recv_sems.at[kind, slot], device_id=dev(),
                device_id_type=mesh_id).wait_recv()

        def keep(kind, which, src, dst):
            copy = pltpu.make_async_copy(src, dst, local_sems.at[kind, which])
            copy.start()
            return copy

        edge = pltpu.make_async_remote_copy(
            src_ref=edge_ref, dst_ref=edge_buf, send_sem=local_sems.at[0, 2],
            recv_sem=local_sems.at[1, 2], device_id=before, device_id_type=mesh_id)
        edge.start()

        def pair_view(ref, lo, size):
            return ref.at[:, :, pl.ds(other_c, 1), pl.ds(lo, size)]

        def pair_slot(ref, lo, size):
            return ref.at[:, :, :, pl.ds(lo, size)]

        for lo_c, lo_r, slot in ((0, 0, 0), (hc, hr, slot_cb)):
            send(0, pair_view(conv_ref, lo_c, hc), pair_slot(rc_conv, lo_c, hc), slot, peers[0])
            send(1, pair_view(res_ref, lo_r, hr), pair_slot(rc_res, lo_r, hr), slot, peers[0])

        def pair_sum(lo_c, lo_r, slot):
            arrive(0, pair_view(conv_ref, lo_c, hc), pair_slot(rc_conv, lo_c, hc), slot)
            arrive(1, pair_view(res_ref, lo_r, hr), pair_slot(rc_res, lo_r, hr), slot)
            for x in range(nx):
                for zh in range(nzh):
                    own_c = conv_ref[x, zh, pl.ds(me_c, 1), pl.ds(lo_c, hc)][0].astype(jnp.float32)
                    got_c = rc_conv[x, zh, 0, pl.ds(lo_c, hc)].astype(jnp.float32)
                    sx_conv[x, zh, pl.ds(lo_c, hc)] = (own_c + got_c).astype(jnp.bfloat16)
                    own_r = res_ref[x, zh, pl.ds(me_c, 1), pl.ds(lo_r, hr)][0].astype(jnp.float32)
                    got_r = rc_res[x, zh, 0, pl.ds(lo_r, hr)].astype(jnp.float32)
                    sx_res[x, zh, pl.ds(lo_r, hr)] = (own_r + got_r).astype(jnp.bfloat16)

        pair_sum(0, 0, 0)

        for d in range(1, nx):
            tx = lax.rem(me_x + d, nx)
            send(0, sx_conv.at[tx, :, pl.ds(0, hc)], rxa_conv.at[me_x], base_xa + me_x, x_peers[d - 1])
            send(1, sx_res.at[tx, :, pl.ds(0, hr)], rxa_res.at[me_x], base_xa + me_x, x_peers[d - 1])
        pair_sum(hc, hr, slot_cb)
        for d in range(1, ny):
            ty = lax.rem(me_y + d, ny)
            send(0, sx_conv.at[:, :, pl.ds(hc, hc), pl.ds(ty * cyc, cyc)], ryb_conv.at[me_y],
                 base_yb + me_y, y_peers[d - 1])
            send(1, sx_res.at[:, :, pl.ds(hr, hr), pl.ds(ty * cyr, cyr)], ryb_res.at[me_y],
                 base_yb + me_y, y_peers[d - 1])
        own_b = [keep(0, 0, sx_conv.at[:, :, pl.ds(hc, hc), pl.ds(me_y * cyc, cyc)], ryb_conv.at[me_y]),
                 keep(1, 0, sx_res.at[:, :, pl.ds(hr, hr), pl.ds(me_y * cyr, cyr)], ryb_res.at[me_y])]

        for d in range(1, nx):
            sx = lax.rem(me_x + nx - d, nx)
            arrive(0, sx_conv.at[sx, :, pl.ds(0, hc)], rxa_conv.at[sx], base_xa + sx)
            arrive(1, sx_res.at[sx, :, pl.ds(0, hr)], rxa_res.at[sx], base_xa + sx)
        acc_c = sx_conv[me_x, :, :hc].astype(jnp.float32)
        acc_r = sx_res[me_x, :, :hr].astype(jnp.float32)
        for d in range(1, nx):
            sx = lax.rem(me_x + nx - d, nx)
            acc_c = acc_c + rxa_conv[sx].astype(jnp.float32)
            acc_r = acc_r + rxa_res[sx].astype(jnp.float32)
        sa_conv[...] = acc_c.astype(jnp.bfloat16)
        sa_res[...] = acc_r.astype(jnp.bfloat16)
        for d in range(1, ny):
            ty = lax.rem(me_y + d, ny)
            send(0, sa_conv.at[:, :, pl.ds(ty * cyc, cyc)], rya_conv.at[me_y], base_ya + me_y, y_peers[d - 1])
            send(1, sa_res.at[:, :, pl.ds(ty * cyr, cyr)], rya_res.at[me_y], base_ya + me_y, y_peers[d - 1])
        own_a = [keep(0, 1, sa_conv.at[:, :, pl.ds(me_y * cyc, cyc)], rya_conv.at[me_y]),
                 keep(1, 1, sa_res.at[:, :, pl.ds(me_y * cyr, cyr)], rya_res.at[me_y])]

        for d in range(1, ny):
            sy = lax.rem(me_y + ny - d, ny)
            arrive(0, sx_conv.at[:, :, pl.ds(hc, hc), pl.ds(0, cyc)], ryb_conv.at[sy], base_yb + sy)
            arrive(1, sx_res.at[:, :, pl.ds(hr, hr), pl.ds(0, cyr)], ryb_res.at[sy], base_yb + sy)
        for copy in own_b:
            copy.wait()
        acc_c = ryb_conv[0].astype(jnp.float32)
        acc_r = ryb_res[0].astype(jnp.float32)
        for s in range(1, ny):
            acc_c = acc_c + ryb_conv[s].astype(jnp.float32)
            acc_r = acc_r + ryb_res[s].astype(jnp.float32)
        sb_conv[...] = acc_c.astype(jnp.bfloat16)
        sb_res[...] = acc_r.astype(jnp.bfloat16)
        for d in range(1, nx):
            tx = lax.rem(me_x + d, nx)
            send(0, sb_conv.at[tx], rxb_conv.at[me_x], base_xb + me_x, x_peers[d - 1])
            send(1, sb_res.at[tx], rxb_res.at[me_x], base_xb + me_x, x_peers[d - 1])

        for d in range(1, ny):
            sy = lax.rem(me_y + ny - d, ny)
            arrive(0, sa_conv.at[:, :, pl.ds(0, cyc)], rya_conv.at[sy], base_ya + sy)
            arrive(1, sa_res.at[:, :, pl.ds(0, cyr)], rya_res.at[sy], base_ya + sy)
        for copy in own_a:
            copy.wait()
        for d in range(1, nx):
            sx = lax.rem(me_x + nx - d, nx)
            arrive(0, sb_conv.at[sx], rxb_conv.at[sx], base_xb + sx)
            arrive(1, sb_res.at[sx], rxb_res.at[sx], base_xb + sx)
        top_c = rya_conv[0].astype(jnp.float32)
        top_r = rya_res[0].astype(jnp.float32)
        for s in range(1, ny):
            top_c = top_c + rya_conv[s].astype(jnp.float32)
            top_r = top_r + rya_res[s].astype(jnp.float32)
        low_c = sb_conv[me_x].astype(jnp.float32)
        low_r = sb_res[me_x].astype(jnp.float32)
        for d in range(1, nx):
            sx = lax.rem(me_x + nx - d, nx)
            low_c = low_c + rxb_conv[sx].astype(jnp.float32)
            low_r = low_r + rxb_res[sx].astype(jnp.float32)
        acc_c = jnp.concatenate([top_c, low_c], axis=1)
        acc_r = jnp.concatenate([top_r, low_r], axis=1)
        for zh in range(nzh):
            flip_c = acc_c[zh].T
            flip_r = acc_r[zh].T
            for zl in range(nzl):
                sz_conv[zh * nzl + zl] = flip_c[zl * cc:(zl + 1) * cc, :].astype(jnp.bfloat16)
                sz_res[zh * nzl + zl] = flip_r[zl * cr:(zl + 1) * cr, :].astype(jnp.bfloat16)

        for d in range(1, nz):
            tz = lax.rem(me_z + d, nz)
            send(0, sz_conv.at[tz], rz_conv.at[me_z], base_z + me_z, z_peers[d - 1])
            send(1, sz_res.at[tz], rz_res.at[me_z], base_z + me_z, z_peers[d - 1])
        for d in range(1, nz):
            sz = lax.rem(me_z + nz - d, nz)
            arrive(0, sz_conv.at[sz], rz_conv.at[sz], base_z + sz)
            arrive(1, sz_res.at[sz], rz_res.at[sz], base_z + sz)
        acc_c = sz_conv[me_z].astype(jnp.float32)
        acc_r = sz_res[me_z].astype(jnp.float32)
        for d in range(1, nz):
            sz = lax.rem(me_z + nz - d, nz)
            acc_c = acc_c + rz_conv[sz].astype(jnp.float32)
            acc_r = acc_r + rz_res[sz].astype(jnp.float32)
        conv_out[...] = acc_c * scale
        res_out[...] = acc_r * scale
        edge.wait_recv()

        @pl.when(t < n_tm - 1)
        def _():
            edge_out[...] = edge_buf[...]

        @pl.when(t == n_tm - 1)
        def _():
            edge_out[...] = jnp.zeros_like(edge_out)

        for copy in sends:
            copy.wait_send()
        edge.wait_send()

    vmem = pl.BlockSpec(memory_space=pltpu.VMEM)
    bf16, f32 = jnp.bfloat16, jnp.float32
    return pl.pallas_call(
        kernel,
        out_shape=(jax.ShapeDtypeStruct((cc, rc), f32), jax.ShapeDtypeStruct((cr, rr), f32),
                   jax.ShapeDtypeStruct(edge_shape, bf16)),
        in_specs=[vmem, vmem, vmem],
        out_specs=(vmem, vmem, vmem),
        scratch_shapes=[
            pltpu.VMEM((nx, nzh, 1, rc, n_conv), bf16),
            pltpu.VMEM((nx, nzh, 1, rr, n_res), bf16),
            pltpu.VMEM((nx, nzh, rc, n_conv), bf16),
            pltpu.VMEM((nx, nzh, rr, n_res), bf16),
            pltpu.VMEM((nx, nzh, hc, n_conv), bf16),
            pltpu.VMEM((nx, nzh, hr, n_res), bf16),
            pltpu.VMEM((ny, nx, nzh, hc, cyc), bf16),
            pltpu.VMEM((ny, nx, nzh, hr, cyr), bf16),
            pltpu.VMEM((nzh, hc, n_conv), bf16),
            pltpu.VMEM((nzh, hr, n_res), bf16),
            pltpu.VMEM((ny, nzh, hc, cyc), bf16),
            pltpu.VMEM((ny, nzh, hr, cyr), bf16),
            pltpu.VMEM((nx, nzh, hc, cyc), bf16),
            pltpu.VMEM((nx, nzh, hr, cyr), bf16),
            pltpu.VMEM((nx, nzh, hc, cyc), bf16),
            pltpu.VMEM((nx, nzh, hr, cyr), bf16),
            pltpu.VMEM((nz, cc, rc), bf16),
            pltpu.VMEM((nz, cr, rr), bf16),
            pltpu.VMEM((nz, cc, rc), bf16),
            pltpu.VMEM((nz, cr, rr), bf16),
            pltpu.VMEM(edge_shape, bf16),
            pltpu.SemaphoreType.DMA((2, n_slots)),
            pltpu.SemaphoreType.DMA((2, n_slots)),
            pltpu.SemaphoreType.DMA((2, 3)),
        ],
        compiler_params=pltpu.CompilerParams(collective_id=0, has_side_effects=True),
    )


def make_body(sizes):
    nx, nzh, nc, ny, nzl = sizes
    n_tm = nx * nzh * nc
    n_rep = ny * nzl

    def body(samples, grad_out, w_conv, w_res, lengths):
        sequence_rows = samples[0]
        cotangent = grad_out[0]
        seq_len = lengths[0]
        count_of_rows = sequence_rows.shape[0]
        channel_count = sequence_rows.shape[1]
        start_row = lax.axis_index(TM) * count_of_rows
        trailing_rows = sequence_rows[count_of_rows - DILATION_STEP :]
        arrived = passed_along(trailing_rows, TM, 1, n_tm)
        prior_samples = jnp.concatenate(
            [arrived, sequence_rows[: count_of_rows - DILATION_STEP]], 0
        )
        inputs = jnp.concatenate([prior_samples, sequence_rows], 1)
        in_length = (start_row + jnp.arange(count_of_rows) < seq_len).astype(jnp.float32)[:, None]
        gated, pre_grad = gate_backward(inputs, cotangent, in_length, w_conv, w_res)
        input_gradient = jnp.dot(pre_grad, w_conv.T, preferred_element_type=jnp.float32)
        term_conv = jnp.einsum("tk,tn->kn", inputs, pre_grad, preferred_element_type=jnp.float32)
        term_res = jnp.einsum("tk,tn->kn", gated, cotangent, preferred_element_type=jnp.float32)
        kc, n_conv = term_conv.shape
        kr, n_res = term_res.shape
        rc, rr = kc // n_tm, kr // n_tm
        all_tokens = count_of_rows * n_tm * n_rep
        edge_rows = input_gradient[:DILATION_STEP, :channel_count].astype(jnp.bfloat16)
        reducer = make_reducer(sizes, rc, n_conv, rr, n_res, float(all_tokens) ** (-0.5), edge_rows.shape)
        split = count_of_rows - DILATION_STEP
        head_rows = jnp.concatenate([
            (cotangent[:split].astype(jnp.float32) + input_gradient[:split, channel_count:]
             + input_gradient[DILATION_STEP:, :channel_count]).astype(jnp.bfloat16),
            jnp.zeros((count_of_rows - split, channel_count), jnp.bfloat16)], 0)
        conv_in = term_conv.astype(jnp.bfloat16).reshape(nx, nzh, nc, rc, n_conv)
        res_in = term_res.astype(jnp.bfloat16).reshape(nx, nzh, nc, rr, n_res)
        head_rows, conv_in, res_in, edge_rows = lax.optimization_barrier((head_rows, conv_in, res_in, edge_rows))
        flip_conv, flip_res, incoming_gradient = reducer(conv_in, res_in, edge_rows)
        tail_rows = (
            cotangent[split:].astype(jnp.float32) + input_gradient[split:, channel_count:]
            + incoming_gradient.astype(jnp.float32)
        ).astype(jnp.bfloat16)
        grad_rows = lax.dynamic_update_slice(head_rows, tail_rows, (split, 0))
        return (grad_rows[None], flip_conv.T, flip_res.T)

    return body


def solution(mesh):
    n_tm, n_rep = mesh.devices.shape
    nc = 2
    nzh = 2
    nx = n_tm // (nc * nzh)
    nzl = 8
    ny = n_rep // nzl
    sizes = (nx, nzh, nc, ny, nzl)
    fine = Mesh(mesh.devices.reshape(sizes), ("x", "zh", "c", "y", "zl"))
    return jax.shard_map(
        make_body(sizes),
        mesh=fine,
        in_specs=(P(REP, TM, None), P(REP, TM, None), P(), P(), P(REP)),
        out_specs=(P(REP, TM, None), P(TM, REP), P(TM, REP)),
        check_vma=False,
    )
```

```python
import jax
import jax.numpy as jnp
from jax import lax
from jax.experimental import pallas as pl
from jax.experimental.pallas import tpu as pltpu
from jax.sharding import Mesh, PartitionSpec as P

DILATION_STEP = 256
TM = ("x", "zh", "c")
REP = ("y", "zl")


def passed_along(array, axis, by, length):
    pairs = [(i, i + by) for i in range(length) if 0 <= i + by < length]
    return lax.ppermute(array, axis, pairs)


def gate_backward(inputs, cotangent, in_length, w_conv, w_res):
    channel_count = w_res.shape[0]
    pre_act = jnp.dot(inputs, w_conv, preferred_element_type=jnp.float32)
    tanh_f = jnp.tanh(pre_act[:, :channel_count])
    sig_g = jax.nn.sigmoid(pre_act[:, channel_count:])
    gated = (in_length * tanh_f * sig_g).astype(jnp.bfloat16)
    gated_grad = in_length * jnp.dot(cotangent, w_res.T, preferred_element_type=jnp.float32)
    pre_grad = jnp.concatenate(
        [gated_grad * sig_g * (1.0 - tanh_f * tanh_f), gated_grad * tanh_f * sig_g * (1.0 - sig_g)],
        1,
    ).astype(jnp.bfloat16)
    return (gated, pre_grad)


def make_reducer(sizes, rc, n_conv, rr, n_res, scale):
    nx, nzh, nc, ny, nzl = sizes
    nz = nzh * nzl
    cyc, cyr = n_conv // ny, n_res // ny
    cc, cr = cyc // nzl, cyr // nzl
    hc, hr = rc // 2, rr // 2
    base_xa, base_yb = 1, 1 + nx
    base_ya, base_xb = 1 + nx + ny, 1 + nx + 2 * ny
    base_z = 1 + 2 * nx + 2 * ny
    n_cw, n_ccw = nz // 2 - 1, nz // 2
    base_ccw = base_z + n_cw
    n_slots = base_ccw + n_ccw
    n_peers = (nc - 1) + (nx - 1) + (ny - 1) + 2
    n_tm = nx * nzh * nc
    mesh_id = pl.DeviceIdType.MESH

    def kernel(conv_ref, res_ref, conv_out, res_out,
               rc_conv, rc_res, sx_conv, sx_res,
               rxa_conv, rxa_res, ryb_conv, ryb_res,
               sa_conv, sa_res, rya_conv, rya_res,
               sb_conv, sb_res, rxb_conv, rxb_res,
               sz_conv, sz_res, cw_in_c, cw_in_r, cw_out_c, cw_out_r,
               ccw_in_c, ccw_in_r, ccw_out_c, ccw_out_r, send_sems, recv_sems, local_sems):
        me_x = lax.axis_index("x")
        me_zh = lax.axis_index("zh")
        me_c = lax.axis_index("c")
        me_y = lax.axis_index("y")
        me_zl = lax.axis_index("zl")
        me_z = me_zh * nzl + me_zl
        other_c = 1 - me_c

        def dev(x=None, zh=None, c=None, y=None, zl=None):
            return (me_x if x is None else x, me_zh if zh is None else zh,
                    me_c if c is None else c, me_y if y is None else y,
                    me_zl if zl is None else zl)

        peers = [dev(c=other_c)]
        x_peers = [dev(x=lax.rem(me_x + d, nx)) for d in range(1, nx)]
        y_peers = [dev(y=lax.rem(me_y + d, ny)) for d in range(1, ny)]
        right = dev(zh=lax.rem(me_z + 1, nz) // nzl, zl=lax.rem(lax.rem(me_z + 1, nz), nzl))
        left = dev(zh=lax.rem(me_z + nz - 1, nz) // nzl, zl=lax.rem(lax.rem(me_z + nz - 1, nz), nzl))
        z_peers = [right, left]
        barrier = pltpu.get_barrier_semaphore()
        for peer in peers + x_peers + y_peers + z_peers:
            pl.semaphore_signal(barrier, inc=1, device_id=peer, device_id_type=mesh_id)
        pl.semaphore_wait(barrier, n_peers)

        sends = []

        def send(kind, src, dst, slot, peer):
            copy = pltpu.make_async_remote_copy(
                src_ref=src, dst_ref=dst, send_sem=send_sems.at[kind, slot],
                recv_sem=recv_sems.at[kind, slot], device_id=peer, device_id_type=mesh_id)
            copy.start()
            sends.append(copy)

        def arrive(kind, src, dst, slot):
            pltpu.make_async_remote_copy(
                src_ref=src, dst_ref=dst, send_sem=send_sems.at[kind, slot],
                recv_sem=recv_sems.at[kind, slot], device_id=dev(),
                device_id_type=mesh_id).wait_recv()

        def keep(kind, which, src, dst):
            copy = pltpu.make_async_copy(src, dst, local_sems.at[kind, which])
            copy.start()
            return copy

        send(0, conv_ref.at[:, :, pl.ds(other_c, 1)], rc_conv, 0, peers[0])
        send(1, res_ref.at[:, :, pl.ds(other_c, 1)], rc_res, 0, peers[0])
        arrive(0, conv_ref.at[:, :, pl.ds(other_c, 1)], rc_conv, 0)
        arrive(1, res_ref.at[:, :, pl.ds(other_c, 1)], rc_res, 0)
        for x in range(nx):
            for zh in range(nzh):
                own_c = conv_ref[x, zh, pl.ds(me_c, 1)][0].astype(jnp.float32)
                sx_conv[x, zh] = (own_c + rc_conv[x, zh, 0].astype(jnp.float32)).astype(jnp.bfloat16)
                own_r = res_ref[x, zh, pl.ds(me_c, 1)][0].astype(jnp.float32)
                sx_res[x, zh] = (own_r + rc_res[x, zh, 0].astype(jnp.float32)).astype(jnp.bfloat16)

        for d in range(1, nx):
            tx = lax.rem(me_x + d, nx)
            send(0, sx_conv.at[tx, :, pl.ds(0, hc)], rxa_conv.at[me_x], base_xa + me_x, x_peers[d - 1])
            send(1, sx_res.at[tx, :, pl.ds(0, hr)], rxa_res.at[me_x], base_xa + me_x, x_peers[d - 1])
        for d in range(1, ny):
            ty = lax.rem(me_y + d, ny)
            send(0, sx_conv.at[:, :, pl.ds(hc, hc), pl.ds(ty * cyc, cyc)], ryb_conv.at[me_y],
                 base_yb + me_y, y_peers[d - 1])
            send(1, sx_res.at[:, :, pl.ds(hr, hr), pl.ds(ty * cyr, cyr)], ryb_res.at[me_y],
                 base_yb + me_y, y_peers[d - 1])
        own_b = [keep(0, 0, sx_conv.at[:, :, pl.ds(hc, hc), pl.ds(me_y * cyc, cyc)], ryb_conv.at[me_y]),
                 keep(1, 0, sx_res.at[:, :, pl.ds(hr, hr), pl.ds(me_y * cyr, cyr)], ryb_res.at[me_y])]

        for d in range(1, nx):
            sx = lax.rem(me_x + nx - d, nx)
            arrive(0, sx_conv.at[sx, :, pl.ds(0, hc)], rxa_conv.at[sx], base_xa + sx)
            arrive(1, sx_res.at[sx, :, pl.ds(0, hr)], rxa_res.at[sx], base_xa + sx)
        acc_c = sx_conv[me_x, :, :hc].astype(jnp.float32)
        acc_r = sx_res[me_x, :, :hr].astype(jnp.float32)
        for d in range(1, nx):
            sx = lax.rem(me_x + nx - d, nx)
            acc_c = acc_c + rxa_conv[sx].astype(jnp.float32)
            acc_r = acc_r + rxa_res[sx].astype(jnp.float32)
        sa_conv[...] = acc_c.astype(jnp.bfloat16)
        sa_res[...] = acc_r.astype(jnp.bfloat16)
        for d in range(1, ny):
            ty = lax.rem(me_y + d, ny)
            send(0, sa_conv.at[:, :, pl.ds(ty * cyc, cyc)], rya_conv.at[me_y], base_ya + me_y, y_peers[d - 1])
            send(1, sa_res.at[:, :, pl.ds(ty * cyr, cyr)], rya_res.at[me_y], base_ya + me_y, y_peers[d - 1])
        own_a = [keep(0, 1, sa_conv.at[:, :, pl.ds(me_y * cyc, cyc)], rya_conv.at[me_y]),
                 keep(1, 1, sa_res.at[:, :, pl.ds(me_y * cyr, cyr)], rya_res.at[me_y])]

        for d in range(1, ny):
            sy = lax.rem(me_y + ny - d, ny)
            arrive(0, sx_conv.at[:, :, pl.ds(hc, hc), pl.ds(0, cyc)], ryb_conv.at[sy], base_yb + sy)
            arrive(1, sx_res.at[:, :, pl.ds(hr, hr), pl.ds(0, cyr)], ryb_res.at[sy], base_yb + sy)
        for copy in own_b:
            copy.wait()
        acc_c = ryb_conv[0].astype(jnp.float32)
        acc_r = ryb_res[0].astype(jnp.float32)
        for s in range(1, ny):
            acc_c = acc_c + ryb_conv[s].astype(jnp.float32)
            acc_r = acc_r + ryb_res[s].astype(jnp.float32)
        sb_conv[...] = acc_c.astype(jnp.bfloat16)
        sb_res[...] = acc_r.astype(jnp.bfloat16)
        for d in range(1, nx):
            tx = lax.rem(me_x + d, nx)
            send(0, sb_conv.at[tx], rxb_conv.at[me_x], base_xb + me_x, x_peers[d - 1])
            send(1, sb_res.at[tx], rxb_res.at[me_x], base_xb + me_x, x_peers[d - 1])

        for d in range(1, ny):
            sy = lax.rem(me_y + ny - d, ny)
            arrive(0, sa_conv.at[:, :, pl.ds(0, cyc)], rya_conv.at[sy], base_ya + sy)
            arrive(1, sa_res.at[:, :, pl.ds(0, cyr)], rya_res.at[sy], base_ya + sy)
        for copy in own_a:
            copy.wait()
        for d in range(1, nx):
            sx = lax.rem(me_x + nx - d, nx)
            arrive(0, sb_conv.at[sx], rxb_conv.at[sx], base_xb + sx)
            arrive(1, sb_res.at[sx], rxb_res.at[sx], base_xb + sx)
        top_c = rya_conv[0].astype(jnp.float32)
        top_r = rya_res[0].astype(jnp.float32)
        for s in range(1, ny):
            top_c = top_c + rya_conv[s].astype(jnp.float32)
            top_r = top_r + rya_res[s].astype(jnp.float32)
        low_c = sb_conv[me_x].astype(jnp.float32)
        low_r = sb_res[me_x].astype(jnp.float32)
        for d in range(1, nx):
            sx = lax.rem(me_x + nx - d, nx)
            low_c = low_c + rxb_conv[sx].astype(jnp.float32)
            low_r = low_r + rxb_res[sx].astype(jnp.float32)
        acc_c = jnp.concatenate([top_c, low_c], axis=1)
        acc_r = jnp.concatenate([top_r, low_r], axis=1)
        for zh in range(nzh):
            flip_c = acc_c[zh].T
            flip_r = acc_r[zh].T
            for zl in range(nzl):
                sz_conv[zh * nzl + zl] = flip_c[zl * cc:(zl + 1) * cc, :]
                sz_res[zh * nzl + zl] = flip_r[zl * cr:(zl + 1) * cr, :]

        chains = ((n_cw, 1, base_z, right, cw_in_c, cw_in_r, cw_out_c, cw_out_r),
                  (n_ccw, -1, base_ccw, left, ccw_in_c, ccw_in_r, ccw_out_c, ccw_out_r))
        for s in range(n_ccw):
            for steps, sign, base, peer, in_c, in_r, out_c, out_r in chains:
                if s >= steps:
                    continue
                q = lax.rem(me_z + nz + sign * (steps - s), nz)
                if s == 0:
                    src_c, src_r = sz_conv.at[q], sz_res.at[q]
                else:
                    arrive(0, sz_conv.at[q], in_c.at[s - 1], base + s - 1)
                    arrive(1, sz_res.at[q], in_r.at[s - 1], base + s - 1)
                    out_c[s] = sz_conv[q] + in_c[s - 1]
                    out_r[s] = sz_res[q] + in_r[s - 1]
                    src_c, src_r = out_c.at[s], out_r.at[s]
                send(0, src_c, in_c.at[s], base + s, peer)
                send(1, src_r, in_r.at[s], base + s, peer)
        for steps, sign, base, peer, in_c, in_r, out_c, out_r in chains:
            arrive(0, sz_conv.at[me_z], in_c.at[steps - 1], base + steps - 1)
            arrive(1, sz_res.at[me_z], in_r.at[steps - 1], base + steps - 1)
        acc_c = sz_conv[me_z] + cw_in_c[n_cw - 1] + ccw_in_c[n_ccw - 1]
        acc_r = sz_res[me_z] + cw_in_r[n_cw - 1] + ccw_in_r[n_ccw - 1]
        conv_out[...] = acc_c * scale
        res_out[...] = acc_r * scale
        for copy in sends:
            copy.wait_send()

    vmem = pl.BlockSpec(memory_space=pltpu.VMEM)
    bf16, f32 = jnp.bfloat16, jnp.float32
    return pl.pallas_call(
        kernel,
        out_shape=(jax.ShapeDtypeStruct((cc, rc), f32), jax.ShapeDtypeStruct((cr, rr), f32)),
        in_specs=[vmem, vmem],
        out_specs=(vmem, vmem),
        scratch_shapes=[
            pltpu.VMEM((nx, nzh, 1, rc, n_conv), bf16),
            pltpu.VMEM((nx, nzh, 1, rr, n_res), bf16),
            pltpu.VMEM((nx, nzh, rc, n_conv), bf16),
            pltpu.VMEM((nx, nzh, rr, n_res), bf16),
            pltpu.VMEM((nx, nzh, hc, n_conv), bf16),
            pltpu.VMEM((nx, nzh, hr, n_res), bf16),
            pltpu.VMEM((ny, nx, nzh, hc, cyc), bf16),
            pltpu.VMEM((ny, nx, nzh, hr, cyr), bf16),
            pltpu.VMEM((nzh, hc, n_conv), bf16),
            pltpu.VMEM((nzh, hr, n_res), bf16),
            pltpu.VMEM((ny, nzh, hc, cyc), bf16),
            pltpu.VMEM((ny, nzh, hr, cyr), bf16),
            pltpu.VMEM((nx, nzh, hc, cyc), bf16),
            pltpu.VMEM((nx, nzh, hr, cyr), bf16),
            pltpu.VMEM((nx, nzh, hc, cyc), bf16),
            pltpu.VMEM((nx, nzh, hr, cyr), bf16),
            pltpu.VMEM((nz, cc, rc), f32),
            pltpu.VMEM((nz, cr, rr), f32),
            pltpu.VMEM((n_cw, cc, rc), f32),
            pltpu.VMEM((n_cw, cr, rr), f32),
            pltpu.VMEM((n_cw, cc, rc), f32),
            pltpu.VMEM((n_cw, cr, rr), f32),
            pltpu.VMEM((n_ccw, cc, rc), f32),
            pltpu.VMEM((n_ccw, cr, rr), f32),
            pltpu.VMEM((n_ccw, cc, rc), f32),
            pltpu.VMEM((n_ccw, cr, rr), f32),
            pltpu.SemaphoreType.DMA((2, n_slots)),
            pltpu.SemaphoreType.DMA((2, n_slots)),
            pltpu.SemaphoreType.DMA((2, 3)),
        ],
        compiler_params=pltpu.CompilerParams(collective_id=0, has_side_effects=True),
    )


def make_body(sizes):
    nx, nzh, nc, ny, nzl = sizes
    n_tm = nx * nzh * nc
    n_rep = ny * nzl

    def body(samples, grad_out, w_conv, w_res, lengths):
        sequence_rows = samples[0]
        cotangent = grad_out[0]
        seq_len = lengths[0]
        count_of_rows = sequence_rows.shape[0]
        channel_count = sequence_rows.shape[1]
        start_row = lax.axis_index(TM) * count_of_rows
        trailing_rows = sequence_rows[count_of_rows - DILATION_STEP :]
        arrived = passed_along(trailing_rows, TM, 1, n_tm)
        prior_samples = jnp.concatenate(
            [arrived, sequence_rows[: count_of_rows - DILATION_STEP]], 0
        )
        inputs = jnp.concatenate([prior_samples, sequence_rows], 1)
        in_length = (start_row + jnp.arange(count_of_rows) < seq_len).astype(jnp.float32)[:, None]
        gated, pre_grad = gate_backward(inputs, cotangent, in_length, w_conv, w_res)
        input_gradient = jnp.dot(pre_grad, w_conv.T, preferred_element_type=jnp.float32)
        term_conv = jnp.einsum("tk,tn->kn", inputs, pre_grad, preferred_element_type=jnp.float32)
        term_res = jnp.einsum("tk,tn->kn", gated, cotangent, preferred_element_type=jnp.float32)
        kc, n_conv = term_conv.shape
        kr, n_res = term_res.shape
        rc, rr = kc // n_tm, kr // n_tm
        all_tokens = count_of_rows * n_tm * n_rep
        incoming_gradient = passed_along(
            input_gradient[:DILATION_STEP, :channel_count].astype(jnp.bfloat16), TM, -1, n_tm
        )
        reducer = make_reducer(sizes, rc, n_conv, rr, n_res, float(all_tokens) ** (-0.5))
        split = count_of_rows - DILATION_STEP
        head_rows = (
            cotangent[:split].astype(jnp.float32) + input_gradient[:split, channel_count:]
            + input_gradient[DILATION_STEP:, :channel_count]
        ).astype(jnp.bfloat16)
        conv_in = term_conv.astype(jnp.bfloat16).reshape(nx, nzh, nc, rc, n_conv)
        res_in = term_res.astype(jnp.bfloat16).reshape(nx, nzh, nc, rr, n_res)
        head_rows, conv_in, res_in = lax.optimization_barrier((head_rows, conv_in, res_in))
        flip_conv, flip_res = reducer(conv_in, res_in)
        tail_rows = (
            cotangent[split:].astype(jnp.float32) + input_gradient[split:, channel_count:]
            + incoming_gradient.astype(jnp.float32)
        ).astype(jnp.bfloat16)
        grad_rows = jnp.concatenate([head_rows, tail_rows], 0)
        return (grad_rows[None], flip_conv.T, flip_res.T)

    return body


def solution(mesh):
    n_tm, n_rep = mesh.devices.shape
    nc = 2
    nzh = 2
    nx = n_tm // (nc * nzh)
    nzl = 8
    ny = n_rep // nzl
    sizes = (nx, nzh, nc, ny, nzl)
    fine = Mesh(mesh.devices.reshape(sizes), ("x", "zh", "c", "y", "zl"))
    return jax.shard_map(
        make_body(sizes),
        mesh=fine,
        in_specs=(P(REP, TM, None), P(REP, TM, None), P(), P(), P(REP)),
        out_specs=(P(REP, TM, None), P(TM, REP), P(TM, REP)),
        check_vma=False,
    )
```

```python
import jax
import jax.numpy as jnp
from jax import lax
from jax.experimental import pallas as pl
from jax.experimental.pallas import tpu as pltpu
from jax.sharding import Mesh, PartitionSpec as P

DILATION_STEP = 256
TM = ("x", "zh", "c")
REP = ("y", "zl")


def passed_along(array, axis, by, length):
    pairs = [(i, i + by) for i in range(length) if 0 <= i + by < length]
    return lax.ppermute(array, axis, pairs)


def gate_backward(inputs, cotangent, in_length, w_conv, w_res):
    channel_count = w_res.shape[0]
    pre_act = jnp.dot(inputs, w_conv, preferred_element_type=jnp.float32)
    tanh_f = jnp.tanh(pre_act[:, :channel_count])
    sig_g = jax.nn.sigmoid(pre_act[:, channel_count:])
    gated = (in_length * tanh_f * sig_g).astype(jnp.bfloat16)
    gated_grad = in_length * jnp.dot(cotangent, w_res.T, preferred_element_type=jnp.float32)
    pre_grad = jnp.concatenate(
        [gated_grad * sig_g * (1.0 - tanh_f * tanh_f), gated_grad * tanh_f * sig_g * (1.0 - sig_g)],
        1,
    ).astype(jnp.bfloat16)
    return (gated, pre_grad)


def make_reducer(sizes, rc, n_conv, rr, n_res, scale, edge_shape):
    nx, nzh, nc, ny, nzl = sizes
    nz = nzh * nzl
    cyc, cyr = n_conv // ny, n_res // ny
    cc, cr = cyc // nzl, cyr // nzl
    hc, hr = rc // 2, rr // 2
    base_xa, base_yb = 1, 1 + nx
    base_ya, base_xb = 1 + nx + ny, 1 + nx + 2 * ny
    base_z = 1 + 2 * nx + 2 * ny
    n_slots = base_z + nz
    n_peers = (nc - 1) + (nx - 1) + (ny - 1) + (nz - 1) + 2
    n_tm = nx * nzh * nc
    mesh_id = pl.DeviceIdType.MESH

    def kernel(conv_ref, res_ref, edge_ref, conv_out, res_out, edge_out,
               rc_conv, rc_res, sx_conv, sx_res,
               rxa_conv, rxa_res, ryb_conv, ryb_res,
               sa_conv, sa_res, rya_conv, rya_res,
               sb_conv, sb_res, rxb_conv, rxb_res,
               sz_both, rz_both,
               edge_buf, send_sems, recv_sems, local_sems):
        me_x = lax.axis_index("x")
        me_zh = lax.axis_index("zh")
        me_c = lax.axis_index("c")
        me_y = lax.axis_index("y")
        me_zl = lax.axis_index("zl")
        me_z = me_zh * nzl + me_zl
        other_c = 1 - me_c

        def dev(x=None, zh=None, c=None, y=None, zl=None):
            return (me_x if x is None else x, me_zh if zh is None else zh,
                    me_c if c is None else c, me_y if y is None else y,
                    me_zl if zl is None else zl)

        peers = [dev(c=other_c)]
        x_peers = [dev(x=lax.rem(me_x + d, nx)) for d in range(1, nx)]
        y_peers = [dev(y=lax.rem(me_y + d, ny)) for d in range(1, ny)]
        z_peers = []
        for d in range(1, nz):
            q = lax.rem(me_z + d, nz)
            z_peers.append(dev(zh=q // nzl, zl=lax.rem(q, nzl)))
        barrier = pltpu.get_barrier_semaphore()
        t = (me_x * nzh + me_zh) * nc + me_c

        def tm_dev(u):
            return dev(x=u // (nzh * nc), zh=lax.rem(u // nc, nzh), c=lax.rem(u, nc))

        before = tm_dev(lax.rem(t + n_tm - 1, n_tm))
        after = tm_dev(lax.rem(t + 1, n_tm))
        for peer in peers + x_peers + y_peers + z_peers + [before, after]:
            pl.semaphore_signal(barrier, inc=1, device_id=peer, device_id_type=mesh_id)
        pl.semaphore_wait(barrier, n_peers)

        sends = []

        def send(kind, src, dst, slot, peer):
            copy = pltpu.make_async_remote_copy(
                src_ref=src, dst_ref=dst, send_sem=send_sems.at[kind, slot],
                recv_sem=recv_sems.at[kind, slot], device_id=peer, device_id_type=mesh_id)
            copy.start()
            sends.append(copy)

        def arrive(kind, src, dst, slot):
            pltpu.make_async_remote_copy(
                src_ref=src, dst_ref=dst, send_sem=send_sems.at[kind, slot],
                recv_sem=recv_sems.at[kind, slot], device_id=dev(),
                device_id_type=mesh_id).wait_recv()

        def keep(kind, which, src, dst):
            copy = pltpu.make_async_copy(src, dst, local_sems.at[kind, which])
            copy.start()
            return copy

        edge = pltpu.make_async_remote_copy(
            src_ref=edge_ref, dst_ref=edge_buf, send_sem=local_sems.at[0, 2],
            recv_sem=local_sems.at[1, 2], device_id=before, device_id_type=mesh_id)
        edge.start()

        send(0, conv_ref.at[:, :, pl.ds(other_c, 1)], rc_conv, 0, peers[0])
        send(1, res_ref.at[:, :, pl.ds(other_c, 1)], rc_res, 0, peers[0])
        arrive(0, conv_ref.at[:, :, pl.ds(other_c, 1)], rc_conv, 0)
        arrive(1, res_ref.at[:, :, pl.ds(other_c, 1)], rc_res, 0)
        for x in range(nx):
            for zh in range(nzh):
                own_c = conv_ref[x, zh, pl.ds(me_c, 1)][0].astype(jnp.float32)
                sx_conv[x, zh] = (own_c + rc_conv[x, zh, 0].astype(jnp.float32)).astype(jnp.bfloat16)
                own_r = res_ref[x, zh, pl.ds(me_c, 1)][0].astype(jnp.float32)
                sx_res[x, zh] = (own_r + rc_res[x, zh, 0].astype(jnp.float32)).astype(jnp.bfloat16)

        for d in range(1, nx):
            tx = lax.rem(me_x + d, nx)
            send(0, sx_conv.at[tx, :, pl.ds(0, hc)], rxa_conv.at[me_x], base_xa + me_x, x_peers[d - 1])
            send(1, sx_res.at[tx, :, pl.ds(0, hr)], rxa_res.at[me_x], base_xa + me_x, x_peers[d - 1])
        for d in range(1, ny):
            ty = lax.rem(me_y + d, ny)
            send(0, sx_conv.at[:, :, pl.ds(hc, hc), pl.ds(ty * cyc, cyc)], ryb_conv.at[me_y],
                 base_yb + me_y, y_peers[d - 1])
            send(1, sx_res.at[:, :, pl.ds(hr, hr), pl.ds(ty * cyr, cyr)], ryb_res.at[me_y],
                 base_yb + me_y, y_peers[d - 1])
        own_b = [keep(0, 0, sx_conv.at[:, :, pl.ds(hc, hc), pl.ds(me_y * cyc, cyc)], ryb_conv.at[me_y]),
                 keep(1, 0, sx_res.at[:, :, pl.ds(hr, hr), pl.ds(me_y * cyr, cyr)], ryb_res.at[me_y])]

        for d in range(1, nx):
            sx = lax.rem(me_x + nx - d, nx)
            arrive(0, sx_conv.at[sx, :, pl.ds(0, hc)], rxa_conv.at[sx], base_xa + sx)
            arrive(1, sx_res.at[sx, :, pl.ds(0, hr)], rxa_res.at[sx], base_xa + sx)
        acc_c = sx_conv[me_x, :, :hc].astype(jnp.float32)
        acc_r = sx_res[me_x, :, :hr].astype(jnp.float32)
        for d in range(1, nx):
            sx = lax.rem(me_x + nx - d, nx)
            acc_c = acc_c + rxa_conv[sx].astype(jnp.float32)
            acc_r = acc_r + rxa_res[sx].astype(jnp.float32)
        sa_conv[...] = acc_c.astype(jnp.bfloat16)
        sa_res[...] = acc_r.astype(jnp.bfloat16)
        for d in range(1, ny):
            ty = lax.rem(me_y + d, ny)
            send(0, sa_conv.at[:, :, pl.ds(ty * cyc, cyc)], rya_conv.at[me_y], base_ya + me_y, y_peers[d - 1])
            send(1, sa_res.at[:, :, pl.ds(ty * cyr, cyr)], rya_res.at[me_y], base_ya + me_y, y_peers[d - 1])
        own_a = [keep(0, 1, sa_conv.at[:, :, pl.ds(me_y * cyc, cyc)], rya_conv.at[me_y]),
                 keep(1, 1, sa_res.at[:, :, pl.ds(me_y * cyr, cyr)], rya_res.at[me_y])]

        for d in range(1, ny):
            sy = lax.rem(me_y + ny - d, ny)
            arrive(0, sx_conv.at[:, :, pl.ds(hc, hc), pl.ds(0, cyc)], ryb_conv.at[sy], base_yb + sy)
            arrive(1, sx_res.at[:, :, pl.ds(hr, hr), pl.ds(0, cyr)], ryb_res.at[sy], base_yb + sy)
        for copy in own_b:
            copy.wait()
        acc_c = ryb_conv[0].astype(jnp.float32)
        acc_r = ryb_res[0].astype(jnp.float32)
        for s in range(1, ny):
            acc_c = acc_c + ryb_conv[s].astype(jnp.float32)
            acc_r = acc_r + ryb_res[s].astype(jnp.float32)
        sb_conv[...] = acc_c.astype(jnp.bfloat16)
        sb_res[...] = acc_r.astype(jnp.bfloat16)
        for d in range(1, nx):
            tx = lax.rem(me_x + d, nx)
            send(0, sb_conv.at[tx], rxb_conv.at[me_x], base_xb + me_x, x_peers[d - 1])
            send(1, sb_res.at[tx], rxb_res.at[me_x], base_xb + me_x, x_peers[d - 1])

        for d in range(1, ny):
            sy = lax.rem(me_y + ny - d, ny)
            arrive(0, sa_conv.at[:, :, pl.ds(0, cyc)], rya_conv.at[sy], base_ya + sy)
            arrive(1, sa_res.at[:, :, pl.ds(0, cyr)], rya_res.at[sy], base_ya + sy)
        for copy in own_a:
            copy.wait()
        for d in range(1, nx):
            sx = lax.rem(me_x + nx - d, nx)
            arrive(0, sb_conv.at[sx], rxb_conv.at[sx], base_xb + sx)
            arrive(1, sb_res.at[sx], rxb_res.at[sx], base_xb + sx)
        top_c = rya_conv[0].astype(jnp.float32)
        top_r = rya_res[0].astype(jnp.float32)
        for s in range(1, ny):
            top_c = top_c + rya_conv[s].astype(jnp.float32)
            top_r = top_r + rya_res[s].astype(jnp.float32)
        low_c = sb_conv[me_x].astype(jnp.float32)
        low_r = sb_res[me_x].astype(jnp.float32)
        for d in range(1, nx):
            sx = lax.rem(me_x + nx - d, nx)
            low_c = low_c + rxb_conv[sx].astype(jnp.float32)
            low_r = low_r + rxb_res[sx].astype(jnp.float32)
        acc_c = jnp.concatenate([top_c, low_c], axis=1)
        acc_r = jnp.concatenate([top_r, low_r], axis=1)
        for zh in range(nzh):
            flip_c = acc_c[zh].T
            flip_r = acc_r[zh].T
            for zl in range(nzl):
                q = zh * nzl + zl
                sz_both[q, :cc, :] = flip_c[zl * cc:(zl + 1) * cc, :].astype(jnp.bfloat16)
                sz_both[q, cc:, :rr] = flip_r[zl * cr:(zl + 1) * cr, :].astype(jnp.bfloat16)
                sz_both[q, cc:, rr:] = jnp.zeros((cr, rc - rr), jnp.bfloat16)

        for d in range(1, nz):
            tz = lax.rem(me_z + d, nz)
            send(0, sz_both.at[tz], rz_both.at[me_z], base_z + me_z, z_peers[d - 1])
        for d in range(1, nz):
            sz = lax.rem(me_z + nz - d, nz)
            arrive(0, sz_both.at[sz], rz_both.at[sz], base_z + sz)
        acc = sz_both[me_z].astype(jnp.float32)
        for d in range(1, nz):
            sz = lax.rem(me_z + nz - d, nz)
            acc = acc + rz_both[sz].astype(jnp.float32)
        conv_out[...] = acc[:cc] * scale
        res_out[...] = acc[cc:, :rr] * scale
        edge.wait_recv()

        @pl.when(t < n_tm - 1)
        def _():
            edge_out[...] = edge_buf[...]

        @pl.when(t == n_tm - 1)
        def _():
            edge_out[...] = jnp.zeros_like(edge_out)

        for copy in sends:
            copy.wait_send()
        edge.wait_send()

    vmem = pl.BlockSpec(memory_space=pltpu.VMEM)
    bf16, f32 = jnp.bfloat16, jnp.float32
    return pl.pallas_call(
        kernel,
        out_shape=(jax.ShapeDtypeStruct((cc, rc), f32), jax.ShapeDtypeStruct((cr, rr), f32),
                   jax.ShapeDtypeStruct(edge_shape, bf16)),
        in_specs=[vmem, vmem, vmem],
        out_specs=(vmem, vmem, vmem),
        scratch_shapes=[
            pltpu.VMEM((nx, nzh, 1, rc, n_conv), bf16),
            pltpu.VMEM((nx, nzh, 1, rr, n_res), bf16),
            pltpu.VMEM((nx, nzh, rc, n_conv), bf16),
            pltpu.VMEM((nx, nzh, rr, n_res), bf16),
            pltpu.VMEM((nx, nzh, hc, n_conv), bf16),
            pltpu.VMEM((nx, nzh, hr, n_res), bf16),
            pltpu.VMEM((ny, nx, nzh, hc, cyc), bf16),
            pltpu.VMEM((ny, nx, nzh, hr, cyr), bf16),
            pltpu.VMEM((nzh, hc, n_conv), bf16),
            pltpu.VMEM((nzh, hr, n_res), bf16),
            pltpu.VMEM((ny, nzh, hc, cyc), bf16),
            pltpu.VMEM((ny, nzh, hr, cyr), bf16),
            pltpu.VMEM((nx, nzh, hc, cyc), bf16),
            pltpu.VMEM((nx, nzh, hr, cyr), bf16),
            pltpu.VMEM((nx, nzh, hc, cyc), bf16),
            pltpu.VMEM((nx, nzh, hr, cyr), bf16),
            pltpu.VMEM((nz, cc + cr, rc), bf16),
            pltpu.VMEM((nz, cc + cr, rc), bf16),
            pltpu.VMEM(edge_shape, bf16),
            pltpu.SemaphoreType.DMA((2, n_slots)),
            pltpu.SemaphoreType.DMA((2, n_slots)),
            pltpu.SemaphoreType.DMA((2, 3)),
        ],
        compiler_params=pltpu.CompilerParams(collective_id=0, has_side_effects=True),
    )


def make_body(sizes):
    nx, nzh, nc, ny, nzl = sizes
    n_tm = nx * nzh * nc
    n_rep = ny * nzl

    def body(samples, grad_out, w_conv, w_res, lengths):
        sequence_rows = samples[0]
        cotangent = grad_out[0]
        seq_len = lengths[0]
        count_of_rows = sequence_rows.shape[0]
        channel_count = sequence_rows.shape[1]
        start_row = lax.axis_index(TM) * count_of_rows
        trailing_rows = sequence_rows[count_of_rows - DILATION_STEP :]
        arrived = passed_along(trailing_rows, TM, 1, n_tm)
        prior_samples = jnp.concatenate(
            [arrived, sequence_rows[: count_of_rows - DILATION_STEP]], 0
        )
        inputs = jnp.concatenate([prior_samples, sequence_rows], 1)
        in_length = (start_row + jnp.arange(count_of_rows) < seq_len).astype(jnp.float32)[:, None]
        gated, pre_grad = gate_backward(inputs, cotangent, in_length, w_conv, w_res)
        input_gradient = jnp.dot(pre_grad, w_conv.T, preferred_element_type=jnp.float32)
        term_conv = jnp.einsum("tk,tn->kn", inputs, pre_grad, preferred_element_type=jnp.float32)
        term_res = jnp.einsum("tk,tn->kn", gated, cotangent, preferred_element_type=jnp.float32)
        kc, n_conv = term_conv.shape
        kr, n_res = term_res.shape
        rc, rr = kc // n_tm, kr // n_tm
        all_tokens = count_of_rows * n_tm * n_rep
        edge_rows = input_gradient[:DILATION_STEP, :channel_count].astype(jnp.bfloat16)
        reducer = make_reducer(sizes, rc, n_conv, rr, n_res, float(all_tokens) ** (-0.5), edge_rows.shape)
        split = count_of_rows - DILATION_STEP
        head_rows = (
            cotangent[:split].astype(jnp.float32) + input_gradient[:split, channel_count:]
            + input_gradient[DILATION_STEP:, :channel_count]
        ).astype(jnp.bfloat16)
        conv_in = term_conv.astype(jnp.bfloat16).reshape(nx, nzh, nc, rc, n_conv)
        res_in = term_res.astype(jnp.bfloat16).reshape(nx, nzh, nc, rr, n_res)
        head_rows, conv_in, res_in, edge_rows = lax.optimization_barrier((head_rows, conv_in, res_in, edge_rows))
        flip_conv, flip_res, incoming_gradient = reducer(conv_in, res_in, edge_rows)
        tail_rows = (
            cotangent[split:].astype(jnp.float32) + input_gradient[split:, channel_count:]
            + incoming_gradient.astype(jnp.float32)
        ).astype(jnp.bfloat16)
        grad_rows = jnp.concatenate([head_rows, tail_rows], 0)
        return (grad_rows[None], flip_conv.T, flip_res.T)

    return body


def solution(mesh):
    n_tm, n_rep = mesh.devices.shape
    nc = 2
    nzh = 2
    nx = n_tm // (nc * nzh)
    nzl = 8
    ny = n_rep // nzl
    sizes = (nx, nzh, nc, ny, nzl)
    fine = Mesh(mesh.devices.reshape(sizes), ("x", "zh", "c", "y", "zl"))
    return jax.shard_map(
        make_body(sizes),
        mesh=fine,
        in_specs=(P(REP, TM, None), P(REP, TM, None), P(), P(), P(REP)),
        out_specs=(P(REP, TM, None), P(TM, REP), P(TM, REP)),
        check_vma=False,
    )
```

```python
import jax
import jax.numpy as jnp
from jax import lax
from jax.experimental import pallas as pl
from jax.experimental.pallas import tpu as pltpu
from jax.sharding import Mesh, PartitionSpec as P

DILATION_STEP = 256
TM = ("x", "zh", "c")
REP = ("y", "zl")


def passed_along(array, axis, by, length):
    pairs = [(i, i + by) for i in range(length) if 0 <= i + by < length]
    return lax.ppermute(array, axis, pairs)


def gate_backward(inputs, cotangent, in_length, w_conv, w_res):
    channel_count = w_res.shape[0]
    pre_act = jnp.dot(inputs, w_conv, preferred_element_type=jnp.float32)
    tanh_f = jnp.tanh(pre_act[:, :channel_count])
    sig_g = jax.nn.sigmoid(pre_act[:, channel_count:])
    gated = (in_length * tanh_f * sig_g).astype(jnp.bfloat16)
    gated_grad = in_length * jnp.dot(cotangent, w_res.T, preferred_element_type=jnp.float32)
    pre_grad = jnp.concatenate(
        [gated_grad * sig_g * (1.0 - tanh_f * tanh_f), gated_grad * tanh_f * sig_g * (1.0 - sig_g)],
        1,
    ).astype(jnp.bfloat16)
    return (gated, pre_grad)


def make_reducer(sizes, rc, n_conv, rr, n_res, scale, edge_shape):
    nx, nzh, nc, ny, nzl = sizes
    nz = nzh * nzl
    cyc, cyr = n_conv // ny, n_res // ny
    cc, cr = cyc // nzl, cyr // nzl
    hc, hr = rc // 2, rr // 2
    base_xa, base_yb = 1, 1 + nx
    base_ya, base_xb = 1 + nx + ny, 1 + nx + 2 * ny
    base_z = 1 + 2 * nx + 2 * ny
    n_slots = base_z + nz
    n_peers = (nc - 1) + (nx - 1) + (ny - 1) + (nz - 1) + 2
    n_tm = nx * nzh * nc
    mesh_id = pl.DeviceIdType.MESH

    def kernel(conv_ref, res_ref, edge_ref, conv_out, res_out, edge_out,
               rc_conv, rc_res, sx_conv, sx_res,
               rxa_conv, rxa_res, ryb_conv, ryb_res,
               sa_conv, sa_res, rya_conv, rya_res,
               sb_conv, sb_res, rxb_conv, rxb_res,
               sz_both, rz_both,
               edge_buf, send_sems, recv_sems, local_sems):
        me_x = lax.axis_index("x")
        me_zh = lax.axis_index("zh")
        me_c = lax.axis_index("c")
        me_y = lax.axis_index("y")
        me_zl = lax.axis_index("zl")
        me_z = me_zh * nzl + me_zl
        other_c = 1 - me_c

        def dev(x=None, zh=None, c=None, y=None, zl=None):
            return (me_x if x is None else x, me_zh if zh is None else zh,
                    me_c if c is None else c, me_y if y is None else y,
                    me_zl if zl is None else zl)

        peers = [dev(c=other_c)]
        x_peers = [dev(x=lax.rem(me_x + d, nx)) for d in range(1, nx)]
        y_peers = [dev(y=lax.rem(me_y + d, ny)) for d in range(1, ny)]
        z_peers = []
        for d in range(1, nz):
            q = lax.rem(me_z + d, nz)
            z_peers.append(dev(zh=q // nzl, zl=lax.rem(q, nzl)))
        barrier = pltpu.get_barrier_semaphore()
        t = (me_x * nzh + me_zh) * nc + me_c

        def tm_dev(u):
            return dev(x=u // (nzh * nc), zh=lax.rem(u // nc, nzh), c=lax.rem(u, nc))

        before = tm_dev(lax.rem(t + n_tm - 1, n_tm))
        after = tm_dev(lax.rem(t + 1, n_tm))
        far_first = sorted(range(1, nz), key=lambda d: -min(d, nz - d))
        for peer in [z_peers[d - 1] for d in far_first] + [before, after] + peers + x_peers + y_peers:
            pl.semaphore_signal(barrier, inc=1, device_id=peer, device_id_type=mesh_id)
        pl.semaphore_wait(barrier, n_peers)

        sends = []

        def send(kind, src, dst, slot, peer):
            copy = pltpu.make_async_remote_copy(
                src_ref=src, dst_ref=dst, send_sem=send_sems.at[kind, slot],
                recv_sem=recv_sems.at[kind, slot], device_id=peer, device_id_type=mesh_id)
            copy.start()
            sends.append(copy)

        def arrive(kind, src, dst, slot):
            pltpu.make_async_remote_copy(
                src_ref=src, dst_ref=dst, send_sem=send_sems.at[kind, slot],
                recv_sem=recv_sems.at[kind, slot], device_id=dev(),
                device_id_type=mesh_id).wait_recv()

        def keep(kind, which, src, dst):
            copy = pltpu.make_async_copy(src, dst, local_sems.at[kind, which])
            copy.start()
            return copy

        edge = pltpu.make_async_remote_copy(
            src_ref=edge_ref, dst_ref=edge_buf, send_sem=local_sems.at[0, 2],
            recv_sem=local_sems.at[1, 2], device_id=before, device_id_type=mesh_id)
        edge.start()

        send(0, conv_ref.at[:, :, pl.ds(other_c, 1)], rc_conv, 0, peers[0])
        send(1, res_ref.at[:, :, pl.ds(other_c, 1)], rc_res, 0, peers[0])
        arrive(0, conv_ref.at[:, :, pl.ds(other_c, 1)], rc_conv, 0)
        arrive(1, res_ref.at[:, :, pl.ds(other_c, 1)], rc_res, 0)
        for x in range(nx):
            for zh in range(nzh):
                own_c = conv_ref[x, zh, pl.ds(me_c, 1)][0].astype(jnp.float32)
                sx_conv[x, zh] = (own_c + rc_conv[x, zh, 0].astype(jnp.float32)).astype(jnp.bfloat16)
                own_r = res_ref[x, zh, pl.ds(me_c, 1)][0].astype(jnp.float32)
                sx_res[x, zh] = (own_r + rc_res[x, zh, 0].astype(jnp.float32)).astype(jnp.bfloat16)

        for d in range(1, nx):
            tx = lax.rem(me_x + d, nx)
            send(0, sx_conv.at[tx, :, pl.ds(0, hc)], rxa_conv.at[me_x], base_xa + me_x, x_peers[d - 1])
            send(1, sx_res.at[tx, :, pl.ds(0, hr)], rxa_res.at[me_x], base_xa + me_x, x_peers[d - 1])
        for d in range(1, ny):
            ty = lax.rem(me_y + d, ny)
            send(0, sx_conv.at[:, :, pl.ds(hc, hc), pl.ds(ty * cyc, cyc)], ryb_conv.at[me_y],
                 base_yb + me_y, y_peers[d - 1])
            send(1, sx_res.at[:, :, pl.ds(hr, hr), pl.ds(ty * cyr, cyr)], ryb_res.at[me_y],
                 base_yb + me_y, y_peers[d - 1])
        own_b = [keep(0, 0, sx_conv.at[:, :, pl.ds(hc, hc), pl.ds(me_y * cyc, cyc)], ryb_conv.at[me_y]),
                 keep(1, 0, sx_res.at[:, :, pl.ds(hr, hr), pl.ds(me_y * cyr, cyr)], ryb_res.at[me_y])]

        for d in range(1, nx):
            sx = lax.rem(me_x + nx - d, nx)
            arrive(0, sx_conv.at[sx, :, pl.ds(0, hc)], rxa_conv.at[sx], base_xa + sx)
            arrive(1, sx_res.at[sx, :, pl.ds(0, hr)], rxa_res.at[sx], base_xa + sx)
        acc_c = sx_conv[me_x, :, :hc].astype(jnp.float32)
        acc_r = sx_res[me_x, :, :hr].astype(jnp.float32)
        for d in range(1, nx):
            sx = lax.rem(me_x + nx - d, nx)
            acc_c = acc_c + rxa_conv[sx].astype(jnp.float32)
            acc_r = acc_r + rxa_res[sx].astype(jnp.float32)
        sa_conv[...] = acc_c.astype(jnp.bfloat16)
        sa_res[...] = acc_r.astype(jnp.bfloat16)
        for d in range(1, ny):
            ty = lax.rem(me_y + d, ny)
            send(0, sa_conv.at[:, :, pl.ds(ty * cyc, cyc)], rya_conv.at[me_y], base_ya + me_y, y_peers[d - 1])
            send(1, sa_res.at[:, :, pl.ds(ty * cyr, cyr)], rya_res.at[me_y], base_ya + me_y, y_peers[d - 1])
        own_a = [keep(0, 1, sa_conv.at[:, :, pl.ds(me_y * cyc, cyc)], rya_conv.at[me_y]),
                 keep(1, 1, sa_res.at[:, :, pl.ds(me_y * cyr, cyr)], rya_res.at[me_y])]

        for d in range(1, ny):
            sy = lax.rem(me_y + ny - d, ny)
            arrive(0, sx_conv.at[:, :, pl.ds(hc, hc), pl.ds(0, cyc)], ryb_conv.at[sy], base_yb + sy)
            arrive(1, sx_res.at[:, :, pl.ds(hr, hr), pl.ds(0, cyr)], ryb_res.at[sy], base_yb + sy)
        for copy in own_b:
            copy.wait()
        acc_c = ryb_conv[0].astype(jnp.float32)
        acc_r = ryb_res[0].astype(jnp.float32)
        for s in range(1, ny):
            acc_c = acc_c + ryb_conv[s].astype(jnp.float32)
            acc_r = acc_r + ryb_res[s].astype(jnp.float32)
        sb_conv[...] = acc_c.astype(jnp.bfloat16)
        sb_res[...] = acc_r.astype(jnp.bfloat16)
        for d in range(1, nx):
            tx = lax.rem(me_x + d, nx)
            send(0, sb_conv.at[tx], rxb_conv.at[me_x], base_xb + me_x, x_peers[d - 1])
            send(1, sb_res.at[tx], rxb_res.at[me_x], base_xb + me_x, x_peers[d - 1])

        for d in range(1, ny):
            sy = lax.rem(me_y + ny - d, ny)
            arrive(0, sa_conv.at[:, :, pl.ds(0, cyc)], rya_conv.at[sy], base_ya + sy)
            arrive(1, sa_res.at[:, :, pl.ds(0, cyr)], rya_res.at[sy], base_ya + sy)
        for copy in own_a:
            copy.wait()
        for d in range(1, nx):
            sx = lax.rem(me_x + nx - d, nx)
            arrive(0, sb_conv.at[sx], rxb_conv.at[sx], base_xb + sx)
            arrive(1, sb_res.at[sx], rxb_res.at[sx], base_xb + sx)
        top_c = rya_conv[0].astype(jnp.float32)
        top_r = rya_res[0].astype(jnp.float32)
        for s in range(1, ny):
            top_c = top_c + rya_conv[s].astype(jnp.float32)
            top_r = top_r + rya_res[s].astype(jnp.float32)
        low_c = sb_conv[me_x].astype(jnp.float32)
        low_r = sb_res[me_x].astype(jnp.float32)
        for d in range(1, nx):
            sx = lax.rem(me_x + nx - d, nx)
            low_c = low_c + rxb_conv[sx].astype(jnp.float32)
            low_r = low_r + rxb_res[sx].astype(jnp.float32)
        acc_c = jnp.concatenate([top_c, low_c], axis=1)
        acc_r = jnp.concatenate([top_r, low_r], axis=1)
        for zh in range(nzh):
            flip_c = acc_c[zh].T
            flip_r = acc_r[zh].T
            for zl in range(nzl):
                q = zh * nzl + zl
                sz_both[q, :cc, :] = flip_c[zl * cc:(zl + 1) * cc, :].astype(jnp.bfloat16)
                sz_both[q, cc:, :rr] = flip_r[zl * cr:(zl + 1) * cr, :].astype(jnp.bfloat16)
                sz_both[q, cc:, rr:] = jnp.zeros((cr, rc - rr), jnp.bfloat16)

        for d in range(1, nz):
            tz = lax.rem(me_z + d, nz)
            send(0, sz_both.at[tz], rz_both.at[me_z], base_z + me_z, z_peers[d - 1])
        for d in range(1, nz):
            sz = lax.rem(me_z + nz - d, nz)
            arrive(0, sz_both.at[sz], rz_both.at[sz], base_z + sz)
        acc = sz_both[me_z].astype(jnp.float32)
        for d in range(1, nz):
            sz = lax.rem(me_z + nz - d, nz)
            acc = acc + rz_both[sz].astype(jnp.float32)
        conv_out[...] = acc[:cc] * scale
        res_out[...] = acc[cc:, :rr] * scale
        edge.wait_recv()

        @pl.when(t < n_tm - 1)
        def _():
            edge_out[...] = edge_buf[...]

        @pl.when(t == n_tm - 1)
        def _():
            edge_out[...] = jnp.zeros_like(edge_out)

        for copy in sends:
            copy.wait_send()
        edge.wait_send()

    vmem = pl.BlockSpec(memory_space=pltpu.VMEM)
    bf16, f32 = jnp.bfloat16, jnp.float32
    return pl.pallas_call(
        kernel,
        out_shape=(jax.ShapeDtypeStruct((cc, rc), f32), jax.ShapeDtypeStruct((cr, rr), f32),
                   jax.ShapeDtypeStruct(edge_shape, bf16)),
        in_specs=[vmem, vmem, vmem],
        out_specs=(vmem, vmem, vmem),
        scratch_shapes=[
            pltpu.VMEM((nx, nzh, 1, rc, n_conv), bf16),
            pltpu.VMEM((nx, nzh, 1, rr, n_res), bf16),
            pltpu.VMEM((nx, nzh, rc, n_conv), bf16),
            pltpu.VMEM((nx, nzh, rr, n_res), bf16),
            pltpu.VMEM((nx, nzh, hc, n_conv), bf16),
            pltpu.VMEM((nx, nzh, hr, n_res), bf16),
            pltpu.VMEM((ny, nx, nzh, hc, cyc), bf16),
            pltpu.VMEM((ny, nx, nzh, hr, cyr), bf16),
            pltpu.VMEM((nzh, hc, n_conv), bf16),
            pltpu.VMEM((nzh, hr, n_res), bf16),
            pltpu.VMEM((ny, nzh, hc, cyc), bf16),
            pltpu.VMEM((ny, nzh, hr, cyr), bf16),
            pltpu.VMEM((nx, nzh, hc, cyc), bf16),
            pltpu.VMEM((nx, nzh, hr, cyr), bf16),
            pltpu.VMEM((nx, nzh, hc, cyc), bf16),
            pltpu.VMEM((nx, nzh, hr, cyr), bf16),
            pltpu.VMEM((nz, cc + cr, rc), bf16),
            pltpu.VMEM((nz, cc + cr, rc), bf16),
            pltpu.VMEM(edge_shape, bf16),
            pltpu.SemaphoreType.DMA((2, n_slots)),
            pltpu.SemaphoreType.DMA((2, n_slots)),
            pltpu.SemaphoreType.DMA((2, 3)),
        ],
        compiler_params=pltpu.CompilerParams(collective_id=0, has_side_effects=True),
    )


def make_body(sizes):
    nx, nzh, nc, ny, nzl = sizes
    n_tm = nx * nzh * nc
    n_rep = ny * nzl

    def body(samples, grad_out, w_conv, w_res, lengths):
        sequence_rows = samples[0]
        cotangent = grad_out[0]
        seq_len = lengths[0]
        count_of_rows = sequence_rows.shape[0]
        channel_count = sequence_rows.shape[1]
        start_row = lax.axis_index(TM) * count_of_rows
        trailing_rows = sequence_rows[count_of_rows - DILATION_STEP :]
        arrived = passed_along(trailing_rows, TM, 1, n_tm)
        prior_samples = jnp.concatenate(
            [arrived, sequence_rows[: count_of_rows - DILATION_STEP]], 0
        )
        inputs = jnp.concatenate([prior_samples, sequence_rows], 1)
        in_length = (start_row + jnp.arange(count_of_rows) < seq_len).astype(jnp.float32)[:, None]
        gated, pre_grad = gate_backward(inputs, cotangent, in_length, w_conv, w_res)
        input_gradient = jnp.dot(pre_grad, w_conv.T, preferred_element_type=jnp.float32)
        term_conv = jnp.einsum("tk,tn->kn", inputs, pre_grad, preferred_element_type=jnp.float32)
        term_res = jnp.einsum("tk,tn->kn", gated, cotangent, preferred_element_type=jnp.float32)
        kc, n_conv = term_conv.shape
        kr, n_res = term_res.shape
        rc, rr = kc // n_tm, kr // n_tm
        all_tokens = count_of_rows * n_tm * n_rep
        edge_rows = input_gradient[:DILATION_STEP, :channel_count].astype(jnp.bfloat16)
        reducer = make_reducer(sizes, rc, n_conv, rr, n_res, float(all_tokens) ** (-0.5), edge_rows.shape)
        split = count_of_rows - DILATION_STEP
        head_rows = (
            cotangent[:split].astype(jnp.float32) + input_gradient[:split, channel_count:]
            + input_gradient[DILATION_STEP:, :channel_count]
        ).astype(jnp.bfloat16)
        conv_in = term_conv.astype(jnp.bfloat16).reshape(nx, nzh, nc, rc, n_conv)
        res_in = term_res.astype(jnp.bfloat16).reshape(nx, nzh, nc, rr, n_res)
        head_rows, conv_in, res_in, edge_rows = lax.optimization_barrier((head_rows, conv_in, res_in, edge_rows))
        flip_conv, flip_res, incoming_gradient = reducer(conv_in, res_in, edge_rows)
        tail_rows = (
            cotangent[split:].astype(jnp.float32) + input_gradient[split:, channel_count:]
            + incoming_gradient.astype(jnp.float32)
        ).astype(jnp.bfloat16)
        grad_rows = jnp.concatenate([head_rows, tail_rows], 0)
        return (grad_rows[None], flip_conv.T, flip_res.T)

    return body


def solution(mesh):
    n_tm, n_rep = mesh.devices.shape
    nc = 2
    nzh = 2
    nx = n_tm // (nc * nzh)
    nzl = 8
    ny = n_rep // nzl
    sizes = (nx, nzh, nc, ny, nzl)
    fine = Mesh(mesh.devices.reshape(sizes), ("x", "zh", "c", "y", "zl"))
    return jax.shard_map(
        make_body(sizes),
        mesh=fine,
        in_specs=(P(REP, TM, None), P(REP, TM, None), P(), P(), P(REP)),
        out_specs=(P(REP, TM, None), P(TM, REP), P(TM, REP)),
        check_vma=False,
    )
```

```python
import jax
import jax.numpy as jnp
from jax import lax
from jax.experimental import pallas as pl
from jax.experimental.pallas import tpu as pltpu
from jax.sharding import Mesh, PartitionSpec as P

DILATION_STEP = 256
TM = ("x", "zh", "c")
REP = ("y", "zl")


def passed_along(array, axis, by, length):
    pairs = [(i, i + by) for i in range(length) if 0 <= i + by < length]
    return lax.ppermute(array, axis, pairs)


def gate_backward(inputs, cotangent, in_length, w_conv, w_res):
    channel_count = w_res.shape[0]
    pre_act = jnp.dot(inputs, w_conv, preferred_element_type=jnp.float32)
    tanh_f = jnp.tanh(pre_act[:, :channel_count])
    sig_g = jax.nn.sigmoid(pre_act[:, channel_count:])
    gated = (in_length * tanh_f * sig_g).astype(jnp.bfloat16)
    gated_grad = in_length * jnp.dot(cotangent, w_res.T, preferred_element_type=jnp.float32)
    pre_grad = jnp.concatenate(
        [gated_grad * sig_g * (1.0 - tanh_f * tanh_f), gated_grad * tanh_f * sig_g * (1.0 - sig_g)],
        1,
    ).astype(jnp.bfloat16)
    return (gated, pre_grad)


def make_reducer(sizes, rc, n_conv, rr, n_res, scale, edge_shape):
    nx, nzh, nc, ny, nzl = sizes
    nz = nzh * nzl
    cyc, cyr = n_conv // ny, n_res // ny
    cc, cr = cyc // nzl, cyr // nzl
    hc, hr = rc // 2, rr // 2
    base_xa, base_yb = 1, 1 + nx
    base_ya, base_xb = 1 + nx + ny, 1 + nx + 2 * ny
    base_z = 1 + 2 * nx + 2 * ny
    n_slots = base_z + nz
    n_peers = (nc - 1) + (nx - 1) + (ny - 1) + (nz - 1) + 2
    n_tm = nx * nzh * nc
    mesh_id = pl.DeviceIdType.MESH

    def kernel(conv_ref, res_ref, edge_ref, conv_out, res_out, edge_out,
               rc_conv, rc_res, sx_conv, sx_res,
               rxa_conv, rxa_res, ryb_conv, ryb_res,
               sa_conv, sa_res, rya_conv, rya_res,
               sb_conv, sb_res, rxb_conv, rxb_res,
               sz_both, rz_both,
               edge_buf, own_conv, own_res, send_sems, recv_sems, local_sems, own_sems):
        me_x = lax.axis_index("x")
        me_zh = lax.axis_index("zh")
        me_c = lax.axis_index("c")
        me_y = lax.axis_index("y")
        me_zl = lax.axis_index("zl")
        me_z = me_zh * nzl + me_zl
        other_c = 1 - me_c

        def dev(x=None, zh=None, c=None, y=None, zl=None):
            return (me_x if x is None else x, me_zh if zh is None else zh,
                    me_c if c is None else c, me_y if y is None else y,
                    me_zl if zl is None else zl)

        peers = [dev(c=other_c)]
        x_peers = [dev(x=lax.rem(me_x + d, nx)) for d in range(1, nx)]
        y_peers = [dev(y=lax.rem(me_y + d, ny)) for d in range(1, ny)]
        z_peers = []
        for d in range(1, nz):
            q = lax.rem(me_z + d, nz)
            z_peers.append(dev(zh=q // nzl, zl=lax.rem(q, nzl)))
        barrier = pltpu.get_barrier_semaphore()
        t = (me_x * nzh + me_zh) * nc + me_c

        def tm_dev(u):
            return dev(x=u // (nzh * nc), zh=lax.rem(u // nc, nzh), c=lax.rem(u, nc))

        before = tm_dev(lax.rem(t + n_tm - 1, n_tm))
        after = tm_dev(lax.rem(t + 1, n_tm))
        far_first = sorted(range(1, nz), key=lambda d: -min(d, nz - d))
        for peer in [z_peers[d - 1] for d in far_first] + [before, after] + peers + x_peers + y_peers:
            pl.semaphore_signal(barrier, inc=1, device_id=peer, device_id_type=mesh_id)
        pl.semaphore_wait(barrier, n_peers)

        sends = []

        def send(kind, src, dst, slot, peer):
            copy = pltpu.make_async_remote_copy(
                src_ref=src, dst_ref=dst, send_sem=send_sems.at[kind, slot],
                recv_sem=recv_sems.at[kind, slot], device_id=peer, device_id_type=mesh_id)
            copy.start()
            sends.append(copy)

        def arrive(kind, src, dst, slot):
            pltpu.make_async_remote_copy(
                src_ref=src, dst_ref=dst, send_sem=send_sems.at[kind, slot],
                recv_sem=recv_sems.at[kind, slot], device_id=dev(),
                device_id_type=mesh_id).wait_recv()

        def keep(kind, which, src, dst):
            copy = pltpu.make_async_copy(src, dst, local_sems.at[kind, which])
            copy.start()
            return copy

        edge = pltpu.make_async_remote_copy(
            src_ref=edge_ref, dst_ref=edge_buf, send_sem=local_sems.at[0, 2],
            recv_sem=local_sems.at[1, 2], device_id=before, device_id_type=mesh_id)
        edge.start()

        send(0, conv_ref.at[:, :, pl.ds(other_c, 1)], rc_conv, 0, peers[0])
        send(1, res_ref.at[:, :, pl.ds(other_c, 1)], rc_res, 0, peers[0])
        own_in = [pltpu.make_async_copy(conv_ref.at[:, :, pl.ds(me_c, 1)], own_conv, own_sems.at[0]),
                  pltpu.make_async_copy(res_ref.at[:, :, pl.ds(me_c, 1)], own_res, own_sems.at[1])]
        for copy in own_in:
            copy.start()
        for copy in own_in:
            copy.wait()
        arrive(0, conv_ref.at[:, :, pl.ds(other_c, 1)], rc_conv, 0)
        arrive(1, res_ref.at[:, :, pl.ds(other_c, 1)], rc_res, 0)
        for x in range(nx):
            for zh in range(nzh):
                own_c = own_conv[x, zh, 0].astype(jnp.float32)
                sx_conv[x, zh] = (own_c + rc_conv[x, zh, 0].astype(jnp.float32)).astype(jnp.bfloat16)
                own_r = own_res[x, zh, 0].astype(jnp.float32)
                sx_res[x, zh] = (own_r + rc_res[x, zh, 0].astype(jnp.float32)).astype(jnp.bfloat16)

        for d in range(1, nx):
            tx = lax.rem(me_x + d, nx)
            send(0, sx_conv.at[tx, :, pl.ds(0, hc)], rxa_conv.at[me_x], base_xa + me_x, x_peers[d - 1])
            send(1, sx_res.at[tx, :, pl.ds(0, hr)], rxa_res.at[me_x], base_xa + me_x, x_peers[d - 1])
        for d in range(1, ny):
            ty = lax.rem(me_y + d, ny)
            send(0, sx_conv.at[:, :, pl.ds(hc, hc), pl.ds(ty * cyc, cyc)], ryb_conv.at[me_y],
                 base_yb + me_y, y_peers[d - 1])
            send(1, sx_res.at[:, :, pl.ds(hr, hr), pl.ds(ty * cyr, cyr)], ryb_res.at[me_y],
                 base_yb + me_y, y_peers[d - 1])
        own_b = [keep(0, 0, sx_conv.at[:, :, pl.ds(hc, hc), pl.ds(me_y * cyc, cyc)], ryb_conv.at[me_y]),
                 keep(1, 0, sx_res.at[:, :, pl.ds(hr, hr), pl.ds(me_y * cyr, cyr)], ryb_res.at[me_y])]

        for d in range(1, nx):
            sx = lax.rem(me_x + nx - d, nx)
            arrive(0, sx_conv.at[sx, :, pl.ds(0, hc)], rxa_conv.at[sx], base_xa + sx)
            arrive(1, sx_res.at[sx, :, pl.ds(0, hr)], rxa_res.at[sx], base_xa + sx)
        acc_c = sx_conv[me_x, :, :hc].astype(jnp.float32)
        acc_r = sx_res[me_x, :, :hr].astype(jnp.float32)
        for d in range(1, nx):
            sx = lax.rem(me_x + nx - d, nx)
            acc_c = acc_c + rxa_conv[sx].astype(jnp.float32)
            acc_r = acc_r + rxa_res[sx].astype(jnp.float32)
        sa_conv[...] = acc_c.astype(jnp.bfloat16)
        sa_res[...] = acc_r.astype(jnp.bfloat16)
        for d in range(1, ny):
            ty = lax.rem(me_y + d, ny)
            send(0, sa_conv.at[:, :, pl.ds(ty * cyc, cyc)], rya_conv.at[me_y], base_ya + me_y, y_peers[d - 1])
            send(1, sa_res.at[:, :, pl.ds(ty * cyr, cyr)], rya_res.at[me_y], base_ya + me_y, y_peers[d - 1])
        own_a = [keep(0, 1, sa_conv.at[:, :, pl.ds(me_y * cyc, cyc)], rya_conv.at[me_y]),
                 keep(1, 1, sa_res.at[:, :, pl.ds(me_y * cyr, cyr)], rya_res.at[me_y])]

        for d in range(1, ny):
            sy = lax.rem(me_y + ny - d, ny)
            arrive(0, sx_conv.at[:, :, pl.ds(hc, hc), pl.ds(0, cyc)], ryb_conv.at[sy], base_yb + sy)
            arrive(1, sx_res.at[:, :, pl.ds(hr, hr), pl.ds(0, cyr)], ryb_res.at[sy], base_yb + sy)
        for copy in own_b:
            copy.wait()
        acc_c = ryb_conv[0].astype(jnp.float32)
        acc_r = ryb_res[0].astype(jnp.float32)
        for s in range(1, ny):
            acc_c = acc_c + ryb_conv[s].astype(jnp.float32)
            acc_r = acc_r + ryb_res[s].astype(jnp.float32)
        sb_conv[...] = acc_c.astype(jnp.bfloat16)
        sb_res[...] = acc_r.astype(jnp.bfloat16)
        for d in range(1, nx):
            tx = lax.rem(me_x + d, nx)
            send(0, sb_conv.at[tx], rxb_conv.at[me_x], base_xb + me_x, x_peers[d - 1])
            send(1, sb_res.at[tx], rxb_res.at[me_x], base_xb + me_x, x_peers[d - 1])

        for d in range(1, ny):
            sy = lax.rem(me_y + ny - d, ny)
            arrive(0, sa_conv.at[:, :, pl.ds(0, cyc)], rya_conv.at[sy], base_ya + sy)
            arrive(1, sa_res.at[:, :, pl.ds(0, cyr)], rya_res.at[sy], base_ya + sy)
        for copy in own_a:
            copy.wait()
        for d in range(1, nx):
            sx = lax.rem(me_x + nx - d, nx)
            arrive(0, sb_conv.at[sx], rxb_conv.at[sx], base_xb + sx)
            arrive(1, sb_res.at[sx], rxb_res.at[sx], base_xb + sx)
        top_c = rya_conv[0].astype(jnp.float32)
        top_r = rya_res[0].astype(jnp.float32)
        for s in range(1, ny):
            top_c = top_c + rya_conv[s].astype(jnp.float32)
            top_r = top_r + rya_res[s].astype(jnp.float32)
        low_c = sb_conv[me_x].astype(jnp.float32)
        low_r = sb_res[me_x].astype(jnp.float32)
        for d in range(1, nx):
            sx = lax.rem(me_x + nx - d, nx)
            low_c = low_c + rxb_conv[sx].astype(jnp.float32)
            low_r = low_r + rxb_res[sx].astype(jnp.float32)
        acc_c = jnp.concatenate([top_c, low_c], axis=1)
        acc_r = jnp.concatenate([top_r, low_r], axis=1)
        for zh in range(nzh):
            flip_c = acc_c[zh].T
            flip_r = acc_r[zh].T
            for zl in range(nzl):
                q = zh * nzl + zl
                sz_both[q, :cc, :] = flip_c[zl * cc:(zl + 1) * cc, :].astype(jnp.bfloat16)
                sz_both[q, cc:, :rr] = flip_r[zl * cr:(zl + 1) * cr, :].astype(jnp.bfloat16)
                sz_both[q, cc:, rr:] = jnp.zeros((cr, rc - rr), jnp.bfloat16)

        for d in range(1, nz):
            tz = lax.rem(me_z + d, nz)
            send(0, sz_both.at[tz], rz_both.at[me_z], base_z + me_z, z_peers[d - 1])
        for d in range(1, nz):
            sz = lax.rem(me_z + nz - d, nz)
            arrive(0, sz_both.at[sz], rz_both.at[sz], base_z + sz)
        acc = sz_both[me_z].astype(jnp.float32)
        for d in range(1, nz):
            sz = lax.rem(me_z + nz - d, nz)
            acc = acc + rz_both[sz].astype(jnp.float32)
        conv_out[...] = acc[:cc] * scale
        res_out[...] = acc[cc:, :rr] * scale
        edge.wait_recv()

        @pl.when(t < n_tm - 1)
        def _():
            edge_out[...] = edge_buf[...]

        @pl.when(t == n_tm - 1)
        def _():
            edge_out[...] = jnp.zeros_like(edge_out)

        for copy in sends:
            copy.wait_send()
        edge.wait_send()

    vmem = pl.BlockSpec(memory_space=pltpu.VMEM)
    bf16, f32 = jnp.bfloat16, jnp.float32
    return pl.pallas_call(
        kernel,
        out_shape=(jax.ShapeDtypeStruct((cc, rc), f32), jax.ShapeDtypeStruct((cr, rr), f32),
                   jax.ShapeDtypeStruct(edge_shape, bf16)),
        in_specs=[pl.BlockSpec(memory_space=pl.ANY), pl.BlockSpec(memory_space=pl.ANY), vmem],
        out_specs=(vmem, vmem, vmem),
        scratch_shapes=[
            pltpu.VMEM((nx, nzh, 1, rc, n_conv), bf16),
            pltpu.VMEM((nx, nzh, 1, rr, n_res), bf16),
            pltpu.VMEM((nx, nzh, rc, n_conv), bf16),
            pltpu.VMEM((nx, nzh, rr, n_res), bf16),
            pltpu.VMEM((nx, nzh, hc, n_conv), bf16),
            pltpu.VMEM((nx, nzh, hr, n_res), bf16),
            pltpu.VMEM((ny, nx, nzh, hc, cyc), bf16),
            pltpu.VMEM((ny, nx, nzh, hr, cyr), bf16),
            pltpu.VMEM((nzh, hc, n_conv), bf16),
            pltpu.VMEM((nzh, hr, n_res), bf16),
            pltpu.VMEM((ny, nzh, hc, cyc), bf16),
            pltpu.VMEM((ny, nzh, hr, cyr), bf16),
            pltpu.VMEM((nx, nzh, hc, cyc), bf16),
            pltpu.VMEM((nx, nzh, hr, cyr), bf16),
            pltpu.VMEM((nx, nzh, hc, cyc), bf16),
            pltpu.VMEM((nx, nzh, hr, cyr), bf16),
            pltpu.VMEM((nz, cc + cr, rc), bf16),
            pltpu.VMEM((nz, cc + cr, rc), bf16),
            pltpu.VMEM(edge_shape, bf16),
            pltpu.VMEM((nx, nzh, 1, rc, n_conv), bf16),
            pltpu.VMEM((nx, nzh, 1, rr, n_res), bf16),
            pltpu.SemaphoreType.DMA((2, n_slots)),
            pltpu.SemaphoreType.DMA((2, n_slots)),
            pltpu.SemaphoreType.DMA((2, 3)),
            pltpu.SemaphoreType.DMA((2,)),
        ],
        compiler_params=pltpu.CompilerParams(collective_id=0, has_side_effects=True),
    )


def make_body(sizes):
    nx, nzh, nc, ny, nzl = sizes
    n_tm = nx * nzh * nc
    n_rep = ny * nzl

    def body(samples, grad_out, w_conv, w_res, lengths):
        sequence_rows = samples[0]
        cotangent = grad_out[0]
        seq_len = lengths[0]
        count_of_rows = sequence_rows.shape[0]
        channel_count = sequence_rows.shape[1]
        start_row = lax.axis_index(TM) * count_of_rows
        trailing_rows = sequence_rows[count_of_rows - DILATION_STEP :]
        arrived = passed_along(trailing_rows, TM, 1, n_tm)
        prior_samples = jnp.concatenate(
            [arrived, sequence_rows[: count_of_rows - DILATION_STEP]], 0
        )
        inputs = jnp.concatenate([prior_samples, sequence_rows], 1)
        in_length = (start_row + jnp.arange(count_of_rows) < seq_len).astype(jnp.float32)[:, None]
        gated, pre_grad = gate_backward(inputs, cotangent, in_length, w_conv, w_res)
        input_gradient = jnp.dot(pre_grad, w_conv.T, preferred_element_type=jnp.float32)
        term_conv = jnp.einsum("tk,tn->kn", inputs, pre_grad, preferred_element_type=jnp.float32)
        term_res = jnp.einsum("tk,tn->kn", gated, cotangent, preferred_element_type=jnp.float32)
        kc, n_conv = term_conv.shape
        kr, n_res = term_res.shape
        rc, rr = kc // n_tm, kr // n_tm
        all_tokens = count_of_rows * n_tm * n_rep
        edge_rows = input_gradient[:DILATION_STEP, :channel_count].astype(jnp.bfloat16)
        reducer = make_reducer(sizes, rc, n_conv, rr, n_res, float(all_tokens) ** (-0.5), edge_rows.shape)
        split = count_of_rows - DILATION_STEP
        head_rows = (
            cotangent[:split].astype(jnp.float32) + input_gradient[:split, channel_count:]
            + input_gradient[DILATION_STEP:, :channel_count]
        ).astype(jnp.bfloat16)
        conv_in = term_conv.astype(jnp.bfloat16).reshape(nx, nzh, nc, rc, n_conv)
        res_in = term_res.astype(jnp.bfloat16).reshape(nx, nzh, nc, rr, n_res)
        head_rows, conv_in, res_in, edge_rows = lax.optimization_barrier((head_rows, conv_in, res_in, edge_rows))
        flip_conv, flip_res, incoming_gradient = reducer(conv_in, res_in, edge_rows)
        tail_rows = (
            cotangent[split:].astype(jnp.float32) + input_gradient[split:, channel_count:]
            + incoming_gradient.astype(jnp.float32)
        ).astype(jnp.bfloat16)
        grad_rows = jnp.concatenate([head_rows, tail_rows], 0)
        return (grad_rows[None], flip_conv.T, flip_res.T)

    return body


def solution(mesh):
    n_tm, n_rep = mesh.devices.shape
    nc = 2
    nzh = 2
    nx = n_tm // (nc * nzh)
    nzl = 8
    ny = n_rep // nzl
    sizes = (nx, nzh, nc, ny, nzl)
    fine = Mesh(mesh.devices.reshape(sizes), ("x", "zh", "c", "y", "zl"))
    return jax.shard_map(
        make_body(sizes),
        mesh=fine,
        in_specs=(P(REP, TM, None), P(REP, TM, None), P(), P(), P(REP)),
        out_specs=(P(REP, TM, None), P(TM, REP), P(TM, REP)),
        check_vma=False,
    )
```

```python
import jax
import jax.numpy as jnp
from jax import lax
from jax.experimental import pallas as pl
from jax.experimental.pallas import tpu as pltpu
from jax.sharding import Mesh, PartitionSpec as P

DILATION_STEP = 256
TM = ("x", "zh", "c")
REP = ("y", "zl")


def passed_along(array, axis, by, length):
    pairs = [(i, i + by) for i in range(length) if 0 <= i + by < length]
    return lax.ppermute(array, axis, pairs)


def gate_backward(inputs, cotangent, in_length, w_conv, w_res):
    channel_count = w_res.shape[0]
    pre_act = jnp.dot(inputs, w_conv, preferred_element_type=jnp.float32)
    tanh_f = jnp.tanh(pre_act[:, :channel_count])
    sig_g = jax.nn.sigmoid(pre_act[:, channel_count:])
    gated = (in_length * tanh_f * sig_g).astype(jnp.bfloat16)
    gated_grad = in_length * jnp.dot(cotangent, w_res.T, preferred_element_type=jnp.float32)
    pre_grad = jnp.concatenate(
        [gated_grad * sig_g * (1.0 - tanh_f * tanh_f), gated_grad * tanh_f * sig_g * (1.0 - sig_g)],
        1,
    ).astype(jnp.bfloat16)
    return (gated, pre_grad)


def make_reducer(sizes, rc, n_conv, rr, n_res, scale, edge_shape, rows_shape):
    nx, nzh, nc, ny, nzl = sizes
    nz = nzh * nzl
    cyc, cyr = n_conv // ny, n_res // ny
    cc, cr = cyc // nzl, cyr // nzl
    hc, hr = rc // 2, rr // 2
    base_xa, base_yb = 1, 1 + nx
    base_ya, base_xb = 1 + nx + ny, 1 + nx + 2 * ny
    base_z = 1 + 2 * nx + 2 * ny
    n_slots = base_z + nz
    n_peers = (nc - 1) + (nx - 1) + (ny - 1) + (nz - 1) + 2
    n_tm = nx * nzh * nc
    mesh_id = pl.DeviceIdType.MESH

    def kernel(conv_ref, res_ref, edge_ref, cot_ref, grad_ref, conv_out, res_out, rows_out,
               rc_conv, rc_res, sx_conv, sx_res,
               rxa_conv, rxa_res, ryb_conv, ryb_res,
               sa_conv, sa_res, rya_conv, rya_res,
               sb_conv, sb_res, rxb_conv, rxb_res,
               sz_both, rz_both,
               edge_buf, own_conv, own_res, cot_v, cur_v, late_v, send_sems, recv_sems, local_sems, own_sems):
        me_x = lax.axis_index("x")
        me_zh = lax.axis_index("zh")
        me_c = lax.axis_index("c")
        me_y = lax.axis_index("y")
        me_zl = lax.axis_index("zl")
        me_z = me_zh * nzl + me_zl
        other_c = 1 - me_c

        def dev(x=None, zh=None, c=None, y=None, zl=None):
            return (me_x if x is None else x, me_zh if zh is None else zh,
                    me_c if c is None else c, me_y if y is None else y,
                    me_zl if zl is None else zl)

        peers = [dev(c=other_c)]
        x_peers = [dev(x=lax.rem(me_x + d, nx)) for d in range(1, nx)]
        y_peers = [dev(y=lax.rem(me_y + d, ny)) for d in range(1, ny)]
        z_peers = []
        for d in range(1, nz):
            q = lax.rem(me_z + d, nz)
            z_peers.append(dev(zh=q // nzl, zl=lax.rem(q, nzl)))
        barrier = pltpu.get_barrier_semaphore()
        t = (me_x * nzh + me_zh) * nc + me_c

        def tm_dev(u):
            return dev(x=u // (nzh * nc), zh=lax.rem(u // nc, nzh), c=lax.rem(u, nc))

        before = tm_dev(lax.rem(t + n_tm - 1, n_tm))
        after = tm_dev(lax.rem(t + 1, n_tm))
        far_first = sorted(range(1, nz), key=lambda d: -min(d, nz - d))
        for peer in [z_peers[d - 1] for d in far_first] + [before, after] + peers + x_peers + y_peers:
            pl.semaphore_signal(barrier, inc=1, device_id=peer, device_id_type=mesh_id)
        pl.semaphore_wait(barrier, n_peers)

        sends = []

        def send(kind, src, dst, slot, peer):
            copy = pltpu.make_async_remote_copy(
                src_ref=src, dst_ref=dst, send_sem=send_sems.at[kind, slot],
                recv_sem=recv_sems.at[kind, slot], device_id=peer, device_id_type=mesh_id)
            copy.start()
            sends.append(copy)

        def arrive(kind, src, dst, slot):
            pltpu.make_async_remote_copy(
                src_ref=src, dst_ref=dst, send_sem=send_sems.at[kind, slot],
                recv_sem=recv_sems.at[kind, slot], device_id=dev(),
                device_id_type=mesh_id).wait_recv()

        def keep(kind, which, src, dst):
            copy = pltpu.make_async_copy(src, dst, local_sems.at[kind, which])
            copy.start()
            return copy

        edge = pltpu.make_async_remote_copy(
            src_ref=edge_ref, dst_ref=edge_buf, send_sem=local_sems.at[0, 2],
            recv_sem=local_sems.at[1, 2], device_id=before, device_id_type=mesh_id)
        edge.start()

        send(0, conv_ref.at[:, :, pl.ds(other_c, 1)], rc_conv, 0, peers[0])
        send(1, res_ref.at[:, :, pl.ds(other_c, 1)], rc_res, 0, peers[0])
        own_in = [pltpu.make_async_copy(conv_ref.at[:, :, pl.ds(me_c, 1)], own_conv, own_sems.at[0]),
                  pltpu.make_async_copy(res_ref.at[:, :, pl.ds(me_c, 1)], own_res, own_sems.at[1])]
        for copy in own_in:
            copy.start()
        step, ch = edge_shape
        count = cot_v.shape[0]
        split = count - step
        row_in = [pltpu.make_async_copy(cot_ref, cot_v, own_sems.at[2]),
                  pltpu.make_async_copy(grad_ref.at[:, pl.ds(ch, ch)], cur_v, own_sems.at[3]),
                  pltpu.make_async_copy(grad_ref.at[pl.ds(step, count - step), pl.ds(0, ch)], late_v, own_sems.at[4])]
        for copy in row_in:
            copy.start()
        for copy in own_in:
            copy.wait()
        arrive(0, conv_ref.at[:, :, pl.ds(other_c, 1)], rc_conv, 0)
        arrive(1, res_ref.at[:, :, pl.ds(other_c, 1)], rc_res, 0)
        for x in range(nx):
            for zh in range(nzh):
                own_c = own_conv[x, zh, 0].astype(jnp.float32)
                sx_conv[x, zh] = (own_c + rc_conv[x, zh, 0].astype(jnp.float32)).astype(jnp.bfloat16)
                own_r = own_res[x, zh, 0].astype(jnp.float32)
                sx_res[x, zh] = (own_r + rc_res[x, zh, 0].astype(jnp.float32)).astype(jnp.bfloat16)

        for d in range(1, nx):
            tx = lax.rem(me_x + d, nx)
            send(0, sx_conv.at[tx, :, pl.ds(0, hc)], rxa_conv.at[me_x], base_xa + me_x, x_peers[d - 1])
            send(1, sx_res.at[tx, :, pl.ds(0, hr)], rxa_res.at[me_x], base_xa + me_x, x_peers[d - 1])
        for d in range(1, ny):
            ty = lax.rem(me_y + d, ny)
            send(0, sx_conv.at[:, :, pl.ds(hc, hc), pl.ds(ty * cyc, cyc)], ryb_conv.at[me_y],
                 base_yb + me_y, y_peers[d - 1])
            send(1, sx_res.at[:, :, pl.ds(hr, hr), pl.ds(ty * cyr, cyr)], ryb_res.at[me_y],
                 base_yb + me_y, y_peers[d - 1])
        for copy in row_in:
            copy.wait()
        rows_out[pl.ds(0, split)] = (cot_v[pl.ds(0, split)].astype(jnp.float32) + cur_v[pl.ds(0, split)]
                                     + late_v[pl.ds(0, split)]).astype(jnp.bfloat16)
        own_b = [keep(0, 0, sx_conv.at[:, :, pl.ds(hc, hc), pl.ds(me_y * cyc, cyc)], ryb_conv.at[me_y]),
                 keep(1, 0, sx_res.at[:, :, pl.ds(hr, hr), pl.ds(me_y * cyr, cyr)], ryb_res.at[me_y])]

        for d in range(1, nx):
            sx = lax.rem(me_x + nx - d, nx)
            arrive(0, sx_conv.at[sx, :, pl.ds(0, hc)], rxa_conv.at[sx], base_xa + sx)
            arrive(1, sx_res.at[sx, :, pl.ds(0, hr)], rxa_res.at[sx], base_xa + sx)
        acc_c = sx_conv[me_x, :, :hc].astype(jnp.float32)
        acc_r = sx_res[me_x, :, :hr].astype(jnp.float32)
        for d in range(1, nx):
            sx = lax.rem(me_x + nx - d, nx)
            acc_c = acc_c + rxa_conv[sx].astype(jnp.float32)
            acc_r = acc_r + rxa_res[sx].astype(jnp.float32)
        sa_conv[...] = acc_c.astype(jnp.bfloat16)
        sa_res[...] = acc_r.astype(jnp.bfloat16)
        for d in range(1, ny):
            ty = lax.rem(me_y + d, ny)
            send(0, sa_conv.at[:, :, pl.ds(ty * cyc, cyc)], rya_conv.at[me_y], base_ya + me_y, y_peers[d - 1])
            send(1, sa_res.at[:, :, pl.ds(ty * cyr, cyr)], rya_res.at[me_y], base_ya + me_y, y_peers[d - 1])
        own_a = [keep(0, 1, sa_conv.at[:, :, pl.ds(me_y * cyc, cyc)], rya_conv.at[me_y]),
                 keep(1, 1, sa_res.at[:, :, pl.ds(me_y * cyr, cyr)], rya_res.at[me_y])]

        for d in range(1, ny):
            sy = lax.rem(me_y + ny - d, ny)
            arrive(0, sx_conv.at[:, :, pl.ds(hc, hc), pl.ds(0, cyc)], ryb_conv.at[sy], base_yb + sy)
            arrive(1, sx_res.at[:, :, pl.ds(hr, hr), pl.ds(0, cyr)], ryb_res.at[sy], base_yb + sy)
        for copy in own_b:
            copy.wait()
        acc_c = ryb_conv[0].astype(jnp.float32)
        acc_r = ryb_res[0].astype(jnp.float32)
        for s in range(1, ny):
            acc_c = acc_c + ryb_conv[s].astype(jnp.float32)
            acc_r = acc_r + ryb_res[s].astype(jnp.float32)
        sb_conv[...] = acc_c.astype(jnp.bfloat16)
        sb_res[...] = acc_r.astype(jnp.bfloat16)
        for d in range(1, nx):
            tx = lax.rem(me_x + d, nx)
            send(0, sb_conv.at[tx], rxb_conv.at[me_x], base_xb + me_x, x_peers[d - 1])
            send(1, sb_res.at[tx], rxb_res.at[me_x], base_xb + me_x, x_peers[d - 1])

        for d in range(1, ny):
            sy = lax.rem(me_y + ny - d, ny)
            arrive(0, sa_conv.at[:, :, pl.ds(0, cyc)], rya_conv.at[sy], base_ya + sy)
            arrive(1, sa_res.at[:, :, pl.ds(0, cyr)], rya_res.at[sy], base_ya + sy)
        for copy in own_a:
            copy.wait()
        for d in range(1, nx):
            sx = lax.rem(me_x + nx - d, nx)
            arrive(0, sb_conv.at[sx], rxb_conv.at[sx], base_xb + sx)
            arrive(1, sb_res.at[sx], rxb_res.at[sx], base_xb + sx)
        top_c = rya_conv[0].astype(jnp.float32)
        top_r = rya_res[0].astype(jnp.float32)
        for s in range(1, ny):
            top_c = top_c + rya_conv[s].astype(jnp.float32)
            top_r = top_r + rya_res[s].astype(jnp.float32)
        low_c = sb_conv[me_x].astype(jnp.float32)
        low_r = sb_res[me_x].astype(jnp.float32)
        for d in range(1, nx):
            sx = lax.rem(me_x + nx - d, nx)
            low_c = low_c + rxb_conv[sx].astype(jnp.float32)
            low_r = low_r + rxb_res[sx].astype(jnp.float32)
        acc_c = jnp.concatenate([top_c, low_c], axis=1)
        acc_r = jnp.concatenate([top_r, low_r], axis=1)
        for zh in range(nzh):
            flip_c = acc_c[zh].T
            flip_r = acc_r[zh].T
            for zl in range(nzl):
                q = zh * nzl + zl
                sz_both[q, :cc, :] = flip_c[zl * cc:(zl + 1) * cc, :].astype(jnp.bfloat16)
                sz_both[q, cc:, :rr] = flip_r[zl * cr:(zl + 1) * cr, :].astype(jnp.bfloat16)
                sz_both[q, cc:, rr:] = jnp.zeros((cr, rc - rr), jnp.bfloat16)

        for d in range(1, nz):
            tz = lax.rem(me_z + d, nz)
            send(0, sz_both.at[tz], rz_both.at[me_z], base_z + me_z, z_peers[d - 1])
        for d in range(1, nz):
            sz = lax.rem(me_z + nz - d, nz)
            arrive(0, sz_both.at[sz], rz_both.at[sz], base_z + sz)
        acc = sz_both[me_z].astype(jnp.float32)
        for d in range(1, nz):
            sz = lax.rem(me_z + nz - d, nz)
            acc = acc + rz_both[sz].astype(jnp.float32)
        conv_out[...] = acc[:cc] * scale
        res_out[...] = acc[cc:, :rr] * scale
        edge.wait_recv()

        tail = cot_v[pl.ds(split, step)].astype(jnp.float32) + cur_v[pl.ds(split, step)]

        @pl.when(t < n_tm - 1)
        def _():
            rows_out[pl.ds(split, step)] = (tail + edge_buf[...].astype(jnp.float32)).astype(jnp.bfloat16)

        @pl.when(t == n_tm - 1)
        def _():
            rows_out[pl.ds(split, step)] = tail.astype(jnp.bfloat16)

        for copy in sends:
            copy.wait_send()
        edge.wait_send()

    vmem = pl.BlockSpec(memory_space=pltpu.VMEM)
    bf16, f32 = jnp.bfloat16, jnp.float32
    return pl.pallas_call(
        kernel,
        out_shape=(jax.ShapeDtypeStruct((cc, rc), f32), jax.ShapeDtypeStruct((cr, rr), f32),
                   jax.ShapeDtypeStruct(rows_shape, bf16)),
        in_specs=[pl.BlockSpec(memory_space=pl.ANY), pl.BlockSpec(memory_space=pl.ANY), vmem,
                  pl.BlockSpec(memory_space=pl.ANY), pl.BlockSpec(memory_space=pl.ANY)],
        out_specs=(vmem, vmem, vmem),
        scratch_shapes=[
            pltpu.VMEM((nx, nzh, 1, rc, n_conv), bf16),
            pltpu.VMEM((nx, nzh, 1, rr, n_res), bf16),
            pltpu.VMEM((nx, nzh, rc, n_conv), bf16),
            pltpu.VMEM((nx, nzh, rr, n_res), bf16),
            pltpu.VMEM((nx, nzh, hc, n_conv), bf16),
            pltpu.VMEM((nx, nzh, hr, n_res), bf16),
            pltpu.VMEM((ny, nx, nzh, hc, cyc), bf16),
            pltpu.VMEM((ny, nx, nzh, hr, cyr), bf16),
            pltpu.VMEM((nzh, hc, n_conv), bf16),
            pltpu.VMEM((nzh, hr, n_res), bf16),
            pltpu.VMEM((ny, nzh, hc, cyc), bf16),
            pltpu.VMEM((ny, nzh, hr, cyr), bf16),
            pltpu.VMEM((nx, nzh, hc, cyc), bf16),
            pltpu.VMEM((nx, nzh, hr, cyr), bf16),
            pltpu.VMEM((nx, nzh, hc, cyc), bf16),
            pltpu.VMEM((nx, nzh, hr, cyr), bf16),
            pltpu.VMEM((nz, cc + cr, rc), bf16),
            pltpu.VMEM((nz, cc + cr, rc), bf16),
            pltpu.VMEM(edge_shape, bf16),
            pltpu.VMEM((nx, nzh, 1, rc, n_conv), bf16),
            pltpu.VMEM((nx, nzh, 1, rr, n_res), bf16),
            pltpu.VMEM(rows_shape, bf16),
            pltpu.VMEM(rows_shape, f32),
            pltpu.VMEM((rows_shape[0] - edge_shape[0], edge_shape[1]), f32),
            pltpu.SemaphoreType.DMA((2, n_slots)),
            pltpu.SemaphoreType.DMA((2, n_slots)),
            pltpu.SemaphoreType.DMA((2, 3)),
            pltpu.SemaphoreType.DMA((5,)),
        ],
        compiler_params=pltpu.CompilerParams(collective_id=0, has_side_effects=True),
    )


def make_body(sizes):
    nx, nzh, nc, ny, nzl = sizes
    n_tm = nx * nzh * nc
    n_rep = ny * nzl

    def body(samples, grad_out, w_conv, w_res, lengths):
        sequence_rows = samples[0]
        cotangent = grad_out[0]
        seq_len = lengths[0]
        count_of_rows = sequence_rows.shape[0]
        channel_count = sequence_rows.shape[1]
        start_row = lax.axis_index(TM) * count_of_rows
        trailing_rows = sequence_rows[count_of_rows - DILATION_STEP :]
        arrived = passed_along(trailing_rows, TM, 1, n_tm)
        prior_samples = jnp.concatenate(
            [arrived, sequence_rows[: count_of_rows - DILATION_STEP]], 0
        )
        inputs = jnp.concatenate([prior_samples, sequence_rows], 1)
        in_length = (start_row + jnp.arange(count_of_rows) < seq_len).astype(jnp.float32)[:, None]
        gated, pre_grad = gate_backward(inputs, cotangent, in_length, w_conv, w_res)
        input_gradient = jnp.dot(pre_grad, w_conv.T, preferred_element_type=jnp.float32)
        term_conv = jnp.einsum("tk,tn->kn", inputs, pre_grad, preferred_element_type=jnp.float32)
        term_res = jnp.einsum("tk,tn->kn", gated, cotangent, preferred_element_type=jnp.float32)
        kc, n_conv = term_conv.shape
        kr, n_res = term_res.shape
        rc, rr = kc // n_tm, kr // n_tm
        all_tokens = count_of_rows * n_tm * n_rep
        edge_rows = input_gradient[:DILATION_STEP, :channel_count].astype(jnp.bfloat16)
        reducer = make_reducer(sizes, rc, n_conv, rr, n_res, float(all_tokens) ** (-0.5), edge_rows.shape,
                               cotangent.shape)
        conv_in = term_conv.astype(jnp.bfloat16).reshape(nx, nzh, nc, rc, n_conv)
        res_in = term_res.astype(jnp.bfloat16).reshape(nx, nzh, nc, rr, n_res)
        flip_conv, flip_res, grad_rows = reducer(conv_in, res_in, edge_rows, cotangent, input_gradient)
        return (grad_rows[None], flip_conv.T, flip_res.T)

    return body


def solution(mesh):
    n_tm, n_rep = mesh.devices.shape
    nc = 2
    nzh = 2
    nx = n_tm // (nc * nzh)
    nzl = 8
    ny = n_rep // nzl
    sizes = (nx, nzh, nc, ny, nzl)
    fine = Mesh(mesh.devices.reshape(sizes), ("x", "zh", "c", "y", "zl"))
    return jax.shard_map(
        make_body(sizes),
        mesh=fine,
        in_specs=(P(REP, TM, None), P(REP, TM, None), P(), P(), P(REP)),
        out_specs=(P(REP, TM, None), P(TM, REP), P(TM, REP)),
        check_vma=False,
    )
```

```python
import jax
import jax.numpy as jnp
from jax import lax
from jax.experimental import pallas as pl
from jax.experimental.pallas import tpu as pltpu
from jax.sharding import Mesh, PartitionSpec as P

DILATION_STEP = 256
TM = ("x", "zh", "c")
REP = ("y", "zl")


def passed_along(array, axis, by, length):
    pairs = [(i, i + by) for i in range(length) if 0 <= i + by < length]
    return lax.ppermute(array, axis, pairs)


def gate_backward(inputs, cotangent, in_length, w_conv, w_res):
    channel_count = w_res.shape[0]
    pre_act = jnp.dot(inputs, w_conv, preferred_element_type=jnp.float32)
    tanh_f = jnp.tanh(pre_act[:, :channel_count])
    sig_g = jax.nn.sigmoid(pre_act[:, channel_count:])
    gated = (in_length * tanh_f * sig_g).astype(jnp.bfloat16)
    gated_grad = in_length * jnp.dot(cotangent, w_res.T, preferred_element_type=jnp.float32)
    pre_grad = jnp.concatenate(
        [gated_grad * sig_g * (1.0 - tanh_f * tanh_f), gated_grad * tanh_f * sig_g * (1.0 - sig_g)],
        1,
    ).astype(jnp.bfloat16)
    return (gated, pre_grad)


def make_reducer(sizes, rc, n_conv, rr, n_res, scale, edge_shape):
    nx, nzh, nc, ny, nzl = sizes
    nz = nzh * nzl
    cyc, cyr = n_conv // ny, n_res // ny
    cc, cr = cyc // nzl, cyr // nzl
    hc, hr = rc // 2, rr // 2
    base_xa, base_yb = 1, 1 + nx
    base_ya, base_xb = 1 + nx + ny, 1 + nx + 2 * ny
    base_z = 1 + 2 * nx + 2 * ny
    n_slots = base_z + nz
    n_peers = (nc - 1) + (nx - 1) + (ny - 1) + (nz - 1) + 2
    n_tm = nx * nzh * nc
    mesh_id = pl.DeviceIdType.MESH

    def kernel(conv_ref, res_ref, edge_ref, conv_out, res_out, edge_out,
               rc_conv, rc_res, sx_conv, sx_res,
               rxa_conv, rxa_res, ryb_conv, ryb_res,
               sa_conv, sa_res, rya_conv, rya_res,
               sb_conv, sb_res, rxb_conv, rxb_res,
               sz_both, rz_both,
               edge_buf, own_conv, own_res, send_sems, recv_sems, local_sems, own_sems):
        me_x = lax.axis_index("x")
        me_zh = lax.axis_index("zh")
        me_c = lax.axis_index("c")
        me_y = lax.axis_index("y")
        me_zl = lax.axis_index("zl")
        me_z = me_zh * nzl + me_zl
        other_c = 1 - me_c

        def dev(x=None, zh=None, c=None, y=None, zl=None):
            return (me_x if x is None else x, me_zh if zh is None else zh,
                    me_c if c is None else c, me_y if y is None else y,
                    me_zl if zl is None else zl)

        peers = [dev(c=other_c)]
        x_peers = [dev(x=lax.rem(me_x + d, nx)) for d in range(1, nx)]
        y_peers = [dev(y=lax.rem(me_y + d, ny)) for d in range(1, ny)]
        z_peers = []
        for d in range(1, nz):
            q = lax.rem(me_z + d, nz)
            z_peers.append(dev(zh=q // nzl, zl=lax.rem(q, nzl)))
        barrier = pltpu.get_barrier_semaphore()
        t = (me_x * nzh + me_zh) * nc + me_c

        def tm_dev(u):
            return dev(x=u // (nzh * nc), zh=lax.rem(u // nc, nzh), c=lax.rem(u, nc))

        before = tm_dev(lax.rem(t + n_tm - 1, n_tm))
        after = tm_dev(lax.rem(t + 1, n_tm))
        far_first = sorted(range(1, nz), key=lambda d: -min(d, nz - d))
        for peer in [z_peers[d - 1] for d in far_first] + [before, after] + peers + x_peers + y_peers:
            pl.semaphore_signal(barrier, inc=1, device_id=peer, device_id_type=mesh_id)
        pl.semaphore_wait(barrier, n_peers)

        sends = []

        def send(kind, src, dst, slot, peer):
            copy = pltpu.make_async_remote_copy(
                src_ref=src, dst_ref=dst, send_sem=send_sems.at[kind, slot],
                recv_sem=recv_sems.at[kind, slot], device_id=peer, device_id_type=mesh_id)
            copy.start()
            sends.append(copy)

        def arrive(kind, src, dst, slot):
            pltpu.make_async_remote_copy(
                src_ref=src, dst_ref=dst, send_sem=send_sems.at[kind, slot],
                recv_sem=recv_sems.at[kind, slot], device_id=dev(),
                device_id_type=mesh_id).wait_recv()

        def keep(kind, which, src, dst):
            copy = pltpu.make_async_copy(src, dst, local_sems.at[kind, which])
            copy.start()
            return copy

        edge = pltpu.make_async_remote_copy(
            src_ref=edge_ref, dst_ref=edge_buf, send_sem=local_sems.at[0, 2],
            recv_sem=local_sems.at[1, 2], device_id=before, device_id_type=mesh_id)
        edge.start()

        send(0, conv_ref.at[:, :, pl.ds(other_c, 1)], rc_conv, 0, peers[0])
        send(1, res_ref.at[:, :, pl.ds(other_c, 1)], rc_res, 0, peers[0])
        own_in = [pltpu.make_async_copy(conv_ref.at[:, :, pl.ds(me_c, 1)], own_conv, own_sems.at[0]),
                  pltpu.make_async_copy(res_ref.at[:, :, pl.ds(me_c, 1)], own_res, own_sems.at[1])]
        for copy in own_in:
            copy.start()
        for copy in own_in:
            copy.wait()
        arrive(0, conv_ref.at[:, :, pl.ds(other_c, 1)], rc_conv, 0)
        arrive(1, res_ref.at[:, :, pl.ds(other_c, 1)], rc_res, 0)
        for x in range(nx):
            for zh in range(nzh):
                own_c = own_conv[x, zh, 0].astype(jnp.float32)
                sx_conv[x, zh] = (own_c + rc_conv[x, zh, 0].astype(jnp.float32)).astype(jnp.bfloat16)
                own_r = own_res[x, zh, 0].astype(jnp.float32)
                sx_res[x, zh] = (own_r + rc_res[x, zh, 0].astype(jnp.float32)).astype(jnp.bfloat16)

        for d in range(1, nx):
            tx = lax.rem(me_x + d, nx)
            send(0, sx_conv.at[tx, :, pl.ds(0, hc)], rxa_conv.at[me_x], base_xa + me_x, x_peers[d - 1])
            send(1, sx_res.at[tx, :, pl.ds(0, hr)], rxa_res.at[me_x], base_xa + me_x, x_peers[d - 1])
        for d in range(1, ny):
            ty = lax.rem(me_y + d, ny)
            send(0, sx_conv.at[:, :, pl.ds(hc, hc), pl.ds(ty * cyc, cyc)], ryb_conv.at[me_y],
                 base_yb + me_y, y_peers[d - 1])
            send(1, sx_res.at[:, :, pl.ds(hr, hr), pl.ds(ty * cyr, cyr)], ryb_res.at[me_y],
                 base_yb + me_y, y_peers[d - 1])
        own_b = [keep(0, 0, sx_conv.at[:, :, pl.ds(hc, hc), pl.ds(me_y * cyc, cyc)], ryb_conv.at[me_y]),
                 keep(1, 0, sx_res.at[:, :, pl.ds(hr, hr), pl.ds(me_y * cyr, cyr)], ryb_res.at[me_y])]

        for d in range(1, nx):
            sx = lax.rem(me_x + nx - d, nx)
            arrive(0, sx_conv.at[sx, :, pl.ds(0, hc)], rxa_conv.at[sx], base_xa + sx)
            arrive(1, sx_res.at[sx, :, pl.ds(0, hr)], rxa_res.at[sx], base_xa + sx)
        acc_c = sx_conv[me_x, :, :hc].astype(jnp.float32)
        acc_r = sx_res[me_x, :, :hr].astype(jnp.float32)
        for d in range(1, nx):
            sx = lax.rem(me_x + nx - d, nx)
            acc_c = acc_c + rxa_conv[sx].astype(jnp.float32)
            acc_r = acc_r + rxa_res[sx].astype(jnp.float32)
        sa_conv[...] = acc_c.astype(jnp.bfloat16)
        sa_res[...] = acc_r.astype(jnp.bfloat16)
        for d in range(1, ny):
            ty = lax.rem(me_y + d, ny)
            send(0, sa_conv.at[:, :, pl.ds(ty * cyc, cyc)], rya_conv.at[me_y], base_ya + me_y, y_peers[d - 1])
            send(1, sa_res.at[:, :, pl.ds(ty * cyr, cyr)], rya_res.at[me_y], base_ya + me_y, y_peers[d - 1])
        own_a = [keep(0, 1, sa_conv.at[:, :, pl.ds(me_y * cyc, cyc)], rya_conv.at[me_y]),
                 keep(1, 1, sa_res.at[:, :, pl.ds(me_y * cyr, cyr)], rya_res.at[me_y])]

        for d in range(1, ny):
            sy = lax.rem(me_y + ny - d, ny)
            arrive(0, sx_conv.at[:, :, pl.ds(hc, hc), pl.ds(0, cyc)], ryb_conv.at[sy], base_yb + sy)
            arrive(1, sx_res.at[:, :, pl.ds(hr, hr), pl.ds(0, cyr)], ryb_res.at[sy], base_yb + sy)
        for copy in own_b:
            copy.wait()
        acc_c = ryb_conv[0].astype(jnp.float32)
        acc_r = ryb_res[0].astype(jnp.float32)
        for s in range(1, ny):
            acc_c = acc_c + ryb_conv[s].astype(jnp.float32)
            acc_r = acc_r + ryb_res[s].astype(jnp.float32)
        sb_conv[...] = acc_c.astype(jnp.bfloat16)
        sb_res[...] = acc_r.astype(jnp.bfloat16)
        for d in range(1, nx):
            tx = lax.rem(me_x + d, nx)
            send(0, sb_conv.at[tx], rxb_conv.at[me_x], base_xb + me_x, x_peers[d - 1])
            send(1, sb_res.at[tx], rxb_res.at[me_x], base_xb + me_x, x_peers[d - 1])

        for d in range(1, ny):
            sy = lax.rem(me_y + ny - d, ny)
            arrive(0, sa_conv.at[:, :, pl.ds(0, cyc)], rya_conv.at[sy], base_ya + sy)
            arrive(1, sa_res.at[:, :, pl.ds(0, cyr)], rya_res.at[sy], base_ya + sy)
        for copy in own_a:
            copy.wait()
        for d in range(1, nx):
            sx = lax.rem(me_x + nx - d, nx)
            arrive(0, sb_conv.at[sx], rxb_conv.at[sx], base_xb + sx)
            arrive(1, sb_res.at[sx], rxb_res.at[sx], base_xb + sx)
        top_c = rya_conv[0].astype(jnp.float32)
        top_r = rya_res[0].astype(jnp.float32)
        for s in range(1, ny):
            top_c = top_c + rya_conv[s].astype(jnp.float32)
            top_r = top_r + rya_res[s].astype(jnp.float32)
        low_c = sb_conv[me_x].astype(jnp.float32)
        low_r = sb_res[me_x].astype(jnp.float32)
        for d in range(1, nx):
            sx = lax.rem(me_x + nx - d, nx)
            low_c = low_c + rxb_conv[sx].astype(jnp.float32)
            low_r = low_r + rxb_res[sx].astype(jnp.float32)
        acc_c = jnp.concatenate([top_c, low_c], axis=1)
        acc_r = jnp.concatenate([top_r, low_r], axis=1)
        for zh in range(nzh):
            flip_c = acc_c[zh].T
            flip_r = acc_r[zh].T
            for zl in range(nzl):
                q = zh * nzl + zl
                sz_both[q, :cc, :] = flip_c[zl * cc:(zl + 1) * cc, :].astype(jnp.bfloat16)
                sz_both[q, cc:, :rr] = flip_r[zl * cr:(zl + 1) * cr, :].astype(jnp.bfloat16)
                sz_both[q, cc:, rr:] = jnp.zeros((cr, rc - rr), jnp.bfloat16)

        for d in range(1, nz):
            tz = lax.rem(me_z + d, nz)
            send(0, sz_both.at[tz], rz_both.at[me_z], base_z + me_z, z_peers[d - 1])
        for d in range(1, nz):
            sz = lax.rem(me_z + nz - d, nz)
            arrive(0, sz_both.at[sz], rz_both.at[sz], base_z + sz)
        acc = sz_both[me_z].astype(jnp.float32)
        for d in range(1, nz):
            sz = lax.rem(me_z + nz - d, nz)
            acc = acc + rz_both[sz].astype(jnp.float32)
        conv_out[...] = acc[:cc] * scale
        res_out[...] = acc[cc:, :rr] * scale
        edge.wait_recv()

        @pl.when(t < n_tm - 1)
        def _():
            edge_out[...] = edge_buf[...]

        @pl.when(t == n_tm - 1)
        def _():
            edge_out[...] = jnp.zeros_like(edge_out)

        for copy in sends:
            copy.wait_send()
        edge.wait_send()

    vmem = pl.BlockSpec(memory_space=pltpu.VMEM)
    bf16, f32 = jnp.bfloat16, jnp.float32
    return pl.pallas_call(
        kernel,
        out_shape=(jax.ShapeDtypeStruct((cc, rc), f32), jax.ShapeDtypeStruct((cr, rr), f32),
                   jax.ShapeDtypeStruct(edge_shape, bf16)),
        in_specs=[pl.BlockSpec(memory_space=pl.ANY), pl.BlockSpec(memory_space=pl.ANY), vmem],
        out_specs=(vmem, vmem, vmem),
        scratch_shapes=[
            pltpu.VMEM((nx, nzh, 1, rc, n_conv), bf16),
            pltpu.VMEM((nx, nzh, 1, rr, n_res), bf16),
            pltpu.VMEM((nx, nzh, rc, n_conv), bf16),
            pltpu.VMEM((nx, nzh, rr, n_res), bf16),
            pltpu.VMEM((nx, nzh, hc, n_conv), bf16),
            pltpu.VMEM((nx, nzh, hr, n_res), bf16),
            pltpu.VMEM((ny, nx, nzh, hc, cyc), bf16),
            pltpu.VMEM((ny, nx, nzh, hr, cyr), bf16),
            pltpu.VMEM((nzh, hc, n_conv), bf16),
            pltpu.VMEM((nzh, hr, n_res), bf16),
            pltpu.VMEM((ny, nzh, hc, cyc), bf16),
            pltpu.VMEM((ny, nzh, hr, cyr), bf16),
            pltpu.VMEM((nx, nzh, hc, cyc), bf16),
            pltpu.VMEM((nx, nzh, hr, cyr), bf16),
            pltpu.VMEM((nx, nzh, hc, cyc), bf16),
            pltpu.VMEM((nx, nzh, hr, cyr), bf16),
            pltpu.VMEM((nz, cc + cr, rc), bf16),
            pltpu.VMEM((nz, cc + cr, rc), bf16),
            pltpu.VMEM(edge_shape, bf16),
            pltpu.VMEM((nx, nzh, 1, rc, n_conv), bf16),
            pltpu.VMEM((nx, nzh, 1, rr, n_res), bf16),
            pltpu.SemaphoreType.DMA((2, n_slots)),
            pltpu.SemaphoreType.DMA((2, n_slots)),
            pltpu.SemaphoreType.DMA((2, 3)),
            pltpu.SemaphoreType.DMA((2,)),
        ],
        compiler_params=pltpu.CompilerParams(collective_id=0, has_side_effects=True),
    )


def make_body(sizes):
    nx, nzh, nc, ny, nzl = sizes
    n_tm = nx * nzh * nc
    n_rep = ny * nzl

    def body(samples, grad_out, w_conv, w_res, lengths):
        sequence_rows = samples[0]
        cotangent = grad_out[0]
        seq_len = lengths[0]
        count_of_rows = sequence_rows.shape[0]
        channel_count = sequence_rows.shape[1]
        start_row = lax.axis_index(TM) * count_of_rows
        trailing_rows = sequence_rows[count_of_rows - DILATION_STEP :]
        arrived = passed_along(trailing_rows, TM, 1, n_tm)
        prior_samples = jnp.concatenate(
            [arrived, sequence_rows[: count_of_rows - DILATION_STEP]], 0
        )
        inputs = jnp.concatenate([prior_samples, sequence_rows], 1)
        in_length = (start_row + jnp.arange(count_of_rows) < seq_len).astype(jnp.float32)[:, None]
        gated, pre_grad = gate_backward(inputs, cotangent, in_length, w_conv, w_res)
        input_gradient = jnp.dot(pre_grad, w_conv.T, preferred_element_type=jnp.float32)
        term_conv = jnp.einsum("tk,tn->kn", inputs, pre_grad, preferred_element_type=jnp.float32)
        term_res = jnp.einsum("tk,tn->kn", gated, cotangent, preferred_element_type=jnp.float32)
        kc, n_conv = term_conv.shape
        kr, n_res = term_res.shape
        rc, rr = kc // n_tm, kr // n_tm
        all_tokens = count_of_rows * n_tm * n_rep
        edge_rows = input_gradient[:DILATION_STEP, :channel_count].astype(jnp.bfloat16)
        reducer = make_reducer(sizes, rc, n_conv, rr, n_res, float(all_tokens) ** (-0.5), edge_rows.shape)
        split = count_of_rows - DILATION_STEP
        head_rows = jnp.concatenate([
            (cotangent[:split].astype(jnp.float32) + input_gradient[:split, channel_count:]
             + input_gradient[DILATION_STEP:, :channel_count]).astype(jnp.bfloat16),
            jnp.zeros((count_of_rows - split, channel_count), jnp.bfloat16)], 0)
        conv_in = term_conv.astype(jnp.bfloat16).reshape(nx, nzh, nc, rc, n_conv)
        res_in = term_res.astype(jnp.bfloat16).reshape(nx, nzh, nc, rr, n_res)
        head_rows, conv_in, res_in, edge_rows = lax.optimization_barrier((head_rows, conv_in, res_in, edge_rows))
        flip_conv, flip_res, incoming_gradient = reducer(conv_in, res_in, edge_rows)
        tail_rows = (
            cotangent[split:].astype(jnp.float32) + input_gradient[split:, channel_count:]
            + incoming_gradient.astype(jnp.float32)
        ).astype(jnp.bfloat16)
        grad_rows = lax.dynamic_update_slice(head_rows, tail_rows, (split, 0))
        return (grad_rows[None], flip_conv.T, flip_res.T)

    return body


def solution(mesh):
    n_tm, n_rep = mesh.devices.shape
    nc = 2
    nzh = 2
    nx = n_tm // (nc * nzh)
    nzl = 8
    ny = n_rep // nzl
    sizes = (nx, nzh, nc, ny, nzl)
    fine = Mesh(mesh.devices.reshape(sizes), ("x", "zh", "c", "y", "zl"))
    return jax.shard_map(
        make_body(sizes),
        mesh=fine,
        in_specs=(P(REP, TM, None), P(REP, TM, None), P(), P(), P(REP)),
        out_specs=(P(REP, TM, None), P(TM, REP), P(TM, REP)),
        check_vma=False,
    )
```

```python
import jax
import jax.numpy as jnp
from jax import lax
from jax.experimental import pallas as pl
from jax.experimental.pallas import tpu as pltpu
from jax.sharding import Mesh, PartitionSpec as P

DILATION_STEP = 256
TM = ("x", "zh", "c")
REP = ("y", "zl")


def passed_along(array, axis, by, length):
    pairs = [(i, i + by) for i in range(length) if 0 <= i + by < length]
    return lax.ppermute(array, axis, pairs)


def gate_backward(inputs, cotangent, in_length, w_conv, w_res):
    channel_count = w_res.shape[0]
    pre_act = jnp.dot(inputs, w_conv, preferred_element_type=jnp.float32)
    tanh_f = jnp.tanh(pre_act[:, :channel_count])
    sig_g = jax.nn.sigmoid(pre_act[:, channel_count:])
    gated = (in_length * tanh_f * sig_g).astype(jnp.bfloat16)
    gated_grad = in_length * jnp.dot(cotangent, w_res.T, preferred_element_type=jnp.float32)
    pre_grad = jnp.concatenate(
        [gated_grad * sig_g * (1.0 - tanh_f * tanh_f), gated_grad * tanh_f * sig_g * (1.0 - sig_g)],
        1,
    ).astype(jnp.bfloat16)
    return (gated, pre_grad)


def make_reducer(sizes, rc, n_conv, rr, n_res, scale, edge_shape):
    nx, nzh, nc, ny, nzl = sizes
    nz = nzh * nzl
    cyc, cyr = n_conv // ny, n_res // ny
    cc, cr = cyc // nzl, cyr // nzl
    hc, hr = rc // 2, rr // 2
    base_xa, base_yb = 1, 1 + nx
    base_ya, base_xb = 1 + nx + ny, 1 + nx + 2 * ny
    base_z = 1 + 2 * nx + 2 * ny
    n_slots = base_z + nz
    n_peers = (nc - 1) + (nx - 1) + (ny - 1) + (nz - 1) + 2
    n_tm = nx * nzh * nc
    mesh_id = pl.DeviceIdType.MESH

    def kernel(conv_ref, res_ref, edge_ref, conv_out, res_out, edge_out,
               rc_conv, rc_res, sx_conv, sx_res,
               rxa_conv, rxa_res, ryb_conv, ryb_res,
               sa_conv, sa_res, rya_conv, rya_res,
               sb_conv, sb_res, rxb_conv, rxb_res,
               sz_both, rz_both,
               edge_buf, own_conv, own_res, send_sems, recv_sems, local_sems, own_sems):
        me_x = lax.axis_index("x")
        me_zh = lax.axis_index("zh")
        me_c = lax.axis_index("c")
        me_y = lax.axis_index("y")
        me_zl = lax.axis_index("zl")
        me_z = me_zh * nzl + me_zl
        other_c = 1 - me_c

        def dev(x=None, zh=None, c=None, y=None, zl=None):
            return (me_x if x is None else x, me_zh if zh is None else zh,
                    me_c if c is None else c, me_y if y is None else y,
                    me_zl if zl is None else zl)

        peers = [dev(c=other_c)]
        x_peers = [dev(x=lax.rem(me_x + d, nx)) for d in range(1, nx)]
        y_peers = [dev(y=lax.rem(me_y + d, ny)) for d in range(1, ny)]
        z_peers = []
        for d in range(1, nz):
            q = lax.rem(me_z + d, nz)
            z_peers.append(dev(zh=q // nzl, zl=lax.rem(q, nzl)))
        barrier = pltpu.get_barrier_semaphore()
        t = (me_x * nzh + me_zh) * nc + me_c

        def tm_dev(u):
            return dev(x=u // (nzh * nc), zh=lax.rem(u // nc, nzh), c=lax.rem(u, nc))

        before = tm_dev(lax.rem(t + n_tm - 1, n_tm))
        after = tm_dev(lax.rem(t + 1, n_tm))
        far_first = sorted(range(1, nz), key=lambda d: -min(d, nz - d))
        for peer in [z_peers[d - 1] for d in far_first] + [before, after] + peers + x_peers + y_peers:
            pl.semaphore_signal(barrier, inc=1, device_id=peer, device_id_type=mesh_id)
        pl.semaphore_wait(barrier, n_peers)

        sends = []

        def send(kind, src, dst, slot, peer):
            copy = pltpu.make_async_remote_copy(
                src_ref=src, dst_ref=dst, send_sem=send_sems.at[kind, slot],
                recv_sem=recv_sems.at[kind, slot], device_id=peer, device_id_type=mesh_id)
            copy.start()
            sends.append(copy)

        def arrive(kind, src, dst, slot):
            pltpu.make_async_remote_copy(
                src_ref=src, dst_ref=dst, send_sem=send_sems.at[kind, slot],
                recv_sem=recv_sems.at[kind, slot], device_id=dev(),
                device_id_type=mesh_id).wait_recv()

        def keep(kind, which, src, dst):
            copy = pltpu.make_async_copy(src, dst, local_sems.at[kind, which])
            copy.start()
            return copy

        edge = pltpu.make_async_remote_copy(
            src_ref=edge_ref, dst_ref=edge_buf, send_sem=local_sems.at[0, 2],
            recv_sem=local_sems.at[1, 2], device_id=before, device_id_type=mesh_id)
        edge.start()

        send(0, conv_ref.at[:, :, pl.ds(other_c, 1)], rc_conv, 0, peers[0])
        send(1, res_ref.at[:, :, pl.ds(other_c, 1)], rc_res, 0, peers[0])
        own_in = [pltpu.make_async_copy(conv_ref.at[:, :, pl.ds(me_c, 1)], own_conv, own_sems.at[0]),
                  pltpu.make_async_copy(res_ref.at[:, :, pl.ds(me_c, 1)], own_res, own_sems.at[1])]
        for copy in own_in:
            copy.start()
        for copy in own_in:
            copy.wait()
        arrive(0, conv_ref.at[:, :, pl.ds(other_c, 1)], rc_conv, 0)
        arrive(1, res_ref.at[:, :, pl.ds(other_c, 1)], rc_res, 0)
        for x in range(nx):
            for zh in range(nzh):
                own_c = own_conv[x, zh, 0].astype(jnp.float32)
                sx_conv[x, zh] = (own_c + rc_conv[x, zh, 0].astype(jnp.float32)).astype(jnp.bfloat16)
                own_r = own_res[x, zh, 0].astype(jnp.float32)
                sx_res[x, zh] = (own_r + rc_res[x, zh, 0].astype(jnp.float32)).astype(jnp.bfloat16)

        for d in range(1, nx):
            tx = lax.rem(me_x + d, nx)
            send(0, sx_conv.at[tx, :, pl.ds(0, hc)], rxa_conv.at[me_x], base_xa + me_x, x_peers[d - 1])
            send(1, sx_res.at[tx, :, pl.ds(0, hr)], rxa_res.at[me_x], base_xa + me_x, x_peers[d - 1])
        for d in range(1, ny):
            ty = lax.rem(me_y + d, ny)
            send(0, sx_conv.at[:, :, pl.ds(hc, hc), pl.ds(ty * cyc, cyc)], ryb_conv.at[me_y],
                 base_yb + me_y, y_peers[d - 1])
            send(1, sx_res.at[:, :, pl.ds(hr, hr), pl.ds(ty * cyr, cyr)], ryb_res.at[me_y],
                 base_yb + me_y, y_peers[d - 1])
        own_b = [keep(0, 0, sx_conv.at[:, :, pl.ds(hc, hc), pl.ds(me_y * cyc, cyc)], ryb_conv.at[me_y]),
                 keep(1, 0, sx_res.at[:, :, pl.ds(hr, hr), pl.ds(me_y * cyr, cyr)], ryb_res.at[me_y])]

        for d in range(1, nx):
            sx = lax.rem(me_x + nx - d, nx)
            arrive(0, sx_conv.at[sx, :, pl.ds(0, hc)], rxa_conv.at[sx], base_xa + sx)
            arrive(1, sx_res.at[sx, :, pl.ds(0, hr)], rxa_res.at[sx], base_xa + sx)
        acc_c = sx_conv[me_x, :, :hc].astype(jnp.float32)
        acc_r = sx_res[me_x, :, :hr].astype(jnp.float32)
        for d in range(1, nx):
            sx = lax.rem(me_x + nx - d, nx)
            acc_c = acc_c + rxa_conv[sx].astype(jnp.float32)
            acc_r = acc_r + rxa_res[sx].astype(jnp.float32)
        sa_conv[...] = acc_c.astype(jnp.bfloat16)
        sa_res[...] = acc_r.astype(jnp.bfloat16)
        for d in range(1, ny):
            ty = lax.rem(me_y + d, ny)
            send(0, sa_conv.at[:, :, pl.ds(ty * cyc, cyc)], rya_conv.at[me_y], base_ya + me_y, y_peers[d - 1])
            send(1, sa_res.at[:, :, pl.ds(ty * cyr, cyr)], rya_res.at[me_y], base_ya + me_y, y_peers[d - 1])
        own_a = [keep(0, 1, sa_conv.at[:, :, pl.ds(me_y * cyc, cyc)], rya_conv.at[me_y]),
                 keep(1, 1, sa_res.at[:, :, pl.ds(me_y * cyr, cyr)], rya_res.at[me_y])]

        for d in range(1, ny):
            sy = lax.rem(me_y + ny - d, ny)
            arrive(0, sx_conv.at[:, :, pl.ds(hc, hc), pl.ds(0, cyc)], ryb_conv.at[sy], base_yb + sy)
            arrive(1, sx_res.at[:, :, pl.ds(hr, hr), pl.ds(0, cyr)], ryb_res.at[sy], base_yb + sy)
        for copy in own_b:
            copy.wait()
        acc_c = ryb_conv[0].astype(jnp.float32)
        acc_r = ryb_res[0].astype(jnp.float32)
        for s in range(1, ny):
            acc_c = acc_c + ryb_conv[s].astype(jnp.float32)
            acc_r = acc_r + ryb_res[s].astype(jnp.float32)
        sb_conv[...] = acc_c.astype(jnp.bfloat16)
        sb_res[...] = acc_r.astype(jnp.bfloat16)
        for d in range(1, nx):
            tx = lax.rem(me_x + d, nx)
            send(0, sb_conv.at[tx], rxb_conv.at[me_x], base_xb + me_x, x_peers[d - 1])
            send(1, sb_res.at[tx], rxb_res.at[me_x], base_xb + me_x, x_peers[d - 1])

        for d in range(1, ny):
            sy = lax.rem(me_y + ny - d, ny)
            arrive(0, sa_conv.at[:, :, pl.ds(0, cyc)], rya_conv.at[sy], base_ya + sy)
            arrive(1, sa_res.at[:, :, pl.ds(0, cyr)], rya_res.at[sy], base_ya + sy)
        for copy in own_a:
            copy.wait()
        for d in range(1, nx):
            sx = lax.rem(me_x + nx - d, nx)
            arrive(0, sb_conv.at[sx], rxb_conv.at[sx], base_xb + sx)
            arrive(1, sb_res.at[sx], rxb_res.at[sx], base_xb + sx)
        top_c = rya_conv[0].astype(jnp.float32)
        top_r = rya_res[0].astype(jnp.float32)
        for s in range(1, ny):
            top_c = top_c + rya_conv[s].astype(jnp.float32)
            top_r = top_r + rya_res[s].astype(jnp.float32)
        low_c = sb_conv[me_x].astype(jnp.float32)
        low_r = sb_res[me_x].astype(jnp.float32)
        for d in range(1, nx):
            sx = lax.rem(me_x + nx - d, nx)
            low_c = low_c + rxb_conv[sx].astype(jnp.float32)
            low_r = low_r + rxb_res[sx].astype(jnp.float32)
        acc_c = jnp.concatenate([top_c, low_c], axis=1)
        acc_r = jnp.concatenate([top_r, low_r], axis=1)
        for zh in range(nzh):
            flip_c = acc_c[zh].T
            flip_r = acc_r[zh].T
            for zl in range(nzl):
                q = zh * nzl + zl
                sz_both[q, :cc, :] = flip_c[zl * cc:(zl + 1) * cc, :].astype(jnp.bfloat16)
                sz_both[q, cc:, :rr] = flip_r[zl * cr:(zl + 1) * cr, :].astype(jnp.bfloat16)
                sz_both[q, cc:, rr:] = jnp.zeros((cr, rc - rr), jnp.bfloat16)

        for d in range(1, nz):
            tz = lax.rem(me_z + d, nz)
            send(0, sz_both.at[tz], rz_both.at[me_z], base_z + me_z, z_peers[d - 1])
        for d in range(1, nz):
            sz = lax.rem(me_z + nz - d, nz)
            arrive(0, sz_both.at[sz], rz_both.at[sz], base_z + sz)
        acc = sz_both[me_z].astype(jnp.float32)
        for d in range(1, nz):
            sz = lax.rem(me_z + nz - d, nz)
            acc = acc + rz_both[sz].astype(jnp.float32)
        conv_out[...] = acc[:cc] * scale
        res_out[...] = acc[cc:, :rr] * scale
        edge.wait_recv()

        @pl.when(t < n_tm - 1)
        def _():
            edge_out[...] = edge_buf[...]

        @pl.when(t == n_tm - 1)
        def _():
            edge_out[...] = jnp.zeros_like(edge_out)

        for copy in sends:
            copy.wait_send()
        edge.wait_send()

    vmem = pl.BlockSpec(memory_space=pltpu.VMEM)
    bf16, f32 = jnp.bfloat16, jnp.float32
    return pl.pallas_call(
        kernel,
        out_shape=(jax.ShapeDtypeStruct((cc, rc), f32), jax.ShapeDtypeStruct((cr, rr), f32),
                   jax.ShapeDtypeStruct(edge_shape, bf16)),
        in_specs=[pl.BlockSpec(memory_space=pl.ANY), pl.BlockSpec(memory_space=pl.ANY), vmem],
        out_specs=(vmem, vmem, vmem),
        scratch_shapes=[
            pltpu.VMEM((nx, nzh, 1, rc, n_conv), bf16),
            pltpu.VMEM((nx, nzh, 1, rr, n_res), bf16),
            pltpu.VMEM((nx, nzh, rc, n_conv), bf16),
            pltpu.VMEM((nx, nzh, rr, n_res), bf16),
            pltpu.VMEM((nx, nzh, hc, n_conv), bf16),
            pltpu.VMEM((nx, nzh, hr, n_res), bf16),
            pltpu.VMEM((ny, nx, nzh, hc, cyc), bf16),
            pltpu.VMEM((ny, nx, nzh, hr, cyr), bf16),
            pltpu.VMEM((nzh, hc, n_conv), bf16),
            pltpu.VMEM((nzh, hr, n_res), bf16),
            pltpu.VMEM((ny, nzh, hc, cyc), bf16),
            pltpu.VMEM((ny, nzh, hr, cyr), bf16),
            pltpu.VMEM((nx, nzh, hc, cyc), bf16),
            pltpu.VMEM((nx, nzh, hr, cyr), bf16),
            pltpu.VMEM((nx, nzh, hc, cyc), bf16),
            pltpu.VMEM((nx, nzh, hr, cyr), bf16),
            pltpu.VMEM((nz, cc + cr, rc), bf16),
            pltpu.VMEM((nz, cc + cr, rc), bf16),
            pltpu.VMEM(edge_shape, bf16),
            pltpu.VMEM((nx, nzh, 1, rc, n_conv), bf16),
            pltpu.VMEM((nx, nzh, 1, rr, n_res), bf16),
            pltpu.SemaphoreType.DMA((2, n_slots)),
            pltpu.SemaphoreType.DMA((2, n_slots)),
            pltpu.SemaphoreType.DMA((2, 3)),
            pltpu.SemaphoreType.DMA((2,)),
        ],
        compiler_params=pltpu.CompilerParams(collective_id=0, has_side_effects=True),
    )


def make_halo(sizes):
    nx, nzh, nc, ny, nzl = sizes
    n_tm = nx * nzh * nc
    mesh_id = pl.DeviceIdType.MESH

    def kernel(block_ref, out_ref, buf, send_sem, recv_sem):
        me_y = lax.axis_index("y")
        me_zl = lax.axis_index("zl")
        t = (lax.axis_index("x") * nzh + lax.axis_index("zh")) * nc + lax.axis_index("c")

        def dev(u):
            return (u // (nzh * nc), lax.rem(u // nc, nzh), lax.rem(u, nc), me_y, me_zl)

        nxt = jnp.minimum(t + 1, n_tm - 1)
        prv = jnp.maximum(t - 1, 0)
        has_next = t < n_tm - 1
        has_prev = t > 0
        rows, step = block_ref.shape[1], out_ref.shape[0]
        src_ref = block_ref.at[0, pl.ds(rows - step, step)]
        barrier = pltpu.get_barrier_semaphore()

        @pl.when(has_next)
        def _():
            pl.semaphore_signal(barrier, inc=1, device_id=dev(nxt), device_id_type=mesh_id)

        @pl.when(has_prev)
        def _():
            pl.semaphore_signal(barrier, inc=1, device_id=dev(prv), device_id_type=mesh_id)

        pl.semaphore_wait(barrier, (1 - (t + 1) // n_tm) + (t + n_tm - 1) // n_tm)

        copy = pltpu.make_async_remote_copy(
            src_ref=src_ref, dst_ref=buf, send_sem=send_sem, recv_sem=recv_sem,
            device_id=dev(nxt), device_id_type=mesh_id)

        @pl.when(has_next)
        def _():
            copy.start()

        @pl.when(has_prev)
        def _():
            copy.wait_recv()
            out_ref[...] = buf[...]

        @pl.when(t == 0)
        def _():
            out_ref[...] = jnp.zeros_like(out_ref)

        @pl.when(has_next)
        def _():
            copy.wait_send()

    vmem = pl.BlockSpec(memory_space=pltpu.VMEM)

    def call(block, step):
        shape = (step, block.shape[2])
        return pl.pallas_call(
            kernel,
            out_shape=jax.ShapeDtypeStruct(shape, block.dtype),
            in_specs=[pl.BlockSpec(memory_space=pl.ANY)],
            out_specs=vmem,
            scratch_shapes=[
                pltpu.VMEM(shape, block.dtype),
                pltpu.SemaphoreType.DMA(()),
                pltpu.SemaphoreType.DMA(()),
            ],
            compiler_params=pltpu.CompilerParams(collective_id=1, has_side_effects=True),
        )(block)

    return call


def make_body(sizes):
    nx, nzh, nc, ny, nzl = sizes
    n_tm = nx * nzh * nc
    n_rep = ny * nzl

    def body(samples, grad_out, w_conv, w_res, lengths):
        sequence_rows = samples[0]
        cotangent = grad_out[0]
        seq_len = lengths[0]
        count_of_rows = sequence_rows.shape[0]
        channel_count = sequence_rows.shape[1]
        start_row = lax.axis_index(TM) * count_of_rows
        trailing_rows = sequence_rows[count_of_rows - DILATION_STEP :]
        arrived = make_halo(sizes)(samples, DILATION_STEP)
        prior_samples = jnp.concatenate(
            [arrived, sequence_rows[: count_of_rows - DILATION_STEP]], 0
        )
        inputs = jnp.concatenate([prior_samples, sequence_rows], 1)
        in_length = (start_row + jnp.arange(count_of_rows) < seq_len).astype(jnp.float32)[:, None]
        gated, pre_grad = gate_backward(inputs, cotangent, in_length, w_conv, w_res)
        input_gradient = jnp.dot(pre_grad, w_conv.T, preferred_element_type=jnp.float32)
        term_conv = jnp.einsum("tk,tn->kn", inputs, pre_grad, preferred_element_type=jnp.float32)
        term_res = jnp.einsum("tk,tn->kn", gated, cotangent, preferred_element_type=jnp.float32)
        kc, n_conv = term_conv.shape
        kr, n_res = term_res.shape
        rc, rr = kc // n_tm, kr // n_tm
        all_tokens = count_of_rows * n_tm * n_rep
        edge_rows = input_gradient[:DILATION_STEP, :channel_count].astype(jnp.bfloat16)
        reducer = make_reducer(sizes, rc, n_conv, rr, n_res, float(all_tokens) ** (-0.5), edge_rows.shape)
        split = count_of_rows - DILATION_STEP
        head_rows = (
            cotangent[:split].astype(jnp.float32) + input_gradient[:split, channel_count:]
            + input_gradient[DILATION_STEP:, :channel_count]
        ).astype(jnp.bfloat16)
        conv_in = term_conv.astype(jnp.bfloat16).reshape(nx, nzh, nc, rc, n_conv)
        res_in = term_res.astype(jnp.bfloat16).reshape(nx, nzh, nc, rr, n_res)
        head_rows, conv_in, res_in, edge_rows = lax.optimization_barrier((head_rows, conv_in, res_in, edge_rows))
        flip_conv, flip_res, incoming_gradient = reducer(conv_in, res_in, edge_rows)
        tail_rows = (
            cotangent[split:].astype(jnp.float32) + input_gradient[split:, channel_count:]
            + incoming_gradient.astype(jnp.float32)
        ).astype(jnp.bfloat16)
        grad_rows = jnp.concatenate([head_rows, tail_rows], 0)
        return (grad_rows[None], flip_conv.T, flip_res.T)

    return body


def solution(mesh):
    n_tm, n_rep = mesh.devices.shape
    nc = 2
    nzh = 2
    nx = n_tm // (nc * nzh)
    nzl = 8
    ny = n_rep // nzl
    sizes = (nx, nzh, nc, ny, nzl)
    fine = Mesh(mesh.devices.reshape(sizes), ("x", "zh", "c", "y", "zl"))
    return jax.shard_map(
        make_body(sizes),
        mesh=fine,
        in_specs=(P(REP, TM, None), P(REP, TM, None), P(), P(), P(REP)),
        out_specs=(P(REP, TM, None), P(TM, REP), P(TM, REP)),
        check_vma=False,
    )
```

```python
import jax
import jax.numpy as jnp
from jax import lax
from jax.experimental import pallas as pl
from jax.experimental.pallas import tpu as pltpu
from jax.sharding import Mesh, PartitionSpec as P

DILATION_STEP = 256
TM = ("x", "zh", "c")
REP = ("y", "zl")


def passed_along(array, axis, by, length):
    pairs = [(i, i + by) for i in range(length) if 0 <= i + by < length]
    return lax.ppermute(array, axis, pairs)


def gate_backward(inputs, cotangent, in_length, w_conv, w_res):
    channel_count = w_res.shape[0]
    pre_act = jnp.dot(inputs, w_conv, preferred_element_type=jnp.float32)
    tanh_f = jnp.tanh(pre_act[:, :channel_count])
    sig_g = jax.nn.sigmoid(pre_act[:, channel_count:])
    gated = (in_length * tanh_f * sig_g).astype(jnp.bfloat16)
    gated_grad = in_length * jnp.dot(cotangent, w_res.T, preferred_element_type=jnp.float32)
    pre_grad = jnp.concatenate(
        [gated_grad * sig_g * (1.0 - tanh_f * tanh_f), gated_grad * tanh_f * sig_g * (1.0 - sig_g)],
        1,
    ).astype(jnp.bfloat16)
    return (gated, pre_grad)


def make_reducer(sizes, rc, n_conv, rr, n_res, scale, edge_shape):
    nx, nzh, nc, ny, nzl = sizes
    nz = nzh * nzl
    cyc, cyr = n_conv // ny, n_res // ny
    cc, cr = cyc // nzl, cyr // nzl
    hc, hr = rc // 2, rr // 2
    base_xa, base_yb = 1, 1 + nx
    base_ya, base_xb = 1 + nx + ny, 1 + nx + 2 * ny
    base_z = 1 + 2 * nx + 2 * ny
    n_slots = base_z + nz
    n_peers = (nc - 1) + (nx - 1) + (ny - 1) + (nz - 1) + 2
    n_tm = nx * nzh * nc
    mesh_id = pl.DeviceIdType.MESH

    def kernel(conv_ref, res_ref, edge_ref, conv_out, res_out, edge_out,
               rc_conv, rc_res, sx_conv, sx_res,
               rxa_conv, rxa_res, ryb_conv, ryb_res,
               sa_conv, sa_res, rya_conv, rya_res,
               sb_conv, sb_res, rxb_conv, rxb_res,
               sz_both, rz_both,
               edge_buf, own_conv, own_res, send_sems, recv_sems, local_sems, own_sems):
        me_x = lax.axis_index("x")
        me_zh = lax.axis_index("zh")
        me_c = lax.axis_index("c")
        me_y = lax.axis_index("y")
        me_zl = lax.axis_index("zl")
        me_z = me_zh * nzl + me_zl
        other_c = 1 - me_c

        def dev(x=None, zh=None, c=None, y=None, zl=None):
            return (me_x if x is None else x, me_zh if zh is None else zh,
                    me_c if c is None else c, me_y if y is None else y,
                    me_zl if zl is None else zl)

        peers = [dev(c=other_c)]
        x_peers = [dev(x=lax.rem(me_x + d, nx)) for d in range(1, nx)]
        y_peers = [dev(y=lax.rem(me_y + d, ny)) for d in range(1, ny)]
        z_peers = []
        for d in range(1, nz):
            q = lax.rem(me_z + d, nz)
            z_peers.append(dev(zh=q // nzl, zl=lax.rem(q, nzl)))
        barrier = pltpu.get_barrier_semaphore()
        t = (me_x * nzh + me_zh) * nc + me_c

        def tm_dev(u):
            return dev(x=u // (nzh * nc), zh=lax.rem(u // nc, nzh), c=lax.rem(u, nc))

        before = tm_dev(lax.rem(t + n_tm - 1, n_tm))
        after = tm_dev(lax.rem(t + 1, n_tm))
        far_first = sorted(range(1, nz), key=lambda d: -min(d, nz - d))
        for peer in [z_peers[d - 1] for d in far_first] + [before, after] + peers + x_peers + y_peers:
            pl.semaphore_signal(barrier, inc=1, device_id=peer, device_id_type=mesh_id)
        pl.semaphore_wait(barrier, n_peers)

        sends = []

        def send(kind, src, dst, slot, peer):
            copy = pltpu.make_async_remote_copy(
                src_ref=src, dst_ref=dst, send_sem=send_sems.at[kind, slot],
                recv_sem=recv_sems.at[kind, slot], device_id=peer, device_id_type=mesh_id)
            copy.start()
            sends.append(copy)

        def arrive(kind, src, dst, slot):
            pltpu.make_async_remote_copy(
                src_ref=src, dst_ref=dst, send_sem=send_sems.at[kind, slot],
                recv_sem=recv_sems.at[kind, slot], device_id=dev(),
                device_id_type=mesh_id).wait_recv()

        def keep(kind, which, src, dst):
            copy = pltpu.make_async_copy(src, dst, local_sems.at[kind, which])
            copy.start()
            return copy

        edge = pltpu.make_async_remote_copy(
            src_ref=edge_ref.at[pl.ds(0, edge_shape[0]), pl.ds(0, edge_shape[1])], dst_ref=edge_buf, send_sem=local_sems.at[0, 2],
            recv_sem=local_sems.at[1, 2], device_id=before, device_id_type=mesh_id)
        edge.start()

        send(0, conv_ref.at[:, :, pl.ds(other_c, 1)], rc_conv, 0, peers[0])
        send(1, res_ref.at[:, :, pl.ds(other_c, 1)], rc_res, 0, peers[0])
        own_in = [pltpu.make_async_copy(conv_ref.at[:, :, pl.ds(me_c, 1)], own_conv, own_sems.at[0]),
                  pltpu.make_async_copy(res_ref.at[:, :, pl.ds(me_c, 1)], own_res, own_sems.at[1])]
        for copy in own_in:
            copy.start()
        for copy in own_in:
            copy.wait()
        arrive(0, conv_ref.at[:, :, pl.ds(other_c, 1)], rc_conv, 0)
        arrive(1, res_ref.at[:, :, pl.ds(other_c, 1)], rc_res, 0)
        for x in range(nx):
            for zh in range(nzh):
                own_c = own_conv[x, zh, 0].astype(jnp.float32)
                sx_conv[x, zh] = (own_c + rc_conv[x, zh, 0].astype(jnp.float32)).astype(jnp.bfloat16)
                own_r = own_res[x, zh, 0].astype(jnp.float32)
                sx_res[x, zh] = (own_r + rc_res[x, zh, 0].astype(jnp.float32)).astype(jnp.bfloat16)

        for d in range(1, nx):
            tx = lax.rem(me_x + d, nx)
            send(0, sx_conv.at[tx, :, pl.ds(0, hc)], rxa_conv.at[me_x], base_xa + me_x, x_peers[d - 1])
            send(1, sx_res.at[tx, :, pl.ds(0, hr)], rxa_res.at[me_x], base_xa + me_x, x_peers[d - 1])
        for d in range(1, ny):
            ty = lax.rem(me_y + d, ny)
            send(0, sx_conv.at[:, :, pl.ds(hc, hc), pl.ds(ty * cyc, cyc)], ryb_conv.at[me_y],
                 base_yb + me_y, y_peers[d - 1])
            send(1, sx_res.at[:, :, pl.ds(hr, hr), pl.ds(ty * cyr, cyr)], ryb_res.at[me_y],
                 base_yb + me_y, y_peers[d - 1])
        own_b = [keep(0, 0, sx_conv.at[:, :, pl.ds(hc, hc), pl.ds(me_y * cyc, cyc)], ryb_conv.at[me_y]),
                 keep(1, 0, sx_res.at[:, :, pl.ds(hr, hr), pl.ds(me_y * cyr, cyr)], ryb_res.at[me_y])]

        for d in range(1, nx):
            sx = lax.rem(me_x + nx - d, nx)
            arrive(0, sx_conv.at[sx, :, pl.ds(0, hc)], rxa_conv.at[sx], base_xa + sx)
            arrive(1, sx_res.at[sx, :, pl.ds(0, hr)], rxa_res.at[sx], base_xa + sx)
        acc_c = sx_conv[me_x, :, :hc].astype(jnp.float32)
        acc_r = sx_res[me_x, :, :hr].astype(jnp.float32)
        for d in range(1, nx):
            sx = lax.rem(me_x + nx - d, nx)
            acc_c = acc_c + rxa_conv[sx].astype(jnp.float32)
            acc_r = acc_r + rxa_res[sx].astype(jnp.float32)
        sa_conv[...] = acc_c.astype(jnp.bfloat16)
        sa_res[...] = acc_r.astype(jnp.bfloat16)
        for d in range(1, ny):
            ty = lax.rem(me_y + d, ny)
            send(0, sa_conv.at[:, :, pl.ds(ty * cyc, cyc)], rya_conv.at[me_y], base_ya + me_y, y_peers[d - 1])
            send(1, sa_res.at[:, :, pl.ds(ty * cyr, cyr)], rya_res.at[me_y], base_ya + me_y, y_peers[d - 1])
        own_a = [keep(0, 1, sa_conv.at[:, :, pl.ds(me_y * cyc, cyc)], rya_conv.at[me_y]),
                 keep(1, 1, sa_res.at[:, :, pl.ds(me_y * cyr, cyr)], rya_res.at[me_y])]

        for d in range(1, ny):
            sy = lax.rem(me_y + ny - d, ny)
            arrive(0, sx_conv.at[:, :, pl.ds(hc, hc), pl.ds(0, cyc)], ryb_conv.at[sy], base_yb + sy)
            arrive(1, sx_res.at[:, :, pl.ds(hr, hr), pl.ds(0, cyr)], ryb_res.at[sy], base_yb + sy)
        for copy in own_b:
            copy.wait()
        acc_c = ryb_conv[0].astype(jnp.float32)
        acc_r = ryb_res[0].astype(jnp.float32)
        for s in range(1, ny):
            acc_c = acc_c + ryb_conv[s].astype(jnp.float32)
            acc_r = acc_r + ryb_res[s].astype(jnp.float32)
        sb_conv[...] = acc_c.astype(jnp.bfloat16)
        sb_res[...] = acc_r.astype(jnp.bfloat16)
        for d in range(1, nx):
            tx = lax.rem(me_x + d, nx)
            send(0, sb_conv.at[tx], rxb_conv.at[me_x], base_xb + me_x, x_peers[d - 1])
            send(1, sb_res.at[tx], rxb_res.at[me_x], base_xb + me_x, x_peers[d - 1])

        for d in range(1, ny):
            sy = lax.rem(me_y + ny - d, ny)
            arrive(0, sa_conv.at[:, :, pl.ds(0, cyc)], rya_conv.at[sy], base_ya + sy)
            arrive(1, sa_res.at[:, :, pl.ds(0, cyr)], rya_res.at[sy], base_ya + sy)
        for copy in own_a:
            copy.wait()
        for d in range(1, nx):
            sx = lax.rem(me_x + nx - d, nx)
            arrive(0, sb_conv.at[sx], rxb_conv.at[sx], base_xb + sx)
            arrive(1, sb_res.at[sx], rxb_res.at[sx], base_xb + sx)
        top_c = rya_conv[0].astype(jnp.float32)
        top_r = rya_res[0].astype(jnp.float32)
        for s in range(1, ny):
            top_c = top_c + rya_conv[s].astype(jnp.float32)
            top_r = top_r + rya_res[s].astype(jnp.float32)
        low_c = sb_conv[me_x].astype(jnp.float32)
        low_r = sb_res[me_x].astype(jnp.float32)
        for d in range(1, nx):
            sx = lax.rem(me_x + nx - d, nx)
            low_c = low_c + rxb_conv[sx].astype(jnp.float32)
            low_r = low_r + rxb_res[sx].astype(jnp.float32)
        acc_c = jnp.concatenate([top_c, low_c], axis=1)
        acc_r = jnp.concatenate([top_r, low_r], axis=1)
        for zh in range(nzh):
            flip_c = acc_c[zh].T
            flip_r = acc_r[zh].T
            for zl in range(nzl):
                q = zh * nzl + zl
                sz_both[q, :cc, :] = flip_c[zl * cc:(zl + 1) * cc, :].astype(jnp.bfloat16)
                sz_both[q, cc:, :rr] = flip_r[zl * cr:(zl + 1) * cr, :].astype(jnp.bfloat16)
                sz_both[q, cc:, rr:] = jnp.zeros((cr, rc - rr), jnp.bfloat16)

        for d in range(1, nz):
            tz = lax.rem(me_z + d, nz)
            send(0, sz_both.at[tz], rz_both.at[me_z], base_z + me_z, z_peers[d - 1])
        for d in range(1, nz):
            sz = lax.rem(me_z + nz - d, nz)
            arrive(0, sz_both.at[sz], rz_both.at[sz], base_z + sz)
        acc = sz_both[me_z].astype(jnp.float32)
        for d in range(1, nz):
            sz = lax.rem(me_z + nz - d, nz)
            acc = acc + rz_both[sz].astype(jnp.float32)
        conv_out[...] = acc[:cc] * scale
        res_out[...] = acc[cc:, :rr] * scale
        edge.wait_recv()

        @pl.when(t < n_tm - 1)
        def _():
            edge_out[...] = edge_buf[...]

        @pl.when(t == n_tm - 1)
        def _():
            edge_out[...] = jnp.zeros_like(edge_out)

        for copy in sends:
            copy.wait_send()
        edge.wait_send()

    vmem = pl.BlockSpec(memory_space=pltpu.VMEM)
    bf16, f32 = jnp.bfloat16, jnp.float32
    return pl.pallas_call(
        kernel,
        out_shape=(jax.ShapeDtypeStruct((cc, rc), f32), jax.ShapeDtypeStruct((cr, rr), f32),
                   jax.ShapeDtypeStruct(edge_shape, f32)),
        in_specs=[pl.BlockSpec(memory_space=pl.ANY)] * 3,
        out_specs=(vmem, vmem, vmem),
        scratch_shapes=[
            pltpu.VMEM((nx, nzh, 1, rc, n_conv), bf16),
            pltpu.VMEM((nx, nzh, 1, rr, n_res), bf16),
            pltpu.VMEM((nx, nzh, rc, n_conv), bf16),
            pltpu.VMEM((nx, nzh, rr, n_res), bf16),
            pltpu.VMEM((nx, nzh, hc, n_conv), bf16),
            pltpu.VMEM((nx, nzh, hr, n_res), bf16),
            pltpu.VMEM((ny, nx, nzh, hc, cyc), bf16),
            pltpu.VMEM((ny, nx, nzh, hr, cyr), bf16),
            pltpu.VMEM((nzh, hc, n_conv), bf16),
            pltpu.VMEM((nzh, hr, n_res), bf16),
            pltpu.VMEM((ny, nzh, hc, cyc), bf16),
            pltpu.VMEM((ny, nzh, hr, cyr), bf16),
            pltpu.VMEM((nx, nzh, hc, cyc), bf16),
            pltpu.VMEM((nx, nzh, hr, cyr), bf16),
            pltpu.VMEM((nx, nzh, hc, cyc), bf16),
            pltpu.VMEM((nx, nzh, hr, cyr), bf16),
            pltpu.VMEM((nz, cc + cr, rc), bf16),
            pltpu.VMEM((nz, cc + cr, rc), bf16),
            pltpu.VMEM(edge_shape, f32),
            pltpu.VMEM((nx, nzh, 1, rc, n_conv), bf16),
            pltpu.VMEM((nx, nzh, 1, rr, n_res), bf16),
            pltpu.SemaphoreType.DMA((2, n_slots)),
            pltpu.SemaphoreType.DMA((2, n_slots)),
            pltpu.SemaphoreType.DMA((2, 3)),
            pltpu.SemaphoreType.DMA((2,)),
        ],
        compiler_params=pltpu.CompilerParams(collective_id=0, has_side_effects=True),
    )


def make_body(sizes):
    nx, nzh, nc, ny, nzl = sizes
    n_tm = nx * nzh * nc
    n_rep = ny * nzl

    def body(samples, grad_out, w_conv, w_res, lengths):
        sequence_rows = samples[0]
        cotangent = grad_out[0]
        seq_len = lengths[0]
        count_of_rows = sequence_rows.shape[0]
        channel_count = sequence_rows.shape[1]
        start_row = lax.axis_index(TM) * count_of_rows
        trailing_rows = sequence_rows[count_of_rows - DILATION_STEP :]
        arrived = passed_along(trailing_rows, TM, 1, n_tm)
        prior_samples = jnp.concatenate(
            [arrived, sequence_rows[: count_of_rows - DILATION_STEP]], 0
        )
        inputs = jnp.concatenate([prior_samples, sequence_rows], 1)
        in_length = (start_row + jnp.arange(count_of_rows) < seq_len).astype(jnp.float32)[:, None]
        gated, pre_grad = gate_backward(inputs, cotangent, in_length, w_conv, w_res)
        input_gradient = jnp.dot(pre_grad, w_conv.T, preferred_element_type=jnp.float32)
        term_conv = jnp.einsum("tk,tn->kn", inputs, pre_grad, preferred_element_type=jnp.float32)
        term_res = jnp.einsum("tk,tn->kn", gated, cotangent, preferred_element_type=jnp.float32)
        kc, n_conv = term_conv.shape
        kr, n_res = term_res.shape
        rc, rr = kc // n_tm, kr // n_tm
        all_tokens = count_of_rows * n_tm * n_rep
        edge_shape = (DILATION_STEP, channel_count)
        reducer = make_reducer(sizes, rc, n_conv, rr, n_res, float(all_tokens) ** (-0.5), edge_shape)
        split = count_of_rows - DILATION_STEP
        head_rows = (
            cotangent[:split].astype(jnp.float32) + input_gradient[:split, channel_count:]
            + input_gradient[DILATION_STEP:, :channel_count]
        ).astype(jnp.bfloat16)
        conv_in = term_conv.astype(jnp.bfloat16).reshape(nx, nzh, nc, rc, n_conv)
        res_in = term_res.astype(jnp.bfloat16).reshape(nx, nzh, nc, rr, n_res)
        head_rows, conv_in, res_in = lax.optimization_barrier((head_rows, conv_in, res_in))
        flip_conv, flip_res, incoming_gradient = reducer(conv_in, res_in, input_gradient)
        tail_rows = (
            cotangent[split:].astype(jnp.float32) + input_gradient[split:, channel_count:]
            + incoming_gradient.astype(jnp.float32)
        ).astype(jnp.bfloat16)
        grad_rows = jnp.concatenate([head_rows, tail_rows], 0)
        return (grad_rows[None], flip_conv.T, flip_res.T)

    return body


def solution(mesh):
    n_tm, n_rep = mesh.devices.shape
    nc = 2
    nzh = 2
    nx = n_tm // (nc * nzh)
    nzl = 8
    ny = n_rep // nzl
    sizes = (nx, nzh, nc, ny, nzl)
    fine = Mesh(mesh.devices.reshape(sizes), ("x", "zh", "c", "y", "zl"))
    return jax.shard_map(
        make_body(sizes),
        mesh=fine,
        in_specs=(P(REP, TM, None), P(REP, TM, None), P(), P(), P(REP)),
        out_specs=(P(REP, TM, None), P(TM, REP), P(TM, REP)),
        check_vma=False,
    )
```

```python
import jax
import jax.numpy as jnp
from jax import lax
from jax.experimental import pallas as pl
from jax.experimental.pallas import tpu as pltpu
from jax.sharding import Mesh, PartitionSpec as P

DILATION_STEP = 256
TM = ("x", "zh", "c")
REP = ("y", "zl")


def passed_along(array, axis, by, length):
    pairs = [(i, i + by) for i in range(length) if 0 <= i + by < length]
    return lax.ppermute(array, axis, pairs)


def gate_backward(inputs, cotangent, in_length, w_conv, w_res):
    channel_count = w_res.shape[0]
    pre_act = jnp.dot(inputs, w_conv, preferred_element_type=jnp.float32)
    tanh_f = jnp.tanh(pre_act[:, :channel_count])
    sig_g = jax.nn.sigmoid(pre_act[:, channel_count:])
    gated = (in_length * tanh_f * sig_g).astype(jnp.bfloat16)
    gated_grad = in_length * jnp.dot(cotangent, w_res.T, preferred_element_type=jnp.float32)
    pre_grad = jnp.concatenate(
        [gated_grad * sig_g * (1.0 - tanh_f * tanh_f), gated_grad * tanh_f * sig_g * (1.0 - sig_g)],
        1,
    ).astype(jnp.bfloat16)
    return (gated, pre_grad)


def make_reducer(sizes, rc, n_conv, rr, n_res, scale, edge_shape):
    nx, nzh, nc, ny, nzl = sizes
    nz = nzh * nzl
    cyc, cyr = n_conv // ny, n_res // ny
    cc, cr = cyc // nzl, cyr // nzl
    hc, hr = rc // 2, rr // 2
    base_xa, base_yb = 1, 1 + nx
    base_ya, base_xb = 1 + nx + ny, 1 + nx + 2 * ny
    base_z = 1 + 2 * nx + 2 * ny
    n_slots = base_z + nz
    n_peers = (nc - 1) + (nx - 1) + (ny - 1) + (nz - 1) + 2
    n_tm = nx * nzh * nc
    mesh_id = pl.DeviceIdType.MESH

    def kernel(conv_ref, res_ref, edge_ref, conv_out, res_out, edge_out,
               rc_conv, rc_res, sx_conv, sx_res,
               rxa_conv, rxa_res, ryb_conv, ryb_res,
               sa_conv, sa_res, rya_conv, rya_res,
               sb_conv, sb_res, rxb_conv, rxb_res,
               sz_both, rz_both,
               edge_buf, own_conv, own_res, send_sems, recv_sems, local_sems, own_sems):
        me_x = lax.axis_index("x")
        me_zh = lax.axis_index("zh")
        me_c = lax.axis_index("c")
        me_y = lax.axis_index("y")
        me_zl = lax.axis_index("zl")
        me_z = me_zh * nzl + me_zl
        other_c = 1 - me_c

        def dev(x=None, zh=None, c=None, y=None, zl=None):
            return (me_x if x is None else x, me_zh if zh is None else zh,
                    me_c if c is None else c, me_y if y is None else y,
                    me_zl if zl is None else zl)

        peers = [dev(c=other_c)]
        x_peers = [dev(x=lax.rem(me_x + d, nx)) for d in range(1, nx)]
        y_peers = [dev(y=lax.rem(me_y + d, ny)) for d in range(1, ny)]
        z_peers = []
        for d in range(1, nz):
            q = lax.rem(me_z + d, nz)
            z_peers.append(dev(zh=q // nzl, zl=lax.rem(q, nzl)))
        barrier = pltpu.get_barrier_semaphore()
        t = (me_x * nzh + me_zh) * nc + me_c

        def tm_dev(u):
            return dev(x=u // (nzh * nc), zh=lax.rem(u // nc, nzh), c=lax.rem(u, nc))

        before = tm_dev(lax.rem(t + n_tm - 1, n_tm))
        after = tm_dev(lax.rem(t + 1, n_tm))
        far_first = sorted(range(1, nz), key=lambda d: -min(d, nz - d))
        for peer in [z_peers[d - 1] for d in far_first] + [before, after] + peers + x_peers + y_peers:
            pl.semaphore_signal(barrier, inc=1, device_id=peer, device_id_type=mesh_id)
        pl.semaphore_wait(barrier, n_peers)

        sends = []

        def send(kind, src, dst, slot, peer):
            copy = pltpu.make_async_remote_copy(
                src_ref=src, dst_ref=dst, send_sem=send_sems.at[kind, slot],
                recv_sem=recv_sems.at[kind, slot], device_id=peer, device_id_type=mesh_id)
            copy.start()
            sends.append(copy)

        def arrive(kind, src, dst, slot):
            pltpu.make_async_remote_copy(
                src_ref=src, dst_ref=dst, send_sem=send_sems.at[kind, slot],
                recv_sem=recv_sems.at[kind, slot], device_id=dev(),
                device_id_type=mesh_id).wait_recv()

        def keep(kind, which, src, dst):
            copy = pltpu.make_async_copy(src, dst, local_sems.at[kind, which])
            copy.start()
            return copy

        edge = pltpu.make_async_remote_copy(
            src_ref=edge_ref, dst_ref=edge_buf, send_sem=local_sems.at[0, 2],
            recv_sem=local_sems.at[1, 2], device_id=before, device_id_type=mesh_id)
        edge.start()

        send(0, conv_ref.at[:, :, pl.ds(other_c, 1)], rc_conv, 0, peers[0])
        send(1, res_ref.at[:, :, pl.ds(other_c, 1)], rc_res, 0, peers[0])
        own_in = [pltpu.make_async_copy(conv_ref.at[:, :, pl.ds(me_c, 1)], own_conv, own_sems.at[0]),
                  pltpu.make_async_copy(res_ref.at[:, :, pl.ds(me_c, 1)], own_res, own_sems.at[1])]
        for copy in own_in:
            copy.start()
        for copy in own_in:
            copy.wait()
        arrive(0, conv_ref.at[:, :, pl.ds(other_c, 1)], rc_conv, 0)
        arrive(1, res_ref.at[:, :, pl.ds(other_c, 1)], rc_res, 0)
        for x in range(nx):
            for zh in range(nzh):
                own_c = own_conv[x, zh, 0].astype(jnp.float32)
                sx_conv[x, zh] = (own_c + rc_conv[x, zh, 0].astype(jnp.float32)).astype(jnp.bfloat16)
                own_r = own_res[x, zh, 0].astype(jnp.float32)
                sx_res[x, zh] = (own_r + rc_res[x, zh, 0].astype(jnp.float32)).astype(jnp.bfloat16)

        for d in range(1, nx):
            tx = lax.rem(me_x + d, nx)
            send(0, sx_conv.at[tx, :, pl.ds(0, hc)], rxa_conv.at[me_x], base_xa + me_x, x_peers[d - 1])
            send(1, sx_res.at[tx, :, pl.ds(0, hr)], rxa_res.at[me_x], base_xa + me_x, x_peers[d - 1])
        for d in range(1, ny):
            ty = lax.rem(me_y + d, ny)
            send(0, sx_conv.at[:, :, pl.ds(hc, hc), pl.ds(ty * cyc, cyc)], ryb_conv.at[me_y],
                 base_yb + me_y, y_peers[d - 1])
            send(1, sx_res.at[:, :, pl.ds(hr, hr), pl.ds(ty * cyr, cyr)], ryb_res.at[me_y],
                 base_yb + me_y, y_peers[d - 1])
        own_b = [keep(0, 0, sx_conv.at[:, :, pl.ds(hc, hc), pl.ds(me_y * cyc, cyc)], ryb_conv.at[me_y]),
                 keep(1, 0, sx_res.at[:, :, pl.ds(hr, hr), pl.ds(me_y * cyr, cyr)], ryb_res.at[me_y])]

        for d in range(1, nx):
            sx = lax.rem(me_x + nx - d, nx)
            arrive(0, sx_conv.at[sx, :, pl.ds(0, hc)], rxa_conv.at[sx], base_xa + sx)
            arrive(1, sx_res.at[sx, :, pl.ds(0, hr)], rxa_res.at[sx], base_xa + sx)
        acc_c = sx_conv[me_x, :, :hc].astype(jnp.float32)
        acc_r = sx_res[me_x, :, :hr].astype(jnp.float32)
        for d in range(1, nx):
            sx = lax.rem(me_x + nx - d, nx)
            acc_c = acc_c + rxa_conv[sx].astype(jnp.float32)
            acc_r = acc_r + rxa_res[sx].astype(jnp.float32)
        sa_conv[...] = acc_c.astype(jnp.bfloat16)
        sa_res[...] = acc_r.astype(jnp.bfloat16)
        for d in range(1, ny):
            ty = lax.rem(me_y + d, ny)
            send(0, sa_conv.at[:, :, pl.ds(ty * cyc, cyc)], rya_conv.at[me_y], base_ya + me_y, y_peers[d - 1])
            send(1, sa_res.at[:, :, pl.ds(ty * cyr, cyr)], rya_res.at[me_y], base_ya + me_y, y_peers[d - 1])
        own_a = [keep(0, 1, sa_conv.at[:, :, pl.ds(me_y * cyc, cyc)], rya_conv.at[me_y]),
                 keep(1, 1, sa_res.at[:, :, pl.ds(me_y * cyr, cyr)], rya_res.at[me_y])]

        for d in range(1, ny):
            sy = lax.rem(me_y + ny - d, ny)
            arrive(0, sx_conv.at[:, :, pl.ds(hc, hc), pl.ds(0, cyc)], ryb_conv.at[sy], base_yb + sy)
            arrive(1, sx_res.at[:, :, pl.ds(hr, hr), pl.ds(0, cyr)], ryb_res.at[sy], base_yb + sy)
        for copy in own_b:
            copy.wait()
        acc_c = ryb_conv[0].astype(jnp.float32)
        acc_r = ryb_res[0].astype(jnp.float32)
        for s in range(1, ny):
            acc_c = acc_c + ryb_conv[s].astype(jnp.float32)
            acc_r = acc_r + ryb_res[s].astype(jnp.float32)
        sb_conv[...] = acc_c.astype(jnp.bfloat16)
        sb_res[...] = acc_r.astype(jnp.bfloat16)
        for d in range(1, nx):
            tx = lax.rem(me_x + d, nx)
            send(0, sb_conv.at[tx], rxb_conv.at[me_x], base_xb + me_x, x_peers[d - 1])
            send(1, sb_res.at[tx], rxb_res.at[me_x], base_xb + me_x, x_peers[d - 1])

        for d in range(1, ny):
            sy = lax.rem(me_y + ny - d, ny)
            arrive(0, sa_conv.at[:, :, pl.ds(0, cyc)], rya_conv.at[sy], base_ya + sy)
            arrive(1, sa_res.at[:, :, pl.ds(0, cyr)], rya_res.at[sy], base_ya + sy)
        for copy in own_a:
            copy.wait()
        for d in range(1, nx):
            sx = lax.rem(me_x + nx - d, nx)
            arrive(0, sb_conv.at[sx], rxb_conv.at[sx], base_xb + sx)
            arrive(1, sb_res.at[sx], rxb_res.at[sx], base_xb + sx)
        top_c = rya_conv[0].astype(jnp.float32)
        top_r = rya_res[0].astype(jnp.float32)
        for s in range(1, ny):
            top_c = top_c + rya_conv[s].astype(jnp.float32)
            top_r = top_r + rya_res[s].astype(jnp.float32)
        low_c = sb_conv[me_x].astype(jnp.float32)
        low_r = sb_res[me_x].astype(jnp.float32)
        for d in range(1, nx):
            sx = lax.rem(me_x + nx - d, nx)
            low_c = low_c + rxb_conv[sx].astype(jnp.float32)
            low_r = low_r + rxb_res[sx].astype(jnp.float32)
        acc_c = jnp.concatenate([top_c, low_c], axis=1)
        acc_r = jnp.concatenate([top_r, low_r], axis=1)
        for zh in range(nzh):
            flip_c = acc_c[zh].T
            flip_r = acc_r[zh].T
            for zl in range(nzl):
                q = zh * nzl + zl
                sz_both[q, :cc, :] = flip_c[zl * cc:(zl + 1) * cc, :].astype(jnp.bfloat16)
                sz_both[q, cc:, :rr] = flip_r[zl * cr:(zl + 1) * cr, :].astype(jnp.bfloat16)
                sz_both[q, cc:, rr:] = jnp.zeros((cr, rc - rr), jnp.bfloat16)

        for d in range(1, nz):
            tz = lax.rem(me_z + d, nz)
            send(0, sz_both.at[tz], rz_both.at[me_z], base_z + me_z, z_peers[d - 1])
        for d in range(1, nz):
            sz = lax.rem(me_z + nz - d, nz)
            arrive(0, sz_both.at[sz], rz_both.at[sz], base_z + sz)
        acc = sz_both[me_z].astype(jnp.float32)
        for d in range(1, nz):
            sz = lax.rem(me_z + nz - d, nz)
            acc = acc + rz_both[sz].astype(jnp.float32)
        conv_out[...] = acc[:cc] * scale
        res_out[...] = acc[cc:, :rr] * scale
        edge.wait_recv()

        @pl.when(t < n_tm - 1)
        def _():
            edge_out[...] = edge_buf[...]

        @pl.when(t == n_tm - 1)
        def _():
            edge_out[...] = jnp.zeros_like(edge_out)

        for copy in sends:
            copy.wait_send()
        edge.wait_send()

    vmem = pl.BlockSpec(memory_space=pltpu.VMEM)
    bf16, f32 = jnp.bfloat16, jnp.float32
    return pl.pallas_call(
        kernel,
        out_shape=(jax.ShapeDtypeStruct((cc, rc), f32), jax.ShapeDtypeStruct((cr, rr), f32),
                   jax.ShapeDtypeStruct(edge_shape, bf16)),
        in_specs=[pl.BlockSpec(memory_space=pl.ANY)] * 3,
        out_specs=(vmem, vmem, vmem),
        scratch_shapes=[
            pltpu.VMEM((nx, nzh, 1, rc, n_conv), bf16),
            pltpu.VMEM((nx, nzh, 1, rr, n_res), bf16),
            pltpu.VMEM((nx, nzh, rc, n_conv), bf16),
            pltpu.VMEM((nx, nzh, rr, n_res), bf16),
            pltpu.VMEM((nx, nzh, hc, n_conv), bf16),
            pltpu.VMEM((nx, nzh, hr, n_res), bf16),
            pltpu.VMEM((ny, nx, nzh, hc, cyc), bf16),
            pltpu.VMEM((ny, nx, nzh, hr, cyr), bf16),
            pltpu.VMEM((nzh, hc, n_conv), bf16),
            pltpu.VMEM((nzh, hr, n_res), bf16),
            pltpu.VMEM((ny, nzh, hc, cyc), bf16),
            pltpu.VMEM((ny, nzh, hr, cyr), bf16),
            pltpu.VMEM((nx, nzh, hc, cyc), bf16),
            pltpu.VMEM((nx, nzh, hr, cyr), bf16),
            pltpu.VMEM((nx, nzh, hc, cyc), bf16),
            pltpu.VMEM((nx, nzh, hr, cyr), bf16),
            pltpu.VMEM((nz, cc + cr, rc), bf16),
            pltpu.VMEM((nz, cc + cr, rc), bf16),
            pltpu.VMEM(edge_shape, bf16),
            pltpu.VMEM((nx, nzh, 1, rc, n_conv), bf16),
            pltpu.VMEM((nx, nzh, 1, rr, n_res), bf16),
            pltpu.SemaphoreType.DMA((2, n_slots)),
            pltpu.SemaphoreType.DMA((2, n_slots)),
            pltpu.SemaphoreType.DMA((2, 3)),
            pltpu.SemaphoreType.DMA((2,)),
        ],
        compiler_params=pltpu.CompilerParams(collective_id=0, has_side_effects=True),
    )


def make_body(sizes):
    nx, nzh, nc, ny, nzl = sizes
    n_tm = nx * nzh * nc
    n_rep = ny * nzl

    def body(samples, grad_out, w_conv, w_res, lengths):
        sequence_rows = samples[0]
        cotangent = grad_out[0]
        seq_len = lengths[0]
        count_of_rows = sequence_rows.shape[0]
        channel_count = sequence_rows.shape[1]
        start_row = lax.axis_index(TM) * count_of_rows
        trailing_rows = sequence_rows[count_of_rows - DILATION_STEP :]
        arrived = passed_along(trailing_rows, TM, 1, n_tm)
        prior_samples = jnp.concatenate(
            [arrived, sequence_rows[: count_of_rows - DILATION_STEP]], 0
        )
        inputs = jnp.concatenate([prior_samples, sequence_rows], 1)
        in_length = (start_row + jnp.arange(count_of_rows) < seq_len).astype(jnp.float32)[:, None]
        gated, pre_grad = gate_backward(inputs, cotangent, in_length, w_conv, w_res)
        input_gradient = jnp.dot(pre_grad, w_conv.T, preferred_element_type=jnp.float32)
        term_conv = jnp.einsum("tk,tn->kn", inputs, pre_grad, preferred_element_type=jnp.float32)
        term_res = jnp.einsum("tk,tn->kn", gated, cotangent, preferred_element_type=jnp.float32)
        kc, n_conv = term_conv.shape
        kr, n_res = term_res.shape
        rc, rr = kc // n_tm, kr // n_tm
        all_tokens = count_of_rows * n_tm * n_rep
        edge_rows = input_gradient[:DILATION_STEP, :channel_count].astype(jnp.bfloat16)
        reducer = make_reducer(sizes, rc, n_conv, rr, n_res, float(all_tokens) ** (-0.5), edge_rows.shape)
        split = count_of_rows - DILATION_STEP
        head_rows = (
            cotangent[:split].astype(jnp.float32) + input_gradient[:split, channel_count:]
            + input_gradient[DILATION_STEP:, :channel_count]
        ).astype(jnp.bfloat16)
        conv_in = term_conv.astype(jnp.bfloat16).reshape(nx, nzh, nc, rc, n_conv)
        res_in = term_res.astype(jnp.bfloat16).reshape(nx, nzh, nc, rr, n_res)
        head_rows, conv_in, res_in, edge_rows = lax.optimization_barrier((head_rows, conv_in, res_in, edge_rows))
        flip_conv, flip_res, incoming_gradient = reducer(conv_in, res_in, edge_rows)
        tail_rows = (
            cotangent[split:].astype(jnp.float32) + input_gradient[split:, channel_count:]
            + incoming_gradient.astype(jnp.float32)
        ).astype(jnp.bfloat16)
        grad_rows = jnp.concatenate([head_rows, tail_rows], 0)
        return (grad_rows[None], flip_conv.T, flip_res.T)

    return body


def solution(mesh):
    n_tm, n_rep = mesh.devices.shape
    nc = 2
    nzh = 2
    nx = n_tm // (nc * nzh)
    nzl = 8
    ny = n_rep // nzl
    sizes = (nx, nzh, nc, ny, nzl)
    fine = Mesh(mesh.devices.reshape(sizes), ("x", "zh", "c", "y", "zl"))
    return jax.shard_map(
        make_body(sizes),
        mesh=fine,
        in_specs=(P(REP, TM, None), P(REP, TM, None), P(), P(), P(REP)),
        out_specs=(P(REP, TM, None), P(TM, REP), P(TM, REP)),
        check_vma=False,
    )
```

```python
import jax
import jax.numpy as jnp
from jax import lax
from jax.experimental import pallas as pl
from jax.experimental.pallas import tpu as pltpu
from jax.sharding import Mesh, PartitionSpec as P

DILATION_STEP = 256
TM = ("x", "zh", "c")
REP = ("y", "zl")


def passed_along(array, axis, by, length):
    pairs = [(i, i + by) for i in range(length) if 0 <= i + by < length]
    return lax.ppermute(array, axis, pairs)


def gate_backward(inputs, cotangent, in_length, w_conv, w_res):
    channel_count = w_res.shape[0]
    pre_act = jnp.dot(inputs, w_conv, preferred_element_type=jnp.float32)
    tanh_f = jnp.tanh(pre_act[:, :channel_count])
    sig_g = jax.nn.sigmoid(pre_act[:, channel_count:])
    gated = (in_length * tanh_f * sig_g).astype(jnp.bfloat16)
    gated_grad = in_length * jnp.dot(cotangent, w_res.T, preferred_element_type=jnp.float32)
    pre_grad = jnp.concatenate(
        [gated_grad * sig_g * (1.0 - tanh_f * tanh_f), gated_grad * tanh_f * sig_g * (1.0 - sig_g)],
        1,
    ).astype(jnp.bfloat16)
    return (gated, pre_grad)


def make_reducer(sizes, rc, n_conv, rr, n_res, scale, edge_shape):
    nx, nzh, nc, ny, nzl = sizes
    nz = nzh * nzl
    cyc, cyr = n_conv // ny, n_res // ny
    cc, cr = cyc // nzl, cyr // nzl
    hc, hr = rc // 2, rr // 2
    base_xa, base_yb = 1, 1 + nx
    base_ya, base_xb = 1 + nx + ny, 1 + nx + 2 * ny
    base_z = 1 + 2 * nx + 2 * ny
    n_slots = base_z + nz
    n_peers = (nc - 1) + (nx - 1) + (ny - 1) + (nz - 1) + 2
    n_tm = nx * nzh * nc
    mesh_id = pl.DeviceIdType.MESH

    def kernel(conv_ref, res_ref, edge_ref, conv_out, res_out, edge_out,
               rc_conv, rc_res, sx_conv, sx_res,
               rxa_conv, rxa_res, ryb_conv, ryb_res,
               sa_conv, sa_res, rya_conv, rya_res,
               sb_conv, sb_res, rxb_conv, rxb_res,
               sz_both, rz_both,
               edge_buf, own_conv, own_res, conv_v, res_v, send_sems, recv_sems, local_sems, own_sems):
        me_x = lax.axis_index("x")
        me_zh = lax.axis_index("zh")
        me_c = lax.axis_index("c")
        me_y = lax.axis_index("y")
        me_zl = lax.axis_index("zl")
        me_z = me_zh * nzl + me_zl
        other_c = 1 - me_c

        def dev(x=None, zh=None, c=None, y=None, zl=None):
            return (me_x if x is None else x, me_zh if zh is None else zh,
                    me_c if c is None else c, me_y if y is None else y,
                    me_zl if zl is None else zl)

        peers = [dev(c=other_c)]
        x_peers = [dev(x=lax.rem(me_x + d, nx)) for d in range(1, nx)]
        y_peers = [dev(y=lax.rem(me_y + d, ny)) for d in range(1, ny)]
        z_peers = []
        for d in range(1, nz):
            q = lax.rem(me_z + d, nz)
            z_peers.append(dev(zh=q // nzl, zl=lax.rem(q, nzl)))
        barrier = pltpu.get_barrier_semaphore()
        t = (me_x * nzh + me_zh) * nc + me_c

        def tm_dev(u):
            return dev(x=u // (nzh * nc), zh=lax.rem(u // nc, nzh), c=lax.rem(u, nc))

        before = tm_dev(lax.rem(t + n_tm - 1, n_tm))
        after = tm_dev(lax.rem(t + 1, n_tm))
        far_first = sorted(range(1, nz), key=lambda d: -min(d, nz - d))
        for peer in [z_peers[d - 1] for d in far_first] + [before, after] + peers + x_peers + y_peers:
            pl.semaphore_signal(barrier, inc=1, device_id=peer, device_id_type=mesh_id)
        pl.semaphore_wait(barrier, n_peers)

        sends = []

        def send(kind, src, dst, slot, peer):
            copy = pltpu.make_async_remote_copy(
                src_ref=src, dst_ref=dst, send_sem=send_sems.at[kind, slot],
                recv_sem=recv_sems.at[kind, slot], device_id=peer, device_id_type=mesh_id)
            copy.start()
            sends.append(copy)

        def arrive(kind, src, dst, slot):
            pltpu.make_async_remote_copy(
                src_ref=src, dst_ref=dst, send_sem=send_sems.at[kind, slot],
                recv_sem=recv_sems.at[kind, slot], device_id=dev(),
                device_id_type=mesh_id).wait_recv()

        def keep(kind, which, src, dst):
            copy = pltpu.make_async_copy(src, dst, local_sems.at[kind, which])
            copy.start()
            return copy

        edge = pltpu.make_async_remote_copy(
            src_ref=edge_ref, dst_ref=edge_buf, send_sem=local_sems.at[0, 2],
            recv_sem=local_sems.at[1, 2], device_id=before, device_id_type=mesh_id)
        edge.start()

        send(0, conv_ref.at[:, :, pl.ds(other_c, 1)], rc_conv, 0, peers[0])
        send(1, res_ref.at[:, :, pl.ds(other_c, 1)], rc_res, 0, peers[0])
        own_in = [pltpu.make_async_copy(conv_ref.at[:, :, pl.ds(me_c, 1)], own_conv, own_sems.at[0]),
                  pltpu.make_async_copy(res_ref.at[:, :, pl.ds(me_c, 1)], own_res, own_sems.at[1])]
        for copy in own_in:
            copy.start()
        for copy in own_in:
            copy.wait()
        arrive(0, conv_ref.at[:, :, pl.ds(other_c, 1)], rc_conv, 0)
        arrive(1, res_ref.at[:, :, pl.ds(other_c, 1)], rc_res, 0)
        for x in range(nx):
            for zh in range(nzh):
                own_c = own_conv[x, zh, 0].astype(jnp.float32)
                sx_conv[x, zh] = (own_c + rc_conv[x, zh, 0].astype(jnp.float32)).astype(jnp.bfloat16)
                own_r = own_res[x, zh, 0].astype(jnp.float32)
                sx_res[x, zh] = (own_r + rc_res[x, zh, 0].astype(jnp.float32)).astype(jnp.bfloat16)

        for d in range(1, nx):
            tx = lax.rem(me_x + d, nx)
            send(0, sx_conv.at[tx, :, pl.ds(0, hc)], rxa_conv.at[me_x], base_xa + me_x, x_peers[d - 1])
            send(1, sx_res.at[tx, :, pl.ds(0, hr)], rxa_res.at[me_x], base_xa + me_x, x_peers[d - 1])
        for d in range(1, ny):
            ty = lax.rem(me_y + d, ny)
            send(0, sx_conv.at[:, :, pl.ds(hc, hc), pl.ds(ty * cyc, cyc)], ryb_conv.at[me_y],
                 base_yb + me_y, y_peers[d - 1])
            send(1, sx_res.at[:, :, pl.ds(hr, hr), pl.ds(ty * cyr, cyr)], ryb_res.at[me_y],
                 base_yb + me_y, y_peers[d - 1])
        own_b = [keep(0, 0, sx_conv.at[:, :, pl.ds(hc, hc), pl.ds(me_y * cyc, cyc)], ryb_conv.at[me_y]),
                 keep(1, 0, sx_res.at[:, :, pl.ds(hr, hr), pl.ds(me_y * cyr, cyr)], ryb_res.at[me_y])]

        for d in range(1, nx):
            sx = lax.rem(me_x + nx - d, nx)
            arrive(0, sx_conv.at[sx, :, pl.ds(0, hc)], rxa_conv.at[sx], base_xa + sx)
            arrive(1, sx_res.at[sx, :, pl.ds(0, hr)], rxa_res.at[sx], base_xa + sx)
        acc_c = sx_conv[me_x, :, :hc].astype(jnp.float32)
        acc_r = sx_res[me_x, :, :hr].astype(jnp.float32)
        for d in range(1, nx):
            sx = lax.rem(me_x + nx - d, nx)
            acc_c = acc_c + rxa_conv[sx].astype(jnp.float32)
            acc_r = acc_r + rxa_res[sx].astype(jnp.float32)
        sa_conv[...] = acc_c.astype(jnp.bfloat16)
        sa_res[...] = acc_r.astype(jnp.bfloat16)
        for d in range(1, ny):
            ty = lax.rem(me_y + d, ny)
            send(0, sa_conv.at[:, :, pl.ds(ty * cyc, cyc)], rya_conv.at[me_y], base_ya + me_y, y_peers[d - 1])
            send(1, sa_res.at[:, :, pl.ds(ty * cyr, cyr)], rya_res.at[me_y], base_ya + me_y, y_peers[d - 1])
        own_a = [keep(0, 1, sa_conv.at[:, :, pl.ds(me_y * cyc, cyc)], rya_conv.at[me_y]),
                 keep(1, 1, sa_res.at[:, :, pl.ds(me_y * cyr, cyr)], rya_res.at[me_y])]

        for d in range(1, ny):
            sy = lax.rem(me_y + ny - d, ny)
            arrive(0, sx_conv.at[:, :, pl.ds(hc, hc), pl.ds(0, cyc)], ryb_conv.at[sy], base_yb + sy)
            arrive(1, sx_res.at[:, :, pl.ds(hr, hr), pl.ds(0, cyr)], ryb_res.at[sy], base_yb + sy)
        for copy in own_b:
            copy.wait()
        acc_c = ryb_conv[0].astype(jnp.float32)
        acc_r = ryb_res[0].astype(jnp.float32)
        for s in range(1, ny):
            acc_c = acc_c + ryb_conv[s].astype(jnp.float32)
            acc_r = acc_r + ryb_res[s].astype(jnp.float32)
        sb_conv[...] = acc_c.astype(jnp.bfloat16)
        sb_res[...] = acc_r.astype(jnp.bfloat16)
        for d in range(1, nx):
            tx = lax.rem(me_x + d, nx)
            send(0, sb_conv.at[tx], rxb_conv.at[me_x], base_xb + me_x, x_peers[d - 1])
            send(1, sb_res.at[tx], rxb_res.at[me_x], base_xb + me_x, x_peers[d - 1])

        for d in range(1, ny):
            sy = lax.rem(me_y + ny - d, ny)
            arrive(0, sa_conv.at[:, :, pl.ds(0, cyc)], rya_conv.at[sy], base_ya + sy)
            arrive(1, sa_res.at[:, :, pl.ds(0, cyr)], rya_res.at[sy], base_ya + sy)
        for copy in own_a:
            copy.wait()
        for d in range(1, nx):
            sx = lax.rem(me_x + nx - d, nx)
            arrive(0, sb_conv.at[sx], rxb_conv.at[sx], base_xb + sx)
            arrive(1, sb_res.at[sx], rxb_res.at[sx], base_xb + sx)
        top_c = rya_conv[0].astype(jnp.float32)
        top_r = rya_res[0].astype(jnp.float32)
        for s in range(1, ny):
            top_c = top_c + rya_conv[s].astype(jnp.float32)
            top_r = top_r + rya_res[s].astype(jnp.float32)
        low_c = sb_conv[me_x].astype(jnp.float32)
        low_r = sb_res[me_x].astype(jnp.float32)
        for d in range(1, nx):
            sx = lax.rem(me_x + nx - d, nx)
            low_c = low_c + rxb_conv[sx].astype(jnp.float32)
            low_r = low_r + rxb_res[sx].astype(jnp.float32)
        acc_c = jnp.concatenate([top_c, low_c], axis=1)
        acc_r = jnp.concatenate([top_r, low_r], axis=1)
        for zh in range(nzh):
            flip_c = acc_c[zh].T
            flip_r = acc_r[zh].T
            for zl in range(nzl):
                q = zh * nzl + zl
                sz_both[q, :cc, :] = flip_c[zl * cc:(zl + 1) * cc, :].astype(jnp.bfloat16)
                sz_both[q, cc:, :rr] = flip_r[zl * cr:(zl + 1) * cr, :].astype(jnp.bfloat16)
                sz_both[q, cc:, rr:] = jnp.zeros((cr, rc - rr), jnp.bfloat16)

        for d in range(1, nz):
            tz = lax.rem(me_z + d, nz)
            send(0, sz_both.at[tz], rz_both.at[me_z], base_z + me_z, z_peers[d - 1])
        for d in range(1, nz):
            sz = lax.rem(me_z + nz - d, nz)
            arrive(0, sz_both.at[sz], rz_both.at[sz], base_z + sz)
        acc = sz_both[me_z].astype(jnp.float32)
        for d in range(1, nz):
            sz = lax.rem(me_z + nz - d, nz)
            acc = acc + rz_both[sz].astype(jnp.float32)
        conv_v[...] = acc[:cc] * scale
        res_v[...] = acc[cc:, :rr] * scale
        edge.wait_recv()

        @pl.when(t == n_tm - 1)
        def _():
            edge_buf[...] = jnp.zeros_like(edge_buf)

        outs = [pltpu.make_async_copy(conv_v, conv_out, own_sems.at[2]),
                pltpu.make_async_copy(res_v, res_out, own_sems.at[3]),
                pltpu.make_async_copy(edge_buf, edge_out, own_sems.at[4])]
        for copy in outs:
            copy.start()
        for copy in outs:
            copy.wait()

        for copy in sends:
            copy.wait_send()
        edge.wait_send()

    vmem = pl.BlockSpec(memory_space=pltpu.VMEM)
    bf16, f32 = jnp.bfloat16, jnp.float32
    return pl.pallas_call(
        kernel,
        out_shape=(jax.ShapeDtypeStruct((cc, rc), f32), jax.ShapeDtypeStruct((cr, rr), f32),
                   jax.ShapeDtypeStruct(edge_shape, bf16)),
        in_specs=[pl.BlockSpec(memory_space=pl.ANY)] * 3,
        out_specs=(pl.BlockSpec(memory_space=pl.ANY),) * 3,
        scratch_shapes=[
            pltpu.VMEM((nx, nzh, 1, rc, n_conv), bf16),
            pltpu.VMEM((nx, nzh, 1, rr, n_res), bf16),
            pltpu.VMEM((nx, nzh, rc, n_conv), bf16),
            pltpu.VMEM((nx, nzh, rr, n_res), bf16),
            pltpu.VMEM((nx, nzh, hc, n_conv), bf16),
            pltpu.VMEM((nx, nzh, hr, n_res), bf16),
            pltpu.VMEM((ny, nx, nzh, hc, cyc), bf16),
            pltpu.VMEM((ny, nx, nzh, hr, cyr), bf16),
            pltpu.VMEM((nzh, hc, n_conv), bf16),
            pltpu.VMEM((nzh, hr, n_res), bf16),
            pltpu.VMEM((ny, nzh, hc, cyc), bf16),
            pltpu.VMEM((ny, nzh, hr, cyr), bf16),
            pltpu.VMEM((nx, nzh, hc, cyc), bf16),
            pltpu.VMEM((nx, nzh, hr, cyr), bf16),
            pltpu.VMEM((nx, nzh, hc, cyc), bf16),
            pltpu.VMEM((nx, nzh, hr, cyr), bf16),
            pltpu.VMEM((nz, cc + cr, rc), bf16),
            pltpu.VMEM((nz, cc + cr, rc), bf16),
            pltpu.VMEM(edge_shape, bf16),
            pltpu.VMEM((nx, nzh, 1, rc, n_conv), bf16),
            pltpu.VMEM((nx, nzh, 1, rr, n_res), bf16),
            pltpu.VMEM((cc, rc), f32),
            pltpu.VMEM((cr, rr), f32),
            pltpu.SemaphoreType.DMA((2, n_slots)),
            pltpu.SemaphoreType.DMA((2, n_slots)),
            pltpu.SemaphoreType.DMA((2, 3)),
            pltpu.SemaphoreType.DMA((5,)),
        ],
        compiler_params=pltpu.CompilerParams(collective_id=0, has_side_effects=True),
    )


def make_body(sizes):
    nx, nzh, nc, ny, nzl = sizes
    n_tm = nx * nzh * nc
    n_rep = ny * nzl

    def body(samples, grad_out, w_conv, w_res, lengths):
        sequence_rows = samples[0]
        cotangent = grad_out[0]
        seq_len = lengths[0]
        count_of_rows = sequence_rows.shape[0]
        channel_count = sequence_rows.shape[1]
        start_row = lax.axis_index(TM) * count_of_rows
        trailing_rows = sequence_rows[count_of_rows - DILATION_STEP :]
        arrived = passed_along(trailing_rows, TM, 1, n_tm)
        prior_samples = jnp.concatenate(
            [arrived, sequence_rows[: count_of_rows - DILATION_STEP]], 0
        )
        inputs = jnp.concatenate([prior_samples, sequence_rows], 1)
        in_length = (start_row + jnp.arange(count_of_rows) < seq_len).astype(jnp.float32)[:, None]
        gated, pre_grad = gate_backward(inputs, cotangent, in_length, w_conv, w_res)
        input_gradient = jnp.dot(pre_grad, w_conv.T, preferred_element_type=jnp.float32)
        term_conv = jnp.einsum("tk,tn->kn", inputs, pre_grad, preferred_element_type=jnp.float32)
        term_res = jnp.einsum("tk,tn->kn", gated, cotangent, preferred_element_type=jnp.float32)
        kc, n_conv = term_conv.shape
        kr, n_res = term_res.shape
        rc, rr = kc // n_tm, kr // n_tm
        all_tokens = count_of_rows * n_tm * n_rep
        edge_rows = input_gradient[:DILATION_STEP, :channel_count].astype(jnp.bfloat16)
        reducer = make_reducer(sizes, rc, n_conv, rr, n_res, float(all_tokens) ** (-0.5), edge_rows.shape)
        split = count_of_rows - DILATION_STEP
        head_rows = (
            cotangent[:split].astype(jnp.float32) + input_gradient[:split, channel_count:]
            + input_gradient[DILATION_STEP:, :channel_count]
        ).astype(jnp.bfloat16)
        conv_in = term_conv.astype(jnp.bfloat16).reshape(nx, nzh, nc, rc, n_conv)
        res_in = term_res.astype(jnp.bfloat16).reshape(nx, nzh, nc, rr, n_res)
        head_rows, conv_in, res_in, edge_rows = lax.optimization_barrier((head_rows, conv_in, res_in, edge_rows))
        flip_conv, flip_res, incoming_gradient = reducer(conv_in, res_in, edge_rows)
        tail_rows = (
            cotangent[split:].astype(jnp.float32) + input_gradient[split:, channel_count:]
            + incoming_gradient.astype(jnp.float32)
        ).astype(jnp.bfloat16)
        grad_rows = jnp.concatenate([head_rows, tail_rows], 0)
        return (grad_rows[None], flip_conv.T, flip_res.T)

    return body


def solution(mesh):
    n_tm, n_rep = mesh.devices.shape
    nc = 2
    nzh = 2
    nx = n_tm // (nc * nzh)
    nzl = 8
    ny = n_rep // nzl
    sizes = (nx, nzh, nc, ny, nzl)
    fine = Mesh(mesh.devices.reshape(sizes), ("x", "zh", "c", "y", "zl"))
    return jax.shard_map(
        make_body(sizes),
        mesh=fine,
        in_specs=(P(REP, TM, None), P(REP, TM, None), P(), P(), P(REP)),
        out_specs=(P(REP, TM, None), P(TM, REP), P(TM, REP)),
        check_vma=False,
    )
```

```python
import jax
import jax.numpy as jnp
from jax import lax
from jax.experimental import pallas as pl
from jax.experimental.pallas import tpu as pltpu
from jax.sharding import Mesh, PartitionSpec as P

DILATION_STEP = 256
TM = ("x", "zh", "c")
REP = ("y", "zl")


def passed_along(array, axis, by, length):
    pairs = [(i, i + by) for i in range(length) if 0 <= i + by < length]
    return lax.ppermute(array, axis, pairs)


def gate_backward(inputs, cotangent, in_length, w_conv, w_res):
    channel_count = w_res.shape[0]
    pre_act = jnp.dot(inputs, w_conv, preferred_element_type=jnp.float32)
    tanh_f = jnp.tanh(pre_act[:, :channel_count])
    sig_g = jax.nn.sigmoid(pre_act[:, channel_count:])
    gated = (in_length * tanh_f * sig_g).astype(jnp.bfloat16)
    gated_grad = in_length * jnp.dot(cotangent, w_res.T, preferred_element_type=jnp.float32)
    pre_grad = jnp.concatenate(
        [gated_grad * sig_g * (1.0 - tanh_f * tanh_f), gated_grad * tanh_f * sig_g * (1.0 - sig_g)],
        1,
    ).astype(jnp.bfloat16)
    return (gated, pre_grad)


def make_reducer(sizes, rc, n_conv, rr, n_res, scale, edge_shape):
    nx, nzh, nc, ny, nzl = sizes
    nz = nzh * nzl
    cyc, cyr = n_conv // ny, n_res // ny
    cc, cr = cyc // nzl, cyr // nzl
    hc, hr = rc // 2, rr // 2
    base_xa, base_yb = 1, 1 + nx
    base_ya, base_xb = 1 + nx + ny, 1 + nx + 2 * ny
    base_z = 1 + 2 * nx + 2 * ny
    n_slots = base_z + nz
    n_peers = (nc - 1) + (nx - 1) + (ny - 1) + (nz - 1) + 2
    n_tm = nx * nzh * nc
    mesh_id = pl.DeviceIdType.MESH

    def kernel(conv_ref, res_ref, edge_ref, conv_out, res_out, edge_out,
               rc_conv, rc_res, sx_conv, sx_res,
               rxa_conv, rxa_res, ryb_conv, ryb_res,
               sa_conv, sa_res, rya_conv, rya_res,
               sb_conv, sb_res, rxb_conv, rxb_res,
               sz_both, rz_both,
               edge_buf, own_conv, own_res, edge_f32, edge_src, send_sems, recv_sems, local_sems, own_sems):
        me_x = lax.axis_index("x")
        me_zh = lax.axis_index("zh")
        me_c = lax.axis_index("c")
        me_y = lax.axis_index("y")
        me_zl = lax.axis_index("zl")
        me_z = me_zh * nzl + me_zl
        other_c = 1 - me_c

        def dev(x=None, zh=None, c=None, y=None, zl=None):
            return (me_x if x is None else x, me_zh if zh is None else zh,
                    me_c if c is None else c, me_y if y is None else y,
                    me_zl if zl is None else zl)

        peers = [dev(c=other_c)]
        x_peers = [dev(x=lax.rem(me_x + d, nx)) for d in range(1, nx)]
        y_peers = [dev(y=lax.rem(me_y + d, ny)) for d in range(1, ny)]
        z_peers = []
        for d in range(1, nz):
            q = lax.rem(me_z + d, nz)
            z_peers.append(dev(zh=q // nzl, zl=lax.rem(q, nzl)))
        barrier = pltpu.get_barrier_semaphore()
        t = (me_x * nzh + me_zh) * nc + me_c

        def tm_dev(u):
            return dev(x=u // (nzh * nc), zh=lax.rem(u // nc, nzh), c=lax.rem(u, nc))

        before = tm_dev(lax.rem(t + n_tm - 1, n_tm))
        after = tm_dev(lax.rem(t + 1, n_tm))
        far_first = sorted(range(1, nz), key=lambda d: -min(d, nz - d))
        for peer in [z_peers[d - 1] for d in far_first] + [before, after] + peers + x_peers + y_peers:
            pl.semaphore_signal(barrier, inc=1, device_id=peer, device_id_type=mesh_id)
        pl.semaphore_wait(barrier, n_peers)

        sends = []

        def send(kind, src, dst, slot, peer):
            copy = pltpu.make_async_remote_copy(
                src_ref=src, dst_ref=dst, send_sem=send_sems.at[kind, slot],
                recv_sem=recv_sems.at[kind, slot], device_id=peer, device_id_type=mesh_id)
            copy.start()
            sends.append(copy)

        def arrive(kind, src, dst, slot):
            pltpu.make_async_remote_copy(
                src_ref=src, dst_ref=dst, send_sem=send_sems.at[kind, slot],
                recv_sem=recv_sems.at[kind, slot], device_id=dev(),
                device_id_type=mesh_id).wait_recv()

        def keep(kind, which, src, dst):
            copy = pltpu.make_async_copy(src, dst, local_sems.at[kind, which])
            copy.start()
            return copy

        edge_in = pltpu.make_async_copy(
            edge_ref.at[pl.ds(0, edge_shape[0]), pl.ds(0, edge_shape[1])], edge_f32, own_sems.at[2])
        edge_in.start()
        edge_in.wait()
        edge_src[...] = edge_f32[...].astype(jnp.bfloat16)
        edge = pltpu.make_async_remote_copy(
            src_ref=edge_src, dst_ref=edge_buf, send_sem=local_sems.at[0, 2],
            recv_sem=local_sems.at[1, 2], device_id=before, device_id_type=mesh_id)
        edge.start()

        send(0, conv_ref.at[:, :, pl.ds(other_c, 1)], rc_conv, 0, peers[0])
        send(1, res_ref.at[:, :, pl.ds(other_c, 1)], rc_res, 0, peers[0])
        own_in = [pltpu.make_async_copy(conv_ref.at[:, :, pl.ds(me_c, 1)], own_conv, own_sems.at[0]),
                  pltpu.make_async_copy(res_ref.at[:, :, pl.ds(me_c, 1)], own_res, own_sems.at[1])]
        for copy in own_in:
            copy.start()
        for copy in own_in:
            copy.wait()
        arrive(0, conv_ref.at[:, :, pl.ds(other_c, 1)], rc_conv, 0)
        arrive(1, res_ref.at[:, :, pl.ds(other_c, 1)], rc_res, 0)
        for x in range(nx):
            for zh in range(nzh):
                own_c = own_conv[x, zh, 0].astype(jnp.float32)
                sx_conv[x, zh] = (own_c + rc_conv[x, zh, 0].astype(jnp.float32)).astype(jnp.bfloat16)
                own_r = own_res[x, zh, 0].astype(jnp.float32)
                sx_res[x, zh] = (own_r + rc_res[x, zh, 0].astype(jnp.float32)).astype(jnp.bfloat16)

        for d in range(1, nx):
            tx = lax.rem(me_x + d, nx)
            send(0, sx_conv.at[tx, :, pl.ds(0, hc)], rxa_conv.at[me_x], base_xa + me_x, x_peers[d - 1])
            send(1, sx_res.at[tx, :, pl.ds(0, hr)], rxa_res.at[me_x], base_xa + me_x, x_peers[d - 1])
        for d in range(1, ny):
            ty = lax.rem(me_y + d, ny)
            send(0, sx_conv.at[:, :, pl.ds(hc, hc), pl.ds(ty * cyc, cyc)], ryb_conv.at[me_y],
                 base_yb + me_y, y_peers[d - 1])
            send(1, sx_res.at[:, :, pl.ds(hr, hr), pl.ds(ty * cyr, cyr)], ryb_res.at[me_y],
                 base_yb + me_y, y_peers[d - 1])
        own_b = [keep(0, 0, sx_conv.at[:, :, pl.ds(hc, hc), pl.ds(me_y * cyc, cyc)], ryb_conv.at[me_y]),
                 keep(1, 0, sx_res.at[:, :, pl.ds(hr, hr), pl.ds(me_y * cyr, cyr)], ryb_res.at[me_y])]

        for d in range(1, nx):
            sx = lax.rem(me_x + nx - d, nx)
            arrive(0, sx_conv.at[sx, :, pl.ds(0, hc)], rxa_conv.at[sx], base_xa + sx)
            arrive(1, sx_res.at[sx, :, pl.ds(0, hr)], rxa_res.at[sx], base_xa + sx)
        acc_c = sx_conv[me_x, :, :hc].astype(jnp.float32)
        acc_r = sx_res[me_x, :, :hr].astype(jnp.float32)
        for d in range(1, nx):
            sx = lax.rem(me_x + nx - d, nx)
            acc_c = acc_c + rxa_conv[sx].astype(jnp.float32)
            acc_r = acc_r + rxa_res[sx].astype(jnp.float32)
        sa_conv[...] = acc_c.astype(jnp.bfloat16)
        sa_res[...] = acc_r.astype(jnp.bfloat16)
        for d in range(1, ny):
            ty = lax.rem(me_y + d, ny)
            send(0, sa_conv.at[:, :, pl.ds(ty * cyc, cyc)], rya_conv.at[me_y], base_ya + me_y, y_peers[d - 1])
            send(1, sa_res.at[:, :, pl.ds(ty * cyr, cyr)], rya_res.at[me_y], base_ya + me_y, y_peers[d - 1])
        own_a = [keep(0, 1, sa_conv.at[:, :, pl.ds(me_y * cyc, cyc)], rya_conv.at[me_y]),
                 keep(1, 1, sa_res.at[:, :, pl.ds(me_y * cyr, cyr)], rya_res.at[me_y])]

        for d in range(1, ny):
            sy = lax.rem(me_y + ny - d, ny)
            arrive(0, sx_conv.at[:, :, pl.ds(hc, hc), pl.ds(0, cyc)], ryb_conv.at[sy], base_yb + sy)
            arrive(1, sx_res.at[:, :, pl.ds(hr, hr), pl.ds(0, cyr)], ryb_res.at[sy], base_yb + sy)
        for copy in own_b:
            copy.wait()
        acc_c = ryb_conv[0].astype(jnp.float32)
        acc_r = ryb_res[0].astype(jnp.float32)
        for s in range(1, ny):
            acc_c = acc_c + ryb_conv[s].astype(jnp.float32)
            acc_r = acc_r + ryb_res[s].astype(jnp.float32)
        sb_conv[...] = acc_c.astype(jnp.bfloat16)
        sb_res[...] = acc_r.astype(jnp.bfloat16)
        for d in range(1, nx):
            tx = lax.rem(me_x + d, nx)
            send(0, sb_conv.at[tx], rxb_conv.at[me_x], base_xb + me_x, x_peers[d - 1])
            send(1, sb_res.at[tx], rxb_res.at[me_x], base_xb + me_x, x_peers[d - 1])

        for d in range(1, ny):
            sy = lax.rem(me_y + ny - d, ny)
            arrive(0, sa_conv.at[:, :, pl.ds(0, cyc)], rya_conv.at[sy], base_ya + sy)
            arrive(1, sa_res.at[:, :, pl.ds(0, cyr)], rya_res.at[sy], base_ya + sy)
        for copy in own_a:
            copy.wait()
        for d in range(1, nx):
            sx = lax.rem(me_x + nx - d, nx)
            arrive(0, sb_conv.at[sx], rxb_conv.at[sx], base_xb + sx)
            arrive(1, sb_res.at[sx], rxb_res.at[sx], base_xb + sx)
        top_c = rya_conv[0].astype(jnp.float32)
        top_r = rya_res[0].astype(jnp.float32)
        for s in range(1, ny):
            top_c = top_c + rya_conv[s].astype(jnp.float32)
            top_r = top_r + rya_res[s].astype(jnp.float32)
        low_c = sb_conv[me_x].astype(jnp.float32)
        low_r = sb_res[me_x].astype(jnp.float32)
        for d in range(1, nx):
            sx = lax.rem(me_x + nx - d, nx)
            low_c = low_c + rxb_conv[sx].astype(jnp.float32)
            low_r = low_r + rxb_res[sx].astype(jnp.float32)
        acc_c = jnp.concatenate([top_c, low_c], axis=1)
        acc_r = jnp.concatenate([top_r, low_r], axis=1)
        for zh in range(nzh):
            flip_c = acc_c[zh].T
            flip_r = acc_r[zh].T
            for zl in range(nzl):
                q = zh * nzl + zl
                sz_both[q, :cc, :] = flip_c[zl * cc:(zl + 1) * cc, :].astype(jnp.bfloat16)
                sz_both[q, cc:, :rr] = flip_r[zl * cr:(zl + 1) * cr, :].astype(jnp.bfloat16)
                sz_both[q, cc:, rr:] = jnp.zeros((cr, rc - rr), jnp.bfloat16)

        for d in range(1, nz):
            tz = lax.rem(me_z + d, nz)
            send(0, sz_both.at[tz], rz_both.at[me_z], base_z + me_z, z_peers[d - 1])
        for d in range(1, nz):
            sz = lax.rem(me_z + nz - d, nz)
            arrive(0, sz_both.at[sz], rz_both.at[sz], base_z + sz)
        acc = sz_both[me_z].astype(jnp.float32)
        for d in range(1, nz):
            sz = lax.rem(me_z + nz - d, nz)
            acc = acc + rz_both[sz].astype(jnp.float32)
        conv_out[...] = acc[:cc] * scale
        res_out[...] = acc[cc:, :rr] * scale
        edge.wait_recv()

        @pl.when(t < n_tm - 1)
        def _():
            edge_out[...] = edge_buf[...]

        @pl.when(t == n_tm - 1)
        def _():
            edge_out[...] = jnp.zeros_like(edge_out)

        for copy in sends:
            copy.wait_send()
        edge.wait_send()

    vmem = pl.BlockSpec(memory_space=pltpu.VMEM)
    bf16, f32 = jnp.bfloat16, jnp.float32
    return pl.pallas_call(
        kernel,
        out_shape=(jax.ShapeDtypeStruct((cc, rc), f32), jax.ShapeDtypeStruct((cr, rr), f32),
                   jax.ShapeDtypeStruct(edge_shape, bf16)),
        in_specs=[pl.BlockSpec(memory_space=pl.ANY)] * 3,
        out_specs=(vmem, vmem, vmem),
        scratch_shapes=[
            pltpu.VMEM((nx, nzh, 1, rc, n_conv), bf16),
            pltpu.VMEM((nx, nzh, 1, rr, n_res), bf16),
            pltpu.VMEM((nx, nzh, rc, n_conv), bf16),
            pltpu.VMEM((nx, nzh, rr, n_res), bf16),
            pltpu.VMEM((nx, nzh, hc, n_conv), bf16),
            pltpu.VMEM((nx, nzh, hr, n_res), bf16),
            pltpu.VMEM((ny, nx, nzh, hc, cyc), bf16),
            pltpu.VMEM((ny, nx, nzh, hr, cyr), bf16),
            pltpu.VMEM((nzh, hc, n_conv), bf16),
            pltpu.VMEM((nzh, hr, n_res), bf16),
            pltpu.VMEM((ny, nzh, hc, cyc), bf16),
            pltpu.VMEM((ny, nzh, hr, cyr), bf16),
            pltpu.VMEM((nx, nzh, hc, cyc), bf16),
            pltpu.VMEM((nx, nzh, hr, cyr), bf16),
            pltpu.VMEM((nx, nzh, hc, cyc), bf16),
            pltpu.VMEM((nx, nzh, hr, cyr), bf16),
            pltpu.VMEM((nz, cc + cr, rc), bf16),
            pltpu.VMEM((nz, cc + cr, rc), bf16),
            pltpu.VMEM(edge_shape, bf16),
            pltpu.VMEM((nx, nzh, 1, rc, n_conv), bf16),
            pltpu.VMEM((nx, nzh, 1, rr, n_res), bf16),
            pltpu.VMEM(edge_shape, f32),
            pltpu.VMEM(edge_shape, bf16),
            pltpu.SemaphoreType.DMA((2, n_slots)),
            pltpu.SemaphoreType.DMA((2, n_slots)),
            pltpu.SemaphoreType.DMA((2, 3)),
            pltpu.SemaphoreType.DMA((3,)),
        ],
        compiler_params=pltpu.CompilerParams(collective_id=0, has_side_effects=True),
    )


def make_body(sizes):
    nx, nzh, nc, ny, nzl = sizes
    n_tm = nx * nzh * nc
    n_rep = ny * nzl

    def body(samples, grad_out, w_conv, w_res, lengths):
        sequence_rows = samples[0]
        cotangent = grad_out[0]
        seq_len = lengths[0]
        count_of_rows = sequence_rows.shape[0]
        channel_count = sequence_rows.shape[1]
        start_row = lax.axis_index(TM) * count_of_rows
        trailing_rows = sequence_rows[count_of_rows - DILATION_STEP :]
        arrived = passed_along(trailing_rows, TM, 1, n_tm)
        prior_samples = jnp.concatenate(
            [arrived, sequence_rows[: count_of_rows - DILATION_STEP]], 0
        )
        inputs = jnp.concatenate([prior_samples, sequence_rows], 1)
        in_length = (start_row + jnp.arange(count_of_rows) < seq_len).astype(jnp.float32)[:, None]
        gated, pre_grad = gate_backward(inputs, cotangent, in_length, w_conv, w_res)
        input_gradient = jnp.dot(pre_grad, w_conv.T, preferred_element_type=jnp.float32)
        term_conv = jnp.einsum("tk,tn->kn", inputs, pre_grad, preferred_element_type=jnp.float32)
        term_res = jnp.einsum("tk,tn->kn", gated, cotangent, preferred_element_type=jnp.float32)
        kc, n_conv = term_conv.shape
        kr, n_res = term_res.shape
        rc, rr = kc // n_tm, kr // n_tm
        all_tokens = count_of_rows * n_tm * n_rep
        edge_shape = (DILATION_STEP, channel_count)
        reducer = make_reducer(sizes, rc, n_conv, rr, n_res, float(all_tokens) ** (-0.5), edge_shape)
        split = count_of_rows - DILATION_STEP
        head_rows = (
            cotangent[:split].astype(jnp.float32) + input_gradient[:split, channel_count:]
            + input_gradient[DILATION_STEP:, :channel_count]
        ).astype(jnp.bfloat16)
        conv_in = term_conv.astype(jnp.bfloat16).reshape(nx, nzh, nc, rc, n_conv)
        res_in = term_res.astype(jnp.bfloat16).reshape(nx, nzh, nc, rr, n_res)
        head_rows, conv_in, res_in = lax.optimization_barrier((head_rows, conv_in, res_in))
        flip_conv, flip_res, incoming_gradient = reducer(conv_in, res_in, input_gradient)
        tail_rows = (
            cotangent[split:].astype(jnp.float32) + input_gradient[split:, channel_count:]
            + incoming_gradient.astype(jnp.float32)
        ).astype(jnp.bfloat16)
        grad_rows = jnp.concatenate([head_rows, tail_rows], 0)
        return (grad_rows[None], flip_conv.T, flip_res.T)

    return body


def solution(mesh):
    n_tm, n_rep = mesh.devices.shape
    nc = 2
    nzh = 2
    nx = n_tm // (nc * nzh)
    nzl = 8
    ny = n_rep // nzl
    sizes = (nx, nzh, nc, ny, nzl)
    fine = Mesh(mesh.devices.reshape(sizes), ("x", "zh", "c", "y", "zl"))
    return jax.shard_map(
        make_body(sizes),
        mesh=fine,
        in_specs=(P(REP, TM, None), P(REP, TM, None), P(), P(), P(REP)),
        out_specs=(P(REP, TM, None), P(TM, REP), P(TM, REP)),
        check_vma=False,
    )
```

```python
import jax
import jax.numpy as jnp
from jax import lax
from jax.experimental import pallas as pl
from jax.experimental.pallas import tpu as pltpu
from jax.sharding import Mesh, PartitionSpec as P

DILATION_STEP = 256
TM = ("x", "zh", "c")
REP = ("y", "zl")


def passed_along(array, axis, by, length):
    pairs = [(i, i + by) for i in range(length) if 0 <= i + by < length]
    return lax.ppermute(array, axis, pairs)


def gate_backward(inputs, cotangent, in_length, w_conv, w_res):
    channel_count = w_res.shape[0]
    pre_act = jnp.dot(inputs, w_conv, preferred_element_type=jnp.float32)
    tanh_f = jnp.tanh(pre_act[:, :channel_count])
    sig_g = jax.nn.sigmoid(pre_act[:, channel_count:])
    gated = (in_length * tanh_f * sig_g).astype(jnp.bfloat16)
    gated_grad = in_length * jnp.dot(cotangent, w_res.T, preferred_element_type=jnp.float32)
    pre_grad = jnp.concatenate(
        [gated_grad * sig_g * (1.0 - tanh_f * tanh_f), gated_grad * tanh_f * sig_g * (1.0 - sig_g)],
        1,
    ).astype(jnp.bfloat16)
    return (gated, pre_grad)


def make_reducer(sizes, rc, n_conv, rr, n_res, scale, edge_shape):
    nx, nzh, nc, ny, nzl = sizes
    nz = nzh * nzl
    cyc, cyr = n_conv // ny, n_res // ny
    cc, cr = cyc // nzl, cyr // nzl
    hc, hr = rc // 2, rr // 2
    base_xa, base_yb = 1, 1 + nx
    base_ya, base_xb = 1 + nx + ny, 1 + nx + 2 * ny
    base_z = 1 + 2 * nx + 2 * ny
    n_slots = base_z + nz
    n_peers = (nc - 1) + (nx - 1) + (ny - 1) + (nz - 1) + 2
    n_tm = nx * nzh * nc
    mesh_id = pl.DeviceIdType.MESH

    def kernel(conv_ref, res_ref, edge_ref, conv_out, res_out, edge_out,
               rc_conv, rc_res, sx_conv, sx_res,
               rxa_conv, rxa_res, ryb_conv, ryb_res,
               sa_conv, sa_res, rya_conv, rya_res,
               sb_conv, sb_res, rxb_conv, rxb_res,
               sz_both, rz_both,
               edge_buf, own_conv, own_res, send_sems, recv_sems, local_sems, own_sems):
        me_x = lax.axis_index("x")
        me_zh = lax.axis_index("zh")
        me_c = lax.axis_index("c")
        me_y = lax.axis_index("y")
        me_zl = lax.axis_index("zl")
        me_z = me_zh * nzl + me_zl
        other_c = 1 - me_c

        def dev(x=None, zh=None, c=None, y=None, zl=None):
            return (me_x if x is None else x, me_zh if zh is None else zh,
                    me_c if c is None else c, me_y if y is None else y,
                    me_zl if zl is None else zl)

        peers = [dev(c=other_c)]
        x_peers = [dev(x=lax.rem(me_x + d, nx)) for d in range(1, nx)]
        y_peers = [dev(y=lax.rem(me_y + d, ny)) for d in range(1, ny)]
        z_peers = []
        for d in range(1, nz):
            q = lax.rem(me_z + d, nz)
            z_peers.append(dev(zh=q // nzl, zl=lax.rem(q, nzl)))
        barrier = pltpu.get_barrier_semaphore()
        t = (me_x * nzh + me_zh) * nc + me_c

        def tm_dev(u):
            return dev(x=u // (nzh * nc), zh=lax.rem(u // nc, nzh), c=lax.rem(u, nc))

        before = tm_dev(lax.rem(t + n_tm - 1, n_tm))
        after = tm_dev(lax.rem(t + 1, n_tm))
        far_first = sorted(range(1, nz), key=lambda d: -min(d, nz - d))
        for peer in [z_peers[d - 1] for d in far_first] + [before, after] + peers + x_peers + y_peers:
            pl.semaphore_signal(barrier, inc=1, device_id=peer, device_id_type=mesh_id)
        pl.semaphore_wait(barrier, n_peers)

        sends = []

        def send(kind, src, dst, slot, peer):
            copy = pltpu.make_async_remote_copy(
                src_ref=src, dst_ref=dst, send_sem=send_sems.at[kind, slot],
                recv_sem=recv_sems.at[kind, slot], device_id=peer, device_id_type=mesh_id)
            copy.start()
            sends.append(copy)

        def arrive(kind, src, dst, slot):
            pltpu.make_async_remote_copy(
                src_ref=src, dst_ref=dst, send_sem=send_sems.at[kind, slot],
                recv_sem=recv_sems.at[kind, slot], device_id=dev(),
                device_id_type=mesh_id).wait_recv()

        def keep(kind, which, src, dst):
            copy = pltpu.make_async_copy(src, dst, local_sems.at[kind, which])
            copy.start()
            return copy

        edge = pltpu.make_async_remote_copy(
            src_ref=edge_ref, dst_ref=edge_buf, send_sem=local_sems.at[0, 2],
            recv_sem=local_sems.at[1, 2], device_id=before, device_id_type=mesh_id)

        send(0, conv_ref.at[:, :, pl.ds(other_c, 1)], rc_conv, 0, peers[0])
        send(1, res_ref.at[:, :, pl.ds(other_c, 1)], rc_res, 0, peers[0])
        own_in = [pltpu.make_async_copy(conv_ref.at[:, :, pl.ds(me_c, 1)], own_conv, own_sems.at[0]),
                  pltpu.make_async_copy(res_ref.at[:, :, pl.ds(me_c, 1)], own_res, own_sems.at[1])]
        for copy in own_in:
            copy.start()
        for copy in own_in:
            copy.wait()
        arrive(0, conv_ref.at[:, :, pl.ds(other_c, 1)], rc_conv, 0)
        arrive(1, res_ref.at[:, :, pl.ds(other_c, 1)], rc_res, 0)
        edge.start()
        for x in range(nx):
            for zh in range(nzh):
                own_c = own_conv[x, zh, 0].astype(jnp.float32)
                sx_conv[x, zh] = (own_c + rc_conv[x, zh, 0].astype(jnp.float32)).astype(jnp.bfloat16)
                own_r = own_res[x, zh, 0].astype(jnp.float32)
                sx_res[x, zh] = (own_r + rc_res[x, zh, 0].astype(jnp.float32)).astype(jnp.bfloat16)

        for d in range(1, nx):
            tx = lax.rem(me_x + d, nx)
            send(0, sx_conv.at[tx, :, pl.ds(0, hc)], rxa_conv.at[me_x], base_xa + me_x, x_peers[d - 1])
            send(1, sx_res.at[tx, :, pl.ds(0, hr)], rxa_res.at[me_x], base_xa + me_x, x_peers[d - 1])
        for d in range(1, ny):
            ty = lax.rem(me_y + d, ny)
            send(0, sx_conv.at[:, :, pl.ds(hc, hc), pl.ds(ty * cyc, cyc)], ryb_conv.at[me_y],
                 base_yb + me_y, y_peers[d - 1])
            send(1, sx_res.at[:, :, pl.ds(hr, hr), pl.ds(ty * cyr, cyr)], ryb_res.at[me_y],
                 base_yb + me_y, y_peers[d - 1])
        own_b = [keep(0, 0, sx_conv.at[:, :, pl.ds(hc, hc), pl.ds(me_y * cyc, cyc)], ryb_conv.at[me_y]),
                 keep(1, 0, sx_res.at[:, :, pl.ds(hr, hr), pl.ds(me_y * cyr, cyr)], ryb_res.at[me_y])]

        for d in range(1, nx):
            sx = lax.rem(me_x + nx - d, nx)
            arrive(0, sx_conv.at[sx, :, pl.ds(0, hc)], rxa_conv.at[sx], base_xa + sx)
            arrive(1, sx_res.at[sx, :, pl.ds(0, hr)], rxa_res.at[sx], base_xa + sx)
        acc_c = sx_conv[me_x, :, :hc].astype(jnp.float32)
        acc_r = sx_res[me_x, :, :hr].astype(jnp.float32)
        for d in range(1, nx):
            sx = lax.rem(me_x + nx - d, nx)
            acc_c = acc_c + rxa_conv[sx].astype(jnp.float32)
            acc_r = acc_r + rxa_res[sx].astype(jnp.float32)
        sa_conv[...] = acc_c.astype(jnp.bfloat16)
        sa_res[...] = acc_r.astype(jnp.bfloat16)
        for d in range(1, ny):
            ty = lax.rem(me_y + d, ny)
            send(0, sa_conv.at[:, :, pl.ds(ty * cyc, cyc)], rya_conv.at[me_y], base_ya + me_y, y_peers[d - 1])
            send(1, sa_res.at[:, :, pl.ds(ty * cyr, cyr)], rya_res.at[me_y], base_ya + me_y, y_peers[d - 1])
        own_a = [keep(0, 1, sa_conv.at[:, :, pl.ds(me_y * cyc, cyc)], rya_conv.at[me_y]),
                 keep(1, 1, sa_res.at[:, :, pl.ds(me_y * cyr, cyr)], rya_res.at[me_y])]

        for d in range(1, ny):
            sy = lax.rem(me_y + ny - d, ny)
            arrive(0, sx_conv.at[:, :, pl.ds(hc, hc), pl.ds(0, cyc)], ryb_conv.at[sy], base_yb + sy)
            arrive(1, sx_res.at[:, :, pl.ds(hr, hr), pl.ds(0, cyr)], ryb_res.at[sy], base_yb + sy)
        for copy in own_b:
            copy.wait()
        acc_c = ryb_conv[0].astype(jnp.float32)
        acc_r = ryb_res[0].astype(jnp.float32)
        for s in range(1, ny):
            acc_c = acc_c + ryb_conv[s].astype(jnp.float32)
            acc_r = acc_r + ryb_res[s].astype(jnp.float32)
        sb_conv[...] = acc_c.astype(jnp.bfloat16)
        sb_res[...] = acc_r.astype(jnp.bfloat16)
        for d in range(1, nx):
            tx = lax.rem(me_x + d, nx)
            send(0, sb_conv.at[tx], rxb_conv.at[me_x], base_xb + me_x, x_peers[d - 1])
            send(1, sb_res.at[tx], rxb_res.at[me_x], base_xb + me_x, x_peers[d - 1])

        for d in range(1, ny):
            sy = lax.rem(me_y + ny - d, ny)
            arrive(0, sa_conv.at[:, :, pl.ds(0, cyc)], rya_conv.at[sy], base_ya + sy)
            arrive(1, sa_res.at[:, :, pl.ds(0, cyr)], rya_res.at[sy], base_ya + sy)
        for copy in own_a:
            copy.wait()
        for d in range(1, nx):
            sx = lax.rem(me_x + nx - d, nx)
            arrive(0, sb_conv.at[sx], rxb_conv.at[sx], base_xb + sx)
            arrive(1, sb_res.at[sx], rxb_res.at[sx], base_xb + sx)
        top_c = rya_conv[0].astype(jnp.float32)
        top_r = rya_res[0].astype(jnp.float32)
        for s in range(1, ny):
            top_c = top_c + rya_conv[s].astype(jnp.float32)
            top_r = top_r + rya_res[s].astype(jnp.float32)
        low_c = sb_conv[me_x].astype(jnp.float32)
        low_r = sb_res[me_x].astype(jnp.float32)
        for d in range(1, nx):
            sx = lax.rem(me_x + nx - d, nx)
            low_c = low_c + rxb_conv[sx].astype(jnp.float32)
            low_r = low_r + rxb_res[sx].astype(jnp.float32)
        acc_c = jnp.concatenate([top_c, low_c], axis=1)
        acc_r = jnp.concatenate([top_r, low_r], axis=1)
        for zh in range(nzh):
            flip_c = acc_c[zh].T
            flip_r = acc_r[zh].T
            for zl in range(nzl):
                q = zh * nzl + zl
                sz_both[q, :cc, :] = flip_c[zl * cc:(zl + 1) * cc, :].astype(jnp.bfloat16)
                sz_both[q, cc:, :rr] = flip_r[zl * cr:(zl + 1) * cr, :].astype(jnp.bfloat16)
                sz_both[q, cc:, rr:] = jnp.zeros((cr, rc - rr), jnp.bfloat16)

        for d in range(1, nz):
            tz = lax.rem(me_z + d, nz)
            send(0, sz_both.at[tz], rz_both.at[me_z], base_z + me_z, z_peers[d - 1])
        for d in range(1, nz):
            sz = lax.rem(me_z + nz - d, nz)
            arrive(0, sz_both.at[sz], rz_both.at[sz], base_z + sz)
        acc = sz_both[me_z].astype(jnp.float32)
        for d in range(1, nz):
            sz = lax.rem(me_z + nz - d, nz)
            acc = acc + rz_both[sz].astype(jnp.float32)
        conv_out[...] = acc[:cc] * scale
        res_out[...] = acc[cc:, :rr] * scale
        edge.wait_recv()

        @pl.when(t < n_tm - 1)
        def _():
            edge_out[...] = edge_buf[...]

        @pl.when(t == n_tm - 1)
        def _():
            edge_out[...] = jnp.zeros_like(edge_out)

        for copy in sends:
            copy.wait_send()
        edge.wait_send()

    vmem = pl.BlockSpec(memory_space=pltpu.VMEM)
    bf16, f32 = jnp.bfloat16, jnp.float32
    return pl.pallas_call(
        kernel,
        out_shape=(jax.ShapeDtypeStruct((cc, rc), f32), jax.ShapeDtypeStruct((cr, rr), f32),
                   jax.ShapeDtypeStruct(edge_shape, bf16)),
        in_specs=[pl.BlockSpec(memory_space=pl.ANY)] * 3,
        out_specs=(vmem, vmem, vmem),
        scratch_shapes=[
            pltpu.VMEM((nx, nzh, 1, rc, n_conv), bf16),
            pltpu.VMEM((nx, nzh, 1, rr, n_res), bf16),
            pltpu.VMEM((nx, nzh, rc, n_conv), bf16),
            pltpu.VMEM((nx, nzh, rr, n_res), bf16),
            pltpu.VMEM((nx, nzh, hc, n_conv), bf16),
            pltpu.VMEM((nx, nzh, hr, n_res), bf16),
            pltpu.VMEM((ny, nx, nzh, hc, cyc), bf16),
            pltpu.VMEM((ny, nx, nzh, hr, cyr), bf16),
            pltpu.VMEM((nzh, hc, n_conv), bf16),
            pltpu.VMEM((nzh, hr, n_res), bf16),
            pltpu.VMEM((ny, nzh, hc, cyc), bf16),
            pltpu.VMEM((ny, nzh, hr, cyr), bf16),
            pltpu.VMEM((nx, nzh, hc, cyc), bf16),
            pltpu.VMEM((nx, nzh, hr, cyr), bf16),
            pltpu.VMEM((nx, nzh, hc, cyc), bf16),
            pltpu.VMEM((nx, nzh, hr, cyr), bf16),
            pltpu.VMEM((nz, cc + cr, rc), bf16),
            pltpu.VMEM((nz, cc + cr, rc), bf16),
            pltpu.VMEM(edge_shape, bf16),
            pltpu.VMEM((nx, nzh, 1, rc, n_conv), bf16),
            pltpu.VMEM((nx, nzh, 1, rr, n_res), bf16),
            pltpu.SemaphoreType.DMA((2, n_slots)),
            pltpu.SemaphoreType.DMA((2, n_slots)),
            pltpu.SemaphoreType.DMA((2, 3)),
            pltpu.SemaphoreType.DMA((2,)),
        ],
        compiler_params=pltpu.CompilerParams(collective_id=0, has_side_effects=True),
    )


def make_body(sizes):
    nx, nzh, nc, ny, nzl = sizes
    n_tm = nx * nzh * nc
    n_rep = ny * nzl

    def body(samples, grad_out, w_conv, w_res, lengths):
        sequence_rows = samples[0]
        cotangent = grad_out[0]
        seq_len = lengths[0]
        count_of_rows = sequence_rows.shape[0]
        channel_count = sequence_rows.shape[1]
        start_row = lax.axis_index(TM) * count_of_rows
        trailing_rows = sequence_rows[count_of_rows - DILATION_STEP :]
        arrived = passed_along(trailing_rows, TM, 1, n_tm)
        prior_samples = jnp.concatenate(
            [arrived, sequence_rows[: count_of_rows - DILATION_STEP]], 0
        )
        inputs = jnp.concatenate([prior_samples, sequence_rows], 1)
        in_length = (start_row + jnp.arange(count_of_rows) < seq_len).astype(jnp.float32)[:, None]
        gated, pre_grad = gate_backward(inputs, cotangent, in_length, w_conv, w_res)
        input_gradient = jnp.dot(pre_grad, w_conv.T, preferred_element_type=jnp.float32)
        term_conv = jnp.einsum("tk,tn->kn", inputs, pre_grad, preferred_element_type=jnp.float32)
        term_res = jnp.einsum("tk,tn->kn", gated, cotangent, preferred_element_type=jnp.float32)
        kc, n_conv = term_conv.shape
        kr, n_res = term_res.shape
        rc, rr = kc // n_tm, kr // n_tm
        all_tokens = count_of_rows * n_tm * n_rep
        edge_rows = input_gradient[:DILATION_STEP, :channel_count].astype(jnp.bfloat16)
        reducer = make_reducer(sizes, rc, n_conv, rr, n_res, float(all_tokens) ** (-0.5), edge_rows.shape)
        split = count_of_rows - DILATION_STEP
        head_rows = (
            cotangent[:split].astype(jnp.float32) + input_gradient[:split, channel_count:]
            + input_gradient[DILATION_STEP:, :channel_count]
        ).astype(jnp.bfloat16)
        conv_in = term_conv.astype(jnp.bfloat16).reshape(nx, nzh, nc, rc, n_conv)
        res_in = term_res.astype(jnp.bfloat16).reshape(nx, nzh, nc, rr, n_res)
        head_rows, conv_in, res_in, edge_rows = lax.optimization_barrier((head_rows, conv_in, res_in, edge_rows))
        flip_conv, flip_res, incoming_gradient = reducer(conv_in, res_in, edge_rows)
        tail_rows = (
            cotangent[split:].astype(jnp.float32) + input_gradient[split:, channel_count:]
            + incoming_gradient.astype(jnp.float32)
        ).astype(jnp.bfloat16)
        grad_rows = jnp.concatenate([head_rows, tail_rows], 0)
        return (grad_rows[None], flip_conv.T, flip_res.T)

    return body


def solution(mesh):
    n_tm, n_rep = mesh.devices.shape
    nc = 2
    nzh = 2
    nx = n_tm // (nc * nzh)
    nzl = 8
    ny = n_rep // nzl
    sizes = (nx, nzh, nc, ny, nzl)
    fine = Mesh(mesh.devices.reshape(sizes), ("x", "zh", "c", "y", "zl"))
    return jax.shard_map(
        make_body(sizes),
        mesh=fine,
        in_specs=(P(REP, TM, None), P(REP, TM, None), P(), P(), P(REP)),
        out_specs=(P(REP, TM, None), P(TM, REP), P(TM, REP)),
        check_vma=False,
    )
```
